32 devices in a mesh: parts: 2 (over y), replica: 4 (over x, core), tensor: 4 (over z).
Axes of the slice: x: 2, y: 2, z: 4, core: 2. Of those that a mesh axis runs over, the one named last changes fastest.
Arguments:
- hidden: bfloat16 [112, 2, 8192], P(('parts', 'replica'), None, 'tensor'), parts along dimension 0, may hold values from -6 to 6
- queries: bfloat16 [112, 2, 64, 128], P(('parts', 'replica'), None, 'tensor'), parts along dimension 0, may hold values from -220 to 220
- kv_cache: bfloat16 [96, 128, 8, 256], P(('parts', 'replica'), None, 'tensor'), parts along dimension 0, may hold values from -6.5 to 6.5
- w_kv: bfloat16 [8192, 8, 256], P(None, 'tensor'), may hold values from -0.0625 to 0.0625
- store_a: bfloat16 [64, 2, 64, 8192], P(('parts', 'replica'), None, None, 'tensor'), parts along dimension 0, may hold values from -0.0625 to 0.0625
- store_b: bfloat16 [64, 2, 64, 1024], P(('parts', 'replica'), None, None, 'tensor'), parts along dimension 0, may hold values from -0.75 to 0.75
- lengths: int32 [96], P('parts'), parts along dimension 0, may hold values from 2 to 128, as said below
- arrival_from: int32 [8, 2], P('parts'), parts along dimension 0, may hold values from 0 to 3, as said below
- arrival_slot: int32 [8, 2], P('parts'), parts along dimension 0, may hold values from 0 to 11, as said below
- resident_adapter: int32 [96], P('parts'), parts along dimension 0, may hold values from 0 to 7
- arrival_adapter: int32 [8, 2], P('parts'), parts along dimension 0, may hold values from 0 to 3
- hot_holder: int32 [32], P('parts'), parts along dimension 0, may hold values from 0 to 31, as said below
- hot_dest: int32 [32, 1], P('parts'), parts along dimension 0, may hold values from 0 to 3, as said below
Outputs:
- attn_out: bfloat16 [112, 2, 8192], P(('parts', 'replica'), None, 'tensor'), parts along dimension 0
- new_kv: bfloat16 [112, 2, 8, 256], P(('parts', 'replica'), None, 'tensor'), parts along dimension 0
- arrival_cache: bfloat16 [16, 128, 8, 256], P(('parts', 'replica'), None, 'tensor'), parts along dimension 0
- installed_a: bfloat16 [32, 2, 64, 8192], P(('parts', 'replica'), None, None, 'tensor'), parts along dimension 0
- installed_b: bfloat16 [32, 2, 64, 1024], P(('parts', 'replica'), None, None, 'tensor'), parts along dimension 0
The draws below stay inside these ranges and needn't reach their ends.
There are 2 independent parts, one for each index of `parts`. The reference program is written for one: setup_inputs(seed, part) draws one part's arguments, and reference() takes and returns one part's arrays. A program takes and returns all parts, laid end to end along the dimension named above; an argument that names none is the same for every part. Nothing has to cross between parts.
Inputs may be any that keep to these rules, and one draw needn't show every extreme that they name: `lengths`: every request listed by arrival_from and arrival_slot holds more than 96 rows; some request holds exactly 128. `arrival_from`: row r lists 2 distinct replicas, none equal to r; each replica appears exactly 2 times in the whole array. `arrival_slot`: no request (replica and slot) is listed twice. `hot_holder`: entry h is the holder's replica times 8 plus its slot; the holder's replica is not in row h of hot_dest; the holders of rows c * 4 to c * 4 + 3 lie on distinct replicas. `hot_dest`: for each c below 4, rows c * 4 to c * 4 + 3 together list every replica exactly once.
All inputs are finite; a program needn't handle non-finite values.
Results may differ from the reference program's by a relative error of at most 0.0071.
Values may be sent and summed in bfloat16 or wider, within the bound.
No kernel may reach another device: no remote copies, remote signals or barrier semaphores. Data moves between devices by JAX's collectives and lax.ppermute only.
A program may use at most 64 MiB of HBM per device.

```python
import math
import jax
import jax.numpy as jnp
from jax import lax

D = 8192
HEADS = 64
KEY_VALUE_HEADS = 8
HEAD_WIDTH = 128
RANK = 64
NEW_TOKEN_COUNT = 2
COPIES = 4
RES = 12
CAP = 128
ASLOT = 8
ARRIVE = 2
FAN = 1
SPANS = 4
N_REPLICA = 4


def plan_draw(key):
    key_list = jax.random.split(jax.random.fold_in(key, 7), 9)
    shuffle = jax.random.permutation(key_list[0], N_REPLICA).astype(jnp.int32)
    inverse = jnp.argsort(shuffle).astype(jnp.int32)
    offsets = (1 + jax.random.permutation(key_list[1], N_REPLICA - 1)[:ARRIVE]).astype(jnp.int32)
    sender = shuffle[(inverse[:, None] + offsets[None, :]) % N_REPLICA]
    slot_keys = jax.random.split(key_list[2], N_REPLICA)
    slot_orders = jax.vmap(lambda sub_key: jax.random.permutation(sub_key, RES))(slot_keys).astype(jnp.int32)
    top_replica = jax.random.randint(key_list[8], (), 0, N_REPLICA)
    shifted = (slot_orders - slot_orders[:, :1] + (RES - 1)) % RES
    is_top = (jnp.arange(N_REPLICA, dtype=jnp.int32) == top_replica)[:, None]
    slot_orders = jnp.where(is_top, shifted, slot_orders).astype(jnp.int32)
    arrive_ids = jnp.arange(ARRIVE, dtype=jnp.int32)
    source_slot = slot_orders[sender, arrive_ids[None, :]]
    ceilings = jax.random.randint(key_list[3], (N_REPLICA, 1), CAP // 8, CAP + 1)
    length_table = jax.random.randint(key_list[4], (N_REPLICA, RES), 2, ceilings + 1)
    long_lengths = jax.random.randint(key_list[5], (N_REPLICA, ARRIVE), 3 * CAP // 4 + 1, CAP + 1)
    length_table = length_table.at[sender, source_slot].set(long_lengths)
    chosen = jax.random.randint(key_list[6], (), 0, N_REPLICA)
    length_table = length_table.at[sender[chosen, 0], source_slot[chosen, 0]].set(CAP)
    dest_rows = []
    holder_rows = []
    for copy_id in range(COPIES):
        copy_key = jax.random.fold_in(key_list[7], copy_id)
        key_perm, key_pick, key_slot = jax.random.split(copy_key, 3)
        shuffled = jax.random.permutation(key_perm, N_REPLICA).astype(jnp.int32)
        dest_rows.append(shuffled.reshape(SPANS, FAN))
        pick_idx = jax.random.randint(key_pick, (SPANS,), 0, FAN)
        next_span = (jnp.arange(SPANS, dtype=jnp.int32) + 1) % SPANS
        holder_rep = shuffled[next_span * FAN + pick_idx]
        holder_slot = jax.random.randint(key_slot, (SPANS,), 0, ASLOT)
        holder_rows.append(holder_rep * ASLOT + holder_slot)
    hot_dest = jnp.concatenate(dest_rows, axis=0).astype(jnp.int32)
    hot_holder = jnp.concatenate(holder_rows, axis=0).astype(jnp.int32)
    return (length_table.reshape(-1).astype(jnp.int32), sender.astype(jnp.int32), source_slot.astype(jnp.int32), hot_holder, hot_dest)


def cache_draw(key):
    drawn = jax.random.truncated_normal(jax.random.fold_in(key, 21), -6.0, 6.0, (N_REPLICA * RES, CAP, KEY_VALUE_HEADS, 2 * HEAD_WIDTH), jnp.float32)
    drawn = drawn.astype(jnp.bfloat16).astype(jnp.float32)
    return drawn


def draw_kv_cache(key, part):
    return cache_draw(key).astype(jnp.bfloat16)


def draw_queries(key, part):
    request_slot_count = N_REPLICA * (RES + ARRIVE)
    drawn = jax.random.truncated_normal(jax.random.fold_in(key, 31), -6.0, 6.0, (request_slot_count, NEW_TOKEN_COUNT, HEADS, HEAD_WIDTH), jnp.float32)
    return drawn.astype(jnp.bfloat16)


def draw_lengths(key, part):
    return plan_draw(key)[0]


def draw_arrival_from(key, part):
    return plan_draw(key)[1]


def draw_arrival_slot(key, part):
    return plan_draw(key)[2]


def draw_hot_holder(key, part):
    return plan_draw(key)[3]


def draw_hot_dest(key, part):
    return plan_draw(key)[4]


def with_ends(array, stream_key, low, high):
    longest = array.shape.index(max(array.shape))
    spots = []
    for shift in (0, 1):
        where = [jax.random.randint(jax.random.fold_in(stream_key, axis), (), 0, length) for axis, length in enumerate(array.shape)]
        where[longest] = (where[longest] + shift) % array.shape[longest]
        spots.append(tuple(where))
    return array.at[spots[0]].set(low).at[spots[1]].set(high)


def levels(rng, extent, pieces, smallest, largest):
    loudness, own = 1.0, jax.random.fold_in(rng, 6)
    for axis_at, shards_of in pieces:
        heights = jnp.exp(jax.random.uniform(jax.random.fold_in(own, axis_at), (shards_of,), jnp.float32, smallest / len(pieces), largest / len(pieces)))
        loudness = loudness * jnp.repeat(heights, extent[axis_at] // shards_of).reshape([-1 if axis == axis_at else 1 for axis in range(len(extent))])
    return loudness


def noise(own_key, shape, width, limit, pieces=(), kind=jnp.bfloat16):
    result = width * jax.random.normal(own_key, shape, jnp.float32)
    if pieces:
        result = result * levels(own_key, shape, pieces, -0.22, 0.18)
    return jnp.clip(result, -limit, limit).astype(kind)


def setup_inputs(seed: int = 0, part: int = 0) -> dict:
    arg_keys = jax.random.split(jax.random.key(seed), 14)
    own_keys = jax.random.split(jax.random.fold_in(arg_keys[13], part), 14)
    hidden = noise(own_keys[0], (N_REPLICA * (RES + ARRIVE), NEW_TOKEN_COUNT, D), 1.0, 6.0, ((0, 4), (2, 4)))
    queries = draw_queries(jax.random.fold_in(jax.random.fold_in(arg_keys[13], part), 71), part)
    kv_cache = draw_kv_cache(jax.random.fold_in(jax.random.fold_in(arg_keys[13], part), 71), part)
    w_kv = noise(arg_keys[3], (D, KEY_VALUE_HEADS, 2 * HEAD_WIDTH), D ** -0.5, 0.0625, ((1, 4),))
    store_a = noise(own_keys[4], (N_REPLICA * ASLOT, 2, RANK, D), D ** -0.5, 0.0625, ((0, 4), (3, 4)))
    store_b = noise(own_keys[5], (N_REPLICA * ASLOT, 2, RANK, KEY_VALUE_HEADS * HEAD_WIDTH), RANK ** -0.5, 0.75, ((0, 4), (3, 4)))
    lengths = draw_lengths(jax.random.fold_in(jax.random.fold_in(arg_keys[13], part), 71), part)
    arrival_from = draw_arrival_from(jax.random.fold_in(jax.random.fold_in(arg_keys[13], part), 71), part)
    arrival_slot = draw_arrival_slot(jax.random.fold_in(jax.random.fold_in(arg_keys[13], part), 71), part)
    resident_adapter = with_ends(jax.random.randint(own_keys[9], (N_REPLICA * RES,), 0, ASLOT), jax.random.fold_in(own_keys[9], 1), 0, ASLOT - 1).astype(jnp.int32)
    arrival_adapter = with_ends(jax.random.randint(own_keys[10], (N_REPLICA, ARRIVE), 0, COPIES), jax.random.fold_in(own_keys[10], 1), 0, COPIES - 1).astype(jnp.int32)
    hot_holder = draw_hot_holder(jax.random.fold_in(jax.random.fold_in(arg_keys[13], part), 71), part)
    hot_dest = draw_hot_dest(jax.random.fold_in(jax.random.fold_in(arg_keys[13], part), 71), part)
    return {"hidden": hidden, "queries": queries, "kv_cache": kv_cache, "w_kv": w_kv, "store_a": store_a, "store_b": store_b, "lengths": lengths, "arrival_from": arrival_from, "arrival_slot": arrival_slot, "resident_adapter": resident_adapter, "arrival_adapter": arrival_adapter, "hot_holder": hot_holder, "hot_dest": hot_dest}


ADAPTER_SCALE = 2.0
ROPE_BASE = 500000.0

def rotate_keys(key_rows, positions):
    half_size = HEAD_WIDTH // 2
    frequency = ROPE_BASE ** (-(jnp.arange(half_size, dtype=jnp.float32) * 2.0 / HEAD_WIDTH))
    angles = positions.astype(jnp.float32)[:, :, None, None] * frequency
    cosine = jnp.cos(angles)
    sine_val = jnp.sin(angles)
    first_half = key_rows[..., :half_size]
    second_half = key_rows[..., half_size:]
    return jnp.concatenate([first_half * cosine - second_half * sine_val, second_half * cosine + first_half * sine_val], axis=-1)

def attend(queries, stored, lengths_now, fresh_kv):
    request_slot_count = queries.shape[0]
    group_size = HEADS // KEY_VALUE_HEADS
    grouped = queries.astype(jnp.float32).reshape(request_slot_count, NEW_TOKEN_COUNT, KEY_VALUE_HEADS, group_size, HEAD_WIDTH)
    score_scale = 1.0 / math.sqrt(HEAD_WIDTH)
    past_scores = jnp.einsum('msgjd,mcgd->msgjc', grouped, stored[..., :HEAD_WIDTH].astype(jnp.float32)) * score_scale
    recent_scores = jnp.einsum('msgjd,mtgd->msgjt', grouped, fresh_kv[..., :HEAD_WIDTH].astype(jnp.float32)) * score_scale
    row_ids = jnp.arange(CAP, dtype=jnp.int32)
    past_ok = (row_ids[None, :] < lengths_now[:, None])[:, None, None, None, :]
    step_ids = jnp.arange(NEW_TOKEN_COUNT, dtype=jnp.int32)
    recent_ok = (step_ids[None, :] <= step_ids[:, None])[None, :, None, None, :]
    past_scores = jnp.where(past_ok, past_scores, -jnp.inf)
    recent_scores = jnp.where(recent_ok, recent_scores, -jnp.inf)
    peak_score = jnp.maximum(lax.optimization_barrier(jnp.max(past_scores, -1)), lax.optimization_barrier(jnp.max(recent_scores, -1)))[..., None]
    past_exp = jnp.exp(past_scores - peak_score)
    recent_exp = jnp.exp(recent_scores - peak_score)
    denom_sum = lax.optimization_barrier(jnp.sum(past_exp, -1, keepdims=True)) + lax.optimization_barrier(jnp.sum(recent_exp, -1, keepdims=True))
    past_w = (past_exp / denom_sum).astype(jnp.bfloat16).astype(jnp.float32)
    recent_w = (recent_exp / denom_sum).astype(jnp.bfloat16).astype(jnp.float32)
    mixed_out = jnp.einsum('msgjc,mcgd->msgjd', past_w, stored[..., HEAD_WIDTH:].astype(jnp.float32))
    mixed_out = mixed_out + jnp.einsum('msgjt,mtgd->msgjd', recent_w, fresh_kv[..., HEAD_WIDTH:].astype(jnp.float32))
    return mixed_out.reshape(request_slot_count, NEW_TOKEN_COUNT, HEADS * HEAD_WIDTH)

def reference(hidden, queries, kv_cache, w_kv, store_a, store_b, lengths, arrival_from, arrival_slot, resident_adapter, arrival_adapter, hot_holder, hot_dest):
    request_slot_count = RES + ARRIVE
    leaving_ids = (arrival_from * RES + arrival_slot).reshape(-1)
    blocks = hot_dest.reshape(COPIES, SPANS, FAN)
    weight_f32 = w_kv.astype(jnp.float32)

    def one_replica(replica):
        own_ids = replica * RES + jnp.arange(RES, dtype=jnp.int32)
        moved_ids = arrival_from[replica] * RES + arrival_slot[replica]
        source_ids = jnp.concatenate([own_ids, moved_ids]).astype(jnp.int32)
        staying = jnp.logical_not(jnp.any(own_ids[:, None] == leaving_ids[None, :], axis=1))
        live_mask = jnp.concatenate([staying, jnp.ones((ARRIVE,), bool)])
        seen_len = lengths[source_ids]
        listed = jnp.any(blocks == replica, axis=2).astype(jnp.int32)
        wanted = jnp.arange(COPIES, dtype=jnp.int32) * SPANS + lax.optimization_barrier(jnp.sum(listed * jnp.arange(SPANS, dtype=jnp.int32)[None, :], axis=1))
        inst_a = store_a[hot_holder[wanted]]
        inst_b = store_b[hot_holder[wanted]]
        own_adapter = lax.dynamic_slice_in_dim(resident_adapter, replica * RES, RES)
        my_choice = arrival_adapter[replica]
        adapt_a = jnp.concatenate([store_a[replica * ASLOT + own_adapter], inst_a[my_choice]])
        adapter_up_weight = jnp.concatenate([store_b[replica * ASLOT + own_adapter], inst_b[my_choice]])
        hidden_f32 = lax.dynamic_slice_in_dim(hidden, replica * request_slot_count, request_slot_count).astype(jnp.float32)
        query_rows = lax.dynamic_slice_in_dim(queries, replica * request_slot_count, request_slot_count)
        base_projection = jnp.einsum('msd,dgc->msgc', hidden_f32, weight_f32)
        down_projected = jnp.einsum('msd,mpkd->mspk', hidden_f32, adapt_a.astype(jnp.float32)).astype(jnp.bfloat16)
        adapter_update = jnp.einsum('gnot,gote->gnoe', down_projected.astype(jnp.float32), adapter_up_weight.astype(jnp.float32))
        adapter_update = adapter_update.reshape(request_slot_count, NEW_TOKEN_COUNT, 2, KEY_VALUE_HEADS, HEAD_WIDTH).transpose(0, 1, 3, 2, 4).reshape(request_slot_count, NEW_TOKEN_COUNT, KEY_VALUE_HEADS, 2 * HEAD_WIDTH)
        unrotated_key_value = base_projection + ADAPTER_SCALE * adapter_update
        positions = seen_len[:, None] + jnp.arange(NEW_TOKEN_COUNT, dtype=jnp.int32)[None, :]
        fresh_kv = jnp.concatenate([rotate_keys(unrotated_key_value[..., :HEAD_WIDTH], positions), unrotated_key_value[..., HEAD_WIDTH:]], axis=-1).astype(jnp.bfloat16)
        stored = kv_cache[source_ids]
        row_ids = jnp.arange(CAP, dtype=jnp.int32)
        arrived = jnp.where((row_ids[None, :] < seen_len[RES:, None])[:, :, None, None], stored[RES:], jnp.zeros((), jnp.bfloat16))
        mixed_out = attend(query_rows, stored, seen_len, fresh_kv)
        attn_rows = jnp.where(live_mask[:, None, None], mixed_out, 0.0).astype(jnp.bfloat16)
        fresh_rows = jnp.where(live_mask[:, None, None, None], fresh_kv, jnp.zeros((), jnp.bfloat16))
        return (attn_rows, fresh_rows, arrived, inst_a, inst_b)
    attn_all, fresh_all, arrived_all, inst_a_all, inst_b_all = lax.map(one_replica, jnp.arange(N_REPLICA, dtype=jnp.int32))
    return (attn_all.reshape(N_REPLICA * request_slot_count, NEW_TOKEN_COUNT, HEADS * HEAD_WIDTH), fresh_all.reshape(N_REPLICA * request_slot_count, NEW_TOKEN_COUNT, KEY_VALUE_HEADS, 2 * HEAD_WIDTH), arrived_all.reshape(N_REPLICA * ARRIVE, CAP, KEY_VALUE_HEADS, 2 * HEAD_WIDTH), inst_a_all.reshape(N_REPLICA * COPIES, 2, RANK, D), inst_b_all.reshape(N_REPLICA * COPIES, 2, RANK, KEY_VALUE_HEADS * HEAD_WIDTH))
```

```python
import functools
import math

import jax
import jax.numpy as jnp
from jax import lax
from jax.experimental import pallas as pl
from jax.experimental.pallas import tpu as pltpu
from jax.sharding import PartitionSpec as P

COPIES = 4


ADAPTER_SCALE = 2.0
ROPE_BASE = 500000.0


def rotate_keys(key_rows, positions):
    head_length = key_rows.shape[-1]
    half_size = head_length // 2
    frequency = ROPE_BASE ** (-(jnp.arange(half_size, dtype=jnp.float32) * 2.0 / head_length))
    angles = positions.astype(jnp.float32)[:, :, None, None] * frequency
    cosine = jnp.cos(angles)
    sine_val = jnp.sin(angles)
    first_half = key_rows[..., :half_size]
    second_half = key_rows[..., half_size:]
    return jnp.concatenate(
        [
            first_half * cosine - second_half * sine_val,
            second_half * cosine + first_half * sine_val,
        ],
        axis=-1,
    )


def attend(queries, stored, lengths_now, fresh_kv):
    request_slot_count, decode_step_count, heads_local, head_length = queries.shape
    local_key_value = stored.shape[2]
    group_size = heads_local // local_key_value
    grouped = queries.reshape(
        request_slot_count, decode_step_count, local_key_value, group_size, head_length
    )
    score_scale = 1.0 / math.sqrt(head_length)
    past_scores = (
        jnp.einsum(
            "msgjd,mcgd->msgjc",
            grouped,
            stored[..., :head_length],
            preferred_element_type=jnp.float32,
        )
        * score_scale
    )
    recent_scores = (
        jnp.einsum(
            "msgjd,mtgd->msgjt",
            grouped,
            fresh_kv[..., :head_length],
            preferred_element_type=jnp.float32,
        )
        * score_scale
    )
    row_ids = jnp.arange(stored.shape[1], dtype=jnp.int32)
    past_ok = (row_ids[None, :] < lengths_now[:, None])[:, None, None, None, :]
    step_ids = jnp.arange(decode_step_count, dtype=jnp.int32)
    recent_ok = (step_ids[None, :] <= step_ids[:, None])[None, :, None, None, :]
    past_scores = jnp.where(past_ok, past_scores, -jnp.inf)
    recent_scores = jnp.where(recent_ok, recent_scores, -jnp.inf)
    peak_score = jnp.maximum(jnp.max(past_scores, -1), jnp.max(recent_scores, -1))[..., None]
    past_exp = jnp.exp(past_scores - peak_score)
    recent_exp = jnp.exp(recent_scores - peak_score)
    denom_sum = jnp.sum(past_exp, -1, keepdims=True) + jnp.sum(recent_exp, -1, keepdims=True)
    past_w = (past_exp / denom_sum).astype(jnp.bfloat16)
    recent_w = (recent_exp / denom_sum).astype(jnp.bfloat16)
    mixed_out = jnp.einsum(
        "msgjc,mcgd->msgjd", past_w, stored[..., head_length:], preferred_element_type=jnp.float32
    )
    mixed_out = mixed_out + jnp.einsum(
        "msgjt,mtgd->msgjd",
        recent_w,
        fresh_kv[..., head_length:],
        preferred_element_type=jnp.float32,
    )
    return mixed_out.reshape(request_slot_count, decode_step_count, heads_local * head_length)


def local_general(
    hidden,
    queries,
    kv_cache,
    w_kv,
    store_a,
    store_b,
    lengths,
    arrival_from,
    arrival_slot,
    resident_adapter,
    arrival_adapter,
    hot_holder,
    hot_dest,
):
    my_index = lax.axis_index("replica")
    replicas = lax.axis_size("replica")
    resident = kv_cache.shape[0]
    arrive = arrival_from.shape[1]
    request_slot_count = resident + arrive
    decode_step_count = hidden.shape[1]
    head_length = queries.shape[3]
    local_key_value = kv_cache.shape[2]
    slot_total = store_a.shape[0]
    hot_total = hot_holder.shape[0]
    spans = hot_total // COPIES
    my_from = lax.dynamic_index_in_dim(arrival_from, my_index, 0, keepdims=False)
    my_slot = lax.dynamic_index_in_dim(arrival_slot, my_index, 0, keepdims=False)
    own_ids = my_index * resident + jnp.arange(resident, dtype=jnp.int32)
    leaving_ids = (arrival_from * resident + arrival_slot).reshape(-1)
    staying = jnp.logical_not(jnp.any(own_ids[:, None] == leaving_ids[None, :], axis=1))
    live_mask = jnp.concatenate([staying, jnp.ones((arrive,), bool)])
    own_len = lax.dynamic_slice_in_dim(lengths, my_index * resident, resident)
    arrival_len = jnp.take(lengths, my_from * resident + my_slot)
    seen_len = jnp.concatenate([own_len, arrival_len])
    takes_mine = arrival_from == my_index
    sends_any = jnp.any(takes_mine, axis=1)
    send_slot = jnp.sum(jnp.where(takes_mine, arrival_slot, 0), axis=1)
    outgoing = jnp.take(kv_cache, send_slot, axis=0)
    outgoing = jnp.where(sends_any[:, None, None, None], outgoing, jnp.zeros((), jnp.bfloat16))
    incoming = lax.all_to_all(outgoing, "replica", split_axis=0, concat_axis=0, tiled=True)
    blocks = hot_dest.reshape(COPIES, spans, hot_dest.shape[1])
    holder_grid = hot_holder.reshape(COPIES, spans)
    holder_rep = holder_grid // slot_total
    mine = holder_rep == my_index
    has_one = jnp.any(mine, axis=1)
    local_pick = jnp.sum(jnp.where(mine, holder_grid % slot_total, 0), axis=1)

    def spread_rows(store):
        rows = jnp.take(store, local_pick, axis=0)
        rows = jnp.where(has_one[:, None, None, None], rows, jnp.zeros((), jnp.bfloat16))
        return rows.reshape(COPIES, replicas, -1).transpose(1, 0, 2)

    got_a, got_b = (
        lax.all_to_all(spread_rows(store_a), "replica", split_axis=0, concat_axis=0, tiled=True),
        lax.all_to_all(spread_rows(store_b), "replica", split_axis=0, concat_axis=0, tiled=True),
    )
    replica_ids = jnp.arange(replicas, dtype=jnp.int32)
    member = jnp.any(blocks[:, :, :, None] == replica_ids[None, None, None, :], axis=2).astype(
        jnp.int32
    )
    source_rep = jnp.sum(member * holder_rep[:, :, None], axis=1)
    copy_ids = jnp.arange(COPIES, dtype=jnp.int32)
    route_a = got_a[source_rep.T, copy_ids[None, :]]
    route_b = got_b[source_rep.T, copy_ids[None, :]]
    recv_a, recv_b = (
        lax.all_to_all(route_a, "replica", split_axis=0, concat_axis=0, tiled=True),
        lax.all_to_all(route_b, "replica", split_axis=0, concat_axis=0, tiled=True),
    )
    installed_a = recv_a.transpose(1, 0, 2).reshape((COPIES,) + store_a.shape[1:])
    installed_b = recv_b.transpose(1, 0, 2).reshape((COPIES,) + store_b.shape[1:])
    own_adapter = lax.dynamic_slice_in_dim(resident_adapter, my_index * resident, resident)
    my_choice = lax.dynamic_index_in_dim(arrival_adapter, my_index, 0, keepdims=False)
    adapt_a = jnp.concatenate(
        [jnp.take(store_a, own_adapter, axis=0), jnp.take(installed_a, my_choice, axis=0)]
    )
    adapter_up_weight = jnp.concatenate(
        [jnp.take(store_b, own_adapter, axis=0), jnp.take(installed_b, my_choice, axis=0)]
    )
    partial_value = jnp.einsum(
        "msd,mpkd->mspk", hidden, adapt_a, preferred_element_type=jnp.float32
    )
    base_projection = jnp.einsum(
        "msd,dgc->msgc",
        lax.all_gather(hidden, "tensor", axis=2, tiled=True),
        w_kv,
        preferred_element_type=jnp.float32,
    )
    down_projected = lax.psum(partial_value, "tensor")
    down_projected = down_projected.astype(jnp.bfloat16)
    adapter_update = jnp.einsum(
        "gnot,gote->gnoe", down_projected, adapter_up_weight, preferred_element_type=jnp.float32
    )
    adapter_update = (
        adapter_update.reshape(
            request_slot_count, decode_step_count, 2, local_key_value, head_length
        )
        .transpose(0, 1, 3, 2, 4)
        .reshape(request_slot_count, decode_step_count, local_key_value, 2 * head_length)
    )
    unrotated_key_value = base_projection + ADAPTER_SCALE * adapter_update
    positions = seen_len[:, None] + jnp.arange(decode_step_count, dtype=jnp.int32)[None, :]
    fresh_kv = jnp.concatenate(
        [
            rotate_keys(unrotated_key_value[..., :head_length], positions),
            unrotated_key_value[..., head_length:],
        ],
        axis=-1,
    ).astype(jnp.bfloat16)
    stay_out = attend(queries[:resident], kv_cache, own_len, fresh_kv[:resident])
    arrived = jnp.take(incoming, my_from, axis=0)
    row_ids = jnp.arange(kv_cache.shape[1], dtype=jnp.int32)
    arrived = jnp.where(
        (row_ids[None, :] < arrival_len[:, None])[:, :, None, None],
        arrived,
        jnp.zeros((), jnp.bfloat16),
    )
    move_out = attend(queries[resident:], arrived, arrival_len, fresh_kv[resident:])
    mixed_out = jnp.concatenate([stay_out, move_out], axis=0)
    attn_out = jnp.where(live_mask[:, None, None], mixed_out, 0.0).astype(jnp.bfloat16)
    new_kv = jnp.where(live_mask[:, None, None, None], fresh_kv, jnp.zeros((), jnp.bfloat16))
    return (attn_out, new_kv, arrived, installed_a, installed_b)


def partner(array, mask):
    return lax.ppermute(array, "replica", [(i, i ^ mask) for i in range(lax.axis_size("replica"))])


def shifted(array, step):
    size = lax.axis_size("tensor")
    return lax.ppermute(array, "tensor", [(i, (i + step) % size) for i in range(size)])


def pick_kernel(count, flags, first, second, out, sem):
    for i in range(count):

        @pl.when(flags[i] != 0)
        def _():
            pltpu.make_async_copy(first.at[i], out.at[i], sem.at[0]).start()

        @pl.when(flags[i] == 0)
        def _():
            pltpu.make_async_copy(second.at[i], out.at[i], sem.at[0]).start()

    pltpu.make_async_copy(first, out, sem.at[0]).wait()


def pick(flags, first, second):
    count = first.shape[0]
    return pl.pallas_call(
        functools.partial(pick_kernel, count),
        out_shape=jax.ShapeDtypeStruct(first.shape, first.dtype),
        grid_spec=pltpu.PrefetchScalarGridSpec(
            num_scalar_prefetch=1,
            in_specs=[pl.BlockSpec(memory_space=pl.ANY)] * 2,
            out_specs=pl.BlockSpec(memory_space=pl.ANY),
            scratch_shapes=[pltpu.SemaphoreType.DMA((1,))],
        ),
        name="pick",
    )(flags.astype(jnp.int32), first, second)


def rows_kernel(count, rows, table, out, sem):
    for i in range(count):
        pltpu.make_async_copy(table.at[rows[i]], out.at[i], sem.at[0]).start()
    pltpu.make_async_copy(out, out, sem.at[0]).wait()


def take_rows(table, rows):
    count = rows.shape[0]
    return pl.pallas_call(
        functools.partial(rows_kernel, count),
        out_shape=jax.ShapeDtypeStruct((count,) + table.shape[1:], table.dtype),
        grid_spec=pltpu.PrefetchScalarGridSpec(
            num_scalar_prefetch=1,
            in_specs=[pl.BlockSpec(memory_space=pl.ANY)],
            out_specs=pl.BlockSpec(memory_space=pl.ANY),
            scratch_shapes=[pltpu.SemaphoreType.DMA((1,))],
        ),
        name="take_rows",
    )(rows.astype(jnp.int32), table)


def local_pairs(
    hidden,
    queries,
    kv_cache,
    w_kv,
    store_a,
    store_b,
    lengths,
    arrival_from,
    arrival_slot,
    resident_adapter,
    arrival_adapter,
    hot_holder,
    hot_dest,
):
    me = lax.axis_index("replica")
    replicas = lax.axis_size("replica")
    shards = lax.axis_size("tensor")
    shard = lax.axis_index("tensor")
    resident = kv_cache.shape[0]
    arrive = arrival_from.shape[1]
    slots = resident + arrive
    steps = hidden.shape[1]
    features = hidden.shape[2]
    head_length = queries.shape[3]
    kv_heads = kv_cache.shape[2]
    slot_total = store_a.shape[0]
    rank = store_a.shape[2]
    spans = hot_holder.shape[0] // COPIES
    columns = store_b.shape[3]

    my_from = lax.dynamic_index_in_dim(arrival_from, me, 0, keepdims=False)
    my_slot = lax.dynamic_index_in_dim(arrival_slot, me, 0, keepdims=False)
    own_ids = me * resident + jnp.arange(resident, dtype=jnp.int32)
    leaving_ids = (arrival_from * resident + arrival_slot).reshape(-1)
    staying = jnp.logical_not(jnp.any(own_ids[:, None] == leaving_ids[None, :], axis=1))
    live_mask = jnp.concatenate([staying, jnp.ones((arrive,), bool)])
    own_len = lax.dynamic_slice_in_dim(lengths, me * resident, resident)
    arrival_len = jnp.take(lengths, my_from * resident + my_slot)
    seen_len = jnp.concatenate([own_len, arrival_len])
    takes_mine = arrival_from == me
    send_slot = jnp.sum(jnp.where(takes_mine, arrival_slot, 0), axis=1)
    holder_grid = hot_holder.reshape(COPIES, spans)
    holder_rep = holder_grid // slot_total
    held = jnp.sum(jnp.where(holder_rep == me, holder_grid % slot_total, 0), axis=1)
    dest = hot_dest.reshape(COPIES, spans)
    replica_ids = jnp.arange(replicas, dtype=jnp.int32)
    wants = dest[None, :, :] == replica_ids[:, None, None]
    holder_of = jnp.sum(jnp.where(wants, holder_rep[None], 0), axis=2)
    slot_of = jnp.sum(jnp.where(wants, (holder_grid % slot_total)[None], 0), axis=2)
    my_holder = lax.dynamic_index_in_dim(holder_of, me, 0, keepdims=False)
    across_holder = lax.dynamic_index_in_dim(holder_of, me ^ 2, 0, keepdims=False)
    from_mine = across_holder == me
    from_sibling = my_holder == (me ^ 1)

    masks = tuple(range(1, replicas))
    out_rows = jnp.stack([send_slot[me ^ mask] for mask in masks])
    leaving = take_rows(kv_cache, out_rows)
    came = jnp.stack([partner(leaving[i], mask) for i, mask in enumerate(masks)])

    arrival_hidden = hidden[resident:].reshape(arrive * steps, features)
    other_hidden = [arrival_hidden] + [partner(arrival_hidden, mask) for mask in masks]
    around = [hidden.reshape(slots * steps, features)]
    around += [shifted(around[0], step) for step in range(1, shards)]

    rows_b = take_rows(store_b, held)
    sibling_b = partner(rows_b, 1)
    across_b = partner(pick(from_mine, rows_b, sibling_b), 2)
    installed_b = pick(from_sibling, sibling_b, across_b)
    rows_a = take_rows(store_a, held)
    sibling_a = partner(rows_a, 1)
    across_a = partner(pick(from_mine, rows_a, sibling_a), 2)
    installed_a = pick(from_sibling, sibling_a, across_a)

    own_adapter = lax.dynamic_slice_in_dim(resident_adapter, me * resident, resident)
    row_count = resident * steps
    left = jnp.concatenate([hidden[:resident].reshape(row_count, features)] + other_hidden)
    products = jnp.einsum(
        "md,ard->mar",
        left,
        store_a.reshape(slot_total, 2 * rank, features),
        preferred_element_type=jnp.float32,
    )
    order = jnp.stack([me ^ mask for mask in (0,) + masks])
    chosen = jnp.take(arrival_adapter, order, axis=0)
    hot_rep = jnp.take_along_axis(jnp.take(holder_of, order, axis=0), chosen, axis=1)
    hot_slot = jnp.take_along_axis(jnp.take(slot_of, order, axis=0), chosen, axis=1)
    arrival_pick = jnp.where(hot_rep == me, hot_slot, -1).reshape(-1)
    row_pick = jnp.repeat(jnp.concatenate([own_adapter, arrival_pick]), steps)
    slot_ids = jnp.arange(slot_total, dtype=jnp.int32)
    partial = jnp.sum(
        jnp.where(row_pick[:, None, None] == slot_ids[None, :, None], products, 0.0), axis=1
    )
    total = partial
    for step in range(1, shards):
        total = total + shifted(partial, step)
    arrival_total = total[row_count:].reshape(replicas, arrive * steps, 2 * rank)
    mine_total = arrival_total[0]
    for i, mask in enumerate(masks):
        mine_total = mine_total + partner(arrival_total[i + 1], mask)
    down = jnp.concatenate([total[:row_count], mine_total]).astype(jnp.bfloat16)
    down = down.reshape(slots, steps, 2, rank)

    doubled = jnp.stack(around[::-1] + around[::-1][:-1])
    full = lax.dynamic_slice_in_dim(doubled, shards - 1 - shard, shards, axis=0)
    full = full.transpose(1, 0, 2).reshape(slots, steps, shards * features)
    base = jnp.einsum("msd,dgc->msgc", full, w_kv, preferred_element_type=jnp.float32)

    my_choice = lax.dynamic_index_in_dim(arrival_adapter, me, 0, keepdims=False)
    up = jnp.concatenate(
        [jnp.take(store_b, own_adapter, axis=0), jnp.take(installed_b, my_choice, axis=0)]
    )
    update = jnp.einsum("gnot,gote->gnoe", down, up, preferred_element_type=jnp.float32)
    update = (
        update.reshape(slots, steps, 2, kv_heads, head_length)
        .transpose(0, 1, 3, 2, 4)
        .reshape(slots, steps, kv_heads, 2 * head_length)
    )
    raw = base + ADAPTER_SCALE * update
    positions = seen_len[:, None] + jnp.arange(steps, dtype=jnp.int32)[None, :]
    fresh_kv = jnp.concatenate(
        [rotate_keys(raw[..., :head_length], positions), raw[..., head_length:]], axis=-1
    ).astype(jnp.bfloat16)

    stay_out = attend(queries[:resident], kv_cache, own_len, fresh_kv[:resident])
    arrived = jnp.take(came, (my_from ^ me) - 1, axis=0)
    row_ids = jnp.arange(kv_cache.shape[1], dtype=jnp.int32)
    arrived = jnp.where(
        (row_ids[None, :] < arrival_len[:, None])[:, :, None, None],
        arrived,
        jnp.zeros((), jnp.bfloat16),
    )
    move_out = attend(queries[resident:], arrived, arrival_len, fresh_kv[resident:])
    mixed_out = jnp.concatenate([stay_out, move_out], axis=0)
    attn_out = jnp.where(live_mask[:, None, None], mixed_out, 0.0).astype(jnp.bfloat16)
    new_kv = jnp.where(live_mask[:, None, None, None], fresh_kv, jnp.zeros((), jnp.bfloat16))
    return (attn_out, new_kv, arrived, installed_a, installed_b)


def local(*args):
    fan = args[-1].shape[1]
    if lax.axis_size("replica") == 4 and fan == 1:
        return local_pairs(*args)
    return local_general(*args)


def solution(mesh):
    in_specs = (
        P(("parts", "replica"), None, "tensor"),
        P(("parts", "replica"), None, "tensor", None),
        P(("parts", "replica"), None, "tensor", None),
        P(None, "tensor", None),
        P(("parts", "replica"), None, None, "tensor"),
        P(("parts", "replica"), None, None, "tensor"),
        P("parts"),
        P("parts", None),
        P("parts", None),
        P("parts"),
        P("parts", None),
        P("parts"),
        P("parts", None),
    )
    out_specs = (
        P(("parts", "replica"), None, "tensor"),
        P(("parts", "replica"), None, "tensor", None),
        P(("parts", "replica"), None, "tensor", None),
        P(("parts", "replica"), None, None, "tensor"),
        P(("parts", "replica"), None, None, "tensor"),
    )
    return jax.shard_map(local, mesh=mesh, in_specs=in_specs, out_specs=out_specs, check_vma=False)
```

```python
import functools
import math

import jax
import jax.numpy as jnp
from jax import lax
from jax.experimental import pallas as pl
from jax.experimental.pallas import tpu as pltpu
from jax.sharding import PartitionSpec as P

COPIES = 4


ADAPTER_SCALE = 2.0
ROPE_BASE = 500000.0


def rotate_keys(key_rows, positions):
    head_length = key_rows.shape[-1]
    half_size = head_length // 2
    frequency = ROPE_BASE ** (-(jnp.arange(half_size, dtype=jnp.float32) * 2.0 / head_length))
    angles = positions.astype(jnp.float32)[:, :, None, None] * frequency
    cosine = jnp.cos(angles)
    sine_val = jnp.sin(angles)
    first_half = key_rows[..., :half_size]
    second_half = key_rows[..., half_size:]
    return jnp.concatenate(
        [
            first_half * cosine - second_half * sine_val,
            second_half * cosine + first_half * sine_val,
        ],
        axis=-1,
    )


def attend(queries, stored, lengths_now, fresh_kv):
    request_slot_count, decode_step_count, heads_local, head_length = queries.shape
    local_key_value = stored.shape[2]
    group_size = heads_local // local_key_value
    grouped = queries.reshape(
        request_slot_count, decode_step_count, local_key_value, group_size, head_length
    )
    score_scale = 1.0 / math.sqrt(head_length)
    past_scores = (
        jnp.einsum(
            "msgjd,mcgd->msgjc",
            grouped,
            stored[..., :head_length],
            preferred_element_type=jnp.float32,
        )
        * score_scale
    )
    recent_scores = (
        jnp.einsum(
            "msgjd,mtgd->msgjt",
            grouped,
            fresh_kv[..., :head_length],
            preferred_element_type=jnp.float32,
        )
        * score_scale
    )
    row_ids = jnp.arange(stored.shape[1], dtype=jnp.int32)
    past_ok = (row_ids[None, :] < lengths_now[:, None])[:, None, None, None, :]
    step_ids = jnp.arange(decode_step_count, dtype=jnp.int32)
    recent_ok = (step_ids[None, :] <= step_ids[:, None])[None, :, None, None, :]
    past_scores = jnp.where(past_ok, past_scores, -jnp.inf)
    recent_scores = jnp.where(recent_ok, recent_scores, -jnp.inf)
    peak_score = jnp.maximum(jnp.max(past_scores, -1), jnp.max(recent_scores, -1))[..., None]
    past_exp = jnp.exp(past_scores - peak_score)
    recent_exp = jnp.exp(recent_scores - peak_score)
    denom_sum = jnp.sum(past_exp, -1, keepdims=True) + jnp.sum(recent_exp, -1, keepdims=True)
    past_w = (past_exp / denom_sum).astype(jnp.bfloat16)
    recent_w = (recent_exp / denom_sum).astype(jnp.bfloat16)
    mixed_out = jnp.einsum(
        "msgjc,mcgd->msgjd", past_w, stored[..., head_length:], preferred_element_type=jnp.float32
    )
    mixed_out = mixed_out + jnp.einsum(
        "msgjt,mtgd->msgjd",
        recent_w,
        fresh_kv[..., head_length:],
        preferred_element_type=jnp.float32,
    )
    return mixed_out.reshape(request_slot_count, decode_step_count, heads_local * head_length)


def local_general(
    hidden,
    queries,
    kv_cache,
    w_kv,
    store_a,
    store_b,
    lengths,
    arrival_from,
    arrival_slot,
    resident_adapter,
    arrival_adapter,
    hot_holder,
    hot_dest,
):
    my_index = lax.axis_index("replica")
    replicas = lax.axis_size("replica")
    resident = kv_cache.shape[0]
    arrive = arrival_from.shape[1]
    request_slot_count = resident + arrive
    decode_step_count = hidden.shape[1]
    head_length = queries.shape[3]
    local_key_value = kv_cache.shape[2]
    slot_total = store_a.shape[0]
    hot_total = hot_holder.shape[0]
    spans = hot_total // COPIES
    my_from = lax.dynamic_index_in_dim(arrival_from, my_index, 0, keepdims=False)
    my_slot = lax.dynamic_index_in_dim(arrival_slot, my_index, 0, keepdims=False)
    own_ids = my_index * resident + jnp.arange(resident, dtype=jnp.int32)
    leaving_ids = (arrival_from * resident + arrival_slot).reshape(-1)
    staying = jnp.logical_not(jnp.any(own_ids[:, None] == leaving_ids[None, :], axis=1))
    live_mask = jnp.concatenate([staying, jnp.ones((arrive,), bool)])
    own_len = lax.dynamic_slice_in_dim(lengths, my_index * resident, resident)
    arrival_len = jnp.take(lengths, my_from * resident + my_slot)
    seen_len = jnp.concatenate([own_len, arrival_len])
    takes_mine = arrival_from == my_index
    sends_any = jnp.any(takes_mine, axis=1)
    send_slot = jnp.sum(jnp.where(takes_mine, arrival_slot, 0), axis=1)
    outgoing = jnp.take(kv_cache, send_slot, axis=0)
    outgoing = jnp.where(sends_any[:, None, None, None], outgoing, jnp.zeros((), jnp.bfloat16))
    incoming = lax.all_to_all(outgoing, "replica", split_axis=0, concat_axis=0, tiled=True)
    blocks = hot_dest.reshape(COPIES, spans, hot_dest.shape[1])
    holder_grid = hot_holder.reshape(COPIES, spans)
    holder_rep = holder_grid // slot_total
    mine = holder_rep == my_index
    has_one = jnp.any(mine, axis=1)
    local_pick = jnp.sum(jnp.where(mine, holder_grid % slot_total, 0), axis=1)

    def spread_rows(store):
        rows = jnp.take(store, local_pick, axis=0)
        rows = jnp.where(has_one[:, None, None, None], rows, jnp.zeros((), jnp.bfloat16))
        return rows.reshape(COPIES, replicas, -1).transpose(1, 0, 2)

    got_a, got_b = (
        lax.all_to_all(spread_rows(store_a), "replica", split_axis=0, concat_axis=0, tiled=True),
        lax.all_to_all(spread_rows(store_b), "replica", split_axis=0, concat_axis=0, tiled=True),
    )
    replica_ids = jnp.arange(replicas, dtype=jnp.int32)
    member = jnp.any(blocks[:, :, :, None] == replica_ids[None, None, None, :], axis=2).astype(
        jnp.int32
    )
    source_rep = jnp.sum(member * holder_rep[:, :, None], axis=1)
    copy_ids = jnp.arange(COPIES, dtype=jnp.int32)
    route_a = got_a[source_rep.T, copy_ids[None, :]]
    route_b = got_b[source_rep.T, copy_ids[None, :]]
    recv_a, recv_b = (
        lax.all_to_all(route_a, "replica", split_axis=0, concat_axis=0, tiled=True),
        lax.all_to_all(route_b, "replica", split_axis=0, concat_axis=0, tiled=True),
    )
    installed_a = recv_a.transpose(1, 0, 2).reshape((COPIES,) + store_a.shape[1:])
    installed_b = recv_b.transpose(1, 0, 2).reshape((COPIES,) + store_b.shape[1:])
    own_adapter = lax.dynamic_slice_in_dim(resident_adapter, my_index * resident, resident)
    my_choice = lax.dynamic_index_in_dim(arrival_adapter, my_index, 0, keepdims=False)
    adapt_a = jnp.concatenate(
        [jnp.take(store_a, own_adapter, axis=0), jnp.take(installed_a, my_choice, axis=0)]
    )
    adapter_up_weight = jnp.concatenate(
        [jnp.take(store_b, own_adapter, axis=0), jnp.take(installed_b, my_choice, axis=0)]
    )
    partial_value = jnp.einsum(
        "msd,mpkd->mspk", hidden, adapt_a, preferred_element_type=jnp.float32
    )
    base_projection = jnp.einsum(
        "msd,dgc->msgc",
        lax.all_gather(hidden, "tensor", axis=2, tiled=True),
        w_kv,
        preferred_element_type=jnp.float32,
    )
    down_projected = lax.psum(partial_value, "tensor")
    down_projected = down_projected.astype(jnp.bfloat16)
    adapter_update = jnp.einsum(
        "gnot,gote->gnoe", down_projected, adapter_up_weight, preferred_element_type=jnp.float32
    )
    adapter_update = (
        adapter_update.reshape(
            request_slot_count, decode_step_count, 2, local_key_value, head_length
        )
        .transpose(0, 1, 3, 2, 4)
        .reshape(request_slot_count, decode_step_count, local_key_value, 2 * head_length)
    )
    unrotated_key_value = base_projection + ADAPTER_SCALE * adapter_update
    positions = seen_len[:, None] + jnp.arange(decode_step_count, dtype=jnp.int32)[None, :]
    fresh_kv = jnp.concatenate(
        [
            rotate_keys(unrotated_key_value[..., :head_length], positions),
            unrotated_key_value[..., head_length:],
        ],
        axis=-1,
    ).astype(jnp.bfloat16)
    stay_out = attend(queries[:resident], kv_cache, own_len, fresh_kv[:resident])
    arrived = jnp.take(incoming, my_from, axis=0)
    row_ids = jnp.arange(kv_cache.shape[1], dtype=jnp.int32)
    arrived = jnp.where(
        (row_ids[None, :] < arrival_len[:, None])[:, :, None, None],
        arrived,
        jnp.zeros((), jnp.bfloat16),
    )
    move_out = attend(queries[resident:], arrived, arrival_len, fresh_kv[resident:])
    mixed_out = jnp.concatenate([stay_out, move_out], axis=0)
    attn_out = jnp.where(live_mask[:, None, None], mixed_out, 0.0).astype(jnp.bfloat16)
    new_kv = jnp.where(live_mask[:, None, None, None], fresh_kv, jnp.zeros((), jnp.bfloat16))
    return (attn_out, new_kv, arrived, installed_a, installed_b)


def partner(array, mask):
    return lax.ppermute(array, "replica", [(i, i ^ mask) for i in range(lax.axis_size("replica"))])


def shifted(array, step):
    size = lax.axis_size("tensor")
    return lax.ppermute(array, "tensor", [(i, (i + step) % size) for i in range(size)])


HEAD_UNITS = 5


def wanted_by(holder, dest, spans, replica, copy_id):
    row = jnp.int32(0)
    for span in range(spans):
        at = copy_id * spans + span
        row += jnp.where(dest[at, 0] == replica, holder[at], 0)
    return row


def crossing(holder, dest, spans, slot_total, chip):
    items, count = [], jnp.int32(0)
    for copy_id in range(COPIES):
        for core in range(2):
            row = wanted_by(holder, dest, spans, 2 * chip + core, copy_id)
            crosses = row // (2 * slot_total) != chip
            items.append((copy_id, core, row, crosses, count))
            count = count + crosses.astype(jnp.int32)
    return items


def collect_kernel(spans, slot_total, masks, *refs):
    (me_ref, arrival_from, arrival_slot, holder, kv_cache, store_a, store_b) = refs[:7]
    leaving, rows_b, rows_a, sems = refs[7 : 7 + len(masks)], refs[-3], refs[-2], refs[-1]
    me = me_ref[0]
    copies = []
    for i, mask in enumerate(masks):
        to = me ^ mask
        slot = jnp.int32(0)
        for a in range(arrival_from.shape[1]):
            slot += jnp.where(arrival_from[to, a] == me, arrival_slot[to, a], 0)
        copies.append((kv_cache.at[slot], leaving[i]))
    for table, rows in ((store_b, rows_b), (store_a, rows_a)):
        for copy_id in range(COPIES):
            slot = jnp.int32(0)
            for span in range(spans):
                row = holder[copy_id * spans + span]
                slot += jnp.where(row // slot_total == me, row % slot_total, 0)
            copies.append((table.at[slot], rows.at[copy_id]))
    started = [
        pltpu.make_async_copy(a, b, sems.at[i]) for i, (a, b) in enumerate(copies)
    ]
    for copy in started:
        copy.start()
    for copy in started:
        copy.wait()


def pack_kernel(spans, slot_total, *refs):
    (me_ref, holder, dest, store_a, store_b, sibling_a, sibling_b) = refs[:7]
    across_b, head, tails, sems, sems_b = refs[7], refs[8], refs[9:-2], refs[-2], refs[-1]
    me = me_ref[0]
    core = me % 2
    chip = 1 - me // 2
    items = crossing(holder, dest, spans, slot_total, chip)

    def each(action):
        for at, (copy_id, _, row, crosses, unit) in enumerate(items):
            own = row // slot_total == me
            sem = sems.at[at]
            for source, right in (
                (store_a.at[row % slot_total, core], own),
                (sibling_a.at[copy_id, core], jnp.logical_not(own)),
            ):
                use = jnp.logical_and(crosses, right)

                @pl.when(jnp.logical_and(use, unit < HEAD_UNITS))
                def _():
                    action(source, head.at[jnp.minimum(unit, HEAD_UNITS - 1)], sem)

                for i, tail in enumerate(tails):
                    if at >= HEAD_UNITS + i:

                        @pl.when(jnp.logical_and(use, unit == HEAD_UNITS + i))
                        def _():
                            action(source, tail, sem)

        for copy_id in range(COPIES):
            row = wanted_by(holder, dest, spans, 2 * chip + core, copy_id)
            own = row // slot_total == me
            sem = sems_b.at[copy_id]

            @pl.when(own)
            def _():
                action(store_b.at[row % slot_total], across_b.at[copy_id], sem)

            @pl.when(jnp.logical_not(own))
            def _():
                action(sibling_b.at[copy_id], across_b.at[copy_id], sem)

    each(lambda a, b, sem: pltpu.make_async_copy(a, b, sem).start())
    each(lambda a, b, sem: pltpu.make_async_copy(a, b, sem).wait())


def place_up_kernel(spans, slot_total, me_ref, holder, dest, sibling_b, across_b, out, sems):
    me = me_ref[0]

    def each(action):
        for copy_id in range(COPIES):
            row = wanted_by(holder, dest, spans, me, copy_id)
            near = row // (2 * slot_total) == me // 2

            @pl.when(near)
            def _():
                action(sibling_b.at[copy_id], out.at[copy_id], sems.at[copy_id])

            @pl.when(jnp.logical_not(near))
            def _():
                action(across_b.at[copy_id], out.at[copy_id], sems.at[copy_id])

    each(lambda a, b, sem: pltpu.make_async_copy(a, b, sem).start())
    each(lambda a, b, sem: pltpu.make_async_copy(a, b, sem).wait())


def place_down_kernel(spans, slot_total, tail_units, *refs):
    (me_ref, holder, dest, sibling_a, head, head_other) = refs[:6]
    tails, tails_other = refs[6 : 6 + tail_units], refs[6 + tail_units : 6 + 2 * tail_units]
    out, sems = refs[-2], refs[-1]
    me = me_ref[0]
    core = me % 2
    items = crossing(holder, dest, spans, slot_total, me // 2)

    def each(action):
        for at, (copy_id, to, row, crosses, unit) in enumerate(items):
            mine = to == core

            @pl.when(jnp.logical_and(mine, jnp.logical_not(crosses)))
            def _():
                action(sibling_a.at[copy_id], out.at[copy_id], sems.at[copy_id, 0])

            use = jnp.logical_and(mine, crosses)
            for side, (group, last) in enumerate(((head, tails), (head_other, tails_other))):
                half = core if side == 0 else 1 - core
                sem = sems.at[copy_id, side]

                @pl.when(jnp.logical_and(use, unit < HEAD_UNITS))
                def _():
                    action(
                        group.at[jnp.minimum(unit, HEAD_UNITS - 1)], out.at[copy_id, half], sem
                    )

                for i, tail in enumerate(last):
                    if at >= HEAD_UNITS + i:

                        @pl.when(jnp.logical_and(use, unit == HEAD_UNITS + i))
                        def _():
                            action(tail, out.at[copy_id, half], sem)

    each(lambda a, b, sem: pltpu.make_async_copy(a, b, sem).start())
    each(lambda a, b, sem: pltpu.make_async_copy(a, b, sem).wait())


def copy_call(kernel, name, tables, arrays, shapes, sems):
    return pl.pallas_call(
        kernel,
        out_shape=[jax.ShapeDtypeStruct(shape, arrays[0].dtype) for shape in shapes],
        in_specs=[pl.BlockSpec(memory_space=pltpu.SMEM)] * len(tables)
        + [pl.BlockSpec(memory_space=pl.ANY)] * len(arrays),
        out_specs=[pl.BlockSpec(memory_space=pltpu.VMEM)] * len(shapes),
        scratch_shapes=[pltpu.SemaphoreType.DMA(shape) for shape in sems],
        name=name,
    )(*tables, *arrays)


def local_pairs(
    hidden,
    queries,
    kv_cache,
    w_kv,
    store_a,
    store_b,
    lengths,
    arrival_from,
    arrival_slot,
    resident_adapter,
    arrival_adapter,
    hot_holder,
    hot_dest,
):
    me = lax.axis_index("replica")
    replicas = lax.axis_size("replica")
    shards = lax.axis_size("tensor")
    shard = lax.axis_index("tensor")
    resident = kv_cache.shape[0]
    arrive = arrival_from.shape[1]
    slots = resident + arrive
    steps = hidden.shape[1]
    features = hidden.shape[2]
    head_length = queries.shape[3]
    kv_heads = kv_cache.shape[2]
    slot_total = store_a.shape[0]
    rank = store_a.shape[2]
    spans = hot_holder.shape[0] // COPIES
    columns = store_b.shape[3]

    my_from = lax.dynamic_index_in_dim(arrival_from, me, 0, keepdims=False)
    my_slot = lax.dynamic_index_in_dim(arrival_slot, me, 0, keepdims=False)
    own_ids = me * resident + jnp.arange(resident, dtype=jnp.int32)
    leaving_ids = (arrival_from * resident + arrival_slot).reshape(-1)
    staying = jnp.logical_not(jnp.any(own_ids[:, None] == leaving_ids[None, :], axis=1))
    live_mask = jnp.concatenate([staying, jnp.ones((arrive,), bool)])
    own_len = lax.dynamic_slice_in_dim(lengths, me * resident, resident)
    arrival_len = jnp.take(lengths, my_from * resident + my_slot)
    seen_len = jnp.concatenate([own_len, arrival_len])
    holder_grid = hot_holder.reshape(COPIES, spans)
    holder_rep = holder_grid // slot_total
    dest = hot_dest.reshape(COPIES, spans)
    replica_ids = jnp.arange(replicas, dtype=jnp.int32)
    wants = dest[None, :, :] == replica_ids[:, None, None]
    holder_of = jnp.sum(jnp.where(wants, holder_rep[None], 0), axis=2)
    slot_of = jnp.sum(jnp.where(wants, (holder_grid % slot_total)[None], 0), axis=2)

    masks = tuple(range(1, replicas))
    me_table = jnp.reshape(me, (1,)).astype(jnp.int32)
    row_a, row_b = store_a.shape[1:], store_b.shape[1:]
    *leaving, rows_b, rows_a = copy_call(
        functools.partial(collect_kernel, spans, slot_total, masks),
        "collect",
        (me_table, arrival_from, arrival_slot, hot_holder),
        (kv_cache, store_a, store_b),
        [kv_cache.shape[1:]] * len(masks) + [(COPIES,) + row_b, (COPIES,) + row_a],
        [(len(masks) + 2 * COPIES,)],
    )
    came = jnp.stack([partner(array, mask) for array, mask in zip(leaving, masks)])
    sibling_b = partner(rows_b, 1)
    sibling_a = partner(rows_a, 1)

    arrival_hidden = hidden[resident:].reshape(arrive * steps, features)
    other_hidden = [arrival_hidden] + [partner(arrival_hidden, mask) for mask in masks]
    around = [hidden.reshape(slots * steps, features)]
    around += [shifted(around[0], step) for step in range(1, shards)]

    unit_shape = row_a[1:]
    tail_units = 2 * COPIES - HEAD_UNITS
    across_b, head, *tails = copy_call(
        functools.partial(pack_kernel, spans, slot_total),
        "pack",
        (me_table, hot_holder, hot_dest),
        (store_a, store_b, sibling_a, sibling_b),
        [(COPIES,) + row_b, (HEAD_UNITS,) + unit_shape] + [unit_shape] * tail_units,
        [(2 * COPIES,), (COPIES,)],
    )
    across_b = partner(across_b, 2)
    head = partner(head, 2)
    (installed_b,) = copy_call(
        functools.partial(place_up_kernel, spans, slot_total),
        "place_up",
        (me_table, hot_holder, hot_dest),
        (sibling_b, across_b),
        [(COPIES,) + row_b],
        [(COPIES,)],
    )

    own_adapter = lax.dynamic_slice_in_dim(resident_adapter, me * resident, resident)
    row_count = resident * steps
    left = jnp.concatenate([hidden[:resident].reshape(row_count, features)] + other_hidden)
    products = jnp.einsum(
        "md,ard->mar",
        left,
        store_a.reshape(slot_total, 2 * rank, features),
        preferred_element_type=jnp.float32,
    )
    order = jnp.stack([me ^ mask for mask in (0,) + masks])
    chosen = jnp.take(arrival_adapter, order, axis=0)
    hot_rep = jnp.take_along_axis(jnp.take(holder_of, order, axis=0), chosen, axis=1)
    hot_slot = jnp.take_along_axis(jnp.take(slot_of, order, axis=0), chosen, axis=1)
    arrival_pick = jnp.where(hot_rep == me, hot_slot, -1).reshape(-1)
    row_pick = jnp.repeat(jnp.concatenate([own_adapter, arrival_pick]), steps)
    slot_ids = jnp.arange(slot_total, dtype=jnp.int32)
    partial = jnp.sum(
        jnp.where(row_pick[:, None, None] == slot_ids[None, :, None], products, 0.0), axis=1
    )
    total = partial
    for step in range(1, shards):
        total = total + shifted(partial, step)
    arrival_total = total[row_count:].reshape(replicas, arrive * steps, 2 * rank)
    mine_total = arrival_total[0]
    for i, mask in enumerate(masks):
        mine_total = mine_total + partner(arrival_total[i + 1], mask)
    down = jnp.concatenate([total[:row_count], mine_total]).astype(jnp.bfloat16)
    down = down.reshape(slots, steps, 2, rank)

    doubled = jnp.stack(around[::-1] + around[::-1][:-1])
    full = lax.dynamic_slice_in_dim(doubled, shards - 1 - shard, shards, axis=0)
    full = full.transpose(1, 0, 2).reshape(slots, steps, shards * features)
    base = jnp.einsum("msd,dgc->msgc", full, w_kv, preferred_element_type=jnp.float32)

    my_choice = lax.dynamic_index_in_dim(arrival_adapter, me, 0, keepdims=False)
    up = jnp.concatenate(
        [jnp.take(store_b, own_adapter, axis=0), jnp.take(installed_b, my_choice, axis=0)]
    )
    update = jnp.einsum("gnot,gote->gnoe", down, up, preferred_element_type=jnp.float32)
    update = (
        update.reshape(slots, steps, 2, kv_heads, head_length)
        .transpose(0, 1, 3, 2, 4)
        .reshape(slots, steps, kv_heads, 2 * head_length)
    )
    raw = base + ADAPTER_SCALE * update
    positions = seen_len[:, None] + jnp.arange(steps, dtype=jnp.int32)[None, :]
    fresh_kv = jnp.concatenate(
        [rotate_keys(raw[..., :head_length], positions), raw[..., head_length:]], axis=-1
    ).astype(jnp.bfloat16)

    stay_out = attend(queries[:resident], kv_cache, own_len, fresh_kv[:resident])
    arrived = jnp.take(came, (my_from ^ me) - 1, axis=0)
    row_ids = jnp.arange(kv_cache.shape[1], dtype=jnp.int32)
    arrived = jnp.where(
        (row_ids[None, :] < arrival_len[:, None])[:, :, None, None],
        arrived,
        jnp.zeros((), jnp.bfloat16),
    )
    move_out = attend(queries[resident:], arrived, arrival_len, fresh_kv[resident:])
    mixed_out = jnp.concatenate([stay_out, move_out], axis=0)
    attn_out = jnp.where(live_mask[:, None, None], mixed_out, 0.0).astype(jnp.bfloat16)
    new_kv = jnp.where(live_mask[:, None, None, None], fresh_kv, jnp.zeros((), jnp.bfloat16))

    far = replica_ids[:2, None] // 2 != holder_of[:2] // 2
    extra = jnp.clip(jnp.sum(far.astype(jnp.int32)) - HEAD_UNITS, 0, tail_units)
    *tails, attn_out = lax.optimization_barrier((*tails, attn_out))

    def send(units):
        def branch(*arrays):
            got = [partner(array, 2) for array in arrays[:units]]
            other = [partner(array, 1) for array in got]
            rest = list(arrays[units:])
            return (*got, *rest, *other, *rest)

        return branch

    ends = lax.switch(extra, [send(units) for units in range(tail_units + 1)], *tails)
    (installed_a,) = copy_call(
        functools.partial(place_down_kernel, spans, slot_total, tail_units),
        "place_down",
        (me_table, hot_holder, hot_dest),
        (sibling_a, head, partner(head, 1), *ends),
        [(COPIES,) + row_a],
        [(COPIES, 2)],
    )
    return (attn_out, new_kv, arrived, installed_a, installed_b)


def local(*args):
    fan = args[-1].shape[1]
    if lax.axis_size("replica") == 4 and fan == 1:
        return local_pairs(*args)
    return local_general(*args)


def solution(mesh):
    in_specs = (
        P(("parts", "replica"), None, "tensor"),
        P(("parts", "replica"), None, "tensor", None),
        P(("parts", "replica"), None, "tensor", None),
        P(None, "tensor", None),
        P(("parts", "replica"), None, None, "tensor"),
        P(("parts", "replica"), None, None, "tensor"),
        P("parts"),
        P("parts", None),
        P("parts", None),
        P("parts"),
        P("parts", None),
        P("parts"),
        P("parts", None),
    )
    out_specs = (
        P(("parts", "replica"), None, "tensor"),
        P(("parts", "replica"), None, "tensor", None),
        P(("parts", "replica"), None, "tensor", None),
        P(("parts", "replica"), None, None, "tensor"),
        P(("parts", "replica"), None, None, "tensor"),
    )
    return jax.shard_map(local, mesh=mesh, in_specs=in_specs, out_specs=out_specs, check_vma=False)
```

```python
import functools
import math

import jax
import jax.numpy as jnp
from jax import lax
from jax.experimental import pallas as pl
from jax.experimental.pallas import tpu as pltpu
from jax.sharding import PartitionSpec as P

COPIES = 4


ADAPTER_SCALE = 2.0
ROPE_BASE = 500000.0


def rotate_keys(key_rows, positions):
    head_length = key_rows.shape[-1]
    half_size = head_length // 2
    frequency = ROPE_BASE ** (-(jnp.arange(half_size, dtype=jnp.float32) * 2.0 / head_length))
    angles = positions.astype(jnp.float32)[:, :, None, None] * frequency
    cosine = jnp.cos(angles)
    sine_val = jnp.sin(angles)
    first_half = key_rows[..., :half_size]
    second_half = key_rows[..., half_size:]
    return jnp.concatenate(
        [
            first_half * cosine - second_half * sine_val,
            second_half * cosine + first_half * sine_val,
        ],
        axis=-1,
    )


def attend(queries, stored, lengths_now, fresh_kv):
    request_slot_count, decode_step_count, heads_local, head_length = queries.shape
    local_key_value = stored.shape[2]
    group_size = heads_local // local_key_value
    grouped = queries.reshape(
        request_slot_count, decode_step_count, local_key_value, group_size, head_length
    )
    score_scale = 1.0 / math.sqrt(head_length)
    past_scores = (
        jnp.einsum(
            "msgjd,mcgd->msgjc",
            grouped,
            stored[..., :head_length],
            preferred_element_type=jnp.float32,
        )
        * score_scale
    )
    recent_scores = (
        jnp.einsum(
            "msgjd,mtgd->msgjt",
            grouped,
            fresh_kv[..., :head_length],
            preferred_element_type=jnp.float32,
        )
        * score_scale
    )
    row_ids = jnp.arange(stored.shape[1], dtype=jnp.int32)
    past_ok = (row_ids[None, :] < lengths_now[:, None])[:, None, None, None, :]
    step_ids = jnp.arange(decode_step_count, dtype=jnp.int32)
    recent_ok = (step_ids[None, :] <= step_ids[:, None])[None, :, None, None, :]
    past_scores = jnp.where(past_ok, past_scores, -jnp.inf)
    recent_scores = jnp.where(recent_ok, recent_scores, -jnp.inf)
    peak_score = jnp.maximum(jnp.max(past_scores, -1), jnp.max(recent_scores, -1))[..., None]
    past_exp = jnp.exp(past_scores - peak_score)
    recent_exp = jnp.exp(recent_scores - peak_score)
    denom_sum = jnp.sum(past_exp, -1, keepdims=True) + jnp.sum(recent_exp, -1, keepdims=True)
    past_w = (past_exp / denom_sum).astype(jnp.bfloat16)
    recent_w = (recent_exp / denom_sum).astype(jnp.bfloat16)
    mixed_out = jnp.einsum(
        "msgjc,mcgd->msgjd", past_w, stored[..., head_length:], preferred_element_type=jnp.float32
    )
    mixed_out = mixed_out + jnp.einsum(
        "msgjt,mtgd->msgjd",
        recent_w,
        fresh_kv[..., head_length:],
        preferred_element_type=jnp.float32,
    )
    return mixed_out.reshape(request_slot_count, decode_step_count, heads_local * head_length)


def local_general(
    hidden,
    queries,
    kv_cache,
    w_kv,
    store_a,
    store_b,
    lengths,
    arrival_from,
    arrival_slot,
    resident_adapter,
    arrival_adapter,
    hot_holder,
    hot_dest,
):
    my_index = lax.axis_index("replica")
    replicas = lax.axis_size("replica")
    resident = kv_cache.shape[0]
    arrive = arrival_from.shape[1]
    request_slot_count = resident + arrive
    decode_step_count = hidden.shape[1]
    head_length = queries.shape[3]
    local_key_value = kv_cache.shape[2]
    slot_total = store_a.shape[0]
    hot_total = hot_holder.shape[0]
    spans = hot_total // COPIES
    my_from = lax.dynamic_index_in_dim(arrival_from, my_index, 0, keepdims=False)
    my_slot = lax.dynamic_index_in_dim(arrival_slot, my_index, 0, keepdims=False)
    own_ids = my_index * resident + jnp.arange(resident, dtype=jnp.int32)
    leaving_ids = (arrival_from * resident + arrival_slot).reshape(-1)
    staying = jnp.logical_not(jnp.any(own_ids[:, None] == leaving_ids[None, :], axis=1))
    live_mask = jnp.concatenate([staying, jnp.ones((arrive,), bool)])
    own_len = lax.dynamic_slice_in_dim(lengths, my_index * resident, resident)
    arrival_len = jnp.take(lengths, my_from * resident + my_slot)
    seen_len = jnp.concatenate([own_len, arrival_len])
    takes_mine = arrival_from == my_index
    sends_any = jnp.any(takes_mine, axis=1)
    send_slot = jnp.sum(jnp.where(takes_mine, arrival_slot, 0), axis=1)
    outgoing = jnp.take(kv_cache, send_slot, axis=0)
    outgoing = jnp.where(sends_any[:, None, None, None], outgoing, jnp.zeros((), jnp.bfloat16))
    incoming = lax.all_to_all(outgoing, "replica", split_axis=0, concat_axis=0, tiled=True)
    blocks = hot_dest.reshape(COPIES, spans, hot_dest.shape[1])
    holder_grid = hot_holder.reshape(COPIES, spans)
    holder_rep = holder_grid // slot_total
    mine = holder_rep == my_index
    has_one = jnp.any(mine, axis=1)
    local_pick = jnp.sum(jnp.where(mine, holder_grid % slot_total, 0), axis=1)

    def spread_rows(store):
        rows = jnp.take(store, local_pick, axis=0)
        rows = jnp.where(has_one[:, None, None, None], rows, jnp.zeros((), jnp.bfloat16))
        return rows.reshape(COPIES, replicas, -1).transpose(1, 0, 2)

    got_a, got_b = (
        lax.all_to_all(spread_rows(store_a), "replica", split_axis=0, concat_axis=0, tiled=True),
        lax.all_to_all(spread_rows(store_b), "replica", split_axis=0, concat_axis=0, tiled=True),
    )
    replica_ids = jnp.arange(replicas, dtype=jnp.int32)
    member = jnp.any(blocks[:, :, :, None] == replica_ids[None, None, None, :], axis=2).astype(
        jnp.int32
    )
    source_rep = jnp.sum(member * holder_rep[:, :, None], axis=1)
    copy_ids = jnp.arange(COPIES, dtype=jnp.int32)
    route_a = got_a[source_rep.T, copy_ids[None, :]]
    route_b = got_b[source_rep.T, copy_ids[None, :]]
    recv_a, recv_b = (
        lax.all_to_all(route_a, "replica", split_axis=0, concat_axis=0, tiled=True),
        lax.all_to_all(route_b, "replica", split_axis=0, concat_axis=0, tiled=True),
    )
    installed_a = recv_a.transpose(1, 0, 2).reshape((COPIES,) + store_a.shape[1:])
    installed_b = recv_b.transpose(1, 0, 2).reshape((COPIES,) + store_b.shape[1:])
    own_adapter = lax.dynamic_slice_in_dim(resident_adapter, my_index * resident, resident)
    my_choice = lax.dynamic_index_in_dim(arrival_adapter, my_index, 0, keepdims=False)
    adapt_a = jnp.concatenate(
        [jnp.take(store_a, own_adapter, axis=0), jnp.take(installed_a, my_choice, axis=0)]
    )
    adapter_up_weight = jnp.concatenate(
        [jnp.take(store_b, own_adapter, axis=0), jnp.take(installed_b, my_choice, axis=0)]
    )
    partial_value = jnp.einsum(
        "msd,mpkd->mspk", hidden, adapt_a, preferred_element_type=jnp.float32
    )
    base_projection = jnp.einsum(
        "msd,dgc->msgc",
        lax.all_gather(hidden, "tensor", axis=2, tiled=True),
        w_kv,
        preferred_element_type=jnp.float32,
    )
    down_projected = lax.psum(partial_value, "tensor")
    down_projected = down_projected.astype(jnp.bfloat16)
    adapter_update = jnp.einsum(
        "gnot,gote->gnoe", down_projected, adapter_up_weight, preferred_element_type=jnp.float32
    )
    adapter_update = (
        adapter_update.reshape(
            request_slot_count, decode_step_count, 2, local_key_value, head_length
        )
        .transpose(0, 1, 3, 2, 4)
        .reshape(request_slot_count, decode_step_count, local_key_value, 2 * head_length)
    )
    unrotated_key_value = base_projection + ADAPTER_SCALE * adapter_update
    positions = seen_len[:, None] + jnp.arange(decode_step_count, dtype=jnp.int32)[None, :]
    fresh_kv = jnp.concatenate(
        [
            rotate_keys(unrotated_key_value[..., :head_length], positions),
            unrotated_key_value[..., head_length:],
        ],
        axis=-1,
    ).astype(jnp.bfloat16)
    stay_out = attend(queries[:resident], kv_cache, own_len, fresh_kv[:resident])
    arrived = jnp.take(incoming, my_from, axis=0)
    row_ids = jnp.arange(kv_cache.shape[1], dtype=jnp.int32)
    arrived = jnp.where(
        (row_ids[None, :] < arrival_len[:, None])[:, :, None, None],
        arrived,
        jnp.zeros((), jnp.bfloat16),
    )
    move_out = attend(queries[resident:], arrived, arrival_len, fresh_kv[resident:])
    mixed_out = jnp.concatenate([stay_out, move_out], axis=0)
    attn_out = jnp.where(live_mask[:, None, None], mixed_out, 0.0).astype(jnp.bfloat16)
    new_kv = jnp.where(live_mask[:, None, None, None], fresh_kv, jnp.zeros((), jnp.bfloat16))
    return (attn_out, new_kv, arrived, installed_a, installed_b)


def partner(array, mask):
    return lax.ppermute(array, "replica", [(i, i ^ mask) for i in range(lax.axis_size("replica"))])


def shifted(array, step):
    size = lax.axis_size("tensor")
    return lax.ppermute(array, "tensor", [(i, (i + step) % size) for i in range(size)])


HEAD_UNITS = 5


def wanted_by(holder, dest, spans, replica, copy_id):
    row = jnp.int32(0)
    for span in range(spans):
        at = copy_id * spans + span
        row += jnp.where(dest[0, at] == replica, holder[at], 0)
    return row


def crossing(holder, dest, spans, slot_total, chip):
    items, count = [], jnp.int32(0)
    for copy_id in range(COPIES):
        for core in range(2):
            row = wanted_by(holder, dest, spans, 2 * chip + core, copy_id)
            crosses = row // (2 * slot_total) != chip
            items.append((copy_id, core, row, crosses, count))
            count = count + crosses.astype(jnp.int32)
    return items


def collect_kernel(spans, slot_total, masks, *refs):
    (me_ref, arrival_from, arrival_slot, holder, kv_cache, store_a, store_b) = refs[:7]
    leaving, rows_b, rows_a, sems = refs[7 : 7 + len(masks)], refs[-3], refs[-2], refs[-1]
    me = me_ref[0]
    copies = []
    for i, mask in enumerate(masks):
        to = me ^ mask
        slot = jnp.int32(0)
        for a in range(arrival_from.shape[0]):
            slot += jnp.where(arrival_from[a, to] == me, arrival_slot[a, to], 0)
        copies.append((kv_cache.at[slot], leaving[i]))
    for table, rows in ((store_b, rows_b), (store_a, rows_a)):
        for copy_id in range(COPIES):
            slot = jnp.int32(0)
            for span in range(spans):
                row = holder[copy_id * spans + span]
                slot += jnp.where(row // slot_total == me, row % slot_total, 0)
            copies.append((table.at[slot], rows.at[copy_id]))
    started = [
        pltpu.make_async_copy(a, b, sems.at[i]) for i, (a, b) in enumerate(copies)
    ]
    for copy in started:
        copy.start()
    for copy in started:
        copy.wait()


def pack_kernel(spans, slot_total, *refs):
    (me_ref, holder, dest, store_a, store_b, sibling_a, sibling_b) = refs[:7]
    across_b, head, tails, sems, sems_b = refs[7], refs[8], refs[9:-2], refs[-2], refs[-1]
    me = me_ref[0]
    core = me % 2
    chip = 1 - me // 2
    items = crossing(holder, dest, spans, slot_total, chip)

    def each(action):
        for at, (copy_id, _, row, crosses, unit) in enumerate(items):
            own = row // slot_total == me
            sem = sems.at[at]
            for source, right in (
                (store_a.at[row % slot_total, core], own),
                (sibling_a.at[copy_id, core], jnp.logical_not(own)),
            ):
                use = jnp.logical_and(crosses, right)

                @pl.when(jnp.logical_and(use, unit < HEAD_UNITS))
                def _():
                    action(source, head.at[jnp.minimum(unit, HEAD_UNITS - 1)], sem)

                for i, tail in enumerate(tails):
                    if at >= HEAD_UNITS + i:

                        @pl.when(jnp.logical_and(use, unit == HEAD_UNITS + i))
                        def _():
                            action(source, tail, sem)

        for copy_id in range(COPIES):
            row = wanted_by(holder, dest, spans, 2 * chip + core, copy_id)
            own = row // slot_total == me
            sem = sems_b.at[copy_id]

            @pl.when(own)
            def _():
                action(store_b.at[row % slot_total], across_b.at[copy_id], sem)

            @pl.when(jnp.logical_not(own))
            def _():
                action(sibling_b.at[copy_id], across_b.at[copy_id], sem)

    each(lambda a, b, sem: pltpu.make_async_copy(a, b, sem).start())
    each(lambda a, b, sem: pltpu.make_async_copy(a, b, sem).wait())


def place_up_kernel(spans, slot_total, me_ref, holder, dest, sibling_b, across_b, out, sems):
    me = me_ref[0]

    def each(action):
        for copy_id in range(COPIES):
            row = wanted_by(holder, dest, spans, me, copy_id)
            near = row // (2 * slot_total) == me // 2

            @pl.when(near)
            def _():
                action(sibling_b.at[copy_id], out.at[copy_id], sems.at[copy_id])

            @pl.when(jnp.logical_not(near))
            def _():
                action(across_b.at[copy_id], out.at[copy_id], sems.at[copy_id])

    each(lambda a, b, sem: pltpu.make_async_copy(a, b, sem).start())
    each(lambda a, b, sem: pltpu.make_async_copy(a, b, sem).wait())


def place_down_kernel(spans, slot_total, tail_units, *refs):
    (me_ref, holder, dest, sibling_a, head, head_other) = refs[:6]
    tails, tails_other = refs[6 : 6 + tail_units], refs[6 + tail_units : 6 + 2 * tail_units]
    out, sems = refs[-2], refs[-1]
    me = me_ref[0]
    core = me % 2
    items = crossing(holder, dest, spans, slot_total, me // 2)

    def each(action):
        for at, (copy_id, to, row, crosses, unit) in enumerate(items):
            mine = to == core

            @pl.when(jnp.logical_and(mine, jnp.logical_not(crosses)))
            def _():
                action(sibling_a.at[copy_id], out.at[copy_id], sems.at[copy_id, 0])

            use = jnp.logical_and(mine, crosses)
            for side, (group, last) in enumerate(((head, tails), (head_other, tails_other))):
                half = core if side == 0 else 1 - core
                sem = sems.at[copy_id, side]

                @pl.when(jnp.logical_and(use, unit < HEAD_UNITS))
                def _():
                    action(
                        group.at[jnp.minimum(unit, HEAD_UNITS - 1)], out.at[copy_id, half], sem
                    )

                for i, tail in enumerate(last):
                    if at >= HEAD_UNITS + i:

                        @pl.when(jnp.logical_and(use, unit == HEAD_UNITS + i))
                        def _():
                            action(tail, out.at[copy_id, half], sem)

    each(lambda a, b, sem: pltpu.make_async_copy(a, b, sem).start())
    each(lambda a, b, sem: pltpu.make_async_copy(a, b, sem).wait())


def copy_call(kernel, name, tables, arrays, shapes, sems):
    return pl.pallas_call(
        kernel,
        out_shape=[jax.ShapeDtypeStruct(shape, arrays[0].dtype) for shape in shapes],
        in_specs=[pl.BlockSpec(memory_space=pltpu.SMEM)] * len(tables)
        + [pl.BlockSpec(memory_space=pl.ANY)] * len(arrays),
        out_specs=[pl.BlockSpec(memory_space=pltpu.VMEM)] * len(shapes),
        scratch_shapes=[pltpu.SemaphoreType.DMA(shape) for shape in sems],
        name=name,
    )(*tables, *arrays)


def project_kernel(spans, slot_total, resident, steps, masks, *refs):
    (me_ref, resident_adapter, arrival_adapter, holder, dest, hidden, *others) = refs[: 6 + len(masks)]
    store, out, left = refs[-3:]
    me = me_ref[0]
    adapter = pl.program_id(0)
    base = hidden.shape[0]
    block = others[0].shape[0]

    @pl.when(adapter == 0)
    def _():
        left[0:base] = hidden[...]
        for i, other in enumerate(others):
            left[base + i * block : base + (i + 1) * block] = other[...]
        out[...] = jnp.zeros_like(out)

    ids = lax.broadcasted_iota(jnp.int32, out.shape, 0) // steps
    picked = jnp.zeros(out.shape, jnp.bool_)
    for slot in range(resident):
        hit = resident_adapter[me * resident + slot] == adapter
        picked = jnp.logical_or(picked, jnp.logical_and(ids == slot, hit))
    for i, mask in enumerate((0,) + masks):
        replica = me ^ mask
        first = resident if i == 0 else (base + (i - 1) * block) // steps
        for a in range(arrival_adapter.shape[0]):
            chosen = arrival_adapter[a, replica]
            row = jnp.int32(0)
            for copy_id in range(COPIES):
                wanted = wanted_by(holder, dest, spans, replica, copy_id)
                row += jnp.where(chosen == copy_id, wanted, 0)
            hit = row == me * slot_total + adapter
            picked = jnp.logical_or(picked, jnp.logical_and(ids == first + a, hit))
    product = lax.dot_general(
        left[...], store[0], (((1,), (1,)), ((), ())), preferred_element_type=jnp.float32
    )
    out[...] += jnp.where(picked, product, 0.0)


def gather_kernel(shard_ref, *refs):
    out = refs[-1]
    count = len(refs) - 1
    width = refs[0].shape[1]
    for step, ref in enumerate(refs[:-1]):
        source = lax.rem(shard_ref[0] + count - step, count)
        out[:, pl.ds(pl.multiple_of(source * width, width), width)] = ref[...]


def attend_kernel(resident, steps, kv_heads, head_length, *refs):
    (me_ref, lengths, arrival_from, arrival_slot, resident_adapter, arrival_adapter) = refs[:6]
    (total, *returned) = refs[6:-9]
    store_b, installed_b, base, queries, cache, arrived, out, new_kv, fresh_ref = refs[-9:]
    me = me_ref[0]
    arrive = arrival_from.shape[0]
    replicas = arrival_from.shape[1]
    slots = resident + arrive
    row_count = base.shape[0]
    rank = store_b.shape[1] // 2
    half = head_length // 2
    seen = [lengths[me * resident + slot] for slot in range(resident)]
    for a in range(arrive):
        seen.append(lengths[arrival_from[a, me] * resident + arrival_slot[a, me]])

    first = resident * steps
    last = total[first:row_count]
    for ref in returned:
        last = last + ref[...]
    down = jnp.concatenate([total[0:first], last], axis=0).astype(jnp.bfloat16)

    ids = lax.broadcasted_iota(jnp.int32, (row_count, 1), 0) // steps
    adapters = jnp.zeros((row_count, 1), jnp.int32)
    position = lax.broadcasted_iota(jnp.int32, (row_count, 1), 0) % steps
    for slot in range(slots):
        if slot < resident:
            adapter = resident_adapter[me * resident + slot]
        else:
            adapter = store_b.shape[0] + arrival_adapter[slot - resident, me]
        adapters = jnp.where(ids == slot, adapter, adapters)
        position = jnp.where(ids == slot, position + seen[slot], position)
    deltas = [jnp.zeros((row_count, store_b.shape[2]), jnp.float32) for _ in range(2)]
    for adapter in range(store_b.shape[0] + COPIES):
        if adapter < store_b.shape[0]:
            table = store_b[adapter]
        else:
            table = installed_b[adapter - store_b.shape[0]]
        for part in range(2):
            product = jnp.dot(
                down[:, part * rank : (part + 1) * rank],
                table[part * rank : (part + 1) * rank],
                preferred_element_type=jnp.float32,
            )
            deltas[part] = jnp.where(adapters == adapter, product, deltas[part])

    lane = lax.broadcasted_iota(jnp.int32, (1, half), 1).astype(jnp.float32)
    frequency = jnp.exp(lane * (-2.0 * math.log(ROPE_BASE) / head_length))
    angles = position.astype(jnp.float32) * frequency
    cosine, sine = jnp.cos(angles), jnp.sin(angles)
    dead = jnp.zeros((row_count, 1), jnp.bool_)
    gone = [jnp.int32(0)] * resident
    for q in range(replicas):
        for a in range(arrive):
            mine = arrival_from[a, q] == me
            slot = arrival_slot[a, q]
            dead = jnp.logical_or(dead, jnp.logical_and(ids == slot, mine))
            for n in range(resident):
                gone[n] = jnp.where(jnp.logical_and(mine, slot == n), 1, gone[n])
    for g in range(kv_heads):
        at = g * 2 * head_length
        columns = slice(g * head_length, (g + 1) * head_length)
        key = base[:, at : at + head_length] + ADAPTER_SCALE * deltas[0][:, columns]
        value = (
            base[:, at + head_length : at + 2 * head_length]
            + ADAPTER_SCALE * deltas[1][:, columns]
        )
        u, w = key[:, :half], key[:, half:]
        key = jnp.concatenate([u * cosine - w * sine, w * cosine + u * sine], axis=1)
        for part, piece in enumerate((key, value)):
            spot = slice(at + part * head_length, at + (part + 1) * head_length)
            rounded = piece.astype(jnp.bfloat16)
            fresh_ref[:, spot] = rounded.astype(jnp.float32)
            new_kv[:, spot] = jnp.where(dead, jnp.zeros_like(rounded), rounded)

    query_rows = queries.shape[1]
    heads = query_rows // steps
    row = lax.broadcasted_iota(jnp.int32, (query_rows, 1), 0)
    step_of = row // heads
    group_of = row % heads // (heads // kv_heads)
    column = lax.broadcasted_iota(jnp.int32, (query_rows, cache.shape[1]), 1)
    same = column % kv_heads == group_of
    past_row = column // kv_heads
    scale = 1.0 / math.sqrt(head_length)
    for n in range(slots):
        stored = cache[n] if n < resident else arrived[n - resident]
        query = queries[n]
        score = (
            lax.dot_general(
                query,
                stored[:, :head_length],
                (((1,), (1,)), ((), ())),
                preferred_element_type=jnp.float32,
            )
            * scale
        )
        score = jnp.where(jnp.logical_and(same, past_row < seen[n]), score, -jnp.inf)
        query = query.astype(jnp.float32)
        recent, values = [], []
        for t in range(steps):
            line = fresh_ref[n * steps + t : n * steps + t + 1]
            key = jnp.zeros((query_rows, head_length), jnp.float32)
            value = key
            for g in range(kv_heads):
                at = g * 2 * head_length
                key = jnp.where(group_of == g, line[:, at : at + head_length], key)
                value = jnp.where(
                    group_of == g, line[:, at + head_length : at + 2 * head_length], value
                )
            fit = jnp.sum(query * key, axis=1, keepdims=True) * scale
            recent.append(jnp.where(step_of >= t, fit, -jnp.inf))
            values.append(value)
        peak = jnp.max(score, axis=1, keepdims=True)
        for fit in recent:
            peak = jnp.maximum(peak, fit)
        past_exp = jnp.exp(score - peak)
        recent_exp = [jnp.exp(fit - peak) for fit in recent]
        denom = jnp.sum(past_exp, axis=1, keepdims=True)
        for term in recent_exp:
            denom = denom + term
        weight = (past_exp / denom).astype(jnp.bfloat16)
        mixed = jnp.dot(weight, stored[:, head_length:], preferred_element_type=jnp.float32)
        for term, value in zip(recent_exp, values):
            mixed = mixed + (term / denom).astype(jnp.bfloat16).astype(jnp.float32) * value
        if n < resident:
            mixed = jnp.where(gone[n] != 0, 0.0, mixed)
        out[n] = mixed.astype(jnp.bfloat16)


SMEM = pl.BlockSpec(memory_space=pltpu.SMEM)
VMEM = pl.BlockSpec(memory_space=pltpu.VMEM)


def local_pairs(
    hidden,
    queries,
    kv_cache,
    w_kv,
    store_a,
    store_b,
    lengths,
    arrival_from,
    arrival_slot,
    resident_adapter,
    arrival_adapter,
    hot_holder,
    hot_dest,
):
    me = lax.axis_index("replica")
    replicas = lax.axis_size("replica")
    shards = lax.axis_size("tensor")
    resident, cap, kv_heads, head_pair = kv_cache.shape
    arrive = arrival_from.shape[1]
    slots = resident + arrive
    steps, features = hidden.shape[1:]
    heads, head_length = queries.shape[2:]
    slot_total = store_a.shape[0]
    rank = store_a.shape[2]
    spans = hot_holder.shape[0] // COPIES
    row_a, row_b = store_a.shape[1:], store_b.shape[1:]
    columns = store_b.shape[3]
    masks = tuple(range(1, replicas))
    me_table = jnp.reshape(me, (1,)).astype(jnp.int32)
    shard_table = jnp.reshape(lax.axis_index("tensor"), (1,)).astype(jnp.int32)
    from_table, slot_table, choice_table = arrival_from.T, arrival_slot.T, arrival_adapter.T
    dest_table = hot_dest.T

    used = slots * steps
    padded = -(-used // 8) * 8
    rows = jnp.pad(hidden.reshape(used, features), ((0, padded - used), (0, 0)))
    first = resident * steps
    other_rows = [partner(rows[first:], mask) for mask in masks]

    *leaving, rows_b, rows_a = copy_call(
        functools.partial(collect_kernel, spans, slot_total, masks),
        "collect",
        (me_table, from_table, slot_table, hot_holder),
        (kv_cache, store_a, store_b),
        [kv_cache.shape[1:]] * len(masks) + [(COPIES,) + row_b, (COPIES,) + row_a],
        [(len(masks) + 2 * COPIES,)],
    )
    sibling_a = partner(rows_a, 1)
    sibling_b = partner(rows_b, 1)
    came = [partner(array, mask) for array, mask in zip(leaving, masks)]
    around = [rows] + [shifted(rows, step) for step in range(1, shards)]

    line_count = padded + len(masks) * (padded - first)
    partial = pl.pallas_call(
        functools.partial(project_kernel, spans, slot_total, resident, steps, masks),
        out_shape=jax.ShapeDtypeStruct((line_count, 2 * rank), jnp.float32),
        grid=(slot_total,),
        in_specs=[SMEM] * 5
        + [pl.BlockSpec((padded, features), lambda i: (0, 0))]
        + [pl.BlockSpec((padded - first, features), lambda i: (0, 0))] * len(masks)
        + [pl.BlockSpec((1, 2 * rank, features), lambda i: (i, 0, 0))],
        out_specs=pl.BlockSpec((line_count, 2 * rank), lambda i: (0, 0)),
        scratch_shapes=[pltpu.VMEM((line_count, features), hidden.dtype)],
        name="project",
    )(
        me_table,
        resident_adapter,
        choice_table,
        hot_holder,
        dest_table,
        rows,
        *other_rows,
        store_a.reshape(slot_total, 2 * rank, features),
    )
    parts = [partial] + [shifted(partial, step) for step in range(1, shards)]

    unit_shape = row_a[1:]
    tail_units = 2 * COPIES - HEAD_UNITS
    across_b, head, *tails = copy_call(
        functools.partial(pack_kernel, spans, slot_total),
        "pack",
        (me_table, hot_holder, dest_table),
        (store_a, store_b, sibling_a, sibling_b),
        [(COPIES,) + row_b, (HEAD_UNITS,) + unit_shape] + [unit_shape] * tail_units,
        [(2 * COPIES,), (COPIES,)],
    )
    *parts, across_b, head = lax.optimization_barrier((*parts, across_b, head))
    across_b = partner(across_b, 2)
    head = partner(head, 2)
    total = parts[0]
    for array in parts[1:]:
        total = total + array
    block = padded - first
    returned = [
        partner(total[padded + i * block : padded + (i + 1) * block], mask)
        for i, mask in enumerate(masks)
    ]

    full = pl.pallas_call(
        gather_kernel,
        out_shape=jax.ShapeDtypeStruct((padded, shards * features), hidden.dtype),
        in_specs=[SMEM] + [VMEM] * shards,
        out_specs=VMEM,
        name="gather",
    )(shard_table, *around)
    base = jnp.einsum("md,dgc->mgc", full, w_kv, preferred_element_type=jnp.float32)
    base = base.reshape(padded, kv_heads * head_pair)

    my_from = lax.dynamic_index_in_dim(from_table, me, 1, keepdims=False)
    my_slot = lax.dynamic_index_in_dim(slot_table, me, 1, keepdims=False)
    row_ids = lax.broadcasted_iota(jnp.int32, kv_cache.shape[1:], 0)
    arrived = []
    for a in range(arrive):
        source = my_from[a]
        length = lax.dynamic_index_in_dim(lengths, source * resident + my_slot[a], 0, False)
        array = came[-1]
        for other, mask in zip(came[:-1], masks):
            array = jnp.where(source == me ^ mask, other, array)
        arrived.append(jnp.where(row_ids < length, array, jnp.zeros((), array.dtype)))
    arrived = jnp.stack(arrived)

    (installed_b,) = copy_call(
        functools.partial(place_up_kernel, spans, slot_total),
        "place_up",
        (me_table, hot_holder, dest_table),
        (sibling_b, across_b),
        [(COPIES,) + row_b],
        [(COPIES,)],
    )
    attn_out, new_kv = pl.pallas_call(
        functools.partial(attend_kernel, resident, steps, kv_heads, head_length),
        out_shape=[
            jax.ShapeDtypeStruct((slots, steps * heads, head_length), jnp.bfloat16),
            jax.ShapeDtypeStruct((padded, kv_heads * head_pair), jnp.bfloat16),
        ],
        in_specs=[SMEM] * 6 + [VMEM] * (1 + len(masks) + 6),
        out_specs=[VMEM] * 2,
        scratch_shapes=[pltpu.VMEM((padded, kv_heads * head_pair), jnp.float32)],
        name="attend",
    )(
        me_table,
        lengths,
        from_table,
        slot_table,
        resident_adapter,
        choice_table,
        total,
        *returned,
        store_b.reshape(slot_total, 2 * rank, columns),
        installed_b.reshape(COPIES, 2 * rank, columns),
        base,
        queries.reshape(slots, steps * heads, head_length),
        kv_cache.reshape(resident, cap * kv_heads, head_pair),
        arrived.reshape(arrive, cap * kv_heads, head_pair),
    )
    attn_out = attn_out.reshape(slots, steps, heads * head_length)
    new_kv = new_kv[:used].reshape(slots, steps, kv_heads, head_pair)

    holder_chip = hot_holder // (2 * slot_total)
    far = jnp.logical_and(hot_dest[:, 0] // 2 == 0, holder_chip != 0)
    extra = jnp.clip(jnp.sum(far.astype(jnp.int32)) - HEAD_UNITS, 0, tail_units)
    *tails, attn_out = lax.optimization_barrier((*tails, attn_out))

    def send(units):
        def branch(*arrays):
            got = [partner(array, 2) for array in arrays[:units]]
            other = [partner(array, 1) for array in got]
            rest = list(arrays[units:])
            return (*got, *rest, *other, *rest)

        return branch

    ends = lax.switch(extra, [send(units) for units in range(tail_units + 1)], *tails)
    (installed_a,) = copy_call(
        functools.partial(place_down_kernel, spans, slot_total, tail_units),
        "place_down",
        (me_table, hot_holder, dest_table),
        (sibling_a, head, partner(head, 1), *ends),
        [(COPIES,) + row_a],
        [(COPIES, 2)],
    )
    return (attn_out, new_kv, arrived, installed_a, installed_b)


def local(*args):
    fan = args[-1].shape[1]
    if lax.axis_size("replica") == 4 and fan == 1:
        return local_pairs(*args)
    return local_general(*args)


def solution(mesh):
    in_specs = (
        P(("parts", "replica"), None, "tensor"),
        P(("parts", "replica"), None, "tensor", None),
        P(("parts", "replica"), None, "tensor", None),
        P(None, "tensor", None),
        P(("parts", "replica"), None, None, "tensor"),
        P(("parts", "replica"), None, None, "tensor"),
        P("parts"),
        P("parts", None),
        P("parts", None),
        P("parts"),
        P("parts", None),
        P("parts"),
        P("parts", None),
    )
    out_specs = (
        P(("parts", "replica"), None, "tensor"),
        P(("parts", "replica"), None, "tensor", None),
        P(("parts", "replica"), None, "tensor", None),
        P(("parts", "replica"), None, None, "tensor"),
        P(("parts", "replica"), None, None, "tensor"),
    )
    return jax.shard_map(local, mesh=mesh, in_specs=in_specs, out_specs=out_specs, check_vma=False)
```

```python
import functools
import math

import jax
import jax.numpy as jnp
from jax import lax
from jax.experimental import pallas as pl
from jax.experimental.pallas import tpu as pltpu
from jax.sharding import PartitionSpec as P


COPIES = 4


ADAPTER_SCALE = 2.0
ROPE_BASE = 500000.0


def rotate_keys(key_rows, positions):
    head_length = key_rows.shape[-1]
    half_size = head_length // 2
    frequency = ROPE_BASE ** (-(jnp.arange(half_size, dtype=jnp.float32) * 2.0 / head_length))
    angles = positions.astype(jnp.float32)[:, :, None, None] * frequency
    cosine = jnp.cos(angles)
    sine_val = jnp.sin(angles)
    first_half = key_rows[..., :half_size]
    second_half = key_rows[..., half_size:]
    return jnp.concatenate(
        [
            first_half * cosine - second_half * sine_val,
            second_half * cosine + first_half * sine_val,
        ],
        axis=-1,
    )


def attend(queries, stored, lengths_now, fresh_kv):
    request_slot_count, decode_step_count, heads_local, head_length = queries.shape
    local_key_value = stored.shape[2]
    group_size = heads_local // local_key_value
    grouped = queries.reshape(
        request_slot_count, decode_step_count, local_key_value, group_size, head_length
    )
    score_scale = 1.0 / math.sqrt(head_length)
    past_scores = (
        jnp.einsum(
            "msgjd,mcgd->msgjc",
            grouped,
            stored[..., :head_length],
            preferred_element_type=jnp.float32,
        )
        * score_scale
    )
    recent_scores = (
        jnp.einsum(
            "msgjd,mtgd->msgjt",
            grouped,
            fresh_kv[..., :head_length],
            preferred_element_type=jnp.float32,
        )
        * score_scale
    )
    row_ids = jnp.arange(stored.shape[1], dtype=jnp.int32)
    past_ok = (row_ids[None, :] < lengths_now[:, None])[:, None, None, None, :]
    step_ids = jnp.arange(decode_step_count, dtype=jnp.int32)
    recent_ok = (step_ids[None, :] <= step_ids[:, None])[None, :, None, None, :]
    past_scores = jnp.where(past_ok, past_scores, -jnp.inf)
    recent_scores = jnp.where(recent_ok, recent_scores, -jnp.inf)
    peak_score = jnp.maximum(jnp.max(past_scores, -1), jnp.max(recent_scores, -1))[..., None]
    past_exp = jnp.exp(past_scores - peak_score)
    recent_exp = jnp.exp(recent_scores - peak_score)
    denom_sum = jnp.sum(past_exp, -1, keepdims=True) + jnp.sum(recent_exp, -1, keepdims=True)
    past_w = (past_exp / denom_sum).astype(jnp.bfloat16)
    recent_w = (recent_exp / denom_sum).astype(jnp.bfloat16)
    mixed_out = jnp.einsum(
        "msgjc,mcgd->msgjd", past_w, stored[..., head_length:], preferred_element_type=jnp.float32
    )
    mixed_out = mixed_out + jnp.einsum(
        "msgjt,mtgd->msgjd",
        recent_w,
        fresh_kv[..., head_length:],
        preferred_element_type=jnp.float32,
    )
    return mixed_out.reshape(request_slot_count, decode_step_count, heads_local * head_length)


def local_general(
    hidden,
    queries,
    kv_cache,
    w_kv,
    store_a,
    store_b,
    lengths,
    arrival_from,
    arrival_slot,
    resident_adapter,
    arrival_adapter,
    hot_holder,
    hot_dest,
):
    my_index = lax.axis_index("replica")
    replicas = lax.axis_size("replica")
    resident = kv_cache.shape[0]
    arrive = arrival_from.shape[1]
    request_slot_count = resident + arrive
    decode_step_count = hidden.shape[1]
    head_length = queries.shape[3]
    local_key_value = kv_cache.shape[2]
    slot_total = store_a.shape[0]
    hot_total = hot_holder.shape[0]
    spans = hot_total // COPIES
    my_from = lax.dynamic_index_in_dim(arrival_from, my_index, 0, keepdims=False)
    my_slot = lax.dynamic_index_in_dim(arrival_slot, my_index, 0, keepdims=False)
    own_ids = my_index * resident + jnp.arange(resident, dtype=jnp.int32)
    leaving_ids = (arrival_from * resident + arrival_slot).reshape(-1)
    staying = jnp.logical_not(jnp.any(own_ids[:, None] == leaving_ids[None, :], axis=1))
    live_mask = jnp.concatenate([staying, jnp.ones((arrive,), bool)])
    own_len = lax.dynamic_slice_in_dim(lengths, my_index * resident, resident)
    arrival_len = jnp.take(lengths, my_from * resident + my_slot)
    seen_len = jnp.concatenate([own_len, arrival_len])
    takes_mine = arrival_from == my_index
    sends_any = jnp.any(takes_mine, axis=1)
    send_slot = jnp.sum(jnp.where(takes_mine, arrival_slot, 0), axis=1)
    outgoing = jnp.take(kv_cache, send_slot, axis=0)
    outgoing = jnp.where(sends_any[:, None, None, None], outgoing, jnp.zeros((), jnp.bfloat16))
    incoming = lax.all_to_all(outgoing, "replica", split_axis=0, concat_axis=0, tiled=True)
    blocks = hot_dest.reshape(COPIES, spans, hot_dest.shape[1])
    holder_grid = hot_holder.reshape(COPIES, spans)
    holder_rep = holder_grid // slot_total
    mine = holder_rep == my_index
    has_one = jnp.any(mine, axis=1)
    local_pick = jnp.sum(jnp.where(mine, holder_grid % slot_total, 0), axis=1)

    def spread_rows(store):
        rows = jnp.take(store, local_pick, axis=0)
        rows = jnp.where(has_one[:, None, None, None], rows, jnp.zeros((), jnp.bfloat16))
        return rows.reshape(COPIES, replicas, -1).transpose(1, 0, 2)

    got_a, got_b = (
        lax.all_to_all(spread_rows(store_a), "replica", split_axis=0, concat_axis=0, tiled=True),
        lax.all_to_all(spread_rows(store_b), "replica", split_axis=0, concat_axis=0, tiled=True),
    )
    replica_ids = jnp.arange(replicas, dtype=jnp.int32)
    member = jnp.any(blocks[:, :, :, None] == replica_ids[None, None, None, :], axis=2).astype(
        jnp.int32
    )
    source_rep = jnp.sum(member * holder_rep[:, :, None], axis=1)
    copy_ids = jnp.arange(COPIES, dtype=jnp.int32)
    route_a = got_a[source_rep.T, copy_ids[None, :]]
    route_b = got_b[source_rep.T, copy_ids[None, :]]
    recv_a, recv_b = (
        lax.all_to_all(route_a, "replica", split_axis=0, concat_axis=0, tiled=True),
        lax.all_to_all(route_b, "replica", split_axis=0, concat_axis=0, tiled=True),
    )
    installed_a = recv_a.transpose(1, 0, 2).reshape((COPIES,) + store_a.shape[1:])
    installed_b = recv_b.transpose(1, 0, 2).reshape((COPIES,) + store_b.shape[1:])
    own_adapter = lax.dynamic_slice_in_dim(resident_adapter, my_index * resident, resident)
    my_choice = lax.dynamic_index_in_dim(arrival_adapter, my_index, 0, keepdims=False)
    adapt_a = jnp.concatenate(
        [jnp.take(store_a, own_adapter, axis=0), jnp.take(installed_a, my_choice, axis=0)]
    )
    adapter_up_weight = jnp.concatenate(
        [jnp.take(store_b, own_adapter, axis=0), jnp.take(installed_b, my_choice, axis=0)]
    )
    partial_value = jnp.einsum(
        "msd,mpkd->mspk", hidden, adapt_a, preferred_element_type=jnp.float32
    )
    base_projection = jnp.einsum(
        "msd,dgc->msgc",
        lax.all_gather(hidden, "tensor", axis=2, tiled=True),
        w_kv,
        preferred_element_type=jnp.float32,
    )
    down_projected = lax.psum(partial_value, "tensor")
    down_projected = down_projected.astype(jnp.bfloat16)
    adapter_update = jnp.einsum(
        "gnot,gote->gnoe", down_projected, adapter_up_weight, preferred_element_type=jnp.float32
    )
    adapter_update = (
        adapter_update.reshape(
            request_slot_count, decode_step_count, 2, local_key_value, head_length
        )
        .transpose(0, 1, 3, 2, 4)
        .reshape(request_slot_count, decode_step_count, local_key_value, 2 * head_length)
    )
    unrotated_key_value = base_projection + ADAPTER_SCALE * adapter_update
    positions = seen_len[:, None] + jnp.arange(decode_step_count, dtype=jnp.int32)[None, :]
    fresh_kv = jnp.concatenate(
        [
            rotate_keys(unrotated_key_value[..., :head_length], positions),
            unrotated_key_value[..., head_length:],
        ],
        axis=-1,
    ).astype(jnp.bfloat16)
    stay_out = attend(queries[:resident], kv_cache, own_len, fresh_kv[:resident])
    arrived = jnp.take(incoming, my_from, axis=0)
    row_ids = jnp.arange(kv_cache.shape[1], dtype=jnp.int32)
    arrived = jnp.where(
        (row_ids[None, :] < arrival_len[:, None])[:, :, None, None],
        arrived,
        jnp.zeros((), jnp.bfloat16),
    )
    move_out = attend(queries[resident:], arrived, arrival_len, fresh_kv[resident:])
    mixed_out = jnp.concatenate([stay_out, move_out], axis=0)
    attn_out = jnp.where(live_mask[:, None, None], mixed_out, 0.0).astype(jnp.bfloat16)
    new_kv = jnp.where(live_mask[:, None, None, None], fresh_kv, jnp.zeros((), jnp.bfloat16))
    return (attn_out, new_kv, arrived, installed_a, installed_b)


def partner(array, mask):
    return lax.ppermute(array, "replica", [(i, i ^ mask) for i in range(lax.axis_size("replica"))])


def shifted(array, step):
    size = lax.axis_size("tensor")
    return lax.ppermute(array, "tensor", [(i, (i + step) % size) for i in range(size)])


HEAD_UNITS = 5
SMEM = pl.BlockSpec(memory_space=pltpu.SMEM)
VMEM = pl.BlockSpec(memory_space=pltpu.VMEM)


def wanted_by(holder, dest, spans, replica, copy_id):
    row = jnp.int32(0)
    for span in range(spans):
        at = copy_id * spans + span
        row += jnp.where(dest[0, at] == replica, holder[at], 0)
    return row


def crossing(holder, dest, spans, slot_total, chip):
    items, count = [], jnp.int32(0)
    for copy_id in range(COPIES):
        for core in range(2):
            row = wanted_by(holder, dest, spans, 2 * chip + core, copy_id)
            crosses = row // (2 * slot_total) != chip
            items.append((copy_id, core, row, crosses, count))
            count = count + crosses.astype(jnp.int32)
    return items


def staged(moves, buffer, sems):
    def when(condition, action):
        if condition is None:
            action()
        else:
            pl.when(condition)(action)

    def begin(at, sources):
        for condition, source in sources:
            when(condition, pltpu.make_async_copy(source, buffer.at[at], sems.at[0, at]).start)

    def forward(at, targets):
        pltpu.make_async_copy(buffer.at[at], buffer.at[at], sems.at[0, at]).wait()
        for condition, target in targets:
            when(condition, pltpu.make_async_copy(buffer.at[at], target, sems.at[1, at]).start)

    def finish(at):
        pltpu.make_async_copy(buffer.at[at], buffer.at[at], sems.at[1, at]).wait()

    for at, (condition, sources, _) in enumerate(moves):
        when(condition, functools.partial(begin, at, sources))
    for at, (condition, _, targets) in enumerate(moves):
        when(condition, functools.partial(forward, at, targets))
    for at, (condition, _, _) in enumerate(moves):
        when(condition, functools.partial(finish, at))


def collect_kernel(spans, slot_total, masks, *refs):
    (me_ref, arrival_from, arrival_slot, holder, kv_cache, store_a, store_b) = refs[:7]
    leaving, (rows_b, rows_a) = refs[7 : 7 + len(masks)], refs[7 + len(masks) : 9 + len(masks)]
    buffers, semaphores = refs[9 + len(masks) : 12 + len(masks)], refs[12 + len(masks) :]
    me = me_ref[0]
    moves = []
    for i, mask in enumerate(masks):
        to = me ^ mask
        slot = jnp.int32(0)
        for a in range(arrival_from.shape[0]):
            slot += jnp.where(arrival_from[a, to] == me, arrival_slot[a, to], 0)
        moves.append((None, [(None, kv_cache.at[slot])], [(None, leaving[i])]))
    groups = [moves]
    held = []
    for copy_id in range(COPIES):
        slot = jnp.int32(0)
        for span in range(spans):
            row = holder[copy_id * spans + span]
            slot += jnp.where(row // slot_total == me, row % slot_total, 0)
        held.append(slot)
    for table, rows in ((store_a, rows_a), (store_b, rows_b)):
        groups.append(
            [
                (None, [(None, table.at[slot])], [(None, rows.at[copy_id])])
                for copy_id, slot in enumerate(held)
            ]
        )
    for moves, buffer, sems in zip(groups, buffers, semaphores):
        for at, (_, ((_, source),), _) in enumerate(moves):
            pltpu.make_async_copy(source, buffer.at[at], sems.at[0, at]).start()
    for moves, buffer, sems in zip(groups, buffers, semaphores):
        for at, (_, _, ((_, target),)) in enumerate(moves):
            pltpu.make_async_copy(buffer.at[at], buffer.at[at], sems.at[0, at]).wait()
            pltpu.make_async_copy(buffer.at[at], target, sems.at[1, at]).start()
    for moves, buffer, sems in zip(groups, buffers, semaphores):
        for at in range(len(moves)):
            pltpu.make_async_copy(buffer.at[at], buffer.at[at], sems.at[1, at]).wait()


def pack_kernel(spans, slot_total, *refs):
    (me_ref, holder, dest, store_a, store_b, sibling_a, sibling_b) = refs[:7]
    across_b, head, *tails = refs[7:-5]
    extra, buffer_b, buffer_a, sems_b, sems_a = refs[-5:]
    me = me_ref[0]
    core = me % 2
    chip = 1 - me // 2
    items = crossing(holder, dest, spans, slot_total, chip)
    moves_b, moves_a = [], []
    for copy_id in range(COPIES):
        row = wanted_by(holder, dest, spans, 2 * chip + core, copy_id)
        own = row // slot_total == me
        sources = [
            (own, store_b.at[row % slot_total]),
            (jnp.logical_not(own), sibling_b.at[copy_id]),
        ]
        moves_b.append((None, sources, [(None, across_b.at[copy_id])]))
    for at, (copy_id, _, row, crosses, unit) in enumerate(items):
        own = row // slot_total == me
        sources = [
            (own, store_a.at[row % slot_total, core]),
            (jnp.logical_not(own), sibling_a.at[copy_id, core]),
        ]
        targets = [(unit < HEAD_UNITS, head.at[jnp.minimum(unit, HEAD_UNITS - 1)])]
        for i, tail in enumerate(tails):
            if at >= HEAD_UNITS + i:
                targets.append((unit == HEAD_UNITS + i, tail))
        moves_a.append((crosses, sources, targets))
    count = items[-1][4] + items[-1][3].astype(jnp.int32)
    extra[0] = jnp.clip(count - HEAD_UNITS, 0, len(tails))
    staged(moves_b, buffer_b, sems_b)
    staged(moves_a, buffer_a, sems_a)


def place_down_kernel(spans, slot_total, tail_units, *refs):
    (me_ref, holder, dest, sibling_a, head, head_other) = refs[:6]
    tails, tails_other = refs[6 : 6 + tail_units], refs[6 + tail_units : 6 + 2 * tail_units]
    out, buffer, sems = refs[-3:]
    me = me_ref[0]
    core = me % 2
    items = crossing(holder, dest, spans, slot_total, me // 2)
    moves = []
    for copy_id in range(COPIES):
        first, second = items[2 * copy_id], items[2 * copy_id + 1]
        crosses = jnp.where(core == 0, first[3].astype(jnp.int32), second[3].astype(jnp.int32))
        unit = jnp.where(core == 0, first[4], second[4])
        near = crosses == 0
        for side, (group, last) in enumerate(((head, tails), (head_other, tails_other))):
            half = core if side == 0 else 1 - core
            early = jnp.logical_and(crosses != 0, unit < HEAD_UNITS)
            sources = [
                (near, sibling_a.at[copy_id, half]),
                (early, group.at[jnp.minimum(unit, HEAD_UNITS - 1)]),
            ]
            for i, tail in enumerate(last):
                sources.append((jnp.logical_and(crosses != 0, unit == HEAD_UNITS + i), tail))
            moves.append((None, sources, [(None, out.at[copy_id, half])]))
    staged(moves, buffer, sems)


def copy_call(kernel, tables, arrays, shapes, scratch, scalars=()):
    hbm = pl.BlockSpec(memory_space=pl.ANY)
    return pl.pallas_call(
        kernel,
        out_shape=[jax.ShapeDtypeStruct(shape, arrays[0].dtype) for shape in shapes]
        + [jax.ShapeDtypeStruct(shape, jnp.int32) for shape in scalars],
        in_specs=[SMEM] * len(tables) + [hbm] * len(arrays),
        out_specs=[hbm] * len(shapes) + [SMEM] * len(scalars),
        scratch_shapes=[pltpu.VMEM(shape, arrays[0].dtype) for shape in scratch]
        + [pltpu.SemaphoreType.DMA((2, shape[0])) for shape in scratch],
    )(*tables, *arrays)


def project_kernel(spans, slot_total, resident, steps, masks, *refs):
    (me_ref, resident_adapter, arrival_adapter, holder, dest, hidden, *others) = refs[: 6 + len(masks)]
    store, out, left, adapters = refs[-4:]
    me = me_ref[0]
    adapter = pl.program_id(0)
    base = hidden.shape[0]
    block = others[0].shape[0]

    @pl.when(adapter == 0)
    def _():
        left[0:base] = hidden[...]
        for i, other in enumerate(others):
            left[base + i * block : base + (i + 1) * block] = other[...]
        out[...] = jnp.zeros_like(out)
        ids = lax.broadcasted_iota(jnp.int32, out.shape, 0) // steps
        own = jnp.full(out.shape, -1, jnp.int32)
        for slot in range(resident):
            own = jnp.where(ids == slot, resident_adapter[me * resident + slot], own)
        for i, mask in enumerate((0,) + masks):
            replica = me ^ mask
            first = resident if i == 0 else (base + (i - 1) * block) // steps
            for a in range(arrival_adapter.shape[0]):
                chosen = arrival_adapter[a, replica]
                row = jnp.int32(0)
                for copy_id in range(COPIES):
                    wanted = wanted_by(holder, dest, spans, replica, copy_id)
                    row += jnp.where(chosen == copy_id, wanted, 0)
                here = jnp.where(row // slot_total == me, row % slot_total, -1)
                own = jnp.where(ids == first + a, here, own)
        adapters[...] = own

    product = lax.dot_general(
        left[...], store[0], (((1,), (1,)), ((), ())), preferred_element_type=jnp.float32
    )
    out[...] += jnp.where(adapters[...] == adapter, product, 0.0)


def gather_kernel(shard_ref, *refs):
    out = refs[-1]
    count = len(refs) - 1
    width = refs[0].shape[1]
    for step, ref in enumerate(refs[:-1]):
        source = lax.rem(shard_ref[0] + count - step, count)
        out[:, pl.ds(pl.multiple_of(source * width, width), width)] = ref[...]


def attend_kernel(spans, masks, resident, steps, kv_heads, head_length, *refs):
    (me_ref, lengths, arrival_from, arrival_slot, resident_adapter, arrival_adapter) = refs[:6]
    holder, dest, total, *returned = refs[6 : 9 + len(masks)]
    came = refs[9 + len(masks) : 9 + 2 * len(masks)]
    store_b, sibling_b, across_b, base, queries, cache = refs[9 + 2 * len(masks) : -5]
    out, new_kv, arrived, installed_b, fresh_ref = refs[-5:]
    me = me_ref[0]
    arrive = arrival_from.shape[0]
    replicas = arrival_from.shape[1]
    slots = resident + arrive
    row_count = base.shape[1]
    rank = store_b.shape[1] // 2
    slot_total = store_b.shape[0]
    half = head_length // 2
    seen = [lengths[me * resident + slot] for slot in range(resident)]
    for a in range(arrive):
        seen.append(lengths[arrival_from[a, me] * resident + arrival_slot[a, me]])

    for a in range(arrive):
        for ref, mask in zip(came, masks):

            @pl.when(arrival_from[a, me] == me ^ mask)
            def _():
                arrived[a] = ref[...]

        def clear(row, carry):
            arrived[a, row] = jnp.zeros(arrived.shape[2:], arrived.dtype)
            return carry

        lax.fori_loop(seen[resident + a], arrived.shape[1], clear, 0)
    for copy_id in range(COPIES):
        near = wanted_by(holder, dest, spans, me, copy_id) // (2 * slot_total) == me // 2

        @pl.when(near)
        def _():
            installed_b[copy_id] = sibling_b[copy_id]

        @pl.when(jnp.logical_not(near))
        def _():
            installed_b[copy_id] = across_b[copy_id]

    first = resident * steps
    last = total[first:row_count]
    for ref in returned:
        last = last + ref[...]
    down = jnp.concatenate([total[0:first], last], axis=0).astype(jnp.bfloat16)

    ids = lax.broadcasted_iota(jnp.int32, (row_count, 1), 0) // steps
    adapters = jnp.zeros((row_count, 1), jnp.int32)
    position = lax.broadcasted_iota(jnp.int32, (row_count, 1), 0) % steps
    for slot in range(slots):
        if slot < resident:
            adapter = resident_adapter[me * resident + slot]
        else:
            adapter = store_b.shape[0] + arrival_adapter[slot - resident, me]
        adapters = jnp.where(ids == slot, adapter, adapters)
        position = jnp.where(ids == slot, position + seen[slot], position)
    deltas = [jnp.zeros((row_count, store_b.shape[2]), jnp.float32) for _ in range(2)]
    for adapter in range(store_b.shape[0] + COPIES):
        if adapter < store_b.shape[0]:
            table = store_b[adapter]
        else:
            table = installed_b[adapter - store_b.shape[0]]
        for part in range(2):
            product = jnp.dot(
                down[:, part * rank : (part + 1) * rank],
                table[part * rank : (part + 1) * rank],
                preferred_element_type=jnp.float32,
            )
            deltas[part] = jnp.where(adapters == adapter, product, deltas[part])

    lane = lax.broadcasted_iota(jnp.int32, (1, half), 1).astype(jnp.float32)
    frequency = jnp.exp(lane * (-2.0 * math.log(ROPE_BASE) / head_length))
    angles = position.astype(jnp.float32) * frequency
    cosine, sine = jnp.cos(angles), jnp.sin(angles)
    dead = jnp.zeros((row_count, 1), jnp.bool_)
    gone = [jnp.int32(0)] * resident
    for q in range(replicas):
        for a in range(arrive):
            mine = arrival_from[a, q] == me
            slot = arrival_slot[a, q]
            dead = jnp.logical_or(dead, jnp.logical_and(ids == slot, mine))
            for n in range(resident):
                gone[n] = jnp.where(jnp.logical_and(mine, slot == n), 1, gone[n])
    for g in range(kv_heads):
        at = g * 2 * head_length
        columns = slice(g * head_length, (g + 1) * head_length)
        key = base[g, :, :head_length] + ADAPTER_SCALE * deltas[0][:, columns]
        value = base[g, :, head_length:] + ADAPTER_SCALE * deltas[1][:, columns]
        u, w = key[:, :half], key[:, half:]
        key = jnp.concatenate([u * cosine - w * sine, w * cosine + u * sine], axis=1)
        for part, piece in enumerate((key, value)):
            spot = slice(at + part * head_length, at + (part + 1) * head_length)
            rounded = piece.astype(jnp.bfloat16)
            fresh_ref[:, spot] = rounded.astype(jnp.float32)
            new_kv[:, spot] = jnp.where(dead, jnp.zeros_like(rounded), rounded)

    query_rows = queries.shape[1]
    heads = query_rows // steps
    row = lax.broadcasted_iota(jnp.int32, (query_rows, 1), 0)
    step_of = row // heads
    group_of = row % heads // (heads // kv_heads)
    cache_rows = cache.shape[1] * kv_heads
    column = lax.broadcasted_iota(jnp.int32, (query_rows, cache_rows), 1)
    same = column % kv_heads == group_of
    past_row = column // kv_heads
    scale = 1.0 / math.sqrt(head_length)
    for n in range(slots):
        stored = cache[n] if n < resident else arrived[n - resident]
        stored = stored.reshape(cache_rows, 2 * head_length)
        query = queries[n]
        score = (
            lax.dot_general(
                query,
                stored[:, :head_length],
                (((1,), (1,)), ((), ())),
                preferred_element_type=jnp.float32,
            )
            * scale
        )
        score = jnp.where(jnp.logical_and(same, past_row < seen[n]), score, -jnp.inf)
        query = query.astype(jnp.float32)
        recent, values = [], []
        for t in range(steps):
            line = fresh_ref[n * steps + t : n * steps + t + 1]
            key = jnp.zeros((query_rows, head_length), jnp.float32)
            value = key
            for g in range(kv_heads):
                at = g * 2 * head_length
                key = jnp.where(group_of == g, line[:, at : at + head_length], key)
                value = jnp.where(
                    group_of == g, line[:, at + head_length : at + 2 * head_length], value
                )
            fit = jnp.sum(query * key, axis=1, keepdims=True) * scale
            recent.append(jnp.where(step_of >= t, fit, -jnp.inf))
            values.append(value)
        peak = jnp.max(score, axis=1, keepdims=True)
        for fit in recent:
            peak = jnp.maximum(peak, fit)
        past_exp = jnp.exp(score - peak)
        recent_exp = [jnp.exp(fit - peak) for fit in recent]
        denom = jnp.sum(past_exp, axis=1, keepdims=True)
        for term in recent_exp:
            denom = denom + term
        weight = (past_exp / denom).astype(jnp.bfloat16)
        mixed = jnp.dot(weight, stored[:, head_length:], preferred_element_type=jnp.float32)
        for term, value in zip(recent_exp, values):
            mixed = mixed + (term / denom).astype(jnp.bfloat16).astype(jnp.float32) * value
        if n < resident:
            mixed = jnp.where(gone[n] != 0, 0.0, mixed)
        out[n] = mixed.astype(jnp.bfloat16)


def pairs_layer(
    hidden,
    queries,
    kv_cache,
    w_kv,
    store_a,
    store_b,
    lengths,
    arrival_from,
    arrival_slot,
    resident_adapter,
    arrival_adapter,
    hot_holder,
    hot_dest,
):
    me = lax.axis_index("replica")
    replicas = lax.axis_size("replica")
    shards = lax.axis_size("tensor")
    resident, _, kv_heads, head_pair = kv_cache.shape
    arrive = arrival_from.shape[1]
    slots = resident + arrive
    steps, features = hidden.shape[1:]
    heads, head_length = queries.shape[2:]
    slot_total = store_a.shape[0]
    rank = store_a.shape[2]
    spans = hot_holder.shape[0] // COPIES
    row_a, row_b = store_a.shape[1:], store_b.shape[1:]
    columns = store_b.shape[3]
    masks = tuple(range(1, replicas))
    me_table = jnp.reshape(me, (1,)).astype(jnp.int32)
    shard_table = jnp.reshape(lax.axis_index("tensor"), (1,)).astype(jnp.int32)
    from_table, slot_table, choice_table = arrival_from.T, arrival_slot.T, arrival_adapter.T
    dest_table = hot_dest.T

    used = slots * steps
    padded = -(-used // 8) * 8
    rows = jnp.pad(hidden.reshape(used, features), ((0, padded - used), (0, 0)))
    first = resident * steps
    block = padded - first
    other_rows = [partner(rows[first:], mask) for mask in masks]

    *leaving, rows_b, rows_a = copy_call(
        functools.partial(collect_kernel, spans, slot_total, masks),
        (me_table, from_table, slot_table, hot_holder),
        (kv_cache, store_a, store_b),
        [kv_cache.shape[1:]] * len(masks) + [(COPIES,) + row_b, (COPIES,) + row_a],
        [(len(masks),) + kv_cache.shape[1:], (COPIES,) + row_a, (COPIES,) + row_b],
    )
    sibling_a = partner(rows_a, 1)
    sibling_b = partner(rows_b, 1)
    came = [partner(array, mask) for array, mask in zip(leaving, masks)]
    around = [rows] + [shifted(rows, step) for step in range(1, shards)]

    line_count = padded + len(masks) * block
    partial = pl.pallas_call(
        functools.partial(project_kernel, spans, slot_total, resident, steps, masks),
        out_shape=jax.ShapeDtypeStruct((line_count, 2 * rank), jnp.float32),
        grid=(slot_total,),
        in_specs=[SMEM] * 5
        + [pl.BlockSpec((padded, features), lambda i: (0, 0))]
        + [pl.BlockSpec((block, features), lambda i: (0, 0))] * len(masks)
        + [pl.BlockSpec((1, 2 * rank, features), lambda i: (i, 0, 0))],
        out_specs=pl.BlockSpec((line_count, 2 * rank), lambda i: (0, 0)),
        scratch_shapes=[
            pltpu.VMEM((line_count, features), hidden.dtype),
            pltpu.VMEM((line_count, 2 * rank), jnp.int32),
        ],
        name="project",
    )(
        me_table,
        resident_adapter,
        choice_table,
        hot_holder,
        dest_table,
        rows,
        *other_rows,
        store_a.reshape(slot_total, 2 * rank, features),
    )
    parts = [partial] + [shifted(partial, step) for step in range(1, shards)]

    unit_shape = row_a[1:]
    tail_units = 2 * COPIES - HEAD_UNITS
    across_b, head, *tails, extra = copy_call(
        functools.partial(pack_kernel, spans, slot_total),
        (me_table, hot_holder, dest_table),
        (store_a, store_b, sibling_a, sibling_b),
        [(COPIES,) + row_b, (HEAD_UNITS,) + unit_shape] + [unit_shape] * tail_units,
        [(COPIES,) + row_b, (2 * COPIES,) + unit_shape],
        [(1,)],
    )
    across_b = partner(across_b, 2)
    head = partner(head, 2)
    total = parts[0]
    for array in parts[1:]:
        total = total + array
    returned = [
        partner(total[padded + i * block : padded + (i + 1) * block], mask)
        for i, mask in enumerate(masks)
    ]

    full = pl.pallas_call(
        gather_kernel,
        out_shape=jax.ShapeDtypeStruct((padded, shards * features), hidden.dtype),
        in_specs=[SMEM] + [VMEM] * shards,
        out_specs=VMEM,
        name="gather",
    )(shard_table, *around)
    base = jnp.einsum("md,dgc->gmc", full, w_kv, preferred_element_type=jnp.float32)

    attn_out, new_kv, arrived, installed_b = pl.pallas_call(
        functools.partial(attend_kernel, spans, masks, resident, steps, kv_heads, head_length),
        out_shape=[
            jax.ShapeDtypeStruct((slots, steps * heads, head_length), jnp.bfloat16),
            jax.ShapeDtypeStruct((padded, kv_heads * head_pair), jnp.bfloat16),
            jax.ShapeDtypeStruct((arrive,) + kv_cache.shape[1:], jnp.bfloat16),
            jax.ShapeDtypeStruct((COPIES, 2 * rank, columns), jnp.bfloat16),
        ],
        in_specs=[SMEM] * 8 + [VMEM] * (1 + 2 * len(masks) + 6),
        out_specs=[VMEM] * 4,
        scratch_shapes=[pltpu.VMEM((padded, kv_heads * head_pair), jnp.float32)],
        name="attend",
    )(
        me_table,
        lengths,
        from_table,
        slot_table,
        resident_adapter,
        choice_table,
        hot_holder,
        dest_table,
        total,
        *returned,
        *came,
        store_b.reshape(slot_total, 2 * rank, columns),
        sibling_b.reshape(COPIES, 2 * rank, columns),
        across_b.reshape(COPIES, 2 * rank, columns),
        base,
        queries.reshape(slots, steps * heads, head_length),
        kv_cache,
    )
    installed_b = installed_b.reshape((COPIES,) + row_b)
    head, attn_out, new_kv = lax.optimization_barrier((head, attn_out, new_kv))
    attn_out = attn_out.reshape(slots, steps, heads * head_length)
    new_kv = new_kv[:used].reshape(slots, steps, kv_heads, head_pair)

    def finish(units):
        def branch(sibling_a, head, *tails):
            got = [partner(array, 2) for array in tails[:units]]
            head_other = partner(head, 1)
            other = [partner(array, 1) for array in got]
            (placed,) = copy_call(
                functools.partial(place_down_kernel, spans, slot_total, units),
                (me_table, hot_holder, dest_table),
                (sibling_a, head, head_other, *got, *other),
                [(COPIES,) + row_a],
                [(2 * COPIES,) + unit_shape],
            )
            return placed

        return branch

    branches = [finish(units) for units in range(tail_units + 1)]
    installed_a = lax.switch(extra[0], branches, sibling_a, head, *tails)
    return (attn_out, new_kv, arrived, installed_a, installed_b)


def local(*args):
    fan = args[-1].shape[1]
    if lax.axis_size("replica") == 4 and fan == 1:
        return pairs_layer(*args)
    return local_general(*args)


def solution(mesh):
    in_specs = (
        P(("parts", "replica"), None, "tensor"),
        P(("parts", "replica"), None, "tensor", None),
        P(("parts", "replica"), None, "tensor", None),
        P(None, "tensor", None),
        P(("parts", "replica"), None, None, "tensor"),
        P(("parts", "replica"), None, None, "tensor"),
        P("parts"),
        P("parts", None),
        P("parts", None),
        P("parts"),
        P("parts", None),
        P("parts"),
        P("parts", None),
    )
    out_specs = (
        P(("parts", "replica"), None, "tensor"),
        P(("parts", "replica"), None, "tensor", None),
        P(("parts", "replica"), None, "tensor", None),
        P(("parts", "replica"), None, None, "tensor"),
        P(("parts", "replica"), None, None, "tensor"),
    )
    return jax.shard_map(local, mesh=mesh, in_specs=in_specs, out_specs=out_specs, check_vma=False)
```

```python
import functools
import math

import jax
import jax.numpy as jnp
from jax import lax
from jax.experimental import pallas as pl
from jax.experimental.pallas import tpu as pltpu
from jax.sharding import PartitionSpec as P


COPIES = 4


ADAPTER_SCALE = 2.0
ROPE_BASE = 500000.0


def rotate_keys(key_rows, positions):
    head_length = key_rows.shape[-1]
    half_size = head_length // 2
    frequency = ROPE_BASE ** (-(jnp.arange(half_size, dtype=jnp.float32) * 2.0 / head_length))
    angles = positions.astype(jnp.float32)[:, :, None, None] * frequency
    cosine = jnp.cos(angles)
    sine_val = jnp.sin(angles)
    first_half = key_rows[..., :half_size]
    second_half = key_rows[..., half_size:]
    return jnp.concatenate(
        [
            first_half * cosine - second_half * sine_val,
            second_half * cosine + first_half * sine_val,
        ],
        axis=-1,
    )


def attend(queries, stored, lengths_now, fresh_kv):
    request_slot_count, decode_step_count, heads_local, head_length = queries.shape
    local_key_value = stored.shape[2]
    group_size = heads_local // local_key_value
    grouped = queries.reshape(
        request_slot_count, decode_step_count, local_key_value, group_size, head_length
    )
    score_scale = 1.0 / math.sqrt(head_length)
    past_scores = (
        jnp.einsum(
            "msgjd,mcgd->msgjc",
            grouped,
            stored[..., :head_length],
            preferred_element_type=jnp.float32,
        )
        * score_scale
    )
    recent_scores = (
        jnp.einsum(
            "msgjd,mtgd->msgjt",
            grouped,
            fresh_kv[..., :head_length],
            preferred_element_type=jnp.float32,
        )
        * score_scale
    )
    row_ids = jnp.arange(stored.shape[1], dtype=jnp.int32)
    past_ok = (row_ids[None, :] < lengths_now[:, None])[:, None, None, None, :]
    step_ids = jnp.arange(decode_step_count, dtype=jnp.int32)
    recent_ok = (step_ids[None, :] <= step_ids[:, None])[None, :, None, None, :]
    past_scores = jnp.where(past_ok, past_scores, -jnp.inf)
    recent_scores = jnp.where(recent_ok, recent_scores, -jnp.inf)
    peak_score = jnp.maximum(jnp.max(past_scores, -1), jnp.max(recent_scores, -1))[..., None]
    past_exp = jnp.exp(past_scores - peak_score)
    recent_exp = jnp.exp(recent_scores - peak_score)
    denom_sum = jnp.sum(past_exp, -1, keepdims=True) + jnp.sum(recent_exp, -1, keepdims=True)
    past_w = (past_exp / denom_sum).astype(jnp.bfloat16)
    recent_w = (recent_exp / denom_sum).astype(jnp.bfloat16)
    mixed_out = jnp.einsum(
        "msgjc,mcgd->msgjd", past_w, stored[..., head_length:], preferred_element_type=jnp.float32
    )
    mixed_out = mixed_out + jnp.einsum(
        "msgjt,mtgd->msgjd",
        recent_w,
        fresh_kv[..., head_length:],
        preferred_element_type=jnp.float32,
    )
    return mixed_out.reshape(request_slot_count, decode_step_count, heads_local * head_length)


def local_general(
    hidden,
    queries,
    kv_cache,
    w_kv,
    store_a,
    store_b,
    lengths,
    arrival_from,
    arrival_slot,
    resident_adapter,
    arrival_adapter,
    hot_holder,
    hot_dest,
):
    my_index = lax.axis_index("replica")
    replicas = lax.axis_size("replica")
    resident = kv_cache.shape[0]
    arrive = arrival_from.shape[1]
    request_slot_count = resident + arrive
    decode_step_count = hidden.shape[1]
    head_length = queries.shape[3]
    local_key_value = kv_cache.shape[2]
    slot_total = store_a.shape[0]
    hot_total = hot_holder.shape[0]
    spans = hot_total // COPIES
    my_from = lax.dynamic_index_in_dim(arrival_from, my_index, 0, keepdims=False)
    my_slot = lax.dynamic_index_in_dim(arrival_slot, my_index, 0, keepdims=False)
    own_ids = my_index * resident + jnp.arange(resident, dtype=jnp.int32)
    leaving_ids = (arrival_from * resident + arrival_slot).reshape(-1)
    staying = jnp.logical_not(jnp.any(own_ids[:, None] == leaving_ids[None, :], axis=1))
    live_mask = jnp.concatenate([staying, jnp.ones((arrive,), bool)])
    own_len = lax.dynamic_slice_in_dim(lengths, my_index * resident, resident)
    arrival_len = jnp.take(lengths, my_from * resident + my_slot)
    seen_len = jnp.concatenate([own_len, arrival_len])
    takes_mine = arrival_from == my_index
    sends_any = jnp.any(takes_mine, axis=1)
    send_slot = jnp.sum(jnp.where(takes_mine, arrival_slot, 0), axis=1)
    outgoing = jnp.take(kv_cache, send_slot, axis=0)
    outgoing = jnp.where(sends_any[:, None, None, None], outgoing, jnp.zeros((), jnp.bfloat16))
    incoming = lax.all_to_all(outgoing, "replica", split_axis=0, concat_axis=0, tiled=True)
    blocks = hot_dest.reshape(COPIES, spans, hot_dest.shape[1])
    holder_grid = hot_holder.reshape(COPIES, spans)
    holder_rep = holder_grid // slot_total
    mine = holder_rep == my_index
    has_one = jnp.any(mine, axis=1)
    local_pick = jnp.sum(jnp.where(mine, holder_grid % slot_total, 0), axis=1)

    def spread_rows(store):
        rows = jnp.take(store, local_pick, axis=0)
        rows = jnp.where(has_one[:, None, None, None], rows, jnp.zeros((), jnp.bfloat16))
        return rows.reshape(COPIES, replicas, -1).transpose(1, 0, 2)

    got_a, got_b = (
        lax.all_to_all(spread_rows(store_a), "replica", split_axis=0, concat_axis=0, tiled=True),
        lax.all_to_all(spread_rows(store_b), "replica", split_axis=0, concat_axis=0, tiled=True),
    )
    replica_ids = jnp.arange(replicas, dtype=jnp.int32)
    member = jnp.any(blocks[:, :, :, None] == replica_ids[None, None, None, :], axis=2).astype(
        jnp.int32
    )
    source_rep = jnp.sum(member * holder_rep[:, :, None], axis=1)
    copy_ids = jnp.arange(COPIES, dtype=jnp.int32)
    route_a = got_a[source_rep.T, copy_ids[None, :]]
    route_b = got_b[source_rep.T, copy_ids[None, :]]
    recv_a, recv_b = (
        lax.all_to_all(route_a, "replica", split_axis=0, concat_axis=0, tiled=True),
        lax.all_to_all(route_b, "replica", split_axis=0, concat_axis=0, tiled=True),
    )
    installed_a = recv_a.transpose(1, 0, 2).reshape((COPIES,) + store_a.shape[1:])
    installed_b = recv_b.transpose(1, 0, 2).reshape((COPIES,) + store_b.shape[1:])
    own_adapter = lax.dynamic_slice_in_dim(resident_adapter, my_index * resident, resident)
    my_choice = lax.dynamic_index_in_dim(arrival_adapter, my_index, 0, keepdims=False)
    adapt_a = jnp.concatenate(
        [jnp.take(store_a, own_adapter, axis=0), jnp.take(installed_a, my_choice, axis=0)]
    )
    adapter_up_weight = jnp.concatenate(
        [jnp.take(store_b, own_adapter, axis=0), jnp.take(installed_b, my_choice, axis=0)]
    )
    partial_value = jnp.einsum(
        "msd,mpkd->mspk", hidden, adapt_a, preferred_element_type=jnp.float32
    )
    base_projection = jnp.einsum(
        "msd,dgc->msgc",
        lax.all_gather(hidden, "tensor", axis=2, tiled=True),
        w_kv,
        preferred_element_type=jnp.float32,
    )
    down_projected = lax.psum(partial_value, "tensor")
    down_projected = down_projected.astype(jnp.bfloat16)
    adapter_update = jnp.einsum(
        "gnot,gote->gnoe", down_projected, adapter_up_weight, preferred_element_type=jnp.float32
    )
    adapter_update = (
        adapter_update.reshape(
            request_slot_count, decode_step_count, 2, local_key_value, head_length
        )
        .transpose(0, 1, 3, 2, 4)
        .reshape(request_slot_count, decode_step_count, local_key_value, 2 * head_length)
    )
    unrotated_key_value = base_projection + ADAPTER_SCALE * adapter_update
    positions = seen_len[:, None] + jnp.arange(decode_step_count, dtype=jnp.int32)[None, :]
    fresh_kv = jnp.concatenate(
        [
            rotate_keys(unrotated_key_value[..., :head_length], positions),
            unrotated_key_value[..., head_length:],
        ],
        axis=-1,
    ).astype(jnp.bfloat16)
    stay_out = attend(queries[:resident], kv_cache, own_len, fresh_kv[:resident])
    arrived = jnp.take(incoming, my_from, axis=0)
    row_ids = jnp.arange(kv_cache.shape[1], dtype=jnp.int32)
    arrived = jnp.where(
        (row_ids[None, :] < arrival_len[:, None])[:, :, None, None],
        arrived,
        jnp.zeros((), jnp.bfloat16),
    )
    move_out = attend(queries[resident:], arrived, arrival_len, fresh_kv[resident:])
    mixed_out = jnp.concatenate([stay_out, move_out], axis=0)
    attn_out = jnp.where(live_mask[:, None, None], mixed_out, 0.0).astype(jnp.bfloat16)
    new_kv = jnp.where(live_mask[:, None, None, None], fresh_kv, jnp.zeros((), jnp.bfloat16))
    return (attn_out, new_kv, arrived, installed_a, installed_b)


def partner(array, mask):
    return lax.ppermute(array, "replica", [(i, i ^ mask) for i in range(lax.axis_size("replica"))])


def shifted(array, step):
    size = lax.axis_size("tensor")
    return lax.ppermute(array, "tensor", [(i, (i + step) % size) for i in range(size)])


HEAD_UNITS = 5
EARLY_UNITS = 4
SMEM = pl.BlockSpec(memory_space=pltpu.SMEM)
VMEM = pl.BlockSpec(memory_space=pltpu.VMEM)


def wanted_by(holder, dest, spans, replica, copy_id):
    row = jnp.int32(0)
    for span in range(spans):
        at = copy_id * spans + span
        row += jnp.where(dest[0, at] == replica, holder[at], 0)
    return row


def crossing(holder, dest, spans, slot_total, chip):
    items, count = [], jnp.int32(0)
    for copy_id in range(COPIES):
        for core in range(2):
            row = wanted_by(holder, dest, spans, 2 * chip + core, copy_id)
            crosses = row // (2 * slot_total) != chip
            items.append((copy_id, core, row, crosses, count))
            count = count + crosses.astype(jnp.int32)
    return items


def staged(groups):
    def when(condition, action):
        if condition is None:
            action()
        else:
            pl.when(condition)(action)

    def begin(at, sources, buffer, sems):
        for condition, source in sources:
            when(condition, pltpu.make_async_copy(source, buffer.at[at], sems.at[0, at]).start)

    def forward(at, targets, buffer, sems):
        pltpu.make_async_copy(buffer.at[at], buffer.at[at], sems.at[0, at]).wait()
        for condition, target in targets:
            when(condition, pltpu.make_async_copy(buffer.at[at], target, sems.at[1, at]).start)

    def finish(at, buffer, sems):
        pltpu.make_async_copy(buffer.at[at], buffer.at[at], sems.at[1, at]).wait()

    for moves, buffer, sems in groups:
        for at, (condition, sources, _) in enumerate(moves):
            when(condition, functools.partial(begin, at, sources, buffer, sems))
    for moves, buffer, sems in groups:
        for at, (condition, _, targets) in enumerate(moves):
            when(condition, functools.partial(forward, at, targets, buffer, sems))
    for moves, buffer, sems in groups:
        for at, (condition, _, _) in enumerate(moves):
            when(condition, functools.partial(finish, at, buffer, sems))


def collect_kernel(spans, slot_total, masks, *refs):
    (me_ref, arrival_from, arrival_slot, holder, kv_cache, store_a, store_b) = refs[:7]
    leaving, (rows_b, rows_a) = refs[7 : 7 + len(masks)], refs[7 + len(masks) : 9 + len(masks)]
    buffers, semaphores = refs[9 + len(masks) : 12 + len(masks)], refs[12 + len(masks) :]
    me = me_ref[0]
    moves = []
    for i, mask in enumerate(masks):
        to = me ^ mask
        slot = jnp.int32(0)
        for a in range(arrival_from.shape[0]):
            slot += jnp.where(arrival_from[a, to] == me, arrival_slot[a, to], 0)
        moves.append((None, [(None, kv_cache.at[slot])], [(None, leaving[i])]))
    groups = [moves]
    held = []
    for copy_id in range(COPIES):
        slot = jnp.int32(0)
        for span in range(spans):
            row = holder[copy_id * spans + span]
            slot += jnp.where(row // slot_total == me, row % slot_total, 0)
        held.append(slot)
    for table, rows in ((store_a, rows_a), (store_b, rows_b)):
        groups.append(
            [
                (None, [(None, table.at[slot])], [(None, rows.at[copy_id])])
                for copy_id, slot in enumerate(held)
            ]
        )
    staged(list(zip(groups, buffers, semaphores)))


def pack_kernel(spans, slot_total, *refs):
    (me_ref, holder, dest, store_a, store_b, sibling_a, sibling_b) = refs[:7]
    across_b, *units = refs[7:-5]
    extra, buffer_b, buffer_a, sems_b, sems_a = refs[-5:]
    me = me_ref[0]
    core = me % 2
    chip = 1 - me // 2
    items = crossing(holder, dest, spans, slot_total, chip)
    moves_b, moves_a = [], []
    for copy_id in range(COPIES):
        row = jnp.where(core == 0, items[2 * copy_id][2], items[2 * copy_id + 1][2])
        own = row // slot_total == me
        sources = [
            (own, store_b.at[row % slot_total]),
            (jnp.logical_not(own), sibling_b.at[copy_id]),
        ]
        moves_b.append((None, sources, [(None, across_b.at[copy_id])]))
    for at, (copy_id, _, row, crosses, unit) in enumerate(items):
        own = row // slot_total == me
        sources = [
            (own, store_a.at[row % slot_total, core]),
            (jnp.logical_not(own), sibling_a.at[copy_id, core]),
        ]
        targets = [(unit == i, units[i]) for i in range(at + 1)]
        moves_a.append((crosses, sources, targets))
    count = items[-1][4] + items[-1][3].astype(jnp.int32)
    extra[0] = jnp.clip(count - HEAD_UNITS, 0, len(units) - HEAD_UNITS)
    staged([(moves_b, buffer_b, sems_b), (moves_a, buffer_a, sems_a)])


def place_kernel(spans, slot_total, first_unit, unit_count, *refs):
    (me_ref, holder, dest, earlier) = refs[:4]
    got, other = refs[4 : 4 + unit_count], refs[4 + unit_count : 4 + 2 * unit_count]
    out, buffer, sems = refs[-3:]
    me = me_ref[0]
    core = me % 2
    items = crossing(holder, dest, spans, slot_total, me // 2)
    moves = []
    for copy_id in range(COPIES):
        one, two = items[2 * copy_id], items[2 * copy_id + 1]
        crosses = jnp.where(core == 0, one[3].astype(jnp.int32), two[3].astype(jnp.int32)) != 0
        unit = jnp.where(core == 0, one[4], two[4])
        possible = [i for i in range(unit_count) if first_unit + i <= 2 * copy_id + 1]
        if first_unit and not possible:
            continue
        for half, arrays in ((core, got), (1 - core, other)):
            sources = []
            if first_unit:
                active = jnp.logical_and(crosses, unit >= first_unit)
            else:
                near = jnp.logical_not(crosses)
                active = jnp.logical_or(near, unit < unit_count)
                sources.append((near, earlier.at[copy_id, half]))
            for i in possible:
                hit = jnp.logical_and(crosses, unit == first_unit + i)
                sources.append((hit, arrays[i]))
            moves.append((active, sources, [(None, out.at[copy_id, half])]))
    staged([(moves, buffer, sems)])


def copy_call(kernel, tables, arrays, shapes, scratch, scalars=(), aliases=None):
    hbm = pl.BlockSpec(memory_space=pltpu.HBM)
    return pl.pallas_call(
        kernel,
        out_shape=[pltpu.HBM(shape, arrays[0].dtype) for shape in shapes]
        + [jax.ShapeDtypeStruct(shape, jnp.int32) for shape in scalars],
        in_specs=[SMEM] * len(tables) + [hbm] * len(arrays),
        out_specs=[hbm] * len(shapes) + [SMEM] * len(scalars),
        scratch_shapes=[pltpu.VMEM(shape, arrays[0].dtype) for shape in scratch]
        + [pltpu.SemaphoreType.DMA((2, shape[0])) for shape in scratch],
        input_output_aliases=aliases or {},
    )(*tables, *arrays)


def project_kernel(spans, slot_total, resident, steps, masks, *refs):
    (me_ref, resident_adapter, arrival_adapter, holder, dest, hidden, *others) = refs[: 6 + len(masks)]
    store, *outs, left, adapters, sums = refs[6 + len(masks) :]
    me = me_ref[0]
    group = pl.program_id(0)
    base = hidden.shape[0]
    block = others[0].shape[0]
    width = sums.shape[1]
    per_step = store.shape[1] // width

    @pl.when(group == 0)
    def _():
        left[0:base] = hidden[...]
        for i, other in enumerate(others):
            left[base + i * block : base + (i + 1) * block] = other[...]
        sums[...] = jnp.zeros_like(sums)
        ids = lax.broadcasted_iota(jnp.int32, sums.shape, 0) // steps
        own = jnp.full(sums.shape, -1, jnp.int32)
        for slot in range(resident):
            own = jnp.where(ids == slot, resident_adapter[me * resident + slot], own)
        for i, mask in enumerate((0,) + masks):
            replica = me ^ mask
            first = resident if i == 0 else (base + (i - 1) * block) // steps
            for a in range(arrival_adapter.shape[0]):
                chosen = arrival_adapter[a, replica]
                row = jnp.int32(0)
                for span in range(spans):
                    at = chosen * spans + span
                    row += jnp.where(dest[0, at] == replica, holder[at], 0)
                here = jnp.where(row // slot_total == me, row % slot_total, -1)
                own = jnp.where(ids == first + a, here, own)
        adapters[...] = own

    product = lax.dot_general(
        left[...], store[0], (((1,), (1,)), ((), ())), preferred_element_type=jnp.float32
    )
    for i in range(per_step):
        hit = adapters[...] == group * per_step + i
        sums[...] += jnp.where(hit, product[:, i * width : (i + 1) * width], 0.0)

    @pl.when(group == pl.num_programs(0) - 1)
    def _():
        outs[0][...] = sums[0:base]
        for i, out in enumerate(outs[1:]):
            out[...] = sums[base + i * block : base + (i + 1) * block]


def gather_kernel(shard_ref, *refs):
    out = refs[-1]
    count = len(refs) - 1
    width = refs[0].shape[1]
    for step, ref in enumerate(refs[:-1]):
        source = lax.rem(shard_ref[0] + count - step, count)
        out[:, pl.ds(pl.multiple_of(source * width, width), width)] = ref[...]


def attend_kernel(spans, masks, resident, steps, kv_heads, head_length, *refs):
    (me_ref, lengths, arrival_from, arrival_slot, resident_adapter, arrival_adapter) = refs[:6]
    holder, dest, *parts = refs[6 : -11 - len(masks)]
    came = refs[-11 - len(masks) : -11]
    store_b, sibling_b, across_b, base, queries, cache = refs[-11:-5]
    out, new_kv, arrived, installed_b, fresh_ref = refs[-5:]
    me = me_ref[0]
    arrive = arrival_from.shape[0]
    replicas = arrival_from.shape[1]
    slots = resident + arrive
    row_count = base.shape[1]
    rank = store_b.shape[1] // 2
    slot_total = store_b.shape[0]
    half = head_length // 2
    seen = [lengths[me * resident + slot] for slot in range(resident)]
    for a in range(arrive):
        seen.append(lengths[arrival_from[a, me] * resident + arrival_slot[a, me]])

    for a in range(arrive):
        for ref, mask in zip(came, masks):

            @pl.when(arrival_from[a, me] == me ^ mask)
            def _():
                arrived[a] = ref[...]

        def clear(row, carry):
            arrived[a, row] = jnp.zeros(arrived.shape[2:], arrived.dtype)
            return carry

        lax.fori_loop(seen[resident + a], arrived.shape[1], clear, 0)
    for copy_id in range(COPIES):
        near = wanted_by(holder, dest, spans, me, copy_id) // (2 * slot_total) == me // 2

        @pl.when(near)
        def _():
            installed_b[copy_id] = sibling_b[copy_id]

        @pl.when(jnp.logical_not(near))
        def _():
            installed_b[copy_id] = across_b[copy_id]

    total = parts[0][...]
    for part in parts[1:]:
        total = total + part[...]
    down = total.astype(jnp.bfloat16)

    ids = lax.broadcasted_iota(jnp.int32, (row_count, 1), 0) // steps
    adapters = jnp.zeros((row_count, 1), jnp.int32)
    position = lax.broadcasted_iota(jnp.int32, (row_count, 1), 0) % steps
    for slot in range(slots):
        if slot < resident:
            adapter = resident_adapter[me * resident + slot]
        else:
            adapter = store_b.shape[0] + arrival_adapter[slot - resident, me]
        adapters = jnp.where(ids == slot, adapter, adapters)
        position = jnp.where(ids == slot, position + seen[slot], position)
    deltas = [jnp.zeros((row_count, store_b.shape[2]), jnp.float32) for _ in range(2)]
    for adapter in range(store_b.shape[0] + COPIES):
        if adapter < store_b.shape[0]:
            table = store_b[adapter]
        else:
            table = installed_b[adapter - store_b.shape[0]]
        for part in range(2):
            product = jnp.dot(
                down[:, part * rank : (part + 1) * rank],
                table[part * rank : (part + 1) * rank],
                preferred_element_type=jnp.float32,
            )
            deltas[part] = jnp.where(adapters == adapter, product, deltas[part])

    lane = lax.broadcasted_iota(jnp.int32, (1, half), 1).astype(jnp.float32)
    frequency = jnp.exp(lane * (-2.0 * math.log(ROPE_BASE) / head_length))
    angles = position.astype(jnp.float32) * frequency
    cosine, sine = jnp.cos(angles), jnp.sin(angles)
    dead = jnp.zeros((row_count, 1), jnp.bool_)
    gone = [jnp.int32(0)] * resident
    for q in range(replicas):
        for a in range(arrive):
            mine = arrival_from[a, q] == me
            slot = arrival_slot[a, q]
            dead = jnp.logical_or(dead, jnp.logical_and(ids == slot, mine))
            for n in range(resident):
                gone[n] = jnp.where(jnp.logical_and(mine, slot == n), 1, gone[n])
    for g in range(kv_heads):
        at = g * 2 * head_length
        columns = slice(g * head_length, (g + 1) * head_length)
        key = base[g, :, :head_length] + ADAPTER_SCALE * deltas[0][:, columns]
        value = base[g, :, head_length:] + ADAPTER_SCALE * deltas[1][:, columns]
        u, w = key[:, :half], key[:, half:]
        key = jnp.concatenate([u * cosine - w * sine, w * cosine + u * sine], axis=1)
        for part, piece in enumerate((key, value)):
            spot = slice(at + part * head_length, at + (part + 1) * head_length)
            rounded = piece.astype(jnp.bfloat16)
            fresh_ref[:, spot] = rounded.astype(jnp.float32)
            new_kv[:, spot] = jnp.where(dead, jnp.zeros_like(rounded), rounded)

    query_rows = queries.shape[1]
    heads = query_rows // steps
    row = lax.broadcasted_iota(jnp.int32, (query_rows, 1), 0)
    step_of = row // heads
    group_of = row % heads // (heads // kv_heads)
    cache_rows = cache.shape[1] * kv_heads
    column = lax.broadcasted_iota(jnp.int32, (query_rows, cache_rows), 1)
    same = column % kv_heads == group_of
    past_row = column // kv_heads
    scale = 1.0 / math.sqrt(head_length)
    for n in range(slots):
        stored = cache[n] if n < resident else arrived[n - resident]
        stored = stored.reshape(cache_rows, 2 * head_length)
        query = queries[n]
        score = (
            lax.dot_general(
                query,
                stored[:, :head_length],
                (((1,), (1,)), ((), ())),
                preferred_element_type=jnp.float32,
            )
            * scale
        )
        score = jnp.where(jnp.logical_and(same, past_row < seen[n]), score, -jnp.inf)
        query = query.astype(jnp.float32)
        recent, values = [], []
        for t in range(steps):
            line = fresh_ref[n * steps + t : n * steps + t + 1]
            key = jnp.zeros((query_rows, head_length), jnp.float32)
            value = key
            for g in range(kv_heads):
                at = g * 2 * head_length
                key = jnp.where(group_of == g, line[:, at : at + head_length], key)
                value = jnp.where(
                    group_of == g, line[:, at + head_length : at + 2 * head_length], value
                )
            fit = jnp.sum(query * key, axis=1, keepdims=True) * scale
            recent.append(jnp.where(step_of >= t, fit, -jnp.inf))
            values.append(value)
        peak = jnp.max(score, axis=1, keepdims=True)
        for fit in recent:
            peak = jnp.maximum(peak, fit)
        past_exp = jnp.exp(score - peak)
        recent_exp = [jnp.exp(fit - peak) for fit in recent]
        denom = jnp.sum(past_exp, axis=1, keepdims=True)
        for term in recent_exp:
            denom = denom + term
        weight = (past_exp / denom).astype(jnp.bfloat16)
        mixed = jnp.dot(weight, stored[:, head_length:], preferred_element_type=jnp.float32)
        for term, value in zip(recent_exp, values):
            mixed = mixed + (term / denom).astype(jnp.bfloat16).astype(jnp.float32) * value
        if n < resident:
            mixed = jnp.where(gone[n] != 0, 0.0, mixed)
        out[n] = mixed.astype(jnp.bfloat16)


def pairs_layer(
    hidden,
    queries,
    kv_cache,
    w_kv,
    store_a,
    store_b,
    lengths,
    arrival_from,
    arrival_slot,
    resident_adapter,
    arrival_adapter,
    hot_holder,
    hot_dest,
):
    me = lax.axis_index("replica")
    replicas = lax.axis_size("replica")
    shards = lax.axis_size("tensor")
    resident, _, kv_heads, head_pair = kv_cache.shape
    arrive = arrival_from.shape[1]
    slots = resident + arrive
    steps, features = hidden.shape[1:]
    heads, head_length = queries.shape[2:]
    slot_total = store_a.shape[0]
    rank = store_a.shape[2]
    spans = hot_holder.shape[0] // COPIES
    row_a, row_b = store_a.shape[1:], store_b.shape[1:]
    columns = store_b.shape[3]
    masks = tuple(range(1, replicas))
    me_table = jnp.reshape(me, (1,)).astype(jnp.int32)
    shard_table = jnp.reshape(lax.axis_index("tensor"), (1,)).astype(jnp.int32)
    from_table, slot_table, choice_table = arrival_from.T, arrival_slot.T, arrival_adapter.T
    dest_table = hot_dest.T

    used = slots * steps
    padded = -(-used // 8) * 8
    rows = jnp.pad(hidden.reshape(used, features), ((0, padded - used), (0, 0)))
    first = resident * steps
    block = padded - first
    other_rows = [partner(rows[first:], mask) for mask in masks]

    *leaving, rows_b, rows_a = copy_call(
        functools.partial(collect_kernel, spans, slot_total, masks),
        (me_table, from_table, slot_table, hot_holder),
        (kv_cache, store_a, store_b),
        [kv_cache.shape[1:]] * len(masks) + [(COPIES,) + row_b, (COPIES,) + row_a],
        [(len(masks),) + kv_cache.shape[1:], (COPIES,) + row_a, (COPIES,) + row_b],
    )
    sibling_a = partner(rows_a, 1)
    sibling_b = partner(rows_b, 1)
    came = [partner(array, mask) for array, mask in zip(leaving, masks)]
    around = [rows] + [shifted(rows, step) for step in range(1, shards)]

    line_count = padded + len(masks) * block
    per_step = 2 if slot_total % 2 == 0 else 1
    partial, *sent = pl.pallas_call(
        functools.partial(project_kernel, spans, slot_total, resident, steps, masks),
        out_shape=[jax.ShapeDtypeStruct((padded, 2 * rank), jnp.float32)]
        + [jax.ShapeDtypeStruct((block, 2 * rank), jnp.float32)] * len(masks),
        grid=(slot_total // per_step,),
        in_specs=[SMEM] * 5
        + [pl.BlockSpec((padded, features), lambda i: (0, 0))]
        + [pl.BlockSpec((block, features), lambda i: (0, 0))] * len(masks)
        + [pl.BlockSpec((1, per_step * 2 * rank, features), lambda i: (i, 0, 0))],
        out_specs=[pl.BlockSpec((padded, 2 * rank), lambda i: (0, 0))]
        + [pl.BlockSpec((block, 2 * rank), lambda i: (0, 0))] * len(masks),
        scratch_shapes=[
            pltpu.VMEM((line_count, features), hidden.dtype),
            pltpu.VMEM((line_count, 2 * rank), jnp.int32),
            pltpu.VMEM((line_count, 2 * rank), jnp.float32),
        ],
        name="project",
    )(
        me_table,
        resident_adapter,
        choice_table,
        hot_holder,
        dest_table,
        rows,
        *other_rows,
        store_a.reshape(slot_total // per_step, per_step * 2 * rank, features),
    )
    returned = [partner(array, mask) for array, mask in zip(sent, masks)]
    last = partial[first:]
    for array in returned:
        last = last + array
    partial = jnp.concatenate([partial[:first], last])
    parts = [partial] + [shifted(partial, step) for step in range(1, shards)]

    unit_shape = row_a[1:]
    unit_total = 2 * COPIES
    across_b, *units, extra = copy_call(
        functools.partial(pack_kernel, spans, slot_total),
        (me_table, hot_holder, dest_table),
        (store_a, store_b, sibling_a, sibling_b),
        [(COPIES,) + row_b] + [unit_shape] * unit_total,
        [(COPIES,) + row_b, (unit_total,) + unit_shape],
        [(1,)],
    )
    across_b = partner(across_b, 2)
    got = [partner(array, 2) for array in units[:EARLY_UNITS]]
    got += [partner(array, 2) for array in units[EARLY_UNITS:HEAD_UNITS]]

    full = pl.pallas_call(
        gather_kernel,
        out_shape=jax.ShapeDtypeStruct((padded, shards * features), hidden.dtype),
        in_specs=[SMEM] + [VMEM] * shards,
        out_specs=VMEM,
        name="gather",
    )(shard_table, *around)
    base = jnp.einsum("md,dgc->gmc", full, w_kv, preferred_element_type=jnp.float32)

    attn_out, new_kv, arrived, installed_b = pl.pallas_call(
        functools.partial(attend_kernel, spans, masks, resident, steps, kv_heads, head_length),
        out_shape=[
            jax.ShapeDtypeStruct((slots, steps * heads, head_length), jnp.bfloat16),
            jax.ShapeDtypeStruct((padded, kv_heads * head_pair), jnp.bfloat16),
            jax.ShapeDtypeStruct((arrive,) + kv_cache.shape[1:], jnp.bfloat16),
            jax.ShapeDtypeStruct((COPIES, 2 * rank, columns), jnp.bfloat16),
        ],
        in_specs=[SMEM] * 8 + [VMEM] * (shards + len(masks) + 6),
        out_specs=[VMEM] * 4,
        scratch_shapes=[pltpu.VMEM((padded, kv_heads * head_pair), jnp.float32)],
        name="attend",
    )(
        me_table,
        lengths,
        from_table,
        slot_table,
        resident_adapter,
        choice_table,
        hot_holder,
        dest_table,
        *parts,
        *came,
        store_b.reshape(slot_total, 2 * rank, columns),
        sibling_b.reshape(COPIES, 2 * rank, columns),
        across_b.reshape(COPIES, 2 * rank, columns),
        base,
        queries.reshape(slots, steps * heads, head_length),
        kv_cache,
    )
    installed_b = installed_b.reshape((COPIES,) + row_b)
    attn_out = attn_out.reshape(slots, steps, heads * head_length)
    new_kv = new_kv[:used].reshape(slots, steps, kv_heads, head_pair)

    tables = (me_table, hot_holder, dest_table)
    other = [partner(array, 1) for array in got[:EARLY_UNITS]]
    (placed,) = copy_call(
        functools.partial(place_kernel, spans, slot_total, 0, EARLY_UNITS),
        tables,
        (sibling_a, *got[:EARLY_UNITS], *other),
        [(COPIES,) + row_a],
        [(unit_total,) + unit_shape],
    )

    def finish(count):
        def branch(placed, *arrays):
            late = list(arrays[: HEAD_UNITS - EARLY_UNITS])
            late += [partner(array, 2) for array in arrays[len(late) :][:count]]
            other = [partner(array, 1) for array in late]
            return copy_call(
                functools.partial(place_kernel, spans, slot_total, EARLY_UNITS, len(late)),
                tables,
                (placed, *late, *other),
                [(COPIES,) + row_a],
                [(unit_total,) + unit_shape],
                aliases={len(tables): 0},
            )[0]

        return branch

    branches = [finish(count) for count in range(unit_total - HEAD_UNITS + 1)]
    installed_a = lax.switch(
        extra[0], branches, placed, *got[EARLY_UNITS:], *units[HEAD_UNITS:]
    )
    return (attn_out, new_kv, arrived, installed_a, installed_b)


def local(*args):
    fan = args[-1].shape[1]
    if lax.axis_size("replica") == 4 and fan == 1:
        return pairs_layer(*args)
    return local_general(*args)


def solution(mesh):
    in_specs = (
        P(("parts", "replica"), None, "tensor"),
        P(("parts", "replica"), None, "tensor", None),
        P(("parts", "replica"), None, "tensor", None),
        P(None, "tensor", None),
        P(("parts", "replica"), None, None, "tensor"),
        P(("parts", "replica"), None, None, "tensor"),
        P("parts"),
        P("parts", None),
        P("parts", None),
        P("parts"),
        P("parts", None),
        P("parts"),
        P("parts", None),
    )
    out_specs = (
        P(("parts", "replica"), None, "tensor"),
        P(("parts", "replica"), None, "tensor", None),
        P(("parts", "replica"), None, "tensor", None),
        P(("parts", "replica"), None, None, "tensor"),
        P(("parts", "replica"), None, None, "tensor"),
    )
    return jax.shard_map(local, mesh=mesh, in_specs=in_specs, out_specs=out_specs, check_vma=False)
```

```python
import functools
import math

import jax
import jax.numpy as jnp
from jax import lax
from jax.experimental import pallas as pl
from jax.experimental.pallas import tpu as pltpu
from jax.sharding import PartitionSpec as P


COPIES = 4


ADAPTER_SCALE = 2.0
ROPE_BASE = 500000.0


def rotate_keys(key_rows, positions):
    head_length = key_rows.shape[-1]
    half_size = head_length // 2
    frequency = ROPE_BASE ** (-(jnp.arange(half_size, dtype=jnp.float32) * 2.0 / head_length))
    angles = positions.astype(jnp.float32)[:, :, None, None] * frequency
    cosine = jnp.cos(angles)
    sine_val = jnp.sin(angles)
    first_half = key_rows[..., :half_size]
    second_half = key_rows[..., half_size:]
    return jnp.concatenate(
        [
            first_half * cosine - second_half * sine_val,
            second_half * cosine + first_half * sine_val,
        ],
        axis=-1,
    )


def attend(queries, stored, lengths_now, fresh_kv):
    request_slot_count, decode_step_count, heads_local, head_length = queries.shape
    local_key_value = stored.shape[2]
    group_size = heads_local // local_key_value
    grouped = queries.reshape(
        request_slot_count, decode_step_count, local_key_value, group_size, head_length
    )
    score_scale = 1.0 / math.sqrt(head_length)
    past_scores = (
        jnp.einsum(
            "msgjd,mcgd->msgjc",
            grouped,
            stored[..., :head_length],
            preferred_element_type=jnp.float32,
        )
        * score_scale
    )
    recent_scores = (
        jnp.einsum(
            "msgjd,mtgd->msgjt",
            grouped,
            fresh_kv[..., :head_length],
            preferred_element_type=jnp.float32,
        )
        * score_scale
    )
    row_ids = jnp.arange(stored.shape[1], dtype=jnp.int32)
    past_ok = (row_ids[None, :] < lengths_now[:, None])[:, None, None, None, :]
    step_ids = jnp.arange(decode_step_count, dtype=jnp.int32)
    recent_ok = (step_ids[None, :] <= step_ids[:, None])[None, :, None, None, :]
    past_scores = jnp.where(past_ok, past_scores, -jnp.inf)
    recent_scores = jnp.where(recent_ok, recent_scores, -jnp.inf)
    peak_score = jnp.maximum(jnp.max(past_scores, -1), jnp.max(recent_scores, -1))[..., None]
    past_exp = jnp.exp(past_scores - peak_score)
    recent_exp = jnp.exp(recent_scores - peak_score)
    denom_sum = jnp.sum(past_exp, -1, keepdims=True) + jnp.sum(recent_exp, -1, keepdims=True)
    past_w = (past_exp / denom_sum).astype(jnp.bfloat16)
    recent_w = (recent_exp / denom_sum).astype(jnp.bfloat16)
    mixed_out = jnp.einsum(
        "msgjc,mcgd->msgjd", past_w, stored[..., head_length:], preferred_element_type=jnp.float32
    )
    mixed_out = mixed_out + jnp.einsum(
        "msgjt,mtgd->msgjd",
        recent_w,
        fresh_kv[..., head_length:],
        preferred_element_type=jnp.float32,
    )
    return mixed_out.reshape(request_slot_count, decode_step_count, heads_local * head_length)


def local_general(
    hidden,
    queries,
    kv_cache,
    w_kv,
    store_a,
    store_b,
    lengths,
    arrival_from,
    arrival_slot,
    resident_adapter,
    arrival_adapter,
    hot_holder,
    hot_dest,
):
    my_index = lax.axis_index("replica")
    replicas = lax.axis_size("replica")
    resident = kv_cache.shape[0]
    arrive = arrival_from.shape[1]
    request_slot_count = resident + arrive
    decode_step_count = hidden.shape[1]
    head_length = queries.shape[3]
    local_key_value = kv_cache.shape[2]
    slot_total = store_a.shape[0]
    hot_total = hot_holder.shape[0]
    spans = hot_total // COPIES
    my_from = lax.dynamic_index_in_dim(arrival_from, my_index, 0, keepdims=False)
    my_slot = lax.dynamic_index_in_dim(arrival_slot, my_index, 0, keepdims=False)
    own_ids = my_index * resident + jnp.arange(resident, dtype=jnp.int32)
    leaving_ids = (arrival_from * resident + arrival_slot).reshape(-1)
    staying = jnp.logical_not(jnp.any(own_ids[:, None] == leaving_ids[None, :], axis=1))
    live_mask = jnp.concatenate([staying, jnp.ones((arrive,), bool)])
    own_len = lax.dynamic_slice_in_dim(lengths, my_index * resident, resident)
    arrival_len = jnp.take(lengths, my_from * resident + my_slot)
    seen_len = jnp.concatenate([own_len, arrival_len])
    takes_mine = arrival_from == my_index
    sends_any = jnp.any(takes_mine, axis=1)
    send_slot = jnp.sum(jnp.where(takes_mine, arrival_slot, 0), axis=1)
    outgoing = jnp.take(kv_cache, send_slot, axis=0)
    outgoing = jnp.where(sends_any[:, None, None, None], outgoing, jnp.zeros((), jnp.bfloat16))
    incoming = lax.all_to_all(outgoing, "replica", split_axis=0, concat_axis=0, tiled=True)
    blocks = hot_dest.reshape(COPIES, spans, hot_dest.shape[1])
    holder_grid = hot_holder.reshape(COPIES, spans)
    holder_rep = holder_grid // slot_total
    mine = holder_rep == my_index
    has_one = jnp.any(mine, axis=1)
    local_pick = jnp.sum(jnp.where(mine, holder_grid % slot_total, 0), axis=1)

    def spread_rows(store):
        rows = jnp.take(store, local_pick, axis=0)
        rows = jnp.where(has_one[:, None, None, None], rows, jnp.zeros((), jnp.bfloat16))
        return rows.reshape(COPIES, replicas, -1).transpose(1, 0, 2)

    got_a, got_b = (
        lax.all_to_all(spread_rows(store_a), "replica", split_axis=0, concat_axis=0, tiled=True),
        lax.all_to_all(spread_rows(store_b), "replica", split_axis=0, concat_axis=0, tiled=True),
    )
    replica_ids = jnp.arange(replicas, dtype=jnp.int32)
    member = jnp.any(blocks[:, :, :, None] == replica_ids[None, None, None, :], axis=2).astype(
        jnp.int32
    )
    source_rep = jnp.sum(member * holder_rep[:, :, None], axis=1)
    copy_ids = jnp.arange(COPIES, dtype=jnp.int32)
    route_a = got_a[source_rep.T, copy_ids[None, :]]
    route_b = got_b[source_rep.T, copy_ids[None, :]]
    recv_a, recv_b = (
        lax.all_to_all(route_a, "replica", split_axis=0, concat_axis=0, tiled=True),
        lax.all_to_all(route_b, "replica", split_axis=0, concat_axis=0, tiled=True),
    )
    installed_a = recv_a.transpose(1, 0, 2).reshape((COPIES,) + store_a.shape[1:])
    installed_b = recv_b.transpose(1, 0, 2).reshape((COPIES,) + store_b.shape[1:])
    own_adapter = lax.dynamic_slice_in_dim(resident_adapter, my_index * resident, resident)
    my_choice = lax.dynamic_index_in_dim(arrival_adapter, my_index, 0, keepdims=False)
    adapt_a = jnp.concatenate(
        [jnp.take(store_a, own_adapter, axis=0), jnp.take(installed_a, my_choice, axis=0)]
    )
    adapter_up_weight = jnp.concatenate(
        [jnp.take(store_b, own_adapter, axis=0), jnp.take(installed_b, my_choice, axis=0)]
    )
    partial_value = jnp.einsum(
        "msd,mpkd->mspk", hidden, adapt_a, preferred_element_type=jnp.float32
    )
    base_projection = jnp.einsum(
        "msd,dgc->msgc",
        lax.all_gather(hidden, "tensor", axis=2, tiled=True),
        w_kv,
        preferred_element_type=jnp.float32,
    )
    down_projected = lax.psum(partial_value, "tensor")
    down_projected = down_projected.astype(jnp.bfloat16)
    adapter_update = jnp.einsum(
        "gnot,gote->gnoe", down_projected, adapter_up_weight, preferred_element_type=jnp.float32
    )
    adapter_update = (
        adapter_update.reshape(
            request_slot_count, decode_step_count, 2, local_key_value, head_length
        )
        .transpose(0, 1, 3, 2, 4)
        .reshape(request_slot_count, decode_step_count, local_key_value, 2 * head_length)
    )
    unrotated_key_value = base_projection + ADAPTER_SCALE * adapter_update
    positions = seen_len[:, None] + jnp.arange(decode_step_count, dtype=jnp.int32)[None, :]
    fresh_kv = jnp.concatenate(
        [
            rotate_keys(unrotated_key_value[..., :head_length], positions),
            unrotated_key_value[..., head_length:],
        ],
        axis=-1,
    ).astype(jnp.bfloat16)
    stay_out = attend(queries[:resident], kv_cache, own_len, fresh_kv[:resident])
    arrived = jnp.take(incoming, my_from, axis=0)
    row_ids = jnp.arange(kv_cache.shape[1], dtype=jnp.int32)
    arrived = jnp.where(
        (row_ids[None, :] < arrival_len[:, None])[:, :, None, None],
        arrived,
        jnp.zeros((), jnp.bfloat16),
    )
    move_out = attend(queries[resident:], arrived, arrival_len, fresh_kv[resident:])
    mixed_out = jnp.concatenate([stay_out, move_out], axis=0)
    attn_out = jnp.where(live_mask[:, None, None], mixed_out, 0.0).astype(jnp.bfloat16)
    new_kv = jnp.where(live_mask[:, None, None, None], fresh_kv, jnp.zeros((), jnp.bfloat16))
    return (attn_out, new_kv, arrived, installed_a, installed_b)


def partner(array, mask):
    return lax.ppermute(array, "replica", [(i, i ^ mask) for i in range(lax.axis_size("replica"))])


def shifted(array, step):
    size = lax.axis_size("tensor")
    return lax.ppermute(array, "tensor", [(i, (i + step) % size) for i in range(size)])


ALWAYS = ((0, 2), (2, 3), (5, 1))
AT_NEED = ((6, 1), (7, 1))
SMEM = pl.BlockSpec(memory_space=pltpu.SMEM)
VMEM = pl.BlockSpec(memory_space=pltpu.VMEM)


def wanted_by(holder, dest, spans, replica, copy_id):
    row = jnp.int32(0)
    for span in range(spans):
        at = copy_id * spans + span
        row += jnp.where(dest[0, at] == replica, holder[at], 0)
    return row


def crossing(holder, dest, spans, slot_total, chip):
    items, count = [], jnp.int32(0)
    for copy_id in range(COPIES):
        for core in range(2):
            row = wanted_by(holder, dest, spans, 2 * chip + core, copy_id)
            crosses = row // (2 * slot_total) != chip
            items.append((copy_id, core, row, crosses, count))
            count = count + crosses.astype(jnp.int32)
    return items


def staged(groups, meanwhile=None):
    def when(condition, action):
        if condition is None:
            action()
        else:
            pl.when(condition)(action)

    def begin(at, sources, buffer, sems):
        for condition, source in sources:
            when(condition, pltpu.make_async_copy(source, buffer.at[at], sems.at[0, at]).start)

    def forward(at, targets, buffer, sems):
        pltpu.make_async_copy(buffer.at[at], buffer.at[at], sems.at[0, at]).wait()
        for condition, target in targets:
            when(condition, pltpu.make_async_copy(buffer.at[at], target, sems.at[1, at]).start)

    def finish(at, buffer, sems):
        pltpu.make_async_copy(buffer.at[at], buffer.at[at], sems.at[1, at]).wait()

    for moves, buffer, sems in groups:
        for at, (condition, sources, _) in enumerate(moves):
            when(condition, functools.partial(begin, at, sources, buffer, sems))
    if meanwhile is not None:
        meanwhile()
    for moves, buffer, sems in groups:
        for at, (condition, _, targets) in enumerate(moves):
            when(condition, functools.partial(forward, at, targets, buffer, sems))
    for moves, buffer, sems in groups:
        for at, (condition, _, _) in enumerate(moves):
            when(condition, functools.partial(finish, at, buffer, sems))


def collect_kernel(spans, slot_total, masks, *refs):
    (me_ref, arrival_from, arrival_slot, holder, kv_cache, store_a, store_b, hidden) = refs[:8]
    *leaving, rows_a, rows_b, rows, asking = refs[8 : 12 + len(masks)]
    buffers, semaphores = refs[12 + len(masks) : 15 + len(masks)], refs[15 + len(masks) :]
    me = me_ref[0]
    moves = []
    for i, mask in enumerate(masks):
        to = me ^ mask
        slot = jnp.int32(0)
        for a in range(arrival_from.shape[0]):
            slot += jnp.where(arrival_from[a, to] == me, arrival_slot[a, to], 0)
        moves.append((None, [(None, kv_cache.at[slot])], [(None, leaving[i])]))
    groups = [moves]
    held = []
    for copy_id in range(COPIES):
        slot = jnp.int32(0)
        for span in range(spans):
            row = holder[copy_id * spans + span]
            slot += jnp.where(row // slot_total == me, row % slot_total, 0)
        held.append(slot)
    for table, target in ((store_a, rows_a), (store_b, rows_b)):
        groups.append(
            [
                (None, [(None, table.at[slot])], [(None, target.at[copy_id])])
                for copy_id, slot in enumerate(held)
            ]
        )

    def regroup():
        count = hidden.shape[0] * hidden.shape[1]
        start = rows.shape[0] - asking.shape[0]
        blank = jnp.zeros((rows.shape[0] - count, rows.shape[1]), rows.dtype)
        every = hidden[...].reshape(count, rows.shape[1])
        rows[...] = jnp.concatenate([every, blank], axis=0)
        asking[...] = rows[start:]

    staged(list(zip(groups, buffers, semaphores)), regroup)


def pack_kernel(spans, slot_total, *refs):
    (me_ref, holder, dest, store_a, store_b, sibling_a, sibling_b) = refs[:7]
    across_b, *units = refs[7:-5]
    spread = ALWAYS + AT_NEED
    extra, buffer_b, buffer_a, sems_b, sems_a = refs[-5:]
    me = me_ref[0]
    core = me % 2
    chip = 1 - me // 2
    items = crossing(holder, dest, spans, slot_total, chip)
    moves_b, moves_a = [], []
    for copy_id in range(COPIES):
        row = jnp.where(core == 0, items[2 * copy_id][2], items[2 * copy_id + 1][2])
        own = row // slot_total == me
        sources = [
            (own, store_b.at[row % slot_total]),
            (jnp.logical_not(own), sibling_b.at[copy_id]),
        ]
        moves_b.append((None, sources, [(None, across_b.at[copy_id])]))
    for at, (copy_id, _, row, crosses, unit) in enumerate(items):
        own = row // slot_total == me
        sources = [
            (own, store_a.at[row % slot_total, core]),
            (jnp.logical_not(own), sibling_a.at[copy_id, core]),
        ]
        targets = [
            (
                jnp.logical_and(unit >= start, unit < start + size),
                array.at[jnp.clip(unit - start, 0, size - 1)],
            )
            for array, (start, size) in zip(units, spread)
            if start <= at
        ]
        moves_a.append((crosses, sources, targets))
    count = items[-1][4] + items[-1][3].astype(jnp.int32)
    extra[0] = jnp.clip(count - AT_NEED[0][0], 0, len(AT_NEED))
    staged([(moves_b, buffer_b, sems_b), (moves_a, buffer_a, sems_a)])


def place_kernel(spans, slot_total, spread, *refs):
    (me_ref, holder, dest, earlier) = refs[:4]
    got, other = refs[4 : 4 + len(spread)], refs[4 + len(spread) : 4 + 2 * len(spread)]
    out, buffer, sems = refs[-3:]
    me = me_ref[0]
    core = me % 2
    first_unit = spread[0][0]
    past_unit = spread[-1][0] + spread[-1][1]
    items = crossing(holder, dest, spans, slot_total, me // 2)
    moves = []
    for copy_id in range(COPIES):
        one, two = items[2 * copy_id], items[2 * copy_id + 1]
        crosses = jnp.where(core == 0, one[3].astype(jnp.int32), two[3].astype(jnp.int32)) != 0
        unit = jnp.where(core == 0, one[4], two[4])
        possible = [i for i, (start, _) in enumerate(spread) if start <= 2 * copy_id + 1]
        if first_unit and not possible:
            continue
        here = jnp.logical_and(unit >= first_unit, unit < past_unit)
        for half, arrays in ((core, got), (1 - core, other)):
            sources = []
            active = jnp.logical_and(crosses, here)
            if not first_unit:
                near = jnp.logical_not(crosses)
                active = jnp.logical_or(near, here)
                sources.append((near, earlier.at[copy_id, half]))
            for i in possible:
                start, size = spread[i]
                hit = jnp.logical_and(unit >= start, unit < start + size)
                source = arrays[i].at[jnp.clip(unit - start, 0, size - 1)]
                sources.append((jnp.logical_and(crosses, hit), source))
            moves.append((active, sources, [(None, out.at[copy_id, half])]))
    staged([(moves, buffer, sems)])


def copy_call(kernel, tables, arrays, shapes, scratch, scalars=(), aliases=None, given=(), made=()):
    hbm = pl.BlockSpec(memory_space=pl.ANY)
    dtype = arrays[0].dtype
    return pl.pallas_call(
        kernel,
        out_shape=[pltpu.HBM(shape, dtype) for shape in shapes]
        + [jax.ShapeDtypeStruct(shape, dtype) for shape in made]
        + [jax.ShapeDtypeStruct(shape, jnp.int32) for shape in scalars],
        in_specs=[SMEM] * len(tables) + [hbm] * len(arrays) + [VMEM] * len(given),
        out_specs=[hbm] * len(shapes) + [VMEM] * len(made) + [SMEM] * len(scalars),
        scratch_shapes=[pltpu.VMEM(shape, dtype) for shape in scratch]
        + [pltpu.SemaphoreType.DMA((2, shape[0])) for shape in scratch],
        input_output_aliases=aliases or {},
    )(*tables, *arrays, *given)


def project_kernel(spans, slot_total, resident, steps, masks, *refs):
    (me_ref, resident_adapter, arrival_adapter, holder, dest, hidden, *others) = refs[: 6 + len(masks)]
    store, *outs, left, adapters, sums = refs[6 + len(masks) :]
    me = me_ref[0]
    group = pl.program_id(0)
    base = hidden.shape[0]
    block = others[0].shape[0]
    width = sums.shape[1]
    per_step = store.shape[1] // width

    @pl.when(group == 0)
    def _():
        left[0:base] = hidden[...]
        for i, other in enumerate(others):
            left[base + i * block : base + (i + 1) * block] = other[...]
        sums[...] = jnp.zeros_like(sums)
        ids = lax.broadcasted_iota(jnp.int32, sums.shape, 0) // steps
        own = jnp.full(sums.shape, -1, jnp.int32)
        for slot in range(resident):
            own = jnp.where(ids == slot, resident_adapter[me * resident + slot], own)
        for i, mask in enumerate((0,) + masks):
            replica = me ^ mask
            first = resident if i == 0 else (base + (i - 1) * block) // steps
            for a in range(arrival_adapter.shape[0]):
                chosen = arrival_adapter[a, replica]
                row = jnp.int32(0)
                for span in range(spans):
                    at = chosen * spans + span
                    row += jnp.where(dest[0, at] == replica, holder[at], 0)
                here = jnp.where(row // slot_total == me, row % slot_total, -1)
                own = jnp.where(ids == first + a, here, own)
        adapters[...] = own

    product = lax.dot_general(
        left[...], store[0], (((1,), (1,)), ((), ())), preferred_element_type=jnp.float32
    )
    for i in range(per_step):
        hit = adapters[...] == group * per_step + i
        sums[...] += jnp.where(hit, product[:, i * width : (i + 1) * width], 0.0)

    @pl.when(group == pl.num_programs(0) - 1)
    def _():
        outs[0][...] = sums[0:base]
        for i, out in enumerate(outs[1:]):
            out[...] = sums[base + i * block : base + (i + 1) * block]


def gather_kernel(shard_ref, *refs):
    out = refs[-1]
    count = len(refs) - 1
    width = refs[0].shape[1]
    for step, ref in enumerate(refs[:-1]):
        source = lax.rem(shard_ref[0] + count - step, count)
        out[:, pl.ds(pl.multiple_of(source * width, width), width)] = ref[...]


def attend_kernel(spans, masks, resident, steps, kv_heads, head_length, *refs):
    (me_ref, lengths, arrival_from, arrival_slot, resident_adapter, arrival_adapter) = refs[:6]
    holder, dest, *parts = refs[6 : -12 - len(masks)]
    came = refs[-12 - len(masks) : -12]
    store_b, sibling_b, across_b, base, queries, cache = refs[-12:-6]
    out, new_kv, arrived, installed_b, fresh_ref, mixed_ref = refs[-6:]
    me = me_ref[0]
    arrive = arrival_from.shape[0]
    replicas = arrival_from.shape[1]
    slots = resident + arrive
    row_count = base.shape[1]
    rank = store_b.shape[1] // 2
    slot_total = store_b.shape[0]
    half = head_length // 2
    seen = [lengths[me * resident + slot] for slot in range(resident)]
    for a in range(arrive):
        seen.append(lengths[arrival_from[a, me] * resident + arrival_slot[a, me]])

    for a in range(arrive):
        for ref, mask in zip(came, masks):

            @pl.when(arrival_from[a, me] == me ^ mask)
            def _():
                arrived[a] = ref[...]

        def clear(row, carry):
            arrived[a, row] = jnp.zeros(arrived.shape[2:], arrived.dtype)
            return carry

        lax.fori_loop(seen[resident + a], arrived.shape[1], clear, 0)
    for copy_id in range(COPIES):
        near = wanted_by(holder, dest, spans, me, copy_id) // (2 * slot_total) == me // 2

        @pl.when(near)
        def _():
            installed_b[copy_id] = sibling_b[copy_id]

        @pl.when(jnp.logical_not(near))
        def _():
            installed_b[copy_id] = across_b[copy_id]

    total = parts[0][...]
    for part in parts[1:]:
        total = total + part[...]
    down = total.astype(jnp.bfloat16)

    ids = lax.broadcasted_iota(jnp.int32, (row_count, 1), 0) // steps
    adapters = jnp.zeros((row_count, 1), jnp.int32)
    position = lax.broadcasted_iota(jnp.int32, (row_count, 1), 0) % steps
    for slot in range(slots):
        if slot < resident:
            adapter = resident_adapter[me * resident + slot]
        else:
            adapter = store_b.shape[0] + arrival_adapter[slot - resident, me]
        adapters = jnp.where(ids == slot, adapter, adapters)
        position = jnp.where(ids == slot, position + seen[slot], position)
    deltas = [jnp.zeros((row_count, store_b.shape[2]), jnp.float32) for _ in range(2)]
    for adapter in range(store_b.shape[0] + COPIES):
        if adapter < store_b.shape[0]:
            table = store_b[adapter]
        else:
            table = installed_b[adapter - store_b.shape[0]]
        for part in range(2):
            product = jnp.dot(
                down[:, part * rank : (part + 1) * rank],
                table[part * rank : (part + 1) * rank],
                preferred_element_type=jnp.float32,
            )
            deltas[part] = jnp.where(adapters == adapter, product, deltas[part])

    lane = lax.broadcasted_iota(jnp.int32, (1, half), 1).astype(jnp.float32)
    frequency = jnp.exp(lane * (-2.0 * math.log(ROPE_BASE) / head_length))
    angles = position.astype(jnp.float32) * frequency
    cosine, sine = jnp.cos(angles), jnp.sin(angles)
    dead = jnp.zeros((row_count, 1), jnp.bool_)
    gone = [jnp.int32(0)] * resident
    for q in range(replicas):
        for a in range(arrive):
            mine = arrival_from[a, q] == me
            slot = arrival_slot[a, q]
            dead = jnp.logical_or(dead, jnp.logical_and(ids == slot, mine))
            for n in range(resident):
                gone[n] = jnp.where(jnp.logical_and(mine, slot == n), 1, gone[n])
    for g in range(kv_heads):
        at = g * 2 * head_length
        columns = slice(g * head_length, (g + 1) * head_length)
        key = base[g, :, :head_length] + ADAPTER_SCALE * deltas[0][:, columns]
        value = base[g, :, head_length:] + ADAPTER_SCALE * deltas[1][:, columns]
        u, w = key[:, :half], key[:, half:]
        key = jnp.concatenate([u * cosine - w * sine, w * cosine + u * sine], axis=1)
        for part, piece in enumerate((key, value)):
            spot = slice(at + part * head_length, at + (part + 1) * head_length)
            rounded = piece.astype(jnp.bfloat16)
            fresh_ref[:, spot] = rounded.astype(jnp.float32)
            kept = jnp.where(dead, 0.0, rounded.astype(jnp.float32))[: slots * steps]
            lanes = slice(part * head_length, (part + 1) * head_length)
            new_kv[:, :, g, lanes] = kept.reshape(slots, steps, head_length).astype(jnp.bfloat16)

    query_rows = queries.shape[1]
    heads = query_rows // steps
    row = lax.broadcasted_iota(jnp.int32, (query_rows, 1), 0)
    step_of = row // heads
    group_of = row % heads // (heads // kv_heads)
    cache_rows = cache.shape[1] * kv_heads
    column = lax.broadcasted_iota(jnp.int32, (query_rows, cache_rows), 1)
    same = column % kv_heads == group_of
    past_row = column // kv_heads
    scale = 1.0 / math.sqrt(head_length)
    for n in range(slots):
        stored = cache[n] if n < resident else arrived[n - resident]
        stored = stored.reshape(cache_rows, 2 * head_length)
        query = queries[n]
        score = (
            lax.dot_general(
                query,
                stored[:, :head_length],
                (((1,), (1,)), ((), ())),
                preferred_element_type=jnp.float32,
            )
            * scale
        )
        score = jnp.where(jnp.logical_and(same, past_row < seen[n]), score, -jnp.inf)
        query = query.astype(jnp.float32)
        recent, values = [], []
        for t in range(steps):
            line = fresh_ref[n * steps + t : n * steps + t + 1]
            key = jnp.zeros((query_rows, head_length), jnp.float32)
            value = key
            for g in range(kv_heads):
                at = g * 2 * head_length
                key = jnp.where(group_of == g, line[:, at : at + head_length], key)
                value = jnp.where(
                    group_of == g, line[:, at + head_length : at + 2 * head_length], value
                )
            fit = jnp.sum(query * key, axis=1, keepdims=True) * scale
            recent.append(jnp.where(step_of >= t, fit, -jnp.inf))
            values.append(value)
        peak = jnp.max(score, axis=1, keepdims=True)
        for fit in recent:
            peak = jnp.maximum(peak, fit)
        past_exp = jnp.exp(score - peak)
        recent_exp = [jnp.exp(fit - peak) for fit in recent]
        denom = jnp.sum(past_exp, axis=1, keepdims=True)
        for term in recent_exp:
            denom = denom + term
        weight = (past_exp / denom).astype(jnp.bfloat16)
        mixed = jnp.dot(weight, stored[:, head_length:], preferred_element_type=jnp.float32)
        for term, value in zip(recent_exp, values):
            mixed = mixed + (term / denom).astype(jnp.bfloat16).astype(jnp.float32) * value
        if n < resident:
            mixed = jnp.where(gone[n] != 0, 0.0, mixed)
        mixed_ref[n * query_rows : (n + 1) * query_rows] = mixed
        for head in range(heads):
            lanes = slice(head * head_length, (head + 1) * head_length)
            pair = mixed_ref[pl.ds(n * query_rows + head, steps, stride=heads)]
            out[n, :, lanes] = pair.astype(jnp.bfloat16)


def pairs_layer(
    hidden,
    queries,
    kv_cache,
    w_kv,
    store_a,
    store_b,
    lengths,
    arrival_from,
    arrival_slot,
    resident_adapter,
    arrival_adapter,
    hot_holder,
    hot_dest,
):
    me = lax.axis_index("replica")
    replicas = lax.axis_size("replica")
    shards = lax.axis_size("tensor")
    resident, _, kv_heads, head_pair = kv_cache.shape
    arrive = arrival_from.shape[1]
    slots = resident + arrive
    steps, features = hidden.shape[1:]
    heads, head_length = queries.shape[2:]
    slot_total = store_a.shape[0]
    rank = store_a.shape[2]
    spans = hot_holder.shape[0] // COPIES
    row_a, row_b = store_a.shape[1:], store_b.shape[1:]
    columns = store_b.shape[3]
    masks = tuple(range(1, replicas))
    me_table = jnp.reshape(me, (1,)).astype(jnp.int32)
    shard_table = jnp.reshape(lax.axis_index("tensor"), (1,)).astype(jnp.int32)
    from_table, slot_table, choice_table = arrival_from.T, arrival_slot.T, arrival_adapter.T
    dest_table = hot_dest.T

    used = slots * steps
    padded = -(-used // 8) * 8
    first = resident * steps
    block = padded - first

    *leaving, rows_a, rows_b, rows, asking = copy_call(
        functools.partial(collect_kernel, spans, slot_total, masks),
        (me_table, from_table, slot_table, hot_holder),
        (kv_cache, store_a, store_b),
        [kv_cache.shape[1:]] * len(masks) + [(COPIES,) + row_a, (COPIES,) + row_b],
        [(len(masks),) + kv_cache.shape[1:], (COPIES,) + row_a, (COPIES,) + row_b],
        given=(hidden,),
        made=[(padded, features), (block, features)],
    )
    sibling_a = partner(rows_a, 1)
    sibling_b = partner(rows_b, 1)
    other_rows = [partner(asking, mask) for mask in masks]
    came = [partner(array, mask) for array, mask in zip(leaving, masks)]
    around = [rows] + [shifted(rows, step) for step in range(1, shards)]

    line_count = padded + len(masks) * block
    per_step = 2 if slot_total % 2 == 0 else 1
    partial, *sent = pl.pallas_call(
        functools.partial(project_kernel, spans, slot_total, resident, steps, masks),
        out_shape=[jax.ShapeDtypeStruct((padded, 2 * rank), jnp.float32)]
        + [jax.ShapeDtypeStruct((block, 2 * rank), jnp.float32)] * len(masks),
        grid=(slot_total // per_step,),
        in_specs=[SMEM] * 5
        + [pl.BlockSpec((padded, features), lambda i: (0, 0))]
        + [pl.BlockSpec((block, features), lambda i: (0, 0))] * len(masks)
        + [pl.BlockSpec((1, per_step * 2 * rank, features), lambda i: (i, 0, 0))],
        out_specs=[pl.BlockSpec((padded, 2 * rank), lambda i: (0, 0))]
        + [pl.BlockSpec((block, 2 * rank), lambda i: (0, 0))] * len(masks),
        scratch_shapes=[
            pltpu.VMEM((line_count, features), hidden.dtype),
            pltpu.VMEM((line_count, 2 * rank), jnp.int32),
            pltpu.VMEM((line_count, 2 * rank), jnp.float32),
        ],
        name="project",
    )(
        me_table,
        resident_adapter,
        choice_table,
        hot_holder,
        dest_table,
        rows,
        *other_rows,
        store_a.reshape(slot_total // per_step, per_step * 2 * rank, features),
    )
    returned = [partner(array, mask) for array, mask in zip(sent, masks)]
    last = partial[first:]
    for array in returned:
        last = last + array
    partial = jnp.concatenate([partial[:first], last])
    parts = [partial] + [shifted(partial, step) for step in range(1, shards)]

    unit_shape = row_a[1:]
    unit_total = 2 * COPIES
    across_b, *units, extra = copy_call(
        functools.partial(pack_kernel, spans, slot_total),
        (me_table, hot_holder, dest_table),
        (store_a, store_b, sibling_a, sibling_b),
        [(COPIES,) + row_b] + [(size,) + unit_shape for _, size in ALWAYS + AT_NEED],
        [(COPIES,) + row_b, (unit_total,) + unit_shape],
        [(1,)],
    )
    across_b = partner(across_b, 2)
    got = []
    for array in units[: len(ALWAYS)]:
        got.append(partner(array, 2))

    full = pl.pallas_call(
        gather_kernel,
        out_shape=jax.ShapeDtypeStruct((padded, shards * features), hidden.dtype),
        in_specs=[SMEM] + [VMEM] * shards,
        out_specs=VMEM,
        name="gather",
    )(shard_table, *around)
    base = jnp.einsum("md,dgc->gmc", full, w_kv, preferred_element_type=jnp.float32)

    attn_out, new_kv, arrived, installed_b = pl.pallas_call(
        functools.partial(attend_kernel, spans, masks, resident, steps, kv_heads, head_length),
        out_shape=[
            jax.ShapeDtypeStruct((slots, steps, heads * head_length), jnp.bfloat16),
            jax.ShapeDtypeStruct((slots, steps, kv_heads, head_pair), jnp.bfloat16),
            jax.ShapeDtypeStruct((arrive,) + kv_cache.shape[1:], jnp.bfloat16),
            jax.ShapeDtypeStruct((COPIES, 2 * rank, columns), jnp.bfloat16),
        ],
        in_specs=[SMEM] * 8 + [VMEM] * (shards + len(masks) + 6),
        out_specs=[VMEM] * 4,
        scratch_shapes=[
            pltpu.VMEM((padded, kv_heads * head_pair), jnp.float32),
            pltpu.VMEM((slots * steps * heads, head_length), jnp.float32),
        ],
        name="attend",
    )(
        me_table,
        lengths,
        from_table,
        slot_table,
        resident_adapter,
        choice_table,
        hot_holder,
        dest_table,
        *parts,
        *came,
        store_b.reshape(slot_total, 2 * rank, columns),
        sibling_b.reshape(COPIES, 2 * rank, columns),
        across_b.reshape(COPIES, 2 * rank, columns),
        base,
        queries.reshape(slots, steps * heads, head_length),
        kv_cache,
    )
    installed_b = installed_b.reshape((COPIES,) + row_b)

    tables = (me_table, hot_holder, dest_table)
    early = len(ALWAYS) - 1
    other = [partner(array, 1) for array in got[:early]]
    (placed,) = copy_call(
        functools.partial(place_kernel, spans, slot_total, ALWAYS[:early]),
        tables,
        (sibling_a, *got[:early], *other),
        [(COPIES,) + row_a],
        [(unit_total,) + unit_shape],
    )

    def finish(count):
        def branch(placed, *arrays):
            late = [arrays[0]] + [partner(array, 2) for array in arrays[1:][:count]]
            other = [partner(array, 1) for array in late]
            spread = (ALWAYS[early:] + AT_NEED)[: len(late)]
            return copy_call(
                functools.partial(place_kernel, spans, slot_total, spread),
                tables,
                (placed, *late, *other),
                [(COPIES,) + row_a],
                [(unit_total,) + unit_shape],
                aliases={len(tables): 0},
            )[0]

        return branch

    branches = [finish(count) for count in range(len(AT_NEED) + 1)]
    installed_a = lax.switch(extra[0], branches, placed, got[early], *units[len(ALWAYS) :])
    return (attn_out, new_kv, arrived, installed_a, installed_b)


def local(*args):
    fan = args[-1].shape[1]
    if lax.axis_size("replica") == 4 and fan == 1:
        return pairs_layer(*args)
    return local_general(*args)


def solution(mesh):
    in_specs = (
        P(("parts", "replica"), None, "tensor"),
        P(("parts", "replica"), None, "tensor", None),
        P(("parts", "replica"), None, "tensor", None),
        P(None, "tensor", None),
        P(("parts", "replica"), None, None, "tensor"),
        P(("parts", "replica"), None, None, "tensor"),
        P("parts"),
        P("parts", None),
        P("parts", None),
        P("parts"),
        P("parts", None),
        P("parts"),
        P("parts", None),
    )
    out_specs = (
        P(("parts", "replica"), None, "tensor"),
        P(("parts", "replica"), None, "tensor", None),
        P(("parts", "replica"), None, "tensor", None),
        P(("parts", "replica"), None, None, "tensor"),
        P(("parts", "replica"), None, None, "tensor"),
    )
    return jax.shard_map(local, mesh=mesh, in_specs=in_specs, out_specs=out_specs, check_vma=False)
```

```python
import functools
import math

import jax
import jax.numpy as jnp
from jax import lax
from jax.experimental import pallas as pl
from jax.experimental.pallas import tpu as pltpu
from jax.sharding import PartitionSpec as P


COPIES = 4


ADAPTER_SCALE = 2.0
ROPE_BASE = 500000.0


def rotate_keys(key_rows, positions):
    head_length = key_rows.shape[-1]
    half_size = head_length // 2
    frequency = ROPE_BASE ** (-(jnp.arange(half_size, dtype=jnp.float32) * 2.0 / head_length))
    angles = positions.astype(jnp.float32)[:, :, None, None] * frequency
    cosine = jnp.cos(angles)
    sine_val = jnp.sin(angles)
    first_half = key_rows[..., :half_size]
    second_half = key_rows[..., half_size:]
    return jnp.concatenate(
        [
            first_half * cosine - second_half * sine_val,
            second_half * cosine + first_half * sine_val,
        ],
        axis=-1,
    )


def attend(queries, stored, lengths_now, fresh_kv):
    request_slot_count, decode_step_count, heads_local, head_length = queries.shape
    local_key_value = stored.shape[2]
    group_size = heads_local // local_key_value
    grouped = queries.reshape(
        request_slot_count, decode_step_count, local_key_value, group_size, head_length
    )
    score_scale = 1.0 / math.sqrt(head_length)
    past_scores = (
        jnp.einsum(
            "msgjd,mcgd->msgjc",
            grouped,
            stored[..., :head_length],
            preferred_element_type=jnp.float32,
        )
        * score_scale
    )
    recent_scores = (
        jnp.einsum(
            "msgjd,mtgd->msgjt",
            grouped,
            fresh_kv[..., :head_length],
            preferred_element_type=jnp.float32,
        )
        * score_scale
    )
    row_ids = jnp.arange(stored.shape[1], dtype=jnp.int32)
    past_ok = (row_ids[None, :] < lengths_now[:, None])[:, None, None, None, :]
    step_ids = jnp.arange(decode_step_count, dtype=jnp.int32)
    recent_ok = (step_ids[None, :] <= step_ids[:, None])[None, :, None, None, :]
    past_scores = jnp.where(past_ok, past_scores, -jnp.inf)
    recent_scores = jnp.where(recent_ok, recent_scores, -jnp.inf)
    peak_score = jnp.maximum(jnp.max(past_scores, -1), jnp.max(recent_scores, -1))[..., None]
    past_exp = jnp.exp(past_scores - peak_score)
    recent_exp = jnp.exp(recent_scores - peak_score)
    denom_sum = jnp.sum(past_exp, -1, keepdims=True) + jnp.sum(recent_exp, -1, keepdims=True)
    past_w = (past_exp / denom_sum).astype(jnp.bfloat16)
    recent_w = (recent_exp / denom_sum).astype(jnp.bfloat16)
    mixed_out = jnp.einsum(
        "msgjc,mcgd->msgjd", past_w, stored[..., head_length:], preferred_element_type=jnp.float32
    )
    mixed_out = mixed_out + jnp.einsum(
        "msgjt,mtgd->msgjd",
        recent_w,
        fresh_kv[..., head_length:],
        preferred_element_type=jnp.float32,
    )
    return mixed_out.reshape(request_slot_count, decode_step_count, heads_local * head_length)


def local_general(
    hidden,
    queries,
    kv_cache,
    w_kv,
    store_a,
    store_b,
    lengths,
    arrival_from,
    arrival_slot,
    resident_adapter,
    arrival_adapter,
    hot_holder,
    hot_dest,
):
    my_index = lax.axis_index("replica")
    replicas = lax.axis_size("replica")
    resident = kv_cache.shape[0]
    arrive = arrival_from.shape[1]
    request_slot_count = resident + arrive
    decode_step_count = hidden.shape[1]
    head_length = queries.shape[3]
    local_key_value = kv_cache.shape[2]
    slot_total = store_a.shape[0]
    hot_total = hot_holder.shape[0]
    spans = hot_total // COPIES
    my_from = lax.dynamic_index_in_dim(arrival_from, my_index, 0, keepdims=False)
    my_slot = lax.dynamic_index_in_dim(arrival_slot, my_index, 0, keepdims=False)
    own_ids = my_index * resident + jnp.arange(resident, dtype=jnp.int32)
    leaving_ids = (arrival_from * resident + arrival_slot).reshape(-1)
    staying = jnp.logical_not(jnp.any(own_ids[:, None] == leaving_ids[None, :], axis=1))
    live_mask = jnp.concatenate([staying, jnp.ones((arrive,), bool)])
    own_len = lax.dynamic_slice_in_dim(lengths, my_index * resident, resident)
    arrival_len = jnp.take(lengths, my_from * resident + my_slot)
    seen_len = jnp.concatenate([own_len, arrival_len])
    takes_mine = arrival_from == my_index
    sends_any = jnp.any(takes_mine, axis=1)
    send_slot = jnp.sum(jnp.where(takes_mine, arrival_slot, 0), axis=1)
    outgoing = jnp.take(kv_cache, send_slot, axis=0)
    outgoing = jnp.where(sends_any[:, None, None, None], outgoing, jnp.zeros((), jnp.bfloat16))
    incoming = lax.all_to_all(outgoing, "replica", split_axis=0, concat_axis=0, tiled=True)
    blocks = hot_dest.reshape(COPIES, spans, hot_dest.shape[1])
    holder_grid = hot_holder.reshape(COPIES, spans)
    holder_rep = holder_grid // slot_total
    mine = holder_rep == my_index
    has_one = jnp.any(mine, axis=1)
    local_pick = jnp.sum(jnp.where(mine, holder_grid % slot_total, 0), axis=1)

    def spread_rows(store):
        rows = jnp.take(store, local_pick, axis=0)
        rows = jnp.where(has_one[:, None, None, None], rows, jnp.zeros((), jnp.bfloat16))
        return rows.reshape(COPIES, replicas, -1).transpose(1, 0, 2)

    got_a, got_b = (
        lax.all_to_all(spread_rows(store_a), "replica", split_axis=0, concat_axis=0, tiled=True),
        lax.all_to_all(spread_rows(store_b), "replica", split_axis=0, concat_axis=0, tiled=True),
    )
    replica_ids = jnp.arange(replicas, dtype=jnp.int32)
    member = jnp.any(blocks[:, :, :, None] == replica_ids[None, None, None, :], axis=2).astype(
        jnp.int32
    )
    source_rep = jnp.sum(member * holder_rep[:, :, None], axis=1)
    copy_ids = jnp.arange(COPIES, dtype=jnp.int32)
    route_a = got_a[source_rep.T, copy_ids[None, :]]
    route_b = got_b[source_rep.T, copy_ids[None, :]]
    recv_a, recv_b = (
        lax.all_to_all(route_a, "replica", split_axis=0, concat_axis=0, tiled=True),
        lax.all_to_all(route_b, "replica", split_axis=0, concat_axis=0, tiled=True),
    )
    installed_a = recv_a.transpose(1, 0, 2).reshape((COPIES,) + store_a.shape[1:])
    installed_b = recv_b.transpose(1, 0, 2).reshape((COPIES,) + store_b.shape[1:])
    own_adapter = lax.dynamic_slice_in_dim(resident_adapter, my_index * resident, resident)
    my_choice = lax.dynamic_index_in_dim(arrival_adapter, my_index, 0, keepdims=False)
    adapt_a = jnp.concatenate(
        [jnp.take(store_a, own_adapter, axis=0), jnp.take(installed_a, my_choice, axis=0)]
    )
    adapter_up_weight = jnp.concatenate(
        [jnp.take(store_b, own_adapter, axis=0), jnp.take(installed_b, my_choice, axis=0)]
    )
    partial_value = jnp.einsum(
        "msd,mpkd->mspk", hidden, adapt_a, preferred_element_type=jnp.float32
    )
    base_projection = jnp.einsum(
        "msd,dgc->msgc",
        lax.all_gather(hidden, "tensor", axis=2, tiled=True),
        w_kv,
        preferred_element_type=jnp.float32,
    )
    down_projected = lax.psum(partial_value, "tensor")
    down_projected = down_projected.astype(jnp.bfloat16)
    adapter_update = jnp.einsum(
        "gnot,gote->gnoe", down_projected, adapter_up_weight, preferred_element_type=jnp.float32
    )
    adapter_update = (
        adapter_update.reshape(
            request_slot_count, decode_step_count, 2, local_key_value, head_length
        )
        .transpose(0, 1, 3, 2, 4)
        .reshape(request_slot_count, decode_step_count, local_key_value, 2 * head_length)
    )
    unrotated_key_value = base_projection + ADAPTER_SCALE * adapter_update
    positions = seen_len[:, None] + jnp.arange(decode_step_count, dtype=jnp.int32)[None, :]
    fresh_kv = jnp.concatenate(
        [
            rotate_keys(unrotated_key_value[..., :head_length], positions),
            unrotated_key_value[..., head_length:],
        ],
        axis=-1,
    ).astype(jnp.bfloat16)
    stay_out = attend(queries[:resident], kv_cache, own_len, fresh_kv[:resident])
    arrived = jnp.take(incoming, my_from, axis=0)
    row_ids = jnp.arange(kv_cache.shape[1], dtype=jnp.int32)
    arrived = jnp.where(
        (row_ids[None, :] < arrival_len[:, None])[:, :, None, None],
        arrived,
        jnp.zeros((), jnp.bfloat16),
    )
    move_out = attend(queries[resident:], arrived, arrival_len, fresh_kv[resident:])
    mixed_out = jnp.concatenate([stay_out, move_out], axis=0)
    attn_out = jnp.where(live_mask[:, None, None], mixed_out, 0.0).astype(jnp.bfloat16)
    new_kv = jnp.where(live_mask[:, None, None, None], fresh_kv, jnp.zeros((), jnp.bfloat16))
    return (attn_out, new_kv, arrived, installed_a, installed_b)


def partner(array, mask):
    return lax.ppermute(array, "replica", [(i, i ^ mask) for i in range(lax.axis_size("replica"))])


def shifted(array, step):
    size = lax.axis_size("tensor")
    return lax.ppermute(array, "tensor", [(i, (i + step) % size) for i in range(size)])


ALWAYS = ((0, 1), (1, 4), (5, 1))
AT_NEED = ((6, 1), (7, 1))
SMEM = pl.BlockSpec(memory_space=pltpu.SMEM)
VMEM = pl.BlockSpec(memory_space=pltpu.VMEM)


def wanted_by(holder, dest, spans, replica, copy_id):
    row = jnp.int32(0)
    for span in range(spans):
        at = copy_id * spans + span
        row += jnp.where(dest[0, at] == replica, holder[at], 0)
    return row


def crossing(holder, dest, spans, slot_total, chip):
    items, count = [], jnp.int32(0)
    for copy_id in range(COPIES):
        for core in range(2):
            row = wanted_by(holder, dest, spans, 2 * chip + core, copy_id)
            crosses = row // (2 * slot_total) != chip
            items.append((copy_id, core, row, crosses, count))
            count = count + crosses.astype(jnp.int32)
    return items


def staged(groups, meanwhile=None):
    def when(condition, action):
        if condition is None:
            action()
        else:
            pl.when(condition)(action)

    def begin(at, sources, buffer, sems):
        for condition, source in sources:
            when(condition, pltpu.make_async_copy(source, buffer.at[at], sems.at[0, at]).start)

    def forward(at, targets, buffer, sems):
        pltpu.make_async_copy(buffer.at[at], buffer.at[at], sems.at[0, at]).wait()
        for condition, target in targets:
            when(condition, pltpu.make_async_copy(buffer.at[at], target, sems.at[1, at]).start)

    def finish(at, buffer, sems):
        pltpu.make_async_copy(buffer.at[at], buffer.at[at], sems.at[1, at]).wait()

    for moves, buffer, sems in groups:
        for at, (condition, sources, _) in enumerate(moves):
            when(condition, functools.partial(begin, at, sources, buffer, sems))
    if meanwhile is not None:
        meanwhile()
    for moves, buffer, sems in groups:
        for at, (condition, _, targets) in enumerate(moves):
            when(condition, functools.partial(forward, at, targets, buffer, sems))
    for moves, buffer, sems in groups:
        for at, (condition, _, _) in enumerate(moves):
            when(condition, functools.partial(finish, at, buffer, sems))


def collect_kernel(spans, slot_total, masks, *refs):
    (me_ref, arrival_from, arrival_slot, holder, kv_cache, store_a, store_b, hidden) = refs[:8]
    *leaving, rows_a, rows_b, rows, asking = refs[8 : 12 + len(masks)]
    buffers, semaphores = refs[12 + len(masks) : 15 + len(masks)], refs[15 + len(masks) :]
    me = me_ref[0]
    moves = []
    for i, mask in enumerate(masks):
        to = me ^ mask
        slot = jnp.int32(0)
        for a in range(arrival_from.shape[0]):
            slot += jnp.where(arrival_from[a, to] == me, arrival_slot[a, to], 0)
        moves.append((None, [(None, kv_cache.at[slot])], [(None, leaving[i])]))
    groups = [moves]
    held = []
    for copy_id in range(COPIES):
        slot = jnp.int32(0)
        for span in range(spans):
            row = holder[copy_id * spans + span]
            slot += jnp.where(row // slot_total == me, row % slot_total, 0)
        held.append(slot)
    for table, target in ((store_a, rows_a), (store_b, rows_b)):
        groups.append(
            [
                (None, [(None, table.at[slot])], [(None, target.at[copy_id])])
                for copy_id, slot in enumerate(held)
            ]
        )

    def regroup():
        count = hidden.shape[0] * hidden.shape[1]
        start = rows.shape[0] - asking.shape[0]
        blank = jnp.zeros((rows.shape[0] - count, rows.shape[1]), rows.dtype)
        every = hidden[...].reshape(count, rows.shape[1])
        rows[...] = jnp.concatenate([every, blank], axis=0)
        asking[...] = rows[start:]

    staged(list(zip(groups, buffers, semaphores)), regroup)


def pack_kernel(spans, slot_total, *refs):
    (me_ref, holder, dest, store_a, store_b, sibling_a, sibling_b) = refs[:7]
    across_b, *units = refs[7:-5]
    spread = ALWAYS + AT_NEED
    extra, buffer_b, buffer_a, sems_b, sems_a = refs[-5:]
    me = me_ref[0]
    core = me % 2
    chip = 1 - me // 2
    items = crossing(holder, dest, spans, slot_total, chip)
    moves_b, moves_a = [], []
    for copy_id in range(COPIES):
        row = jnp.where(core == 0, items[2 * copy_id][2], items[2 * copy_id + 1][2])
        own = row // slot_total == me
        sources = [
            (own, store_b.at[row % slot_total]),
            (jnp.logical_not(own), sibling_b.at[copy_id]),
        ]
        moves_b.append((None, sources, [(None, across_b.at[copy_id])]))
    for at, (copy_id, _, row, crosses, unit) in enumerate(items):
        own = row // slot_total == me
        sources = [
            (own, store_a.at[row % slot_total, core]),
            (jnp.logical_not(own), sibling_a.at[copy_id, core]),
        ]
        targets = [
            (
                jnp.logical_and(unit >= start, unit < start + size),
                array.at[jnp.clip(unit - start, 0, size - 1)],
            )
            for array, (start, size) in zip(units, spread)
            if start <= at
        ]
        moves_a.append((crosses, sources, targets))
    count = items[-1][4] + items[-1][3].astype(jnp.int32)
    extra[0] = jnp.clip(count - AT_NEED[0][0], 0, len(AT_NEED))
    staged([(moves_b, buffer_b, sems_b), (moves_a, buffer_a, sems_a)])


def place_kernel(spans, slot_total, spread, *refs):
    (me_ref, holder, dest, earlier) = refs[:4]
    got, other = refs[4 : 4 + len(spread)], refs[4 + len(spread) : 4 + 2 * len(spread)]
    out, buffer, sems = refs[-3:]
    me = me_ref[0]
    core = me % 2
    first_unit = spread[0][0]
    past_unit = spread[-1][0] + spread[-1][1]
    items = crossing(holder, dest, spans, slot_total, me // 2)
    moves = []
    for copy_id in range(COPIES):
        one, two = items[2 * copy_id], items[2 * copy_id + 1]
        crosses = jnp.where(core == 0, one[3].astype(jnp.int32), two[3].astype(jnp.int32)) != 0
        unit = jnp.where(core == 0, one[4], two[4])
        possible = [i for i, (start, _) in enumerate(spread) if start <= 2 * copy_id + 1]
        if first_unit and not possible:
            continue
        here = jnp.logical_and(unit >= first_unit, unit < past_unit)
        for half, arrays in ((core, got), (1 - core, other)):
            sources = []
            active = jnp.logical_and(crosses, here)
            if not first_unit:
                near = jnp.logical_not(crosses)
                active = jnp.logical_or(near, here)
                sources.append((near, earlier.at[copy_id, half]))
            for i in possible:
                start, size = spread[i]
                hit = jnp.logical_and(unit >= start, unit < start + size)
                source = arrays[i].at[jnp.clip(unit - start, 0, size - 1)]
                sources.append((jnp.logical_and(crosses, hit), source))
            moves.append((active, sources, [(None, out.at[copy_id, half])]))
    staged([(moves, buffer, sems)])


def copy_call(kernel, tables, arrays, shapes, scratch, scalars=(), aliases=None, given=(), made=()):
    hbm = pl.BlockSpec(memory_space=pl.ANY)
    dtype = arrays[0].dtype
    return pl.pallas_call(
        kernel,
        out_shape=[pltpu.HBM(shape, dtype) for shape in shapes]
        + [jax.ShapeDtypeStruct(shape, dtype) for shape in made]
        + [jax.ShapeDtypeStruct(shape, jnp.int32) for shape in scalars],
        in_specs=[SMEM] * len(tables) + [hbm] * len(arrays) + [VMEM] * len(given),
        out_specs=[hbm] * len(shapes) + [VMEM] * len(made) + [SMEM] * len(scalars),
        scratch_shapes=[pltpu.VMEM(shape, dtype) for shape in scratch]
        + [pltpu.SemaphoreType.DMA((2, shape[0])) for shape in scratch],
        input_output_aliases=aliases or {},
    )(*tables, *arrays, *given)


def project_kernel(spans, slot_total, resident, steps, masks, *refs):
    (me_ref, resident_adapter, arrival_adapter, holder, dest, hidden, *others) = refs[: 6 + len(masks)]
    store, *outs, left, adapters, sums = refs[6 + len(masks) :]
    me = me_ref[0]
    group = pl.program_id(0)
    base = hidden.shape[0]
    block = others[0].shape[0]
    width = sums.shape[1]
    per_step = store.shape[1] // width

    @pl.when(group == 0)
    def _():
        left[0:base] = hidden[...]
        for i, other in enumerate(others):
            left[base + i * block : base + (i + 1) * block] = other[...]
        sums[...] = jnp.zeros_like(sums)
        ids = lax.broadcasted_iota(jnp.int32, sums.shape, 0) // steps
        own = jnp.full(sums.shape, -1, jnp.int32)
        for slot in range(resident):
            own = jnp.where(ids == slot, resident_adapter[me * resident + slot], own)
        for i, mask in enumerate((0,) + masks):
            replica = me ^ mask
            first = resident if i == 0 else (base + (i - 1) * block) // steps
            for a in range(arrival_adapter.shape[0]):
                chosen = arrival_adapter[a, replica]
                row = jnp.int32(0)
                for span in range(spans):
                    at = chosen * spans + span
                    row += jnp.where(dest[0, at] == replica, holder[at], 0)
                here = jnp.where(row // slot_total == me, row % slot_total, -1)
                own = jnp.where(ids == first + a, here, own)
        adapters[...] = own

    product = lax.dot_general(
        left[...], store[0], (((1,), (1,)), ((), ())), preferred_element_type=jnp.float32
    )
    for i in range(per_step):
        hit = adapters[...] == group * per_step + i
        sums[...] += jnp.where(hit, product[:, i * width : (i + 1) * width], 0.0)

    @pl.when(group == pl.num_programs(0) - 1)
    def _():
        outs[0][...] = sums[0:base]
        for i, out in enumerate(outs[1:]):
            out[...] = sums[base + i * block : base + (i + 1) * block]


def gather_kernel(shard_ref, *refs):
    out = refs[-1]
    count = len(refs) - 1
    width = refs[0].shape[1]
    for step, ref in enumerate(refs[:-1]):
        source = lax.rem(shard_ref[0] + count - step, count)
        out[:, pl.ds(pl.multiple_of(source * width, width), width)] = ref[...]


def attend_kernel(spans, masks, resident, steps, kv_heads, head_length, *refs):
    (me_ref, lengths, arrival_from, arrival_slot, resident_adapter, arrival_adapter) = refs[:6]
    holder, dest, *parts = refs[6 : -14 - len(masks)]
    came = refs[-14 - len(masks) : -14]
    store_b, sibling_b, across_b, base, queries, cache = refs[-14:-8]
    out, new_kv, arrived, installed_b = refs[-8:-4]
    fresh_ref, mixed_ref, score_ref, weight_ref = refs[-4:]
    me = me_ref[0]
    arrive = arrival_from.shape[0]
    replicas = arrival_from.shape[1]
    slots = resident + arrive
    row_count = base.shape[1]
    rank = store_b.shape[1] // 2
    slot_total = store_b.shape[0]
    half = head_length // 2
    seen = [lengths[me * resident + slot] for slot in range(resident)]
    for a in range(arrive):
        seen.append(lengths[arrival_from[a, me] * resident + arrival_slot[a, me]])

    for a in range(arrive):
        for ref, mask in zip(came, masks):

            @pl.when(arrival_from[a, me] == me ^ mask)
            def _():
                arrived[a] = ref[...]

        def clear(row, carry):
            arrived[a, row] = jnp.zeros(arrived.shape[2:], arrived.dtype)
            return carry

        lax.fori_loop(seen[resident + a], arrived.shape[1], clear, 0)
    for copy_id in range(COPIES):
        near = wanted_by(holder, dest, spans, me, copy_id) // (2 * slot_total) == me // 2

        @pl.when(near)
        def _():
            installed_b[copy_id] = sibling_b[copy_id]

        @pl.when(jnp.logical_not(near))
        def _():
            installed_b[copy_id] = across_b[copy_id]

    total = parts[0][...]
    for part in parts[1:]:
        total = total + part[...]
    down = total.astype(jnp.bfloat16)

    ids = lax.broadcasted_iota(jnp.int32, (row_count, 1), 0) // steps
    adapters = jnp.zeros((row_count, 1), jnp.int32)
    position = lax.broadcasted_iota(jnp.int32, (row_count, 1), 0) % steps
    for slot in range(slots):
        if slot < resident:
            adapter = resident_adapter[me * resident + slot]
        else:
            adapter = store_b.shape[0] + arrival_adapter[slot - resident, me]
        adapters = jnp.where(ids == slot, adapter, adapters)
        position = jnp.where(ids == slot, position + seen[slot], position)
    deltas = [jnp.zeros((row_count, store_b.shape[2]), jnp.float32) for _ in range(2)]
    for adapter in range(store_b.shape[0] + COPIES):
        if adapter < store_b.shape[0]:
            table = store_b[adapter]
        else:
            table = installed_b[adapter - store_b.shape[0]]
        for part in range(2):
            product = jnp.dot(
                down[:, part * rank : (part + 1) * rank],
                table[part * rank : (part + 1) * rank],
                preferred_element_type=jnp.float32,
            )
            deltas[part] = jnp.where(adapters == adapter, product, deltas[part])

    lane = lax.broadcasted_iota(jnp.int32, (1, half), 1).astype(jnp.float32)
    frequency = jnp.exp(lane * (-2.0 * math.log(ROPE_BASE) / head_length))
    angles = position.astype(jnp.float32) * frequency
    cosine, sine = jnp.cos(angles), jnp.sin(angles)
    dead = jnp.zeros((row_count, 1), jnp.bool_)
    gone = [jnp.int32(0)] * resident
    for q in range(replicas):
        for a in range(arrive):
            mine = arrival_from[a, q] == me
            slot = arrival_slot[a, q]
            dead = jnp.logical_or(dead, jnp.logical_and(ids == slot, mine))
            for n in range(resident):
                gone[n] = jnp.where(jnp.logical_and(mine, slot == n), 1, gone[n])
    for g in range(kv_heads):
        columns = slice(g * head_length, (g + 1) * head_length)
        key = base[g, :, :head_length] + ADAPTER_SCALE * deltas[0][:, columns]
        value = base[g, :, head_length:] + ADAPTER_SCALE * deltas[1][:, columns]
        u, w = key[:, :half], key[:, half:]
        key = jnp.concatenate([u * cosine - w * sine, w * cosine + u * sine], axis=1)
        for part, piece in enumerate((key, value)):
            rounded = piece.astype(jnp.bfloat16).astype(jnp.float32)
            lanes = slice(part * head_length, (part + 1) * head_length)
            fresh_ref[part, pl.ds(g, row_count, stride=kv_heads)] = rounded
            kept = jnp.where(dead, 0.0, rounded)[: slots * steps]
            new_kv[:, :, g, lanes] = kept.reshape(slots, steps, head_length).astype(jnp.bfloat16)

    query_rows = queries.shape[1]
    heads = query_rows // steps
    cache_rows = cache.shape[1] * kv_heads
    new_rows = steps * kv_heads
    pad_rows = 16 - new_rows
    row = lax.broadcasted_iota(jnp.int32, (query_rows, 1), 0)
    step_of = row // heads
    group_of = row % heads // (heads // kv_heads)
    column = lax.broadcasted_iota(jnp.int32, (query_rows, cache_rows), 1)
    same = column % kv_heads == group_of
    past_row = column // kv_heads
    late = lax.broadcasted_iota(jnp.int32, (query_rows, 128), 1)
    allowed = jnp.logical_and(late % kv_heads == group_of, late // kv_heads <= step_of)
    allowed = jnp.logical_and(allowed, late < new_rows)
    scale = 1.0 / math.sqrt(head_length)

    def cached(n):
        stored = cache[n] if n < resident else arrived[n - resident]
        return stored.reshape(cache_rows, 2 * head_length)

    def fresh_rows(n, part):
        lines = fresh_ref[part, n * new_rows : (n + 1) * new_rows]
        blank = jnp.zeros((pad_rows, head_length), jnp.float32)
        return jnp.concatenate([lines, blank], axis=0).astype(jnp.bfloat16)

    def against(query, keys):
        return lax.dot_general(
            query, keys, (((1,), (1,)), ((), ())), preferred_element_type=jnp.float32
        )

    for n in range(slots):
        lines = slice(n * query_rows, (n + 1) * query_rows)
        query = queries[n]
        score = against(query, cached(n)[:, :head_length]) * scale
        score = jnp.where(jnp.logical_and(same, past_row < seen[n]), score, -jnp.inf)
        score_ref[lines, :cache_rows] = score
        keys = jnp.concatenate(
            [fresh_rows(n, 0), jnp.zeros((128 - 16, head_length), jnp.bfloat16)], axis=0
        )
        score = against(query, keys) * scale
        score_ref[lines, cache_rows:] = jnp.where(allowed, score, -jnp.inf)
    for n in range(slots):
        lines = slice(n * query_rows, (n + 1) * query_rows)
        score = score_ref[lines]
        term = jnp.exp(score - jnp.max(score, axis=1, keepdims=True))
        inverse = 1.0 / jnp.sum(term, axis=1, keepdims=True)
        weight_ref[lines] = (term * inverse).astype(jnp.bfloat16)
    for n in range(slots):
        lines = slice(n * query_rows, (n + 1) * query_rows)
        weight = weight_ref[lines]
        mixed = jnp.dot(
            weight[:, :cache_rows], cached(n)[:, head_length:], preferred_element_type=jnp.float32
        )
        mixed = mixed + jnp.dot(
            weight[:, cache_rows : cache_rows + 16],
            fresh_rows(n, 1),
            preferred_element_type=jnp.float32,
        )
        if n < resident:
            mixed = jnp.where(gone[n] != 0, 0.0, mixed)
        mixed_ref[lines] = mixed
    for n in range(slots):
        for head in range(heads):
            lanes = slice(head * head_length, (head + 1) * head_length)
            pair = mixed_ref[pl.ds(n * query_rows + head, steps, stride=heads)]
            out[n, :, lanes] = pair.astype(jnp.bfloat16)


def pairs_layer(
    hidden,
    queries,
    kv_cache,
    w_kv,
    store_a,
    store_b,
    lengths,
    arrival_from,
    arrival_slot,
    resident_adapter,
    arrival_adapter,
    hot_holder,
    hot_dest,
):
    me = lax.axis_index("replica")
    replicas = lax.axis_size("replica")
    shards = lax.axis_size("tensor")
    resident, cap, kv_heads, head_pair = kv_cache.shape
    arrive = arrival_from.shape[1]
    slots = resident + arrive
    steps, features = hidden.shape[1:]
    heads, head_length = queries.shape[2:]
    slot_total = store_a.shape[0]
    rank = store_a.shape[2]
    spans = hot_holder.shape[0] // COPIES
    row_a, row_b = store_a.shape[1:], store_b.shape[1:]
    columns = store_b.shape[3]
    masks = tuple(range(1, replicas))
    me_table = jnp.reshape(me, (1,)).astype(jnp.int32)
    shard_table = jnp.reshape(lax.axis_index("tensor"), (1,)).astype(jnp.int32)
    from_table, slot_table, choice_table = arrival_from.T, arrival_slot.T, arrival_adapter.T
    dest_table = hot_dest.T

    used = slots * steps
    padded = -(-used // 8) * 8
    first = resident * steps
    block = padded - first

    *leaving, rows_a, rows_b, rows, asking = copy_call(
        functools.partial(collect_kernel, spans, slot_total, masks),
        (me_table, from_table, slot_table, hot_holder),
        (kv_cache, store_a, store_b),
        [kv_cache.shape[1:]] * len(masks) + [(COPIES,) + row_a, (COPIES,) + row_b],
        [(len(masks),) + kv_cache.shape[1:], (COPIES,) + row_a, (COPIES,) + row_b],
        given=(hidden,),
        made=[(padded, features), (block, features)],
    )
    sibling_a = partner(rows_a, 1)
    sibling_b = partner(rows_b, 1)
    other_rows = [partner(asking, mask) for mask in masks]
    came = [partner(array, mask) for array, mask in zip(leaving, masks)]
    around = [rows] + [shifted(rows, step) for step in range(1, shards)]

    line_count = padded + len(masks) * block
    per_step = 2 if slot_total % 2 == 0 else 1
    partial, *sent = pl.pallas_call(
        functools.partial(project_kernel, spans, slot_total, resident, steps, masks),
        out_shape=[jax.ShapeDtypeStruct((padded, 2 * rank), jnp.float32)]
        + [jax.ShapeDtypeStruct((block, 2 * rank), jnp.float32)] * len(masks),
        grid=(slot_total // per_step,),
        in_specs=[SMEM] * 5
        + [pl.BlockSpec((padded, features), lambda i: (0, 0))]
        + [pl.BlockSpec((block, features), lambda i: (0, 0))] * len(masks)
        + [pl.BlockSpec((1, per_step * 2 * rank, features), lambda i: (i, 0, 0))],
        out_specs=[pl.BlockSpec((padded, 2 * rank), lambda i: (0, 0))]
        + [pl.BlockSpec((block, 2 * rank), lambda i: (0, 0))] * len(masks),
        scratch_shapes=[
            pltpu.VMEM((line_count, features), hidden.dtype),
            pltpu.VMEM((line_count, 2 * rank), jnp.int32),
            pltpu.VMEM((line_count, 2 * rank), jnp.float32),
        ],
        name="project",
    )(
        me_table,
        resident_adapter,
        choice_table,
        hot_holder,
        dest_table,
        rows,
        *other_rows,
        store_a.reshape(slot_total // per_step, per_step * 2 * rank, features),
    )
    returned = [partner(array, mask) for array, mask in zip(sent, masks)]
    last = partial[first:]
    for array in returned:
        last = last + array
    partial = jnp.concatenate([partial[:first], last])
    parts = [partial] + [shifted(partial, step) for step in range(1, shards)]

    unit_shape = row_a[1:]
    unit_total = 2 * COPIES
    across_b, *units, extra = copy_call(
        functools.partial(pack_kernel, spans, slot_total),
        (me_table, hot_holder, dest_table),
        (store_a, store_b, sibling_a, sibling_b),
        [(COPIES,) + row_b] + [(size,) + unit_shape for _, size in ALWAYS + AT_NEED],
        [(COPIES,) + row_b, (unit_total,) + unit_shape],
        [(1,)],
    )
    across_b = partner(across_b, 2)
    got = []
    for array in units[: len(ALWAYS)]:
        got.append(partner(array, 2))

    full = pl.pallas_call(
        gather_kernel,
        out_shape=jax.ShapeDtypeStruct((padded, shards * features), hidden.dtype),
        in_specs=[SMEM] + [VMEM] * shards,
        out_specs=VMEM,
        name="gather",
    )(shard_table, *around)
    base = jnp.einsum("md,dgc->gmc", full, w_kv, preferred_element_type=jnp.float32)

    attn_out, new_kv, arrived, installed_b = pl.pallas_call(
        functools.partial(attend_kernel, spans, masks, resident, steps, kv_heads, head_length),
        out_shape=[
            jax.ShapeDtypeStruct((slots, steps, heads * head_length), jnp.bfloat16),
            jax.ShapeDtypeStruct((slots, steps, kv_heads, head_pair), jnp.bfloat16),
            jax.ShapeDtypeStruct((arrive,) + kv_cache.shape[1:], jnp.bfloat16),
            jax.ShapeDtypeStruct((COPIES, 2 * rank, columns), jnp.bfloat16),
        ],
        in_specs=[SMEM] * 8 + [VMEM] * (shards + len(masks) + 6),
        out_specs=[VMEM] * 4,
        scratch_shapes=[
            pltpu.VMEM((2, padded * kv_heads, head_length), jnp.float32),
            pltpu.VMEM((slots * steps * heads, head_length), jnp.float32),
            pltpu.VMEM((slots * steps * heads, cap * kv_heads + 128), jnp.float32),
            pltpu.VMEM((slots * steps * heads, cap * kv_heads + 128), jnp.bfloat16),
        ],
        name="attend",
    )(
        me_table,
        lengths,
        from_table,
        slot_table,
        resident_adapter,
        choice_table,
        hot_holder,
        dest_table,
        *parts,
        *came,
        store_b.reshape(slot_total, 2 * rank, columns),
        sibling_b.reshape(COPIES, 2 * rank, columns),
        across_b.reshape(COPIES, 2 * rank, columns),
        base,
        queries.reshape(slots, steps * heads, head_length),
        kv_cache,
    )
    installed_b = installed_b.reshape((COPIES,) + row_b)

    tables = (me_table, hot_holder, dest_table)
    early = len(ALWAYS) - 1
    other = [partner(array, 1) for array in got[:early]]
    (placed,) = copy_call(
        functools.partial(place_kernel, spans, slot_total, ALWAYS[:early]),
        tables,
        (sibling_a, *got[:early], *other),
        [(COPIES,) + row_a],
        [(unit_total,) + unit_shape],
    )

    def finish(count):
        def branch(placed, *arrays):
            late = [arrays[0]] + [partner(array, 2) for array in arrays[1:][:count]]
            other = [partner(array, 1) for array in late]
            spread = (ALWAYS[early:] + AT_NEED)[: len(late)]
            return copy_call(
                functools.partial(place_kernel, spans, slot_total, spread),
                tables,
                (placed, *late, *other),
                [(COPIES,) + row_a],
                [(unit_total,) + unit_shape],
                aliases={len(tables): 0},
            )[0]

        return branch

    branches = [finish(count) for count in range(len(AT_NEED) + 1)]
    installed_a = lax.switch(extra[0], branches, placed, got[early], *units[len(ALWAYS) :])
    return (attn_out, new_kv, arrived, installed_a, installed_b)


def local(*args):
    fan = args[-1].shape[1]
    if lax.axis_size("replica") == 4 and fan == 1:
        return pairs_layer(*args)
    return local_general(*args)


def solution(mesh):
    in_specs = (
        P(("parts", "replica"), None, "tensor"),
        P(("parts", "replica"), None, "tensor", None),
        P(("parts", "replica"), None, "tensor", None),
        P(None, "tensor", None),
        P(("parts", "replica"), None, None, "tensor"),
        P(("parts", "replica"), None, None, "tensor"),
        P("parts"),
        P("parts", None),
        P("parts", None),
        P("parts"),
        P("parts", None),
        P("parts"),
        P("parts", None),
    )
    out_specs = (
        P(("parts", "replica"), None, "tensor"),
        P(("parts", "replica"), None, "tensor", None),
        P(("parts", "replica"), None, "tensor", None),
        P(("parts", "replica"), None, None, "tensor"),
        P(("parts", "replica"), None, None, "tensor"),
    )
    return jax.shard_map(local, mesh=mesh, in_specs=in_specs, out_specs=out_specs, check_vma=False)
```

```python
import functools
import math

import jax
import jax.numpy as jnp
from jax import lax
from jax.experimental import pallas as pl
from jax.experimental.pallas import tpu as pltpu
from jax.sharding import PartitionSpec as P


COPIES = 4


ADAPTER_SCALE = 2.0
ROPE_BASE = 500000.0


def rotate_keys(key_rows, positions):
    head_length = key_rows.shape[-1]
    half_size = head_length // 2
    frequency = ROPE_BASE ** (-(jnp.arange(half_size, dtype=jnp.float32) * 2.0 / head_length))
    angles = positions.astype(jnp.float32)[:, :, None, None] * frequency
    cosine = jnp.cos(angles)
    sine_val = jnp.sin(angles)
    first_half = key_rows[..., :half_size]
    second_half = key_rows[..., half_size:]
    return jnp.concatenate(
        [
            first_half * cosine - second_half * sine_val,
            second_half * cosine + first_half * sine_val,
        ],
        axis=-1,
    )


def attend(queries, stored, lengths_now, fresh_kv):
    request_slot_count, decode_step_count, heads_local, head_length = queries.shape
    local_key_value = stored.shape[2]
    group_size = heads_local // local_key_value
    grouped = queries.reshape(
        request_slot_count, decode_step_count, local_key_value, group_size, head_length
    )
    score_scale = 1.0 / math.sqrt(head_length)
    past_scores = (
        jnp.einsum(
            "msgjd,mcgd->msgjc",
            grouped,
            stored[..., :head_length],
            preferred_element_type=jnp.float32,
        )
        * score_scale
    )
    recent_scores = (
        jnp.einsum(
            "msgjd,mtgd->msgjt",
            grouped,
            fresh_kv[..., :head_length],
            preferred_element_type=jnp.float32,
        )
        * score_scale
    )
    row_ids = jnp.arange(stored.shape[1], dtype=jnp.int32)
    past_ok = (row_ids[None, :] < lengths_now[:, None])[:, None, None, None, :]
    step_ids = jnp.arange(decode_step_count, dtype=jnp.int32)
    recent_ok = (step_ids[None, :] <= step_ids[:, None])[None, :, None, None, :]
    past_scores = jnp.where(past_ok, past_scores, -jnp.inf)
    recent_scores = jnp.where(recent_ok, recent_scores, -jnp.inf)
    peak_score = jnp.maximum(jnp.max(past_scores, -1), jnp.max(recent_scores, -1))[..., None]
    past_exp = jnp.exp(past_scores - peak_score)
    recent_exp = jnp.exp(recent_scores - peak_score)
    denom_sum = jnp.sum(past_exp, -1, keepdims=True) + jnp.sum(recent_exp, -1, keepdims=True)
    past_w = (past_exp / denom_sum).astype(jnp.bfloat16)
    recent_w = (recent_exp / denom_sum).astype(jnp.bfloat16)
    mixed_out = jnp.einsum(
        "msgjc,mcgd->msgjd", past_w, stored[..., head_length:], preferred_element_type=jnp.float32
    )
    mixed_out = mixed_out + jnp.einsum(
        "msgjt,mtgd->msgjd",
        recent_w,
        fresh_kv[..., head_length:],
        preferred_element_type=jnp.float32,
    )
    return mixed_out.reshape(request_slot_count, decode_step_count, heads_local * head_length)


def local_general(
    hidden,
    queries,
    kv_cache,
    w_kv,
    store_a,
    store_b,
    lengths,
    arrival_from,
    arrival_slot,
    resident_adapter,
    arrival_adapter,
    hot_holder,
    hot_dest,
):
    my_index = lax.axis_index("replica")
    replicas = lax.axis_size("replica")
    resident = kv_cache.shape[0]
    arrive = arrival_from.shape[1]
    request_slot_count = resident + arrive
    decode_step_count = hidden.shape[1]
    head_length = queries.shape[3]
    local_key_value = kv_cache.shape[2]
    slot_total = store_a.shape[0]
    hot_total = hot_holder.shape[0]
    spans = hot_total // COPIES
    my_from = lax.dynamic_index_in_dim(arrival_from, my_index, 0, keepdims=False)
    my_slot = lax.dynamic_index_in_dim(arrival_slot, my_index, 0, keepdims=False)
    own_ids = my_index * resident + jnp.arange(resident, dtype=jnp.int32)
    leaving_ids = (arrival_from * resident + arrival_slot).reshape(-1)
    staying = jnp.logical_not(jnp.any(own_ids[:, None] == leaving_ids[None, :], axis=1))
    live_mask = jnp.concatenate([staying, jnp.ones((arrive,), bool)])
    own_len = lax.dynamic_slice_in_dim(lengths, my_index * resident, resident)
    arrival_len = jnp.take(lengths, my_from * resident + my_slot)
    seen_len = jnp.concatenate([own_len, arrival_len])
    takes_mine = arrival_from == my_index
    sends_any = jnp.any(takes_mine, axis=1)
    send_slot = jnp.sum(jnp.where(takes_mine, arrival_slot, 0), axis=1)
    outgoing = jnp.take(kv_cache, send_slot, axis=0)
    outgoing = jnp.where(sends_any[:, None, None, None], outgoing, jnp.zeros((), jnp.bfloat16))
    incoming = lax.all_to_all(outgoing, "replica", split_axis=0, concat_axis=0, tiled=True)
    blocks = hot_dest.reshape(COPIES, spans, hot_dest.shape[1])
    holder_grid = hot_holder.reshape(COPIES, spans)
    holder_rep = holder_grid // slot_total
    mine = holder_rep == my_index
    has_one = jnp.any(mine, axis=1)
    local_pick = jnp.sum(jnp.where(mine, holder_grid % slot_total, 0), axis=1)

    def spread_rows(store):
        rows = jnp.take(store, local_pick, axis=0)
        rows = jnp.where(has_one[:, None, None, None], rows, jnp.zeros((), jnp.bfloat16))
        return rows.reshape(COPIES, replicas, -1).transpose(1, 0, 2)

    got_a, got_b = (
        lax.all_to_all(spread_rows(store_a), "replica", split_axis=0, concat_axis=0, tiled=True),
        lax.all_to_all(spread_rows(store_b), "replica", split_axis=0, concat_axis=0, tiled=True),
    )
    replica_ids = jnp.arange(replicas, dtype=jnp.int32)
    member = jnp.any(blocks[:, :, :, None] == replica_ids[None, None, None, :], axis=2).astype(
        jnp.int32
    )
    source_rep = jnp.sum(member * holder_rep[:, :, None], axis=1)
    copy_ids = jnp.arange(COPIES, dtype=jnp.int32)
    route_a = got_a[source_rep.T, copy_ids[None, :]]
    route_b = got_b[source_rep.T, copy_ids[None, :]]
    recv_a, recv_b = (
        lax.all_to_all(route_a, "replica", split_axis=0, concat_axis=0, tiled=True),
        lax.all_to_all(route_b, "replica", split_axis=0, concat_axis=0, tiled=True),
    )
    installed_a = recv_a.transpose(1, 0, 2).reshape((COPIES,) + store_a.shape[1:])
    installed_b = recv_b.transpose(1, 0, 2).reshape((COPIES,) + store_b.shape[1:])
    own_adapter = lax.dynamic_slice_in_dim(resident_adapter, my_index * resident, resident)
    my_choice = lax.dynamic_index_in_dim(arrival_adapter, my_index, 0, keepdims=False)
    adapt_a = jnp.concatenate(
        [jnp.take(store_a, own_adapter, axis=0), jnp.take(installed_a, my_choice, axis=0)]
    )
    adapter_up_weight = jnp.concatenate(
        [jnp.take(store_b, own_adapter, axis=0), jnp.take(installed_b, my_choice, axis=0)]
    )
    partial_value = jnp.einsum(
        "msd,mpkd->mspk", hidden, adapt_a, preferred_element_type=jnp.float32
    )
    base_projection = jnp.einsum(
        "msd,dgc->msgc",
        lax.all_gather(hidden, "tensor", axis=2, tiled=True),
        w_kv,
        preferred_element_type=jnp.float32,
    )
    down_projected = lax.psum(partial_value, "tensor")
    down_projected = down_projected.astype(jnp.bfloat16)
    adapter_update = jnp.einsum(
        "gnot,gote->gnoe", down_projected, adapter_up_weight, preferred_element_type=jnp.float32
    )
    adapter_update = (
        adapter_update.reshape(
            request_slot_count, decode_step_count, 2, local_key_value, head_length
        )
        .transpose(0, 1, 3, 2, 4)
        .reshape(request_slot_count, decode_step_count, local_key_value, 2 * head_length)
    )
    unrotated_key_value = base_projection + ADAPTER_SCALE * adapter_update
    positions = seen_len[:, None] + jnp.arange(decode_step_count, dtype=jnp.int32)[None, :]
    fresh_kv = jnp.concatenate(
        [
            rotate_keys(unrotated_key_value[..., :head_length], positions),
            unrotated_key_value[..., head_length:],
        ],
        axis=-1,
    ).astype(jnp.bfloat16)
    stay_out = attend(queries[:resident], kv_cache, own_len, fresh_kv[:resident])
    arrived = jnp.take(incoming, my_from, axis=0)
    row_ids = jnp.arange(kv_cache.shape[1], dtype=jnp.int32)
    arrived = jnp.where(
        (row_ids[None, :] < arrival_len[:, None])[:, :, None, None],
        arrived,
        jnp.zeros((), jnp.bfloat16),
    )
    move_out = attend(queries[resident:], arrived, arrival_len, fresh_kv[resident:])
    mixed_out = jnp.concatenate([stay_out, move_out], axis=0)
    attn_out = jnp.where(live_mask[:, None, None], mixed_out, 0.0).astype(jnp.bfloat16)
    new_kv = jnp.where(live_mask[:, None, None, None], fresh_kv, jnp.zeros((), jnp.bfloat16))
    return (attn_out, new_kv, arrived, installed_a, installed_b)


def partner(array, mask):
    return lax.ppermute(array, "replica", [(i, i ^ mask) for i in range(lax.axis_size("replica"))])


def shifted(array, step):
    size = lax.axis_size("tensor")
    return lax.ppermute(array, "tensor", [(i, (i + step) % size) for i in range(size)])


ALWAYS = ((0, 2), (2, 3))
AT_NEED = ((5, 1), (6, 1), (7, 1))
SMEM = pl.BlockSpec(memory_space=pltpu.SMEM)
VMEM = pl.BlockSpec(memory_space=pltpu.VMEM)


def wanted_by(holder, dest, spans, replica, copy_id):
    row = jnp.int32(0)
    for span in range(spans):
        at = copy_id * spans + span
        row += jnp.where(dest[0, at] == replica, holder[at], 0)
    return row


def crossing(holder, dest, spans, slot_total, chip):
    items, count = [], jnp.int32(0)
    for copy_id in range(COPIES):
        for core in range(2):
            row = wanted_by(holder, dest, spans, 2 * chip + core, copy_id)
            crosses = row // (2 * slot_total) != chip
            items.append((copy_id, core, row, crosses, count))
            count = count + crosses.astype(jnp.int32)
    return items


def staged(groups, meanwhile=None):
    def when(condition, action):
        if condition is None:
            action()
        else:
            pl.when(condition)(action)

    def begin(at, sources, buffer, sems):
        for condition, source in sources:
            when(condition, pltpu.make_async_copy(source, buffer.at[at], sems.at[0, at]).start)

    def forward(at, targets, buffer, sems):
        pltpu.make_async_copy(buffer.at[at], buffer.at[at], sems.at[0, at]).wait()
        for condition, target in targets:
            when(condition, pltpu.make_async_copy(buffer.at[at], target, sems.at[1, at]).start)

    def finish(at, buffer, sems):
        pltpu.make_async_copy(buffer.at[at], buffer.at[at], sems.at[1, at]).wait()

    for moves, buffer, sems in groups:
        for at, (condition, sources, _) in enumerate(moves):
            when(condition, functools.partial(begin, at, sources, buffer, sems))
    if meanwhile is not None:
        meanwhile()
    for moves, buffer, sems in groups:
        for at, (condition, _, targets) in enumerate(moves):
            when(condition, functools.partial(forward, at, targets, buffer, sems))
    for moves, buffer, sems in groups:
        for at, (condition, _, _) in enumerate(moves):
            when(condition, functools.partial(finish, at, buffer, sems))


def collect_kernel(spans, slot_total, masks, *refs):
    (me_ref, arrival_from, arrival_slot, holder, kv_cache, store_a, store_b, hidden) = refs[:8]
    *leaving, rows_a, rows_b, rows, asking = refs[8 : 12 + len(masks)]
    *buffers, raw, even = refs[12 + len(masks) : 17 + len(masks)]
    *semaphores, raw_sems, even_sems = refs[17 + len(masks) :]
    me = me_ref[0]
    moves = []
    for i, mask in enumerate(masks):
        to = me ^ mask
        slot = jnp.int32(0)
        for a in range(arrival_from.shape[0]):
            slot += jnp.where(arrival_from[a, to] == me, arrival_slot[a, to], 0)
        moves.append((None, [(None, kv_cache.at[slot])], [(None, leaving[i])]))
    groups = [moves]
    held = []
    for copy_id in range(COPIES):
        slot = jnp.int32(0)
        for span in range(spans):
            row = holder[copy_id * spans + span]
            slot += jnp.where(row // slot_total == me, row % slot_total, 0)
        held.append(slot)
    for table, target in ((store_a, rows_a), (store_b, rows_b)):
        groups.append(
            [
                (None, [(None, table.at[slot])], [(None, target.at[copy_id])])
                for copy_id, slot in enumerate(held)
            ]
        )

    start = rows.shape[0] - asking.shape[0]
    fetch = pltpu.make_async_copy(hidden, raw, raw_sems.at[0, 0])
    puts = [
        pltpu.make_async_copy(even, rows, even_sems.at[0, 0]),
        pltpu.make_async_copy(even.at[start:], asking, even_sems.at[1, 0]),
    ]

    def regroup():
        count = raw.shape[0] * raw.shape[1]
        blank = jnp.zeros((rows.shape[0] - count, rows.shape[1]), rows.dtype)
        fetch.wait()
        every = raw[...].reshape(count, rows.shape[1])
        even[...] = jnp.concatenate([every, blank], axis=0)
        for put in puts:
            put.start()

    fetch.start()
    staged(list(zip(groups, buffers, semaphores)), regroup)
    for put in puts:
        put.wait()


def pack_kernel(spans, slot_total, *refs):
    (me_ref, holder, dest, store_a, store_b, sibling_a, sibling_b) = refs[:7]
    across_b, *units = refs[7:-5]
    spread = ALWAYS + AT_NEED
    extra, buffer_b, buffer_a, sems_b, sems_a = refs[-5:]
    me = me_ref[0]
    core = me % 2
    chip = 1 - me // 2
    items = crossing(holder, dest, spans, slot_total, chip)
    moves_b, moves_a = [], []
    for copy_id in range(COPIES):
        row = jnp.where(core == 0, items[2 * copy_id][2], items[2 * copy_id + 1][2])
        own = row // slot_total == me
        sources = [
            (own, store_b.at[row % slot_total]),
            (jnp.logical_not(own), sibling_b.at[copy_id]),
        ]
        moves_b.append((None, sources, [(None, across_b.at[copy_id])]))
    for at, (copy_id, _, row, crosses, unit) in enumerate(items):
        own = row // slot_total == me
        sources = [
            (own, store_a.at[row % slot_total, core]),
            (jnp.logical_not(own), sibling_a.at[copy_id, core]),
        ]
        targets = [
            (
                jnp.logical_and(unit >= start, unit < start + size),
                array.at[jnp.clip(unit - start, 0, size - 1)],
            )
            for array, (start, size) in zip(units, spread)
            if start <= at
        ]
        moves_a.append((crosses, sources, targets))
    count = items[-1][4] + items[-1][3].astype(jnp.int32)
    extra[0] = jnp.clip(count - AT_NEED[0][0], 0, len(AT_NEED))
    staged([(moves_b, buffer_b, sems_b), (moves_a, buffer_a, sems_a)])


def place_kernel(spans, slot_total, spread, *refs):
    (me_ref, holder, dest, earlier) = refs[:4]
    got, other = refs[4 : 4 + len(spread)], refs[4 + len(spread) : 4 + 2 * len(spread)]
    out, buffer, sems = refs[-3:]
    me = me_ref[0]
    core = me % 2
    first_unit = spread[0][0]
    past_unit = spread[-1][0] + spread[-1][1]
    items = crossing(holder, dest, spans, slot_total, me // 2)
    moves = []
    for copy_id in range(COPIES):
        one, two = items[2 * copy_id], items[2 * copy_id + 1]
        crosses = jnp.where(core == 0, one[3].astype(jnp.int32), two[3].astype(jnp.int32)) != 0
        unit = jnp.where(core == 0, one[4], two[4])
        possible = [i for i, (start, _) in enumerate(spread) if start <= 2 * copy_id + 1]
        if first_unit and not possible:
            continue
        here = jnp.logical_and(unit >= first_unit, unit < past_unit)
        for half, arrays in ((core, got), (1 - core, other)):
            sources = []
            active = jnp.logical_and(crosses, here)
            if not first_unit:
                near = jnp.logical_not(crosses)
                active = jnp.logical_or(near, here)
                sources.append((near, earlier.at[copy_id, half]))
            for i in possible:
                start, size = spread[i]
                hit = jnp.logical_and(unit >= start, unit < start + size)
                source = arrays[i].at[jnp.clip(unit - start, 0, size - 1)]
                sources.append((jnp.logical_and(crosses, hit), source))
            moves.append((active, sources, [(None, out.at[copy_id, half])]))
    staged([(moves, buffer, sems)])


def copy_call(kernel, tables, arrays, shapes, scratch, scalars=(), aliases=None):
    hbm = pl.BlockSpec(memory_space=pl.ANY)
    dtype = arrays[0].dtype
    return pl.pallas_call(
        kernel,
        out_shape=[pltpu.HBM(shape, dtype) for shape in shapes]
        + [jax.ShapeDtypeStruct(shape, jnp.int32) for shape in scalars],
        in_specs=[SMEM] * len(tables) + [hbm] * len(arrays),
        out_specs=[hbm] * len(shapes) + [SMEM] * len(scalars),
        scratch_shapes=[pltpu.VMEM(shape, dtype) for shape in scratch]
        + [pltpu.SemaphoreType.DMA((2, shape[0])) for shape in scratch],
        input_output_aliases=aliases or {},
    )(*tables, *arrays)


def project_kernel(spans, slot_total, resident, steps, masks, *refs):
    (me_ref, resident_adapter, arrival_adapter, holder, dest, hidden, *others) = refs[: 6 + len(masks)]
    store, *outs, left, adapters, sums = refs[6 + len(masks) :]
    me = me_ref[0]
    group = pl.program_id(0)
    base = hidden.shape[0]
    block = others[0].shape[0]
    width = sums.shape[1]
    per_step = store.shape[1] // width

    @pl.when(group == 0)
    def _():
        left[0:base] = hidden[...]
        for i, other in enumerate(others):
            left[base + i * block : base + (i + 1) * block] = other[...]
        sums[...] = jnp.zeros_like(sums)
        ids = lax.broadcasted_iota(jnp.int32, sums.shape, 0) // steps
        own = jnp.full(sums.shape, -1, jnp.int32)
        for slot in range(resident):
            own = jnp.where(ids == slot, resident_adapter[me * resident + slot], own)
        for i, mask in enumerate((0,) + masks):
            replica = me ^ mask
            first = resident if i == 0 else (base + (i - 1) * block) // steps
            for a in range(arrival_adapter.shape[0]):
                chosen = arrival_adapter[a, replica]
                row = jnp.int32(0)
                for span in range(spans):
                    at = chosen * spans + span
                    row += jnp.where(dest[0, at] == replica, holder[at], 0)
                here = jnp.where(row // slot_total == me, row % slot_total, -1)
                own = jnp.where(ids == first + a, here, own)
        adapters[...] = own

    product = lax.dot_general(
        left[...], store[0], (((1,), (1,)), ((), ())), preferred_element_type=jnp.float32
    )
    for i in range(per_step):
        hit = adapters[...] == group * per_step + i
        sums[...] += jnp.where(hit, product[:, i * width : (i + 1) * width], 0.0)

    @pl.when(group == pl.num_programs(0) - 1)
    def _():
        outs[0][...] = sums[0:base]
        for i, out in enumerate(outs[1:]):
            out[...] = sums[base + i * block : base + (i + 1) * block]


def gather_kernel(shard_ref, *refs):
    out = refs[-1]
    count = len(refs) - 1
    width = refs[0].shape[1]
    for step, ref in enumerate(refs[:-1]):
        source = lax.rem(shard_ref[0] + count - step, count)
        out[:, pl.ds(pl.multiple_of(source * width, width), width)] = ref[...]


def attend_kernel(spans, masks, resident, steps, kv_heads, head_length, *refs):
    (me_ref, lengths, arrival_from, arrival_slot, resident_adapter, arrival_adapter) = refs[:6]
    holder, dest, *parts = refs[6 : -14 - len(masks)]
    came = refs[-14 - len(masks) : -14]
    store_b, sibling_b, across_b, base, queries, cache = refs[-14:-8]
    out, new_kv, arrived, installed_b = refs[-8:-4]
    fresh_ref, mixed_ref, score_ref, weight_ref = refs[-4:]
    me = me_ref[0]
    arrive = arrival_from.shape[0]
    replicas = arrival_from.shape[1]
    slots = resident + arrive
    row_count = base.shape[1]
    rank = store_b.shape[1] // 2
    slot_total = store_b.shape[0]
    half = head_length // 2
    seen = [lengths[me * resident + slot] for slot in range(resident)]
    for a in range(arrive):
        seen.append(lengths[arrival_from[a, me] * resident + arrival_slot[a, me]])

    for a in range(arrive):
        for ref, mask in zip(came, masks):

            @pl.when(arrival_from[a, me] == me ^ mask)
            def _():
                arrived[a] = ref[...]

        def clear(row, carry):
            arrived[a, row] = jnp.zeros(arrived.shape[2:], arrived.dtype)
            return carry

        lax.fori_loop(seen[resident + a], arrived.shape[1], clear, 0)
    for copy_id in range(COPIES):
        near = wanted_by(holder, dest, spans, me, copy_id) // (2 * slot_total) == me // 2

        @pl.when(near)
        def _():
            installed_b[copy_id] = sibling_b[copy_id]

        @pl.when(jnp.logical_not(near))
        def _():
            installed_b[copy_id] = across_b[copy_id]

    total = parts[0][...]
    for part in parts[1:]:
        total = total + part[...]
    down = total.astype(jnp.bfloat16)

    ids = lax.broadcasted_iota(jnp.int32, (row_count, 1), 0) // steps
    adapters = jnp.zeros((row_count, 1), jnp.int32)
    position = lax.broadcasted_iota(jnp.int32, (row_count, 1), 0) % steps
    for slot in range(slots):
        if slot < resident:
            adapter = resident_adapter[me * resident + slot]
        else:
            adapter = store_b.shape[0] + arrival_adapter[slot - resident, me]
        adapters = jnp.where(ids == slot, adapter, adapters)
        position = jnp.where(ids == slot, position + seen[slot], position)
    deltas = [jnp.zeros((row_count, store_b.shape[2]), jnp.float32) for _ in range(2)]
    for adapter in range(store_b.shape[0] + COPIES):
        if adapter < store_b.shape[0]:
            table = store_b[adapter]
        else:
            table = installed_b[adapter - store_b.shape[0]]
        for part in range(2):
            product = jnp.dot(
                down[:, part * rank : (part + 1) * rank],
                table[part * rank : (part + 1) * rank],
                preferred_element_type=jnp.float32,
            )
            deltas[part] = jnp.where(adapters == adapter, product, deltas[part])

    lane = lax.broadcasted_iota(jnp.int32, (1, half), 1).astype(jnp.float32)
    frequency = jnp.exp(lane * (-2.0 * math.log(ROPE_BASE) / head_length))
    angles = position.astype(jnp.float32) * frequency
    cosine, sine = jnp.cos(angles), jnp.sin(angles)
    dead = jnp.zeros((row_count, 1), jnp.bool_)
    gone = [jnp.int32(0)] * resident
    for q in range(replicas):
        for a in range(arrive):
            mine = arrival_from[a, q] == me
            slot = arrival_slot[a, q]
            dead = jnp.logical_or(dead, jnp.logical_and(ids == slot, mine))
            for n in range(resident):
                gone[n] = jnp.where(jnp.logical_and(mine, slot == n), 1, gone[n])
    for g in range(kv_heads):
        columns = slice(g * head_length, (g + 1) * head_length)
        key = base[g, :, :head_length] + ADAPTER_SCALE * deltas[0][:, columns]
        value = base[g, :, head_length:] + ADAPTER_SCALE * deltas[1][:, columns]
        u, w = key[:, :half], key[:, half:]
        key = jnp.concatenate([u * cosine - w * sine, w * cosine + u * sine], axis=1)
        for part, piece in enumerate((key, value)):
            rounded = piece.astype(jnp.bfloat16).astype(jnp.float32)
            lanes = slice(part * head_length, (part + 1) * head_length)
            fresh_ref[part, pl.ds(g, row_count, stride=kv_heads)] = rounded
            kept = jnp.where(dead, 0.0, rounded)[: slots * steps]
            new_kv[:, :, g, lanes] = kept.reshape(slots, steps, head_length).astype(jnp.bfloat16)

    query_rows = queries.shape[1]
    heads = query_rows // steps
    cache_rows = cache.shape[1] * kv_heads
    new_rows = steps * kv_heads
    pad_rows = 16 - new_rows
    row = lax.broadcasted_iota(jnp.int32, (query_rows, 1), 0)
    step_of = row // heads
    group_of = row % heads // (heads // kv_heads)
    column = lax.broadcasted_iota(jnp.int32, (query_rows, cache_rows), 1)
    same = column % kv_heads == group_of
    past_row = column // kv_heads
    late = lax.broadcasted_iota(jnp.int32, (query_rows, 128), 1)
    allowed = jnp.logical_and(late % kv_heads == group_of, late // kv_heads <= step_of)
    allowed = jnp.logical_and(allowed, late < new_rows)
    scale = 1.0 / math.sqrt(head_length)

    def cached(n):
        stored = cache[n] if n < resident else arrived[n - resident]
        return stored.reshape(cache_rows, 2 * head_length)

    def fresh_rows(n, part):
        lines = fresh_ref[part, n * new_rows : (n + 1) * new_rows]
        blank = jnp.zeros((pad_rows, head_length), jnp.float32)
        return jnp.concatenate([lines, blank], axis=0).astype(jnp.bfloat16)

    def against(query, keys):
        return lax.dot_general(
            query, keys, (((1,), (1,)), ((), ())), preferred_element_type=jnp.float32
        )

    for n in range(slots):
        lines = slice(n * query_rows, (n + 1) * query_rows)
        query = queries[n]
        score = against(query, cached(n)[:, :head_length]) * scale
        score = jnp.where(jnp.logical_and(same, past_row < seen[n]), score, -jnp.inf)
        score_ref[lines, :cache_rows] = score
        keys = jnp.concatenate(
            [fresh_rows(n, 0), jnp.zeros((128 - 16, head_length), jnp.bfloat16)], axis=0
        )
        score = against(query, keys) * scale
        score_ref[lines, cache_rows:] = jnp.where(allowed, score, -jnp.inf)
    for n in range(slots):
        lines = slice(n * query_rows, (n + 1) * query_rows)
        score = score_ref[lines]
        term = jnp.exp(score - jnp.max(score, axis=1, keepdims=True))
        inverse = 1.0 / jnp.sum(term, axis=1, keepdims=True)
        weight_ref[lines] = (term * inverse).astype(jnp.bfloat16)
    for n in range(slots):
        lines = slice(n * query_rows, (n + 1) * query_rows)
        weight = weight_ref[lines]
        mixed = jnp.dot(
            weight[:, :cache_rows], cached(n)[:, head_length:], preferred_element_type=jnp.float32
        )
        mixed = mixed + jnp.dot(
            weight[:, cache_rows : cache_rows + 16],
            fresh_rows(n, 1),
            preferred_element_type=jnp.float32,
        )
        if n < resident:
            mixed = jnp.where(gone[n] != 0, 0.0, mixed)
        mixed_ref[lines] = mixed
    for n in range(slots):
        for head in range(heads):
            lanes = slice(head * head_length, (head + 1) * head_length)
            pair = mixed_ref[pl.ds(n * query_rows + head, steps, stride=heads)]
            out[n, :, lanes] = pair.astype(jnp.bfloat16)


def pairs_layer(
    hidden,
    queries,
    kv_cache,
    w_kv,
    store_a,
    store_b,
    lengths,
    arrival_from,
    arrival_slot,
    resident_adapter,
    arrival_adapter,
    hot_holder,
    hot_dest,
):
    me = lax.axis_index("replica")
    replicas = lax.axis_size("replica")
    shards = lax.axis_size("tensor")
    resident, cap, kv_heads, head_pair = kv_cache.shape
    arrive = arrival_from.shape[1]
    slots = resident + arrive
    steps, features = hidden.shape[1:]
    heads, head_length = queries.shape[2:]
    slot_total = store_a.shape[0]
    rank = store_a.shape[2]
    spans = hot_holder.shape[0] // COPIES
    row_a, row_b = store_a.shape[1:], store_b.shape[1:]
    columns = store_b.shape[3]
    masks = tuple(range(1, replicas))
    me_table = jnp.reshape(me, (1,)).astype(jnp.int32)
    shard_table = jnp.reshape(lax.axis_index("tensor"), (1,)).astype(jnp.int32)
    from_table, slot_table, choice_table = arrival_from.T, arrival_slot.T, arrival_adapter.T
    dest_table = hot_dest.T

    used = slots * steps
    padded = -(-used // 8) * 8
    first = resident * steps
    block = padded - first

    *leaving, rows_a, rows_b, rows, asking = copy_call(
        functools.partial(collect_kernel, spans, slot_total, masks),
        (me_table, from_table, slot_table, hot_holder),
        (kv_cache, store_a, store_b, hidden),
        [kv_cache.shape[1:]] * len(masks)
        + [(COPIES,) + row_a, (COPIES,) + row_b, (padded, features), (block, features)],
        [
            (len(masks),) + kv_cache.shape[1:],
            (COPIES,) + row_a,
            (COPIES,) + row_b,
            hidden.shape,
            (padded, features),
        ],
    )
    sibling_a = partner(rows_a, 1)
    sibling_b = partner(rows_b, 1)
    other_rows = [partner(asking, mask) for mask in masks]
    came = [partner(array, mask) for array, mask in zip(leaving, masks)]
    around = [rows] + [shifted(rows, step) for step in range(1, shards)]

    line_count = padded + len(masks) * block
    per_step = 2 if slot_total % 2 == 0 else 1
    partial, *sent = pl.pallas_call(
        functools.partial(project_kernel, spans, slot_total, resident, steps, masks),
        out_shape=[jax.ShapeDtypeStruct((padded, 2 * rank), jnp.float32)]
        + [jax.ShapeDtypeStruct((block, 2 * rank), jnp.float32)] * len(masks),
        grid=(slot_total // per_step,),
        in_specs=[SMEM] * 5
        + [pl.BlockSpec((padded, features), lambda i: (0, 0))]
        + [pl.BlockSpec((block, features), lambda i: (0, 0))] * len(masks)
        + [pl.BlockSpec((1, per_step * 2 * rank, features), lambda i: (i, 0, 0))],
        out_specs=[pl.BlockSpec((padded, 2 * rank), lambda i: (0, 0))]
        + [pl.BlockSpec((block, 2 * rank), lambda i: (0, 0))] * len(masks),
        scratch_shapes=[
            pltpu.VMEM((line_count, features), hidden.dtype),
            pltpu.VMEM((line_count, 2 * rank), jnp.int32),
            pltpu.VMEM((line_count, 2 * rank), jnp.float32),
        ],
        name="project",
    )(
        me_table,
        resident_adapter,
        choice_table,
        hot_holder,
        dest_table,
        rows,
        *other_rows,
        store_a.reshape(slot_total // per_step, per_step * 2 * rank, features),
    )
    returned = [partner(array, mask) for array, mask in zip(sent, masks)]
    last = partial[first:]
    for array in returned:
        last = last + array
    partial = jnp.concatenate([partial[:first], last])
    parts = [partial] + [shifted(partial, step) for step in range(1, shards)]

    unit_shape = row_a[1:]
    unit_total = 2 * COPIES
    across_b, *units, extra = copy_call(
        functools.partial(pack_kernel, spans, slot_total),
        (me_table, hot_holder, dest_table),
        (store_a, store_b, sibling_a, sibling_b),
        [(COPIES,) + row_b] + [(size,) + unit_shape for _, size in ALWAYS + AT_NEED],
        [(COPIES,) + row_b, (unit_total,) + unit_shape],
        [(1,)],
    )
    across_b = partner(across_b, 2)
    got = []
    for array in units[: len(ALWAYS)]:
        got.append(partner(array, 2))

    full = pl.pallas_call(
        gather_kernel,
        out_shape=jax.ShapeDtypeStruct((padded, shards * features), hidden.dtype),
        in_specs=[SMEM] + [VMEM] * shards,
        out_specs=VMEM,
        name="gather",
    )(shard_table, *around)
    base = jnp.einsum("md,dgc->gmc", full, w_kv, preferred_element_type=jnp.float32)

    attn_out, new_kv, arrived, installed_b = pl.pallas_call(
        functools.partial(attend_kernel, spans, masks, resident, steps, kv_heads, head_length),
        out_shape=[
            jax.ShapeDtypeStruct((slots, steps, heads * head_length), jnp.bfloat16),
            jax.ShapeDtypeStruct((slots, steps, kv_heads, head_pair), jnp.bfloat16),
            jax.ShapeDtypeStruct((arrive,) + kv_cache.shape[1:], jnp.bfloat16),
            jax.ShapeDtypeStruct((COPIES, 2 * rank, columns), jnp.bfloat16),
        ],
        in_specs=[SMEM] * 8 + [VMEM] * (shards + len(masks) + 6),
        out_specs=[VMEM] * 4,
        scratch_shapes=[
            pltpu.VMEM((2, padded * kv_heads, head_length), jnp.float32),
            pltpu.VMEM((slots * steps * heads, head_length), jnp.float32),
            pltpu.VMEM((slots * steps * heads, cap * kv_heads + 128), jnp.float32),
            pltpu.VMEM((slots * steps * heads, cap * kv_heads + 128), jnp.bfloat16),
        ],
        name="attend",
    )(
        me_table,
        lengths,
        from_table,
        slot_table,
        resident_adapter,
        choice_table,
        hot_holder,
        dest_table,
        *parts,
        *came,
        store_b.reshape(slot_total, 2 * rank, columns),
        sibling_b.reshape(COPIES, 2 * rank, columns),
        across_b.reshape(COPIES, 2 * rank, columns),
        base,
        queries.reshape(slots, steps * heads, head_length),
        kv_cache,
    )
    installed_b = installed_b.reshape((COPIES,) + row_b)

    tables = (me_table, hot_holder, dest_table)

    def finish(count):
        def branch(sibling_a, first_other, *arrays):
            got, rest = list(arrays[: len(ALWAYS)]), arrays[len(ALWAYS) :]
            late = [partner(array, 2) for array in rest[:count]]
            other = [first_other] + [partner(array, 1) for array in got[1:]]
            (placed,) = copy_call(
                functools.partial(place_kernel, spans, slot_total, ALWAYS),
                tables,
                (sibling_a, *got, *other),
                [(COPIES,) + row_a],
                [(unit_total,) + unit_shape],
            )
            if not count:
                return placed
            other = [partner(array, 1) for array in late]
            (placed,) = copy_call(
                functools.partial(place_kernel, spans, slot_total, AT_NEED[:count]),
                tables,
                (placed, *late, *other),
                [(COPIES,) + row_a],
                [(unit_total,) + unit_shape],
                aliases={len(tables): 0},
            )
            return placed

        return branch

    branches = [finish(count) for count in range(len(AT_NEED) + 1)]
    first_other = partner(got[0], 1)
    *rest, attn_out = lax.optimization_barrier((*units[len(ALWAYS) :], attn_out))
    installed_a = lax.switch(extra[0], branches, sibling_a, first_other, *got, *rest)
    return (attn_out, new_kv, arrived, installed_a, installed_b)


def local(*args):
    fan = args[-1].shape[1]
    if lax.axis_size("replica") == 4 and fan == 1:
        return pairs_layer(*args)
    return local_general(*args)


def solution(mesh):
    in_specs = (
        P(("parts", "replica"), None, "tensor"),
        P(("parts", "replica"), None, "tensor", None),
        P(("parts", "replica"), None, "tensor", None),
        P(None, "tensor", None),
        P(("parts", "replica"), None, None, "tensor"),
        P(("parts", "replica"), None, None, "tensor"),
        P("parts"),
        P("parts", None),
        P("parts", None),
        P("parts"),
        P("parts", None),
        P("parts"),
        P("parts", None),
    )
    out_specs = (
        P(("parts", "replica"), None, "tensor"),
        P(("parts", "replica"), None, "tensor", None),
        P(("parts", "replica"), None, "tensor", None),
        P(("parts", "replica"), None, None, "tensor"),
        P(("parts", "replica"), None, None, "tensor"),
    )
    return jax.shard_map(local, mesh=mesh, in_specs=in_specs, out_specs=out_specs, check_vma=False)
```

```python
import functools
import math

import jax
import jax.numpy as jnp
from jax import lax
from jax.experimental import pallas as pl
from jax.experimental.pallas import tpu as pltpu
from jax.sharding import PartitionSpec as P


COPIES = 4


ADAPTER_SCALE = 2.0
ROPE_BASE = 500000.0


def rotate_keys(key_rows, positions):
    head_length = key_rows.shape[-1]
    half_size = head_length // 2
    frequency = ROPE_BASE ** (-(jnp.arange(half_size, dtype=jnp.float32) * 2.0 / head_length))
    angles = positions.astype(jnp.float32)[:, :, None, None] * frequency
    cosine = jnp.cos(angles)
    sine_val = jnp.sin(angles)
    first_half = key_rows[..., :half_size]
    second_half = key_rows[..., half_size:]
    return jnp.concatenate(
        [
            first_half * cosine - second_half * sine_val,
            second_half * cosine + first_half * sine_val,
        ],
        axis=-1,
    )


def attend(queries, stored, lengths_now, fresh_kv):
    request_slot_count, decode_step_count, heads_local, head_length = queries.shape
    local_key_value = stored.shape[2]
    group_size = heads_local // local_key_value
    grouped = queries.reshape(
        request_slot_count, decode_step_count, local_key_value, group_size, head_length
    )
    score_scale = 1.0 / math.sqrt(head_length)
    past_scores = (
        jnp.einsum(
            "msgjd,mcgd->msgjc",
            grouped,
            stored[..., :head_length],
            preferred_element_type=jnp.float32,
        )
        * score_scale
    )
    recent_scores = (
        jnp.einsum(
            "msgjd,mtgd->msgjt",
            grouped,
            fresh_kv[..., :head_length],
            preferred_element_type=jnp.float32,
        )
        * score_scale
    )
    row_ids = jnp.arange(stored.shape[1], dtype=jnp.int32)
    past_ok = (row_ids[None, :] < lengths_now[:, None])[:, None, None, None, :]
    step_ids = jnp.arange(decode_step_count, dtype=jnp.int32)
    recent_ok = (step_ids[None, :] <= step_ids[:, None])[None, :, None, None, :]
    past_scores = jnp.where(past_ok, past_scores, -jnp.inf)
    recent_scores = jnp.where(recent_ok, recent_scores, -jnp.inf)
    peak_score = jnp.maximum(jnp.max(past_scores, -1), jnp.max(recent_scores, -1))[..., None]
    past_exp = jnp.exp(past_scores - peak_score)
    recent_exp = jnp.exp(recent_scores - peak_score)
    denom_sum = jnp.sum(past_exp, -1, keepdims=True) + jnp.sum(recent_exp, -1, keepdims=True)
    past_w = (past_exp / denom_sum).astype(jnp.bfloat16)
    recent_w = (recent_exp / denom_sum).astype(jnp.bfloat16)
    mixed_out = jnp.einsum(
        "msgjc,mcgd->msgjd", past_w, stored[..., head_length:], preferred_element_type=jnp.float32
    )
    mixed_out = mixed_out + jnp.einsum(
        "msgjt,mtgd->msgjd",
        recent_w,
        fresh_kv[..., head_length:],
        preferred_element_type=jnp.float32,
    )
    return mixed_out.reshape(request_slot_count, decode_step_count, heads_local * head_length)


def local_general(
    hidden,
    queries,
    kv_cache,
    w_kv,
    store_a,
    store_b,
    lengths,
    arrival_from,
    arrival_slot,
    resident_adapter,
    arrival_adapter,
    hot_holder,
    hot_dest,
):
    my_index = lax.axis_index("replica")
    replicas = lax.axis_size("replica")
    resident = kv_cache.shape[0]
    arrive = arrival_from.shape[1]
    request_slot_count = resident + arrive
    decode_step_count = hidden.shape[1]
    head_length = queries.shape[3]
    local_key_value = kv_cache.shape[2]
    slot_total = store_a.shape[0]
    hot_total = hot_holder.shape[0]
    spans = hot_total // COPIES
    my_from = lax.dynamic_index_in_dim(arrival_from, my_index, 0, keepdims=False)
    my_slot = lax.dynamic_index_in_dim(arrival_slot, my_index, 0, keepdims=False)
    own_ids = my_index * resident + jnp.arange(resident, dtype=jnp.int32)
    leaving_ids = (arrival_from * resident + arrival_slot).reshape(-1)
    staying = jnp.logical_not(jnp.any(own_ids[:, None] == leaving_ids[None, :], axis=1))
    live_mask = jnp.concatenate([staying, jnp.ones((arrive,), bool)])
    own_len = lax.dynamic_slice_in_dim(lengths, my_index * resident, resident)
    arrival_len = jnp.take(lengths, my_from * resident + my_slot)
    seen_len = jnp.concatenate([own_len, arrival_len])
    takes_mine = arrival_from == my_index
    sends_any = jnp.any(takes_mine, axis=1)
    send_slot = jnp.sum(jnp.where(takes_mine, arrival_slot, 0), axis=1)
    outgoing = jnp.take(kv_cache, send_slot, axis=0)
    outgoing = jnp.where(sends_any[:, None, None, None], outgoing, jnp.zeros((), jnp.bfloat16))
    incoming = lax.all_to_all(outgoing, "replica", split_axis=0, concat_axis=0, tiled=True)
    blocks = hot_dest.reshape(COPIES, spans, hot_dest.shape[1])
    holder_grid = hot_holder.reshape(COPIES, spans)
    holder_rep = holder_grid // slot_total
    mine = holder_rep == my_index
    has_one = jnp.any(mine, axis=1)
    local_pick = jnp.sum(jnp.where(mine, holder_grid % slot_total, 0), axis=1)

    def spread_rows(store):
        rows = jnp.take(store, local_pick, axis=0)
        rows = jnp.where(has_one[:, None, None, None], rows, jnp.zeros((), jnp.bfloat16))
        return rows.reshape(COPIES, replicas, -1).transpose(1, 0, 2)

    got_a, got_b = (
        lax.all_to_all(spread_rows(store_a), "replica", split_axis=0, concat_axis=0, tiled=True),
        lax.all_to_all(spread_rows(store_b), "replica", split_axis=0, concat_axis=0, tiled=True),
    )
    replica_ids = jnp.arange(replicas, dtype=jnp.int32)
    member = jnp.any(blocks[:, :, :, None] == replica_ids[None, None, None, :], axis=2).astype(
        jnp.int32
    )
    source_rep = jnp.sum(member * holder_rep[:, :, None], axis=1)
    copy_ids = jnp.arange(COPIES, dtype=jnp.int32)
    route_a = got_a[source_rep.T, copy_ids[None, :]]
    route_b = got_b[source_rep.T, copy_ids[None, :]]
    recv_a, recv_b = (
        lax.all_to_all(route_a, "replica", split_axis=0, concat_axis=0, tiled=True),
        lax.all_to_all(route_b, "replica", split_axis=0, concat_axis=0, tiled=True),
    )
    installed_a = recv_a.transpose(1, 0, 2).reshape((COPIES,) + store_a.shape[1:])
    installed_b = recv_b.transpose(1, 0, 2).reshape((COPIES,) + store_b.shape[1:])
    own_adapter = lax.dynamic_slice_in_dim(resident_adapter, my_index * resident, resident)
    my_choice = lax.dynamic_index_in_dim(arrival_adapter, my_index, 0, keepdims=False)
    adapt_a = jnp.concatenate(
        [jnp.take(store_a, own_adapter, axis=0), jnp.take(installed_a, my_choice, axis=0)]
    )
    adapter_up_weight = jnp.concatenate(
        [jnp.take(store_b, own_adapter, axis=0), jnp.take(installed_b, my_choice, axis=0)]
    )
    partial_value = jnp.einsum(
        "msd,mpkd->mspk", hidden, adapt_a, preferred_element_type=jnp.float32
    )
    base_projection = jnp.einsum(
        "msd,dgc->msgc",
        lax.all_gather(hidden, "tensor", axis=2, tiled=True),
        w_kv,
        preferred_element_type=jnp.float32,
    )
    down_projected = lax.psum(partial_value, "tensor")
    down_projected = down_projected.astype(jnp.bfloat16)
    adapter_update = jnp.einsum(
        "gnot,gote->gnoe", down_projected, adapter_up_weight, preferred_element_type=jnp.float32
    )
    adapter_update = (
        adapter_update.reshape(
            request_slot_count, decode_step_count, 2, local_key_value, head_length
        )
        .transpose(0, 1, 3, 2, 4)
        .reshape(request_slot_count, decode_step_count, local_key_value, 2 * head_length)
    )
    unrotated_key_value = base_projection + ADAPTER_SCALE * adapter_update
    positions = seen_len[:, None] + jnp.arange(decode_step_count, dtype=jnp.int32)[None, :]
    fresh_kv = jnp.concatenate(
        [
            rotate_keys(unrotated_key_value[..., :head_length], positions),
            unrotated_key_value[..., head_length:],
        ],
        axis=-1,
    ).astype(jnp.bfloat16)
    stay_out = attend(queries[:resident], kv_cache, own_len, fresh_kv[:resident])
    arrived = jnp.take(incoming, my_from, axis=0)
    row_ids = jnp.arange(kv_cache.shape[1], dtype=jnp.int32)
    arrived = jnp.where(
        (row_ids[None, :] < arrival_len[:, None])[:, :, None, None],
        arrived,
        jnp.zeros((), jnp.bfloat16),
    )
    move_out = attend(queries[resident:], arrived, arrival_len, fresh_kv[resident:])
    mixed_out = jnp.concatenate([stay_out, move_out], axis=0)
    attn_out = jnp.where(live_mask[:, None, None], mixed_out, 0.0).astype(jnp.bfloat16)
    new_kv = jnp.where(live_mask[:, None, None, None], fresh_kv, jnp.zeros((), jnp.bfloat16))
    return (attn_out, new_kv, arrived, installed_a, installed_b)


def partner(array, mask):
    return lax.ppermute(array, "replica", [(i, i ^ mask) for i in range(lax.axis_size("replica"))])


def shifted(array, step):
    size = lax.axis_size("tensor")
    return lax.ppermute(array, "tensor", [(i, (i + step) % size) for i in range(size)])


ALWAYS = ((0, 2), (2, 3))
AT_NEED = ((5, 1), (6, 1), (7, 1))
SMEM = pl.BlockSpec(memory_space=pltpu.SMEM)
VMEM = pl.BlockSpec(memory_space=pltpu.VMEM)


def wanted_by(holder, dest, spans, replica, copy_id):
    row = jnp.int32(0)
    for span in range(spans):
        at = copy_id * spans + span
        row += jnp.where(dest[0, at] == replica, holder[at], 0)
    return row


def crossing(holder, dest, spans, slot_total, chip):
    items, count = [], jnp.int32(0)
    for copy_id in range(COPIES):
        for core in range(2):
            row = wanted_by(holder, dest, spans, 2 * chip + core, copy_id)
            crosses = row // (2 * slot_total) != chip
            items.append((copy_id, core, row, crosses, count))
            count = count + crosses.astype(jnp.int32)
    return items


def staged(groups, meanwhile=None):
    def when(condition, action):
        if condition is None:
            action()
        else:
            pl.when(condition)(action)

    def begin(at, sources, buffer, sems):
        for condition, source in sources:
            when(condition, pltpu.make_async_copy(source, buffer.at[at], sems.at[0, at]).start)

    def forward(at, targets, buffer, sems):
        pltpu.make_async_copy(buffer.at[at], buffer.at[at], sems.at[0, at]).wait()
        for condition, target in targets:
            when(condition, pltpu.make_async_copy(buffer.at[at], target, sems.at[1, at]).start)

    def finish(at, buffer, sems):
        pltpu.make_async_copy(buffer.at[at], buffer.at[at], sems.at[1, at]).wait()

    for moves, buffer, sems in groups:
        for at, (condition, sources, _) in enumerate(moves):
            when(condition, functools.partial(begin, at, sources, buffer, sems))
    if meanwhile is not None:
        meanwhile()
    for moves, buffer, sems in groups:
        for at, (condition, _, targets) in enumerate(moves):
            when(condition, functools.partial(forward, at, targets, buffer, sems))
    for moves, buffer, sems in groups:
        for at, (condition, _, _) in enumerate(moves):
            when(condition, functools.partial(finish, at, buffer, sems))


def collect_kernel(spans, slot_total, masks, *refs):
    (me_ref, arrival_from, arrival_slot, holder, kv_cache, store_a, store_b, hidden) = refs[:8]
    *leaving, rows_a, rows_b, rows, asking = refs[8 : 12 + len(masks)]
    *buffers, raw, even = refs[12 + len(masks) : 17 + len(masks)]
    *semaphores, raw_sems, even_sems = refs[17 + len(masks) :]
    me = me_ref[0]
    moves = []
    for i, mask in enumerate(masks):
        to = me ^ mask
        slot = jnp.int32(0)
        for a in range(arrival_from.shape[0]):
            slot += jnp.where(arrival_from[a, to] == me, arrival_slot[a, to], 0)
        moves.append((None, [(None, kv_cache.at[slot])], [(None, leaving[i])]))
    groups = [moves]
    held = []
    for copy_id in range(COPIES):
        slot = jnp.int32(0)
        for span in range(spans):
            row = holder[copy_id * spans + span]
            slot += jnp.where(row // slot_total == me, row % slot_total, 0)
        held.append(slot)
    for table, target in ((store_a, rows_a), (store_b, rows_b)):
        groups.append(
            [
                (None, [(None, table.at[slot])], [(None, target.at[copy_id])])
                for copy_id, slot in enumerate(held)
            ]
        )

    start = rows.shape[0] - asking.shape[0]
    fetch = pltpu.make_async_copy(hidden, raw, raw_sems.at[0, 0])
    puts = [
        pltpu.make_async_copy(even, rows, even_sems.at[0, 0]),
        pltpu.make_async_copy(even.at[start:], asking, even_sems.at[1, 0]),
    ]

    def regroup():
        count = raw.shape[0] * raw.shape[1]
        blank = jnp.zeros((rows.shape[0] - count, rows.shape[1]), rows.dtype)
        fetch.wait()
        every = raw[...].reshape(count, rows.shape[1])
        even[...] = jnp.concatenate([every, blank], axis=0)
        for put in puts:
            put.start()

    fetch.start()
    staged(list(zip(groups, buffers, semaphores)), regroup)
    for put in puts:
        put.wait()


def pack_kernel(spans, slot_total, *refs):
    (me_ref, holder, dest, store_a, store_b, sibling_a, sibling_b) = refs[:7]
    across_b, *units = refs[7:-5]
    spread = ALWAYS + AT_NEED
    extra, buffer_b, buffer_a, sems_b, sems_a = refs[-5:]
    me = me_ref[0]
    core = me % 2
    chip = 1 - me // 2
    items = crossing(holder, dest, spans, slot_total, chip)
    moves_b, moves_a = [], []
    for copy_id in range(COPIES):
        row = jnp.where(core == 0, items[2 * copy_id][2], items[2 * copy_id + 1][2])
        own = row // slot_total == me
        sources = [
            (own, store_b.at[row % slot_total]),
            (jnp.logical_not(own), sibling_b.at[copy_id]),
        ]
        moves_b.append((None, sources, [(None, across_b.at[copy_id])]))
    for at, (copy_id, _, row, crosses, unit) in enumerate(items):
        own = row // slot_total == me
        sources = [
            (own, store_a.at[row % slot_total, core]),
            (jnp.logical_not(own), sibling_a.at[copy_id, core]),
        ]
        targets = [
            (
                jnp.logical_and(unit >= start, unit < start + size),
                array.at[jnp.clip(unit - start, 0, size - 1)],
            )
            for array, (start, size) in zip(units, spread)
            if start <= at
        ]
        moves_a.append((crosses, sources, targets))
    count = items[-1][4] + items[-1][3].astype(jnp.int32)
    extra[0] = jnp.clip(count - AT_NEED[0][0], 0, len(AT_NEED))
    staged([(moves_b, buffer_b, sems_b), (moves_a, buffer_a, sems_a)])


def place_kernel(spans, slot_total, spread, *refs):
    (me_ref, holder, dest, earlier) = refs[:4]
    got, other = refs[4 : 4 + len(spread)], refs[4 + len(spread) : 4 + 2 * len(spread)]
    out, buffer, sems = refs[-3:]
    me = me_ref[0]
    core = me % 2
    first_unit = spread[0][0]
    past_unit = spread[-1][0] + spread[-1][1]
    items = crossing(holder, dest, spans, slot_total, me // 2)
    moves = []
    for copy_id in range(COPIES):
        one, two = items[2 * copy_id], items[2 * copy_id + 1]
        crosses = jnp.where(core == 0, one[3].astype(jnp.int32), two[3].astype(jnp.int32)) != 0
        unit = jnp.where(core == 0, one[4], two[4])
        possible = [i for i, (start, _) in enumerate(spread) if start <= 2 * copy_id + 1]
        if first_unit and not possible:
            continue
        here = jnp.logical_and(unit >= first_unit, unit < past_unit)
        for half, arrays in ((core, got), (1 - core, other)):
            sources = []
            active = jnp.logical_and(crosses, here)
            if not first_unit:
                near = jnp.logical_not(crosses)
                active = jnp.logical_or(near, here)
                sources.append((near, earlier.at[copy_id, half]))
            for i in possible:
                start, size = spread[i]
                hit = jnp.logical_and(unit >= start, unit < start + size)
                source = arrays[i].at[jnp.clip(unit - start, 0, size - 1)]
                sources.append((jnp.logical_and(crosses, hit), source))
            moves.append((active, sources, [(None, out.at[copy_id, half])]))
    staged([(moves, buffer, sems)])


def copy_call(kernel, tables, arrays, shapes, scratch, scalars=(), aliases=None):
    hbm = pl.BlockSpec(memory_space=pl.ANY)
    dtype = arrays[0].dtype
    return pl.pallas_call(
        kernel,
        out_shape=[pltpu.HBM(shape, dtype) for shape in shapes]
        + [jax.ShapeDtypeStruct(shape, jnp.int32) for shape in scalars],
        in_specs=[SMEM] * len(tables) + [hbm] * len(arrays),
        out_specs=[hbm] * len(shapes) + [SMEM] * len(scalars),
        scratch_shapes=[pltpu.VMEM(shape, dtype) for shape in scratch]
        + [pltpu.SemaphoreType.DMA((2, shape[0])) for shape in scratch],
        input_output_aliases=aliases or {},
    )(*tables, *arrays)


def project_kernel(spans, slot_total, resident, steps, masks, *refs):
    (me_ref, resident_adapter, arrival_adapter, holder, dest, hidden, *others) = refs[: 6 + len(masks)]
    store, *outs, left, adapters, sums = refs[6 + len(masks) :]
    me = me_ref[0]
    group = pl.program_id(0)
    base = hidden.shape[0]
    block = others[0].shape[0]
    width = sums.shape[1]
    per_step = store.shape[1] // width

    @pl.when(group == 0)
    def _():
        left[0:base] = hidden[...]
        for i, other in enumerate(others):
            left[base + i * block : base + (i + 1) * block] = other[...]
        sums[...] = jnp.zeros_like(sums)
        ids = lax.broadcasted_iota(jnp.int32, sums.shape, 0) // steps
        own = jnp.full(sums.shape, -1, jnp.int32)
        for slot in range(resident):
            own = jnp.where(ids == slot, resident_adapter[me * resident + slot], own)
        for i, mask in enumerate((0,) + masks):
            replica = me ^ mask
            first = resident if i == 0 else (base + (i - 1) * block) // steps
            for a in range(arrival_adapter.shape[0]):
                chosen = arrival_adapter[a, replica]
                row = jnp.int32(0)
                for span in range(spans):
                    at = chosen * spans + span
                    row += jnp.where(dest[0, at] == replica, holder[at], 0)
                here = jnp.where(row // slot_total == me, row % slot_total, -1)
                own = jnp.where(ids == first + a, here, own)
        adapters[...] = own

    product = lax.dot_general(
        left[...], store[0], (((1,), (1,)), ((), ())), preferred_element_type=jnp.float32
    )
    for i in range(per_step):
        hit = adapters[...] == group * per_step + i
        sums[...] += jnp.where(hit, product[:, i * width : (i + 1) * width], 0.0)

    @pl.when(group == pl.num_programs(0) - 1)
    def _():
        outs[0][...] = sums[0:base]
        for i, out in enumerate(outs[1:]):
            out[...] = sums[base + i * block : base + (i + 1) * block]


def gather_kernel(chunks, shard_ref, *refs):
    partial, *returned, out, total = refs[chunks:]
    width = refs[0].shape[1]
    for step, ref in enumerate(refs[:chunks]):
        source = lax.rem(shard_ref[0] + chunks - step, chunks)
        out[:, pl.ds(pl.multiple_of(source * width, width), width)] = ref[...]
    first = partial.shape[0] - returned[0].shape[0]
    last = partial[first:]
    for ref in returned:
        last = last + ref[...]
    total[:first] = partial[:first]
    total[first:] = last


def attend_kernel(spans, masks, resident, steps, kv_heads, head_length, *refs):
    (me_ref, lengths, arrival_from, arrival_slot, resident_adapter, arrival_adapter) = refs[:6]
    holder, dest, *parts = refs[6 : -14 - len(masks)]
    came = refs[-14 - len(masks) : -14]
    store_b, sibling_b, across_b, base, queries, cache = refs[-14:-8]
    out, new_kv, arrived, installed_b = refs[-8:-4]
    fresh_ref, mixed_ref, score_ref, weight_ref = refs[-4:]
    me = me_ref[0]
    arrive = arrival_from.shape[0]
    replicas = arrival_from.shape[1]
    slots = resident + arrive
    row_count = base.shape[1]
    rank = store_b.shape[1] // 2
    slot_total = store_b.shape[0]
    half = head_length // 2
    seen = [lengths[me * resident + slot] for slot in range(resident)]
    for a in range(arrive):
        seen.append(lengths[arrival_from[a, me] * resident + arrival_slot[a, me]])

    for a in range(arrive):
        for ref, mask in zip(came, masks):

            @pl.when(arrival_from[a, me] == me ^ mask)
            def _():
                arrived[a] = ref[...]

        def clear(row, carry):
            arrived[a, row] = jnp.zeros(arrived.shape[2:], arrived.dtype)
            return carry

        lax.fori_loop(seen[resident + a], arrived.shape[1], clear, 0)
    for copy_id in range(COPIES):
        near = wanted_by(holder, dest, spans, me, copy_id) // (2 * slot_total) == me // 2

        @pl.when(near)
        def _():
            installed_b[copy_id] = sibling_b[copy_id]

        @pl.when(jnp.logical_not(near))
        def _():
            installed_b[copy_id] = across_b[copy_id]

    total = parts[0][...]
    for part in parts[1:]:
        total = total + part[...]
    down = total.astype(jnp.bfloat16)

    ids = lax.broadcasted_iota(jnp.int32, (row_count, 1), 0) // steps
    adapters = jnp.zeros((row_count, 1), jnp.int32)
    position = lax.broadcasted_iota(jnp.int32, (row_count, 1), 0) % steps
    for slot in range(slots):
        if slot < resident:
            adapter = resident_adapter[me * resident + slot]
        else:
            adapter = store_b.shape[0] + arrival_adapter[slot - resident, me]
        adapters = jnp.where(ids == slot, adapter, adapters)
        position = jnp.where(ids == slot, position + seen[slot], position)
    deltas = [jnp.zeros((row_count, store_b.shape[2]), jnp.float32) for _ in range(2)]
    for adapter in range(store_b.shape[0] + COPIES):
        if adapter < store_b.shape[0]:
            table = store_b[adapter]
        else:
            table = installed_b[adapter - store_b.shape[0]]
        for part in range(2):
            product = jnp.dot(
                down[:, part * rank : (part + 1) * rank],
                table[part * rank : (part + 1) * rank],
                preferred_element_type=jnp.float32,
            )
            deltas[part] = jnp.where(adapters == adapter, product, deltas[part])

    lane = lax.broadcasted_iota(jnp.int32, (1, half), 1).astype(jnp.float32)
    frequency = jnp.exp(lane * (-2.0 * math.log(ROPE_BASE) / head_length))
    angles = position.astype(jnp.float32) * frequency
    cosine, sine = jnp.cos(angles), jnp.sin(angles)
    dead = jnp.zeros((row_count, 1), jnp.bool_)
    gone = [jnp.int32(0)] * resident
    for q in range(replicas):
        for a in range(arrive):
            mine = arrival_from[a, q] == me
            slot = arrival_slot[a, q]
            dead = jnp.logical_or(dead, jnp.logical_and(ids == slot, mine))
            for n in range(resident):
                gone[n] = jnp.where(jnp.logical_and(mine, slot == n), 1, gone[n])
    for g in range(kv_heads):
        columns = slice(g * head_length, (g + 1) * head_length)
        key = base[g, :, :head_length] + ADAPTER_SCALE * deltas[0][:, columns]
        value = base[g, :, head_length:] + ADAPTER_SCALE * deltas[1][:, columns]
        u, w = key[:, :half], key[:, half:]
        key = jnp.concatenate([u * cosine - w * sine, w * cosine + u * sine], axis=1)
        for part, piece in enumerate((key, value)):
            rounded = piece.astype(jnp.bfloat16).astype(jnp.float32)
            lanes = slice(part * head_length, (part + 1) * head_length)
            fresh_ref[part, pl.ds(g, row_count, stride=kv_heads)] = rounded
            kept = jnp.where(dead, 0.0, rounded)[: slots * steps]
            new_kv[:, :, g, lanes] = kept.reshape(slots, steps, head_length).astype(jnp.bfloat16)

    query_rows = queries.shape[1]
    heads = query_rows // steps
    cache_rows = cache.shape[1] * kv_heads
    new_rows = steps * kv_heads
    pad_rows = 16 - new_rows
    row = lax.broadcasted_iota(jnp.int32, (query_rows, 1), 0)
    step_of = row // heads
    group_of = row % heads // (heads // kv_heads)
    column = lax.broadcasted_iota(jnp.int32, (query_rows, cache_rows), 1)
    same = column % kv_heads == group_of
    past_row = column // kv_heads
    late = lax.broadcasted_iota(jnp.int32, (query_rows, 128), 1)
    allowed = jnp.logical_and(late % kv_heads == group_of, late // kv_heads <= step_of)
    allowed = jnp.logical_and(allowed, late < new_rows)
    scale = 1.0 / math.sqrt(head_length)

    def cached(n):
        stored = cache[n] if n < resident else arrived[n - resident]
        return stored.reshape(cache_rows, 2 * head_length)

    def fresh_rows(n, part):
        lines = fresh_ref[part, n * new_rows : (n + 1) * new_rows]
        blank = jnp.zeros((pad_rows, head_length), jnp.float32)
        return jnp.concatenate([lines, blank], axis=0).astype(jnp.bfloat16)

    def against(query, keys):
        return lax.dot_general(
            query, keys, (((1,), (1,)), ((), ())), preferred_element_type=jnp.float32
        )

    for n in range(slots):
        lines = slice(n * query_rows, (n + 1) * query_rows)
        query = queries[n]
        score = against(query, cached(n)[:, :head_length]) * scale
        score = jnp.where(jnp.logical_and(same, past_row < seen[n]), score, -jnp.inf)
        score_ref[lines, :cache_rows] = score
        keys = jnp.concatenate(
            [fresh_rows(n, 0), jnp.zeros((128 - 16, head_length), jnp.bfloat16)], axis=0
        )
        score = against(query, keys) * scale
        score_ref[lines, cache_rows:] = jnp.where(allowed, score, -jnp.inf)
    for n in range(slots):
        lines = slice(n * query_rows, (n + 1) * query_rows)
        score = score_ref[lines]
        term = jnp.exp(score - jnp.max(score, axis=1, keepdims=True))
        inverse = 1.0 / jnp.sum(term, axis=1, keepdims=True)
        weight_ref[lines] = (term * inverse).astype(jnp.bfloat16)
    for n in range(slots):
        lines = slice(n * query_rows, (n + 1) * query_rows)
        weight = weight_ref[lines]
        mixed = jnp.dot(
            weight[:, :cache_rows], cached(n)[:, head_length:], preferred_element_type=jnp.float32
        )
        mixed = mixed + jnp.dot(
            weight[:, cache_rows : cache_rows + 16],
            fresh_rows(n, 1),
            preferred_element_type=jnp.float32,
        )
        if n < resident:
            mixed = jnp.where(gone[n] != 0, 0.0, mixed)
        mixed_ref[lines] = mixed
    for n in range(slots):
        for head in range(heads):
            lanes = slice(head * head_length, (head + 1) * head_length)
            pair = mixed_ref[pl.ds(n * query_rows + head, steps, stride=heads)]
            out[n, :, lanes] = pair.astype(jnp.bfloat16)


def pairs_layer(
    hidden,
    queries,
    kv_cache,
    w_kv,
    store_a,
    store_b,
    lengths,
    arrival_from,
    arrival_slot,
    resident_adapter,
    arrival_adapter,
    hot_holder,
    hot_dest,
):
    me = lax.axis_index("replica")
    replicas = lax.axis_size("replica")
    shards = lax.axis_size("tensor")
    resident, cap, kv_heads, head_pair = kv_cache.shape
    arrive = arrival_from.shape[1]
    slots = resident + arrive
    steps, features = hidden.shape[1:]
    heads, head_length = queries.shape[2:]
    slot_total = store_a.shape[0]
    rank = store_a.shape[2]
    spans = hot_holder.shape[0] // COPIES
    row_a, row_b = store_a.shape[1:], store_b.shape[1:]
    columns = store_b.shape[3]
    masks = tuple(range(1, replicas))
    me_table = jnp.reshape(me, (1,)).astype(jnp.int32)
    shard_table = jnp.reshape(lax.axis_index("tensor"), (1,)).astype(jnp.int32)
    from_table, slot_table, choice_table = arrival_from.T, arrival_slot.T, arrival_adapter.T
    dest_table = hot_dest.T

    used = slots * steps
    padded = -(-used // 8) * 8
    first = resident * steps
    block = padded - first

    *leaving, rows_a, rows_b, rows, asking = copy_call(
        functools.partial(collect_kernel, spans, slot_total, masks),
        (me_table, from_table, slot_table, hot_holder),
        (kv_cache, store_a, store_b, hidden),
        [kv_cache.shape[1:]] * len(masks)
        + [(COPIES,) + row_a, (COPIES,) + row_b, (padded, features), (block, features)],
        [
            (len(masks),) + kv_cache.shape[1:],
            (COPIES,) + row_a,
            (COPIES,) + row_b,
            hidden.shape,
            (padded, features),
        ],
    )
    sibling_a = partner(rows_a, 1)
    sibling_b = partner(rows_b, 1)
    other_rows = [partner(asking, mask) for mask in masks]
    came = [partner(array, mask) for array, mask in zip(leaving, masks)]
    around = [rows] + [shifted(rows, step) for step in range(1, shards)]

    line_count = padded + len(masks) * block
    per_step = 2 if slot_total % 2 == 0 else 1
    partial, *sent = pl.pallas_call(
        functools.partial(project_kernel, spans, slot_total, resident, steps, masks),
        out_shape=[jax.ShapeDtypeStruct((padded, 2 * rank), jnp.float32)]
        + [jax.ShapeDtypeStruct((block, 2 * rank), jnp.float32)] * len(masks),
        grid=(slot_total // per_step,),
        in_specs=[SMEM] * 5
        + [pl.BlockSpec((padded, features), lambda i: (0, 0))]
        + [pl.BlockSpec((block, features), lambda i: (0, 0))] * len(masks)
        + [pl.BlockSpec((1, per_step * 2 * rank, features), lambda i: (i, 0, 0))],
        out_specs=[pl.BlockSpec((padded, 2 * rank), lambda i: (0, 0))]
        + [pl.BlockSpec((block, 2 * rank), lambda i: (0, 0))] * len(masks),
        scratch_shapes=[
            pltpu.VMEM((line_count, features), hidden.dtype),
            pltpu.VMEM((line_count, 2 * rank), jnp.int32),
            pltpu.VMEM((line_count, 2 * rank), jnp.float32),
        ],
        name="project",
    )(
        me_table,
        resident_adapter,
        choice_table,
        hot_holder,
        dest_table,
        rows,
        *other_rows,
        store_a.reshape(slot_total // per_step, per_step * 2 * rank, features),
    )
    returned = [partner(array, mask) for array, mask in zip(sent, masks)]
    unit_shape = row_a[1:]
    unit_total = 2 * COPIES
    across_b, *units, extra = copy_call(
        functools.partial(pack_kernel, spans, slot_total),
        (me_table, hot_holder, dest_table),
        (store_a, store_b, sibling_a, sibling_b),
        [(COPIES,) + row_b] + [(size,) + unit_shape for _, size in ALWAYS + AT_NEED],
        [(COPIES,) + row_b, (unit_total,) + unit_shape],
        [(1,)],
    )
    across_b = partner(across_b, 2)
    got = []
    for array in units[: len(ALWAYS)]:
        got.append(partner(array, 2))

    full, partial = pl.pallas_call(
        functools.partial(gather_kernel, shards),
        out_shape=[
            jax.ShapeDtypeStruct((padded, shards * features), hidden.dtype),
            jax.ShapeDtypeStruct(partial.shape, jnp.float32),
        ],
        in_specs=[SMEM] + [VMEM] * (shards + 1 + len(masks)),
        out_specs=[VMEM] * 2,
        name="gather",
    )(shard_table, *around, partial, *returned)
    parts = [partial] + [shifted(partial, step) for step in range(1, shards)]
    base = jnp.einsum("md,dgc->gmc", full, w_kv, preferred_element_type=jnp.float32)

    attn_out, new_kv, arrived, installed_b = pl.pallas_call(
        functools.partial(attend_kernel, spans, masks, resident, steps, kv_heads, head_length),
        out_shape=[
            jax.ShapeDtypeStruct((slots, steps, heads * head_length), jnp.bfloat16),
            jax.ShapeDtypeStruct((slots, steps, kv_heads, head_pair), jnp.bfloat16),
            jax.ShapeDtypeStruct((arrive,) + kv_cache.shape[1:], jnp.bfloat16),
            jax.ShapeDtypeStruct((COPIES, 2 * rank, columns), jnp.bfloat16),
        ],
        in_specs=[SMEM] * 8 + [VMEM] * (shards + len(masks) + 6),
        out_specs=[VMEM] * 4,
        scratch_shapes=[
            pltpu.VMEM((2, padded * kv_heads, head_length), jnp.float32),
            pltpu.VMEM((slots * steps * heads, head_length), jnp.float32),
            pltpu.VMEM((slots * steps * heads, cap * kv_heads + 128), jnp.float32),
            pltpu.VMEM((slots * steps * heads, cap * kv_heads + 128), jnp.bfloat16),
        ],
        name="attend",
    )(
        me_table,
        lengths,
        from_table,
        slot_table,
        resident_adapter,
        choice_table,
        hot_holder,
        dest_table,
        *parts,
        *came,
        store_b.reshape(slot_total, 2 * rank, columns),
        sibling_b.reshape(COPIES, 2 * rank, columns),
        across_b.reshape(COPIES, 2 * rank, columns),
        base,
        queries.reshape(slots, steps * heads, head_length),
        kv_cache,
    )
    installed_b = installed_b.reshape((COPIES,) + row_b)

    tables = (me_table, hot_holder, dest_table)

    def finish(count):
        def branch(sibling_a, first_other, *arrays):
            got, rest = list(arrays[: len(ALWAYS)]), arrays[len(ALWAYS) :]
            late = [partner(array, 2) for array in rest[:count]]
            other = [first_other] + [partner(array, 1) for array in got[1:]]
            (placed,) = copy_call(
                functools.partial(place_kernel, spans, slot_total, ALWAYS),
                tables,
                (sibling_a, *got, *other),
                [(COPIES,) + row_a],
                [(unit_total,) + unit_shape],
            )
            if not count:
                return placed
            other = [partner(array, 1) for array in late]
            (placed,) = copy_call(
                functools.partial(place_kernel, spans, slot_total, AT_NEED[:count]),
                tables,
                (placed, *late, *other),
                [(COPIES,) + row_a],
                [(unit_total,) + unit_shape],
                aliases={len(tables): 0},
            )
            return placed

        return branch

    branches = [finish(count) for count in range(len(AT_NEED) + 1)]
    first_other = partner(got[0], 1)
    *rest, attn_out = lax.optimization_barrier((*units[len(ALWAYS) :], attn_out))
    installed_a = lax.switch(extra[0], branches, sibling_a, first_other, *got, *rest)
    return (attn_out, new_kv, arrived, installed_a, installed_b)


def local(*args):
    fan = args[-1].shape[1]
    if lax.axis_size("replica") == 4 and fan == 1:
        return pairs_layer(*args)
    return local_general(*args)


def solution(mesh):
    in_specs = (
        P(("parts", "replica"), None, "tensor"),
        P(("parts", "replica"), None, "tensor", None),
        P(("parts", "replica"), None, "tensor", None),
        P(None, "tensor", None),
        P(("parts", "replica"), None, None, "tensor"),
        P(("parts", "replica"), None, None, "tensor"),
        P("parts"),
        P("parts", None),
        P("parts", None),
        P("parts"),
        P("parts", None),
        P("parts"),
        P("parts", None),
    )
    out_specs = (
        P(("parts", "replica"), None, "tensor"),
        P(("parts", "replica"), None, "tensor", None),
        P(("parts", "replica"), None, "tensor", None),
        P(("parts", "replica"), None, None, "tensor"),
        P(("parts", "replica"), None, None, "tensor"),
    )
    return jax.shard_map(local, mesh=mesh, in_specs=in_specs, out_specs=out_specs, check_vma=False)
```

```python
import functools
import math

import jax
import jax.numpy as jnp
from jax import lax
from jax.experimental import pallas as pl
from jax.experimental.pallas import tpu as pltpu
from jax.sharding import PartitionSpec as P


COPIES = 4


ADAPTER_SCALE = 2.0
ROPE_BASE = 500000.0


def rotate_keys(key_rows, positions):
    head_length = key_rows.shape[-1]
    half_size = head_length // 2
    frequency = ROPE_BASE ** (-(jnp.arange(half_size, dtype=jnp.float32) * 2.0 / head_length))
    angles = positions.astype(jnp.float32)[:, :, None, None] * frequency
    cosine = jnp.cos(angles)
    sine_val = jnp.sin(angles)
    first_half = key_rows[..., :half_size]
    second_half = key_rows[..., half_size:]
    return jnp.concatenate(
        [
            first_half * cosine - second_half * sine_val,
            second_half * cosine + first_half * sine_val,
        ],
        axis=-1,
    )


def attend(queries, stored, lengths_now, fresh_kv):
    request_slot_count, decode_step_count, heads_local, head_length = queries.shape
    local_key_value = stored.shape[2]
    group_size = heads_local // local_key_value
    grouped = queries.reshape(
        request_slot_count, decode_step_count, local_key_value, group_size, head_length
    )
    score_scale = 1.0 / math.sqrt(head_length)
    past_scores = (
        jnp.einsum(
            "msgjd,mcgd->msgjc",
            grouped,
            stored[..., :head_length],
            preferred_element_type=jnp.float32,
        )
        * score_scale
    )
    recent_scores = (
        jnp.einsum(
            "msgjd,mtgd->msgjt",
            grouped,
            fresh_kv[..., :head_length],
            preferred_element_type=jnp.float32,
        )
        * score_scale
    )
    row_ids = jnp.arange(stored.shape[1], dtype=jnp.int32)
    past_ok = (row_ids[None, :] < lengths_now[:, None])[:, None, None, None, :]
    step_ids = jnp.arange(decode_step_count, dtype=jnp.int32)
    recent_ok = (step_ids[None, :] <= step_ids[:, None])[None, :, None, None, :]
    past_scores = jnp.where(past_ok, past_scores, -jnp.inf)
    recent_scores = jnp.where(recent_ok, recent_scores, -jnp.inf)
    peak_score = jnp.maximum(jnp.max(past_scores, -1), jnp.max(recent_scores, -1))[..., None]
    past_exp = jnp.exp(past_scores - peak_score)
    recent_exp = jnp.exp(recent_scores - peak_score)
    denom_sum = jnp.sum(past_exp, -1, keepdims=True) + jnp.sum(recent_exp, -1, keepdims=True)
    past_w = (past_exp / denom_sum).astype(jnp.bfloat16)
    recent_w = (recent_exp / denom_sum).astype(jnp.bfloat16)
    mixed_out = jnp.einsum(
        "msgjc,mcgd->msgjd", past_w, stored[..., head_length:], preferred_element_type=jnp.float32
    )
    mixed_out = mixed_out + jnp.einsum(
        "msgjt,mtgd->msgjd",
        recent_w,
        fresh_kv[..., head_length:],
        preferred_element_type=jnp.float32,
    )
    return mixed_out.reshape(request_slot_count, decode_step_count, heads_local * head_length)


def local_general(
    hidden,
    queries,
    kv_cache,
    w_kv,
    store_a,
    store_b,
    lengths,
    arrival_from,
    arrival_slot,
    resident_adapter,
    arrival_adapter,
    hot_holder,
    hot_dest,
):
    my_index = lax.axis_index("replica")
    replicas = lax.axis_size("replica")
    resident = kv_cache.shape[0]
    arrive = arrival_from.shape[1]
    request_slot_count = resident + arrive
    decode_step_count = hidden.shape[1]
    head_length = queries.shape[3]
    local_key_value = kv_cache.shape[2]
    slot_total = store_a.shape[0]
    hot_total = hot_holder.shape[0]
    spans = hot_total // COPIES
    my_from = lax.dynamic_index_in_dim(arrival_from, my_index, 0, keepdims=False)
    my_slot = lax.dynamic_index_in_dim(arrival_slot, my_index, 0, keepdims=False)
    own_ids = my_index * resident + jnp.arange(resident, dtype=jnp.int32)
    leaving_ids = (arrival_from * resident + arrival_slot).reshape(-1)
    staying = jnp.logical_not(jnp.any(own_ids[:, None] == leaving_ids[None, :], axis=1))
    live_mask = jnp.concatenate([staying, jnp.ones((arrive,), bool)])
    own_len = lax.dynamic_slice_in_dim(lengths, my_index * resident, resident)
    arrival_len = jnp.take(lengths, my_from * resident + my_slot)
    seen_len = jnp.concatenate([own_len, arrival_len])
    takes_mine = arrival_from == my_index
    sends_any = jnp.any(takes_mine, axis=1)
    send_slot = jnp.sum(jnp.where(takes_mine, arrival_slot, 0), axis=1)
    outgoing = jnp.take(kv_cache, send_slot, axis=0)
    outgoing = jnp.where(sends_any[:, None, None, None], outgoing, jnp.zeros((), jnp.bfloat16))
    incoming = lax.all_to_all(outgoing, "replica", split_axis=0, concat_axis=0, tiled=True)
    blocks = hot_dest.reshape(COPIES, spans, hot_dest.shape[1])
    holder_grid = hot_holder.reshape(COPIES, spans)
    holder_rep = holder_grid // slot_total
    mine = holder_rep == my_index
    has_one = jnp.any(mine, axis=1)
    local_pick = jnp.sum(jnp.where(mine, holder_grid % slot_total, 0), axis=1)

    def spread_rows(store):
        rows = jnp.take(store, local_pick, axis=0)
        rows = jnp.where(has_one[:, None, None, None], rows, jnp.zeros((), jnp.bfloat16))
        return rows.reshape(COPIES, replicas, -1).transpose(1, 0, 2)

    got_a, got_b = (
        lax.all_to_all(spread_rows(store_a), "replica", split_axis=0, concat_axis=0, tiled=True),
        lax.all_to_all(spread_rows(store_b), "replica", split_axis=0, concat_axis=0, tiled=True),
    )
    replica_ids = jnp.arange(replicas, dtype=jnp.int32)
    member = jnp.any(blocks[:, :, :, None] == replica_ids[None, None, None, :], axis=2).astype(
        jnp.int32
    )
    source_rep = jnp.sum(member * holder_rep[:, :, None], axis=1)
    copy_ids = jnp.arange(COPIES, dtype=jnp.int32)
    route_a = got_a[source_rep.T, copy_ids[None, :]]
    route_b = got_b[source_rep.T, copy_ids[None, :]]
    recv_a, recv_b = (
        lax.all_to_all(route_a, "replica", split_axis=0, concat_axis=0, tiled=True),
        lax.all_to_all(route_b, "replica", split_axis=0, concat_axis=0, tiled=True),
    )
    installed_a = recv_a.transpose(1, 0, 2).reshape((COPIES,) + store_a.shape[1:])
    installed_b = recv_b.transpose(1, 0, 2).reshape((COPIES,) + store_b.shape[1:])
    own_adapter = lax.dynamic_slice_in_dim(resident_adapter, my_index * resident, resident)
    my_choice = lax.dynamic_index_in_dim(arrival_adapter, my_index, 0, keepdims=False)
    adapt_a = jnp.concatenate(
        [jnp.take(store_a, own_adapter, axis=0), jnp.take(installed_a, my_choice, axis=0)]
    )
    adapter_up_weight = jnp.concatenate(
        [jnp.take(store_b, own_adapter, axis=0), jnp.take(installed_b, my_choice, axis=0)]
    )
    partial_value = jnp.einsum(
        "msd,mpkd->mspk", hidden, adapt_a, preferred_element_type=jnp.float32
    )
    base_projection = jnp.einsum(
        "msd,dgc->msgc",
        lax.all_gather(hidden, "tensor", axis=2, tiled=True),
        w_kv,
        preferred_element_type=jnp.float32,
    )
    down_projected = lax.psum(partial_value, "tensor")
    down_projected = down_projected.astype(jnp.bfloat16)
    adapter_update = jnp.einsum(
        "gnot,gote->gnoe", down_projected, adapter_up_weight, preferred_element_type=jnp.float32
    )
    adapter_update = (
        adapter_update.reshape(
            request_slot_count, decode_step_count, 2, local_key_value, head_length
        )
        .transpose(0, 1, 3, 2, 4)
        .reshape(request_slot_count, decode_step_count, local_key_value, 2 * head_length)
    )
    unrotated_key_value = base_projection + ADAPTER_SCALE * adapter_update
    positions = seen_len[:, None] + jnp.arange(decode_step_count, dtype=jnp.int32)[None, :]
    fresh_kv = jnp.concatenate(
        [
            rotate_keys(unrotated_key_value[..., :head_length], positions),
            unrotated_key_value[..., head_length:],
        ],
        axis=-1,
    ).astype(jnp.bfloat16)
    stay_out = attend(queries[:resident], kv_cache, own_len, fresh_kv[:resident])
    arrived = jnp.take(incoming, my_from, axis=0)
    row_ids = jnp.arange(kv_cache.shape[1], dtype=jnp.int32)
    arrived = jnp.where(
        (row_ids[None, :] < arrival_len[:, None])[:, :, None, None],
        arrived,
        jnp.zeros((), jnp.bfloat16),
    )
    move_out = attend(queries[resident:], arrived, arrival_len, fresh_kv[resident:])
    mixed_out = jnp.concatenate([stay_out, move_out], axis=0)
    attn_out = jnp.where(live_mask[:, None, None], mixed_out, 0.0).astype(jnp.bfloat16)
    new_kv = jnp.where(live_mask[:, None, None, None], fresh_kv, jnp.zeros((), jnp.bfloat16))
    return (attn_out, new_kv, arrived, installed_a, installed_b)


def partner(array, mask):
    return lax.ppermute(array, "replica", [(i, i ^ mask) for i in range(lax.axis_size("replica"))])


def shifted(array, step):
    size = lax.axis_size("tensor")
    return lax.ppermute(array, "tensor", [(i, (i + step) % size) for i in range(size)])


ALWAYS = ((0, 2), (2, 3))
AT_NEED = ((5, 1), (6, 1), (7, 1))
SMEM = pl.BlockSpec(memory_space=pltpu.SMEM)
VMEM = pl.BlockSpec(memory_space=pltpu.VMEM)


def wanted_by(holder, dest, spans, replica, copy_id):
    row = jnp.int32(0)
    for span in range(spans):
        at = copy_id * spans + span
        row += jnp.where(dest[0, at] == replica, holder[at], 0)
    return row


def crossing(holder, dest, spans, slot_total, chip):
    items, count = [], jnp.int32(0)
    for copy_id in range(COPIES):
        for core in range(2):
            row = wanted_by(holder, dest, spans, 2 * chip + core, copy_id)
            crosses = row // (2 * slot_total) != chip
            items.append((copy_id, core, row, crosses, count))
            count = count + crosses.astype(jnp.int32)
    return items


def staged(groups, meanwhile=None):
    def when(condition, action):
        if condition is None:
            action()
        else:
            pl.when(condition)(action)

    def begin(at, sources, buffer, sems):
        for condition, source in sources:
            when(condition, pltpu.make_async_copy(source, buffer.at[at], sems.at[0, at]).start)

    def forward(at, targets, buffer, sems):
        pltpu.make_async_copy(buffer.at[at], buffer.at[at], sems.at[0, at]).wait()
        for condition, target in targets:
            when(condition, pltpu.make_async_copy(buffer.at[at], target, sems.at[1, at]).start)

    def finish(at, buffer, sems):
        pltpu.make_async_copy(buffer.at[at], buffer.at[at], sems.at[1, at]).wait()

    for moves, buffer, sems in groups:
        for at, (condition, sources, _) in enumerate(moves):
            when(condition, functools.partial(begin, at, sources, buffer, sems))
    if meanwhile is not None:
        meanwhile()
    for moves, buffer, sems in groups:
        for at, (condition, _, targets) in enumerate(moves):
            when(condition, functools.partial(forward, at, targets, buffer, sems))
    for moves, buffer, sems in groups:
        for at, (condition, _, _) in enumerate(moves):
            when(condition, functools.partial(finish, at, buffer, sems))


def held_slots(me, holder, spans, slot_total):
    slots = []
    for copy_id in range(COPIES):
        slot = jnp.int32(0)
        for span in range(spans):
            row = holder[copy_id * spans + span]
            slot += jnp.where(row // slot_total == me, row % slot_total, 0)
        slots.append(slot)
    return slots


def collect_down_kernel(spans, slot_total, me_ref, holder, store_a, rows_a, buffer, sems):
    moves = [
        (None, [(None, store_a.at[slot])], [(None, rows_a.at[copy_id])])
        for copy_id, slot in enumerate(held_slots(me_ref[0], holder, spans, slot_total))
    ]
    staged([(moves, buffer, sems)])


def collect_kernel(spans, slot_total, masks, *refs):
    (me_ref, arrival_from, arrival_slot, holder, kv_cache, store_b, hidden) = refs[:7]
    *leaving, rows_b, rows, asking = refs[7 : 10 + len(masks)]
    *buffers, raw, even = refs[10 + len(masks) : 14 + len(masks)]
    *semaphores, raw_sems, even_sems = refs[14 + len(masks) :]
    me = me_ref[0]
    moves = []
    for i, mask in enumerate(masks):
        to = me ^ mask
        slot = jnp.int32(0)
        for a in range(arrival_from.shape[0]):
            slot += jnp.where(arrival_from[a, to] == me, arrival_slot[a, to], 0)
        moves.append((None, [(None, kv_cache.at[slot])], [(None, leaving[i])]))
    groups = [
        moves,
        [
            (None, [(None, store_b.at[slot])], [(None, rows_b.at[copy_id])])
            for copy_id, slot in enumerate(held_slots(me, holder, spans, slot_total))
        ],
    ]

    start = rows.shape[0] - asking.shape[0]
    fetch = pltpu.make_async_copy(hidden, raw, raw_sems.at[0, 0])
    puts = [
        pltpu.make_async_copy(even, rows, even_sems.at[0, 0]),
        pltpu.make_async_copy(even.at[start:], asking, even_sems.at[1, 0]),
    ]

    def regroup():
        count = raw.shape[0] * raw.shape[1]
        blank = jnp.zeros((rows.shape[0] - count, rows.shape[1]), rows.dtype)
        fetch.wait()
        every = raw[...].reshape(count, rows.shape[1])
        even[...] = jnp.concatenate([every, blank], axis=0)
        for put in puts:
            put.start()

    fetch.start()
    staged(list(zip(groups, buffers, semaphores)), regroup)
    for put in puts:
        put.wait()


def pack_kernel(spans, slot_total, *refs):
    (me_ref, holder, dest, store_a, store_b, sibling_a, sibling_b) = refs[:7]
    across_b, *units = refs[7:-5]
    spread = ALWAYS + AT_NEED
    extra, buffer_b, buffer_a, sems_b, sems_a = refs[-5:]
    me = me_ref[0]
    core = me % 2
    chip = 1 - me // 2
    items = crossing(holder, dest, spans, slot_total, chip)
    moves_b, moves_a = [], []
    for copy_id in range(COPIES):
        row = jnp.where(core == 0, items[2 * copy_id][2], items[2 * copy_id + 1][2])
        own = row // slot_total == me
        sources = [
            (own, store_b.at[row % slot_total]),
            (jnp.logical_not(own), sibling_b.at[copy_id]),
        ]
        moves_b.append((None, sources, [(None, across_b.at[copy_id])]))
    for at, (copy_id, _, row, crosses, unit) in enumerate(items):
        own = row // slot_total == me
        sources = [
            (own, store_a.at[row % slot_total, core]),
            (jnp.logical_not(own), sibling_a.at[copy_id, core]),
        ]
        targets = [
            (
                jnp.logical_and(unit >= start, unit < start + size),
                array.at[jnp.clip(unit - start, 0, size - 1)],
            )
            for array, (start, size) in zip(units, spread)
            if start <= at
        ]
        moves_a.append((crosses, sources, targets))
    count = items[-1][4] + items[-1][3].astype(jnp.int32)
    extra[0] = jnp.clip(count - AT_NEED[0][0], 0, len(AT_NEED))
    staged([(moves_b, buffer_b, sems_b), (moves_a, buffer_a, sems_a)])


def place_kernel(spans, slot_total, spread, *refs):
    (me_ref, holder, dest, earlier) = refs[:4]
    got, other = refs[4 : 4 + len(spread)], refs[4 + len(spread) : 4 + 2 * len(spread)]
    out, buffer, sems = refs[-3:]
    me = me_ref[0]
    core = me % 2
    first_unit = spread[0][0]
    past_unit = spread[-1][0] + spread[-1][1]
    items = crossing(holder, dest, spans, slot_total, me // 2)
    moves = []
    for copy_id in range(COPIES):
        one, two = items[2 * copy_id], items[2 * copy_id + 1]
        crosses = jnp.where(core == 0, one[3].astype(jnp.int32), two[3].astype(jnp.int32)) != 0
        unit = jnp.where(core == 0, one[4], two[4])
        possible = [i for i, (start, _) in enumerate(spread) if start <= 2 * copy_id + 1]
        if first_unit and not possible:
            continue
        here = jnp.logical_and(unit >= first_unit, unit < past_unit)
        for half, arrays in ((core, got), (1 - core, other)):
            sources = []
            active = jnp.logical_and(crosses, here)
            if not first_unit:
                near = jnp.logical_not(crosses)
                active = jnp.logical_or(near, here)
                sources.append((near, earlier.at[copy_id, half]))
            for i in possible:
                start, size = spread[i]
                hit = jnp.logical_and(unit >= start, unit < start + size)
                source = arrays[i].at[jnp.clip(unit - start, 0, size - 1)]
                sources.append((jnp.logical_and(crosses, hit), source))
            moves.append((active, sources, [(None, out.at[copy_id, half])]))
    staged([(moves, buffer, sems)])


def copy_call(kernel, tables, arrays, shapes, scratch, scalars=(), aliases=None):
    hbm = pl.BlockSpec(memory_space=pl.ANY)
    dtype = arrays[0].dtype
    return pl.pallas_call(
        kernel,
        out_shape=[pltpu.HBM(shape, dtype) for shape in shapes]
        + [jax.ShapeDtypeStruct(shape, jnp.int32) for shape in scalars],
        in_specs=[SMEM] * len(tables) + [hbm] * len(arrays),
        out_specs=[hbm] * len(shapes) + [SMEM] * len(scalars),
        scratch_shapes=[pltpu.VMEM(shape, dtype) for shape in scratch]
        + [pltpu.SemaphoreType.DMA((2, shape[0])) for shape in scratch],
        input_output_aliases=aliases or {},
    )(*tables, *arrays)


def project_kernel(spans, slot_total, resident, steps, masks, *refs):
    (me_ref, resident_adapter, arrival_adapter, holder, dest, hidden, *others) = refs[: 6 + len(masks)]
    store, *outs, left, adapters, sums = refs[6 + len(masks) :]
    me = me_ref[0]
    group = pl.program_id(0)
    base = hidden.shape[0]
    block = others[0].shape[0]
    width = sums.shape[1]
    per_step = store.shape[1] // width

    @pl.when(group == 0)
    def _():
        left[0:base] = hidden[...]
        for i, other in enumerate(others):
            left[base + i * block : base + (i + 1) * block] = other[...]
        sums[...] = jnp.zeros_like(sums)
        ids = lax.broadcasted_iota(jnp.int32, sums.shape, 0) // steps
        own = jnp.full(sums.shape, -1, jnp.int32)
        for slot in range(resident):
            own = jnp.where(ids == slot, resident_adapter[me * resident + slot], own)
        for i, mask in enumerate((0,) + masks):
            replica = me ^ mask
            first = resident if i == 0 else (base + (i - 1) * block) // steps
            for a in range(arrival_adapter.shape[0]):
                chosen = arrival_adapter[a, replica]
                row = jnp.int32(0)
                for span in range(spans):
                    at = chosen * spans + span
                    row += jnp.where(dest[0, at] == replica, holder[at], 0)
                here = jnp.where(row // slot_total == me, row % slot_total, -1)
                own = jnp.where(ids == first + a, here, own)
        adapters[...] = own

    product = lax.dot_general(
        left[...], store[0], (((1,), (1,)), ((), ())), preferred_element_type=jnp.float32
    )
    for i in range(per_step):
        hit = adapters[...] == group * per_step + i
        sums[...] += jnp.where(hit, product[:, i * width : (i + 1) * width], 0.0)

    @pl.when(group == pl.num_programs(0) - 1)
    def _():
        outs[0][...] = sums[0:base]
        for i, out in enumerate(outs[1:]):
            out[...] = sums[base + i * block : base + (i + 1) * block]


def gather_kernel(chunks, shard_ref, *refs):
    partial, *returned, out, total = refs[chunks:]
    width = refs[0].shape[1]
    for step, ref in enumerate(refs[:chunks]):
        source = lax.rem(shard_ref[0] + chunks - step, chunks)
        out[:, pl.ds(pl.multiple_of(source * width, width), width)] = ref[...]
    first = partial.shape[0] - returned[0].shape[0]
    last = partial[first:]
    for ref in returned:
        last = last + ref[...]
    total[:first] = partial[:first]
    total[first:] = last


def attend_kernel(spans, masks, resident, steps, kv_heads, head_length, *refs):
    (me_ref, lengths, arrival_from, arrival_slot, resident_adapter, arrival_adapter) = refs[:6]
    holder, dest, *parts = refs[6 : -14 - len(masks)]
    came = refs[-14 - len(masks) : -14]
    store_b, sibling_b, across_b, base, queries, cache = refs[-14:-8]
    out, new_kv, arrived, installed_b = refs[-8:-4]
    fresh_ref, mixed_ref, score_ref, weight_ref = refs[-4:]
    me = me_ref[0]
    arrive = arrival_from.shape[0]
    replicas = arrival_from.shape[1]
    slots = resident + arrive
    row_count = base.shape[1]
    rank = store_b.shape[1] // 2
    slot_total = store_b.shape[0]
    half = head_length // 2
    seen = [lengths[me * resident + slot] for slot in range(resident)]
    for a in range(arrive):
        seen.append(lengths[arrival_from[a, me] * resident + arrival_slot[a, me]])

    for a in range(arrive):
        for ref, mask in zip(came, masks):

            @pl.when(arrival_from[a, me] == me ^ mask)
            def _():
                arrived[a] = ref[...]

        def clear(row, carry):
            arrived[a, row] = jnp.zeros(arrived.shape[2:], arrived.dtype)
            return carry

        lax.fori_loop(seen[resident + a], arrived.shape[1], clear, 0)
    for copy_id in range(COPIES):
        near = wanted_by(holder, dest, spans, me, copy_id) // (2 * slot_total) == me // 2

        @pl.when(near)
        def _():
            installed_b[copy_id] = sibling_b[copy_id]

        @pl.when(jnp.logical_not(near))
        def _():
            installed_b[copy_id] = across_b[copy_id]

    total = parts[0][...]
    for part in parts[1:]:
        total = total + part[...]
    down = total.astype(jnp.bfloat16)

    ids = lax.broadcasted_iota(jnp.int32, (row_count, 1), 0) // steps
    adapters = jnp.zeros((row_count, 1), jnp.int32)
    position = lax.broadcasted_iota(jnp.int32, (row_count, 1), 0) % steps
    for slot in range(slots):
        if slot < resident:
            adapter = resident_adapter[me * resident + slot]
        else:
            adapter = store_b.shape[0] + arrival_adapter[slot - resident, me]
        adapters = jnp.where(ids == slot, adapter, adapters)
        position = jnp.where(ids == slot, position + seen[slot], position)
    deltas = [jnp.zeros((row_count, store_b.shape[2]), jnp.float32) for _ in range(2)]
    for adapter in range(store_b.shape[0] + COPIES):
        if adapter < store_b.shape[0]:
            table = store_b[adapter]
        else:
            table = installed_b[adapter - store_b.shape[0]]
        for part in range(2):
            product = jnp.dot(
                down[:, part * rank : (part + 1) * rank],
                table[part * rank : (part + 1) * rank],
                preferred_element_type=jnp.float32,
            )
            deltas[part] = jnp.where(adapters == adapter, product, deltas[part])

    lane = lax.broadcasted_iota(jnp.int32, (1, half), 1).astype(jnp.float32)
    frequency = jnp.exp(lane * (-2.0 * math.log(ROPE_BASE) / head_length))
    angles = position.astype(jnp.float32) * frequency
    cosine, sine = jnp.cos(angles), jnp.sin(angles)
    dead = jnp.zeros((row_count, 1), jnp.bool_)
    gone = [jnp.int32(0)] * resident
    for q in range(replicas):
        for a in range(arrive):
            mine = arrival_from[a, q] == me
            slot = arrival_slot[a, q]
            dead = jnp.logical_or(dead, jnp.logical_and(ids == slot, mine))
            for n in range(resident):
                gone[n] = jnp.where(jnp.logical_and(mine, slot == n), 1, gone[n])
    for g in range(kv_heads):
        columns = slice(g * head_length, (g + 1) * head_length)
        key = base[g, :, :head_length] + ADAPTER_SCALE * deltas[0][:, columns]
        value = base[g, :, head_length:] + ADAPTER_SCALE * deltas[1][:, columns]
        u, w = key[:, :half], key[:, half:]
        key = jnp.concatenate([u * cosine - w * sine, w * cosine + u * sine], axis=1)
        for part, piece in enumerate((key, value)):
            rounded = piece.astype(jnp.bfloat16).astype(jnp.float32)
            lanes = slice(part * head_length, (part + 1) * head_length)
            fresh_ref[part, pl.ds(g, row_count, stride=kv_heads)] = rounded
            kept = jnp.where(dead, 0.0, rounded)[: slots * steps]
            new_kv[:, :, g, lanes] = kept.reshape(slots, steps, head_length).astype(jnp.bfloat16)

    query_rows = queries.shape[1]
    heads = query_rows // steps
    cache_rows = cache.shape[1] * kv_heads
    new_rows = steps * kv_heads
    pad_rows = 16 - new_rows
    row = lax.broadcasted_iota(jnp.int32, (query_rows, 1), 0)
    step_of = row // heads
    group_of = row % heads // (heads // kv_heads)
    column = lax.broadcasted_iota(jnp.int32, (query_rows, cache_rows), 1)
    same = column % kv_heads == group_of
    past_row = column // kv_heads
    late = lax.broadcasted_iota(jnp.int32, (query_rows, 128), 1)
    allowed = jnp.logical_and(late % kv_heads == group_of, late // kv_heads <= step_of)
    allowed = jnp.logical_and(allowed, late < new_rows)
    scale = 1.0 / math.sqrt(head_length)

    def cached(n):
        stored = cache[n] if n < resident else arrived[n - resident]
        return stored.reshape(cache_rows, 2 * head_length)

    def fresh_rows(n, part):
        lines = fresh_ref[part, n * new_rows : (n + 1) * new_rows]
        blank = jnp.zeros((pad_rows, head_length), jnp.float32)
        return jnp.concatenate([lines, blank], axis=0).astype(jnp.bfloat16)

    def against(query, keys):
        return lax.dot_general(
            query, keys, (((1,), (1,)), ((), ())), preferred_element_type=jnp.float32
        )

    for n in range(slots):
        lines = slice(n * query_rows, (n + 1) * query_rows)
        query = queries[n]
        score = against(query, cached(n)[:, :head_length]) * scale
        score = jnp.where(jnp.logical_and(same, past_row < seen[n]), score, -jnp.inf)
        score_ref[lines, :cache_rows] = score
        keys = jnp.concatenate(
            [fresh_rows(n, 0), jnp.zeros((128 - 16, head_length), jnp.bfloat16)], axis=0
        )
        score = against(query, keys) * scale
        score_ref[lines, cache_rows:] = jnp.where(allowed, score, -jnp.inf)
    for n in range(slots):
        lines = slice(n * query_rows, (n + 1) * query_rows)
        score = score_ref[lines]
        term = jnp.exp(score - jnp.max(score, axis=1, keepdims=True))
        inverse = 1.0 / jnp.sum(term, axis=1, keepdims=True)
        weight_ref[lines] = (term * inverse).astype(jnp.bfloat16)
    for n in range(slots):
        lines = slice(n * query_rows, (n + 1) * query_rows)
        weight = weight_ref[lines]
        mixed = jnp.dot(
            weight[:, :cache_rows], cached(n)[:, head_length:], preferred_element_type=jnp.float32
        )
        mixed = mixed + jnp.dot(
            weight[:, cache_rows : cache_rows + 16],
            fresh_rows(n, 1),
            preferred_element_type=jnp.float32,
        )
        if n < resident:
            mixed = jnp.where(gone[n] != 0, 0.0, mixed)
        mixed_ref[lines] = mixed
    for n in range(slots):
        for head in range(heads):
            lanes = slice(head * head_length, (head + 1) * head_length)
            pair = mixed_ref[pl.ds(n * query_rows + head, steps, stride=heads)]
            out[n, :, lanes] = pair.astype(jnp.bfloat16)


def pairs_layer(
    hidden,
    queries,
    kv_cache,
    w_kv,
    store_a,
    store_b,
    lengths,
    arrival_from,
    arrival_slot,
    resident_adapter,
    arrival_adapter,
    hot_holder,
    hot_dest,
):
    me = lax.axis_index("replica")
    replicas = lax.axis_size("replica")
    shards = lax.axis_size("tensor")
    resident, cap, kv_heads, head_pair = kv_cache.shape
    arrive = arrival_from.shape[1]
    slots = resident + arrive
    steps, features = hidden.shape[1:]
    heads, head_length = queries.shape[2:]
    slot_total = store_a.shape[0]
    rank = store_a.shape[2]
    spans = hot_holder.shape[0] // COPIES
    row_a, row_b = store_a.shape[1:], store_b.shape[1:]
    columns = store_b.shape[3]
    masks = tuple(range(1, replicas))
    me_table = jnp.reshape(me, (1,)).astype(jnp.int32)
    shard_table = jnp.reshape(lax.axis_index("tensor"), (1,)).astype(jnp.int32)
    from_table, slot_table, choice_table = arrival_from.T, arrival_slot.T, arrival_adapter.T
    dest_table = hot_dest.T

    used = slots * steps
    padded = -(-used // 8) * 8
    first = resident * steps
    block = padded - first

    (rows_a,) = copy_call(
        functools.partial(collect_down_kernel, spans, slot_total),
        (me_table, hot_holder),
        (store_a,),
        [(COPIES,) + row_a],
        [(COPIES,) + row_a],
    )
    sibling_a = partner(rows_a, 1)
    *leaving, rows_b, rows, asking = copy_call(
        functools.partial(collect_kernel, spans, slot_total, masks),
        (me_table, from_table, slot_table, hot_holder),
        (kv_cache, store_b, hidden),
        [kv_cache.shape[1:]] * len(masks)
        + [(COPIES,) + row_b, (padded, features), (block, features)],
        [(len(masks),) + kv_cache.shape[1:], (COPIES,) + row_b, hidden.shape, (padded, features)],
    )
    sibling_b = partner(rows_b, 1)
    other_rows = [partner(asking, mask) for mask in masks]
    came = [partner(array, mask) for array, mask in zip(leaving, masks)]
    around = [rows] + [shifted(rows, step) for step in range(1, shards)]

    line_count = padded + len(masks) * block
    per_step = 2 if slot_total % 2 == 0 else 1
    partial, *sent = pl.pallas_call(
        functools.partial(project_kernel, spans, slot_total, resident, steps, masks),
        out_shape=[jax.ShapeDtypeStruct((padded, 2 * rank), jnp.float32)]
        + [jax.ShapeDtypeStruct((block, 2 * rank), jnp.float32)] * len(masks),
        grid=(slot_total // per_step,),
        in_specs=[SMEM] * 5
        + [pl.BlockSpec((padded, features), lambda i: (0, 0))]
        + [pl.BlockSpec((block, features), lambda i: (0, 0))] * len(masks)
        + [pl.BlockSpec((1, per_step * 2 * rank, features), lambda i: (i, 0, 0))],
        out_specs=[pl.BlockSpec((padded, 2 * rank), lambda i: (0, 0))]
        + [pl.BlockSpec((block, 2 * rank), lambda i: (0, 0))] * len(masks),
        scratch_shapes=[
            pltpu.VMEM((line_count, features), hidden.dtype),
            pltpu.VMEM((line_count, 2 * rank), jnp.int32),
            pltpu.VMEM((line_count, 2 * rank), jnp.float32),
        ],
        name="project",
    )(
        me_table,
        resident_adapter,
        choice_table,
        hot_holder,
        dest_table,
        rows,
        *other_rows,
        store_a.reshape(slot_total // per_step, per_step * 2 * rank, features),
    )
    returned = [partner(array, mask) for array, mask in zip(sent, masks)]
    unit_shape = row_a[1:]
    unit_total = 2 * COPIES
    across_b, *units, extra = copy_call(
        functools.partial(pack_kernel, spans, slot_total),
        (me_table, hot_holder, dest_table),
        (store_a, store_b, sibling_a, sibling_b),
        [(COPIES,) + row_b] + [(size,) + unit_shape for _, size in ALWAYS + AT_NEED],
        [(COPIES,) + row_b, (unit_total,) + unit_shape],
        [(1,)],
    )
    across_b = partner(across_b, 2)
    got = []
    for array in units[: len(ALWAYS)]:
        got.append(partner(array, 2))

    full, partial = pl.pallas_call(
        functools.partial(gather_kernel, shards),
        out_shape=[
            jax.ShapeDtypeStruct((padded, shards * features), hidden.dtype),
            jax.ShapeDtypeStruct(partial.shape, jnp.float32),
        ],
        in_specs=[SMEM] + [VMEM] * (shards + 1 + len(masks)),
        out_specs=[VMEM] * 2,
        name="gather",
    )(shard_table, *around, partial, *returned)
    parts = [partial] + [shifted(partial, step) for step in range(1, shards)]
    base = jnp.einsum("md,dgc->gmc", full, w_kv, preferred_element_type=jnp.float32)

    attn_out, new_kv, arrived, installed_b = pl.pallas_call(
        functools.partial(attend_kernel, spans, masks, resident, steps, kv_heads, head_length),
        out_shape=[
            jax.ShapeDtypeStruct((slots, steps, heads * head_length), jnp.bfloat16),
            jax.ShapeDtypeStruct((slots, steps, kv_heads, head_pair), jnp.bfloat16),
            jax.ShapeDtypeStruct((arrive,) + kv_cache.shape[1:], jnp.bfloat16),
            jax.ShapeDtypeStruct((COPIES, 2 * rank, columns), jnp.bfloat16),
        ],
        in_specs=[SMEM] * 8 + [VMEM] * (shards + len(masks) + 6),
        out_specs=[VMEM] * 4,
        scratch_shapes=[
            pltpu.VMEM((2, padded * kv_heads, head_length), jnp.float32),
            pltpu.VMEM((slots * steps * heads, head_length), jnp.float32),
            pltpu.VMEM((slots * steps * heads, cap * kv_heads + 128), jnp.float32),
            pltpu.VMEM((slots * steps * heads, cap * kv_heads + 128), jnp.bfloat16),
        ],
        name="attend",
    )(
        me_table,
        lengths,
        from_table,
        slot_table,
        resident_adapter,
        choice_table,
        hot_holder,
        dest_table,
        *parts,
        *came,
        store_b.reshape(slot_total, 2 * rank, columns),
        sibling_b.reshape(COPIES, 2 * rank, columns),
        across_b.reshape(COPIES, 2 * rank, columns),
        base,
        queries.reshape(slots, steps * heads, head_length),
        kv_cache,
    )
    installed_b = installed_b.reshape((COPIES,) + row_b)

    tables = (me_table, hot_holder, dest_table)

    def finish(count):
        def branch(sibling_a, first_other, *arrays):
            got, rest = list(arrays[: len(ALWAYS)]), arrays[len(ALWAYS) :]
            late = [partner(array, 2) for array in rest[:count]]
            other = [first_other] + [partner(array, 1) for array in got[1:]]
            (placed,) = copy_call(
                functools.partial(place_kernel, spans, slot_total, ALWAYS),
                tables,
                (sibling_a, *got, *other),
                [(COPIES,) + row_a],
                [(unit_total,) + unit_shape],
            )
            if not count:
                return placed
            other = [partner(array, 1) for array in late]
            (placed,) = copy_call(
                functools.partial(place_kernel, spans, slot_total, AT_NEED[:count]),
                tables,
                (placed, *late, *other),
                [(COPIES,) + row_a],
                [(unit_total,) + unit_shape],
                aliases={len(tables): 0},
            )
            return placed

        return branch

    branches = [finish(count) for count in range(len(AT_NEED) + 1)]
    first_other = partner(got[0], 1)
    *rest, attn_out = lax.optimization_barrier((*units[len(ALWAYS) :], attn_out))
    installed_a = lax.switch(extra[0], branches, sibling_a, first_other, *got, *rest)
    return (attn_out, new_kv, arrived, installed_a, installed_b)


def local(*args):
    fan = args[-1].shape[1]
    if lax.axis_size("replica") == 4 and fan == 1:
        return pairs_layer(*args)
    return local_general(*args)


def solution(mesh):
    in_specs = (
        P(("parts", "replica"), None, "tensor"),
        P(("parts", "replica"), None, "tensor", None),
        P(("parts", "replica"), None, "tensor", None),
        P(None, "tensor", None),
        P(("parts", "replica"), None, None, "tensor"),
        P(("parts", "replica"), None, None, "tensor"),
        P("parts"),
        P("parts", None),
        P("parts", None),
        P("parts"),
        P("parts", None),
        P("parts"),
        P("parts", None),
    )
    out_specs = (
        P(("parts", "replica"), None, "tensor"),
        P(("parts", "replica"), None, "tensor", None),
        P(("parts", "replica"), None, "tensor", None),
        P(("parts", "replica"), None, None, "tensor"),
        P(("parts", "replica"), None, None, "tensor"),
    )
    return jax.shard_map(local, mesh=mesh, in_specs=in_specs, out_specs=out_specs, check_vma=False)
```

```python
import functools
import math

import jax
import jax.numpy as jnp
from jax import lax
from jax.experimental import pallas as pl
from jax.experimental.pallas import tpu as pltpu
from jax.sharding import PartitionSpec as P


COPIES = 4


ADAPTER_SCALE = 2.0
ROPE_BASE = 500000.0


def rotate_keys(key_rows, positions):
    head_length = key_rows.shape[-1]
    half_size = head_length // 2
    frequency = ROPE_BASE ** (-(jnp.arange(half_size, dtype=jnp.float32) * 2.0 / head_length))
    angles = positions.astype(jnp.float32)[:, :, None, None] * frequency
    cosine = jnp.cos(angles)
    sine_val = jnp.sin(angles)
    first_half = key_rows[..., :half_size]
    second_half = key_rows[..., half_size:]
    return jnp.concatenate(
        [
            first_half * cosine - second_half * sine_val,
            second_half * cosine + first_half * sine_val,
        ],
        axis=-1,
    )


def attend(queries, stored, lengths_now, fresh_kv):
    request_slot_count, decode_step_count, heads_local, head_length = queries.shape
    local_key_value = stored.shape[2]
    group_size = heads_local // local_key_value
    grouped = queries.reshape(
        request_slot_count, decode_step_count, local_key_value, group_size, head_length
    )
    score_scale = 1.0 / math.sqrt(head_length)
    past_scores = (
        jnp.einsum(
            "msgjd,mcgd->msgjc",
            grouped,
            stored[..., :head_length],
            preferred_element_type=jnp.float32,
        )
        * score_scale
    )
    recent_scores = (
        jnp.einsum(
            "msgjd,mtgd->msgjt",
            grouped,
            fresh_kv[..., :head_length],
            preferred_element_type=jnp.float32,
        )
        * score_scale
    )
    row_ids = jnp.arange(stored.shape[1], dtype=jnp.int32)
    past_ok = (row_ids[None, :] < lengths_now[:, None])[:, None, None, None, :]
    step_ids = jnp.arange(decode_step_count, dtype=jnp.int32)
    recent_ok = (step_ids[None, :] <= step_ids[:, None])[None, :, None, None, :]
    past_scores = jnp.where(past_ok, past_scores, -jnp.inf)
    recent_scores = jnp.where(recent_ok, recent_scores, -jnp.inf)
    peak_score = jnp.maximum(jnp.max(past_scores, -1), jnp.max(recent_scores, -1))[..., None]
    past_exp = jnp.exp(past_scores - peak_score)
    recent_exp = jnp.exp(recent_scores - peak_score)
    denom_sum = jnp.sum(past_exp, -1, keepdims=True) + jnp.sum(recent_exp, -1, keepdims=True)
    past_w = (past_exp / denom_sum).astype(jnp.bfloat16)
    recent_w = (recent_exp / denom_sum).astype(jnp.bfloat16)
    mixed_out = jnp.einsum(
        "msgjc,mcgd->msgjd", past_w, stored[..., head_length:], preferred_element_type=jnp.float32
    )
    mixed_out = mixed_out + jnp.einsum(
        "msgjt,mtgd->msgjd",
        recent_w,
        fresh_kv[..., head_length:],
        preferred_element_type=jnp.float32,
    )
    return mixed_out.reshape(request_slot_count, decode_step_count, heads_local * head_length)


def local_general(
    hidden,
    queries,
    kv_cache,
    w_kv,
    store_a,
    store_b,
    lengths,
    arrival_from,
    arrival_slot,
    resident_adapter,
    arrival_adapter,
    hot_holder,
    hot_dest,
):
    my_index = lax.axis_index("replica")
    replicas = lax.axis_size("replica")
    resident = kv_cache.shape[0]
    arrive = arrival_from.shape[1]
    request_slot_count = resident + arrive
    decode_step_count = hidden.shape[1]
    head_length = queries.shape[3]
    local_key_value = kv_cache.shape[2]
    slot_total = store_a.shape[0]
    hot_total = hot_holder.shape[0]
    spans = hot_total // COPIES
    my_from = lax.dynamic_index_in_dim(arrival_from, my_index, 0, keepdims=False)
    my_slot = lax.dynamic_index_in_dim(arrival_slot, my_index, 0, keepdims=False)
    own_ids = my_index * resident + jnp.arange(resident, dtype=jnp.int32)
    leaving_ids = (arrival_from * resident + arrival_slot).reshape(-1)
    staying = jnp.logical_not(jnp.any(own_ids[:, None] == leaving_ids[None, :], axis=1))
    live_mask = jnp.concatenate([staying, jnp.ones((arrive,), bool)])
    own_len = lax.dynamic_slice_in_dim(lengths, my_index * resident, resident)
    arrival_len = jnp.take(lengths, my_from * resident + my_slot)
    seen_len = jnp.concatenate([own_len, arrival_len])
    takes_mine = arrival_from == my_index
    sends_any = jnp.any(takes_mine, axis=1)
    send_slot = jnp.sum(jnp.where(takes_mine, arrival_slot, 0), axis=1)
    outgoing = jnp.take(kv_cache, send_slot, axis=0)
    outgoing = jnp.where(sends_any[:, None, None, None], outgoing, jnp.zeros((), jnp.bfloat16))
    incoming = lax.all_to_all(outgoing, "replica", split_axis=0, concat_axis=0, tiled=True)
    blocks = hot_dest.reshape(COPIES, spans, hot_dest.shape[1])
    holder_grid = hot_holder.reshape(COPIES, spans)
    holder_rep = holder_grid // slot_total
    mine = holder_rep == my_index
    has_one = jnp.any(mine, axis=1)
    local_pick = jnp.sum(jnp.where(mine, holder_grid % slot_total, 0), axis=1)

    def spread_rows(store):
        rows = jnp.take(store, local_pick, axis=0)
        rows = jnp.where(has_one[:, None, None, None], rows, jnp.zeros((), jnp.bfloat16))
        return rows.reshape(COPIES, replicas, -1).transpose(1, 0, 2)

    got_a, got_b = (
        lax.all_to_all(spread_rows(store_a), "replica", split_axis=0, concat_axis=0, tiled=True),
        lax.all_to_all(spread_rows(store_b), "replica", split_axis=0, concat_axis=0, tiled=True),
    )
    replica_ids = jnp.arange(replicas, dtype=jnp.int32)
    member = jnp.any(blocks[:, :, :, None] == replica_ids[None, None, None, :], axis=2).astype(
        jnp.int32
    )
    source_rep = jnp.sum(member * holder_rep[:, :, None], axis=1)
    copy_ids = jnp.arange(COPIES, dtype=jnp.int32)
    route_a = got_a[source_rep.T, copy_ids[None, :]]
    route_b = got_b[source_rep.T, copy_ids[None, :]]
    recv_a, recv_b = (
        lax.all_to_all(route_a, "replica", split_axis=0, concat_axis=0, tiled=True),
        lax.all_to_all(route_b, "replica", split_axis=0, concat_axis=0, tiled=True),
    )
    installed_a = recv_a.transpose(1, 0, 2).reshape((COPIES,) + store_a.shape[1:])
    installed_b = recv_b.transpose(1, 0, 2).reshape((COPIES,) + store_b.shape[1:])
    own_adapter = lax.dynamic_slice_in_dim(resident_adapter, my_index * resident, resident)
    my_choice = lax.dynamic_index_in_dim(arrival_adapter, my_index, 0, keepdims=False)
    adapt_a = jnp.concatenate(
        [jnp.take(store_a, own_adapter, axis=0), jnp.take(installed_a, my_choice, axis=0)]
    )
    adapter_up_weight = jnp.concatenate(
        [jnp.take(store_b, own_adapter, axis=0), jnp.take(installed_b, my_choice, axis=0)]
    )
    partial_value = jnp.einsum(
        "msd,mpkd->mspk", hidden, adapt_a, preferred_element_type=jnp.float32
    )
    base_projection = jnp.einsum(
        "msd,dgc->msgc",
        lax.all_gather(hidden, "tensor", axis=2, tiled=True),
        w_kv,
        preferred_element_type=jnp.float32,
    )
    down_projected = lax.psum(partial_value, "tensor")
    down_projected = down_projected.astype(jnp.bfloat16)
    adapter_update = jnp.einsum(
        "gnot,gote->gnoe", down_projected, adapter_up_weight, preferred_element_type=jnp.float32
    )
    adapter_update = (
        adapter_update.reshape(
            request_slot_count, decode_step_count, 2, local_key_value, head_length
        )
        .transpose(0, 1, 3, 2, 4)
        .reshape(request_slot_count, decode_step_count, local_key_value, 2 * head_length)
    )
    unrotated_key_value = base_projection + ADAPTER_SCALE * adapter_update
    positions = seen_len[:, None] + jnp.arange(decode_step_count, dtype=jnp.int32)[None, :]
    fresh_kv = jnp.concatenate(
        [
            rotate_keys(unrotated_key_value[..., :head_length], positions),
            unrotated_key_value[..., head_length:],
        ],
        axis=-1,
    ).astype(jnp.bfloat16)
    stay_out = attend(queries[:resident], kv_cache, own_len, fresh_kv[:resident])
    arrived = jnp.take(incoming, my_from, axis=0)
    row_ids = jnp.arange(kv_cache.shape[1], dtype=jnp.int32)
    arrived = jnp.where(
        (row_ids[None, :] < arrival_len[:, None])[:, :, None, None],
        arrived,
        jnp.zeros((), jnp.bfloat16),
    )
    move_out = attend(queries[resident:], arrived, arrival_len, fresh_kv[resident:])
    mixed_out = jnp.concatenate([stay_out, move_out], axis=0)
    attn_out = jnp.where(live_mask[:, None, None], mixed_out, 0.0).astype(jnp.bfloat16)
    new_kv = jnp.where(live_mask[:, None, None, None], fresh_kv, jnp.zeros((), jnp.bfloat16))
    return (attn_out, new_kv, arrived, installed_a, installed_b)


def partner(array, mask):
    return lax.ppermute(array, "replica", [(i, i ^ mask) for i in range(lax.axis_size("replica"))])


def shifted(array, step):
    size = lax.axis_size("tensor")
    return lax.ppermute(array, "tensor", [(i, (i + step) % size) for i in range(size)])


ALWAYS = ((0, 2), (2, 2), (4, 1))
AT_NEED = ((5, 1), (6, 1), (7, 1))
SMEM = pl.BlockSpec(memory_space=pltpu.SMEM)
VMEM = pl.BlockSpec(memory_space=pltpu.VMEM)


def wanted_by(holder, dest, spans, replica, copy_id):
    row = jnp.int32(0)
    for span in range(spans):
        at = copy_id * spans + span
        row += jnp.where(dest[0, at] == replica, holder[at], 0)
    return row


def crossing(holder, dest, spans, slot_total, chip):
    items, count = [], jnp.int32(0)
    for copy_id in range(COPIES):
        for core in range(2):
            row = wanted_by(holder, dest, spans, 2 * chip + core, copy_id)
            crosses = row // (2 * slot_total) != chip
            items.append((copy_id, core, row, crosses, count))
            count = count + crosses.astype(jnp.int32)
    return items


def staged(groups, meanwhile=None):
    def when(condition, action):
        if condition is None:
            action()
        else:
            pl.when(condition)(action)

    def begin(at, sources, buffer, sems):
        for condition, source in sources:
            when(condition, pltpu.make_async_copy(source, buffer.at[at], sems.at[0, at]).start)

    def forward(at, targets, buffer, sems):
        pltpu.make_async_copy(buffer.at[at], buffer.at[at], sems.at[0, at]).wait()
        for condition, target in targets:
            when(condition, pltpu.make_async_copy(buffer.at[at], target, sems.at[1, at]).start)

    def finish(at, buffer, sems):
        pltpu.make_async_copy(buffer.at[at], buffer.at[at], sems.at[1, at]).wait()

    for moves, buffer, sems in groups:
        for at, (condition, sources, _) in enumerate(moves):
            when(condition, functools.partial(begin, at, sources, buffer, sems))
    if meanwhile is not None:
        meanwhile()
    for moves, buffer, sems in groups:
        for at, (condition, _, targets) in enumerate(moves):
            when(condition, functools.partial(forward, at, targets, buffer, sems))
    for moves, buffer, sems in groups:
        for at, (condition, _, _) in enumerate(moves):
            when(condition, functools.partial(finish, at, buffer, sems))


def collect_kernel(spans, slot_total, masks, *refs):
    (me_ref, arrival_from, arrival_slot, holder, kv_cache, store_a, store_b, hidden) = refs[:8]
    *leaving, rows_a, rows_b, rows, asking = refs[8 : 12 + len(masks)]
    *buffers, raw, even = refs[12 + len(masks) : 17 + len(masks)]
    *semaphores, raw_sems, even_sems = refs[17 + len(masks) :]
    me = me_ref[0]
    moves = []
    for i, mask in enumerate(masks):
        to = me ^ mask
        slot = jnp.int32(0)
        for a in range(arrival_from.shape[0]):
            slot += jnp.where(arrival_from[a, to] == me, arrival_slot[a, to], 0)
        moves.append((None, [(None, kv_cache.at[slot])], [(None, leaving[i])]))
    groups = [moves]
    held = []
    for copy_id in range(COPIES):
        slot = jnp.int32(0)
        for span in range(spans):
            row = holder[copy_id * spans + span]
            slot += jnp.where(row // slot_total == me, row % slot_total, 0)
        held.append(slot)
    for table, target in ((store_a, rows_a), (store_b, rows_b)):
        groups.append(
            [
                (None, [(None, table.at[slot])], [(None, target.at[copy_id])])
                for copy_id, slot in enumerate(held)
            ]
        )

    start = rows.shape[0] - asking.shape[0]
    fetch = pltpu.make_async_copy(hidden, raw, raw_sems.at[0, 0])
    puts = [
        pltpu.make_async_copy(even, rows, even_sems.at[0, 0]),
        pltpu.make_async_copy(even.at[start:], asking, even_sems.at[1, 0]),
    ]

    def regroup():
        count = raw.shape[0] * raw.shape[1]
        blank = jnp.zeros((rows.shape[0] - count, rows.shape[1]), rows.dtype)
        fetch.wait()
        every = raw[...].reshape(count, rows.shape[1])
        even[...] = jnp.concatenate([every, blank], axis=0)
        for put in puts:
            put.start()

    fetch.start()
    staged(list(zip(groups, buffers, semaphores)), regroup)
    for put in puts:
        put.wait()


def pack_kernel(spans, slot_total, *refs):
    (me_ref, holder, dest, store_a, store_b, sibling_a, sibling_b) = refs[:7]
    across_b, *units = refs[7:-5]
    spread = ALWAYS + AT_NEED
    extra, buffer_b, buffer_a, sems_b, sems_a = refs[-5:]
    me = me_ref[0]
    core = me % 2
    chip = 1 - me // 2
    items = crossing(holder, dest, spans, slot_total, chip)
    moves_b, moves_a = [], []
    for copy_id in range(COPIES):
        row = jnp.where(core == 0, items[2 * copy_id][2], items[2 * copy_id + 1][2])
        own = row // slot_total == me
        sources = [
            (own, store_b.at[row % slot_total]),
            (jnp.logical_not(own), sibling_b.at[copy_id]),
        ]
        moves_b.append((None, sources, [(None, across_b.at[copy_id])]))
    for at, (copy_id, _, row, crosses, unit) in enumerate(items):
        own = row // slot_total == me
        sources = [
            (own, store_a.at[row % slot_total, core]),
            (jnp.logical_not(own), sibling_a.at[copy_id, core]),
        ]
        targets = [
            (
                jnp.logical_and(unit >= start, unit < start + size),
                array.at[jnp.clip(unit - start, 0, size - 1)],
            )
            for array, (start, size) in zip(units, spread)
            if start <= at
        ]
        moves_a.append((crosses, sources, targets))
    count = items[-1][4] + items[-1][3].astype(jnp.int32)
    extra[0] = jnp.clip(count - AT_NEED[0][0], 0, len(AT_NEED))
    staged([(moves_b, buffer_b, sems_b), (moves_a, buffer_a, sems_a)])


def place_kernel(spans, slot_total, spread, *refs):
    (me_ref, holder, dest, earlier) = refs[:4]
    got, other = refs[4 : 4 + len(spread)], refs[4 + len(spread) : 4 + 2 * len(spread)]
    out, buffer, sems = refs[-3:]
    me = me_ref[0]
    core = me % 2
    first_unit = spread[0][0]
    past_unit = spread[-1][0] + spread[-1][1]
    items = crossing(holder, dest, spans, slot_total, me // 2)
    moves = []
    for copy_id in range(COPIES):
        one, two = items[2 * copy_id], items[2 * copy_id + 1]
        crosses = jnp.where(core == 0, one[3].astype(jnp.int32), two[3].astype(jnp.int32)) != 0
        unit = jnp.where(core == 0, one[4], two[4])
        possible = [i for i, (start, _) in enumerate(spread) if start <= 2 * copy_id + 1]
        if first_unit and not possible:
            continue
        here = jnp.logical_and(unit >= first_unit, unit < past_unit)
        for half, arrays in ((core, got), (1 - core, other)):
            sources = []
            active = jnp.logical_and(crosses, here)
            if not first_unit:
                near = jnp.logical_not(crosses)
                active = jnp.logical_or(near, here)
                sources.append((near, earlier.at[copy_id, half]))
            for i in possible:
                start, size = spread[i]
                hit = jnp.logical_and(unit >= start, unit < start + size)
                source = arrays[i].at[jnp.clip(unit - start, 0, size - 1)]
                sources.append((jnp.logical_and(crosses, hit), source))
            moves.append((active, sources, [(None, out.at[copy_id, half])]))
    staged([(moves, buffer, sems)])


def copy_call(kernel, tables, arrays, shapes, scratch, scalars=(), aliases=None):
    hbm = pl.BlockSpec(memory_space=pl.ANY)
    dtype = arrays[0].dtype
    return pl.pallas_call(
        kernel,
        out_shape=[pltpu.HBM(shape, dtype) for shape in shapes]
        + [jax.ShapeDtypeStruct(shape, jnp.int32) for shape in scalars],
        in_specs=[SMEM] * len(tables) + [hbm] * len(arrays),
        out_specs=[hbm] * len(shapes) + [SMEM] * len(scalars),
        scratch_shapes=[pltpu.VMEM(shape, dtype) for shape in scratch]
        + [pltpu.SemaphoreType.DMA((2, shape[0])) for shape in scratch],
        input_output_aliases=aliases or {},
    )(*tables, *arrays)


def project_kernel(spans, slot_total, resident, steps, masks, *refs):
    (me_ref, resident_adapter, arrival_adapter, holder, dest, hidden, *others) = refs[: 6 + len(masks)]
    store, *outs, left, adapters, sums = refs[6 + len(masks) :]
    me = me_ref[0]
    group = pl.program_id(0)
    base = hidden.shape[0]
    block = others[0].shape[0]
    width = sums.shape[1]
    per_step = store.shape[1] // width

    @pl.when(group == 0)
    def _():
        left[0:base] = hidden[...]
        for i, other in enumerate(others):
            left[base + i * block : base + (i + 1) * block] = other[...]
        sums[...] = jnp.zeros_like(sums)
        ids = lax.broadcasted_iota(jnp.int32, sums.shape, 0) // steps
        own = jnp.full(sums.shape, -1, jnp.int32)
        for slot in range(resident):
            own = jnp.where(ids == slot, resident_adapter[me * resident + slot], own)
        for i, mask in enumerate((0,) + masks):
            replica = me ^ mask
            first = resident if i == 0 else (base + (i - 1) * block) // steps
            for a in range(arrival_adapter.shape[0]):
                chosen = arrival_adapter[a, replica]
                row = jnp.int32(0)
                for span in range(spans):
                    at = chosen * spans + span
                    row += jnp.where(dest[0, at] == replica, holder[at], 0)
                here = jnp.where(row // slot_total == me, row % slot_total, -1)
                own = jnp.where(ids == first + a, here, own)
        adapters[...] = own

    product = lax.dot_general(
        left[...], store[0], (((1,), (1,)), ((), ())), preferred_element_type=jnp.float32
    )
    for i in range(per_step):
        hit = adapters[...] == group * per_step + i
        sums[...] += jnp.where(hit, product[:, i * width : (i + 1) * width], 0.0)

    @pl.when(group == pl.num_programs(0) - 1)
    def _():
        outs[0][...] = sums[0:base]
        for i, out in enumerate(outs[1:]):
            out[...] = sums[base + i * block : base + (i + 1) * block]


def gather_kernel(chunks, shard_ref, *refs):
    partial, *returned, out, total = refs[chunks:]
    width = refs[0].shape[1]
    for step, ref in enumerate(refs[:chunks]):
        source = lax.rem(shard_ref[0] + chunks - step, chunks)
        out[:, pl.ds(pl.multiple_of(source * width, width), width)] = ref[...]
    first = partial.shape[0] - returned[0].shape[0]
    last = partial[first:]
    for ref in returned:
        last = last + ref[...]
    total[:first] = partial[:first]
    total[first:] = last


def attend_kernel(spans, masks, resident, steps, kv_heads, head_length, *refs):
    (me_ref, lengths, arrival_from, arrival_slot, resident_adapter, arrival_adapter) = refs[:6]
    holder, dest, *parts = refs[6 : -14 - len(masks)]
    came = refs[-14 - len(masks) : -14]
    store_b, sibling_b, across_b, base, queries, cache = refs[-14:-8]
    out, new_kv, arrived, installed_b = refs[-8:-4]
    fresh_ref, mixed_ref, score_ref, weight_ref = refs[-4:]
    me = me_ref[0]
    arrive = arrival_from.shape[0]
    replicas = arrival_from.shape[1]
    slots = resident + arrive
    row_count = base.shape[1]
    rank = store_b.shape[1] // 2
    slot_total = store_b.shape[0]
    half = head_length // 2
    seen = [lengths[me * resident + slot] for slot in range(resident)]
    for a in range(arrive):
        seen.append(lengths[arrival_from[a, me] * resident + arrival_slot[a, me]])

    for a in range(arrive):
        for ref, mask in zip(came, masks):

            @pl.when(arrival_from[a, me] == me ^ mask)
            def _():
                arrived[a] = ref[...]

        def clear(row, carry):
            arrived[a, row] = jnp.zeros(arrived.shape[2:], arrived.dtype)
            return carry

        lax.fori_loop(seen[resident + a], arrived.shape[1], clear, 0)
    for copy_id in range(COPIES):
        near = wanted_by(holder, dest, spans, me, copy_id) // (2 * slot_total) == me // 2

        @pl.when(near)
        def _():
            installed_b[copy_id] = sibling_b[copy_id]

        @pl.when(jnp.logical_not(near))
        def _():
            installed_b[copy_id] = across_b[copy_id]

    total = parts[0][...]
    for part in parts[1:]:
        total = total + part[...]
    down = total.astype(jnp.bfloat16)

    ids = lax.broadcasted_iota(jnp.int32, (row_count, 1), 0) // steps
    adapters = jnp.zeros((row_count, 1), jnp.int32)
    position = lax.broadcasted_iota(jnp.int32, (row_count, 1), 0) % steps
    for slot in range(slots):
        if slot < resident:
            adapter = resident_adapter[me * resident + slot]
        else:
            adapter = store_b.shape[0] + arrival_adapter[slot - resident, me]
        adapters = jnp.where(ids == slot, adapter, adapters)
        position = jnp.where(ids == slot, position + seen[slot], position)
    deltas = [jnp.zeros((row_count, store_b.shape[2]), jnp.float32) for _ in range(2)]
    for adapter in range(store_b.shape[0] + COPIES):
        if adapter < store_b.shape[0]:
            table = store_b[adapter]
        else:
            table = installed_b[adapter - store_b.shape[0]]
        for part in range(2):
            product = jnp.dot(
                down[:, part * rank : (part + 1) * rank],
                table[part * rank : (part + 1) * rank],
                preferred_element_type=jnp.float32,
            )
            deltas[part] = jnp.where(adapters == adapter, product, deltas[part])

    lane = lax.broadcasted_iota(jnp.int32, (1, half), 1).astype(jnp.float32)
    frequency = jnp.exp(lane * (-2.0 * math.log(ROPE_BASE) / head_length))
    angles = position.astype(jnp.float32) * frequency
    cosine, sine = jnp.cos(angles), jnp.sin(angles)
    dead = jnp.zeros((row_count, 1), jnp.bool_)
    gone = [jnp.int32(0)] * resident
    for q in range(replicas):
        for a in range(arrive):
            mine = arrival_from[a, q] == me
            slot = arrival_slot[a, q]
            dead = jnp.logical_or(dead, jnp.logical_and(ids == slot, mine))
            for n in range(resident):
                gone[n] = jnp.where(jnp.logical_and(mine, slot == n), 1, gone[n])
    for g in range(kv_heads):
        columns = slice(g * head_length, (g + 1) * head_length)
        key = base[g, :, :head_length] + ADAPTER_SCALE * deltas[0][:, columns]
        value = base[g, :, head_length:] + ADAPTER_SCALE * deltas[1][:, columns]
        u, w = key[:, :half], key[:, half:]
        key = jnp.concatenate([u * cosine - w * sine, w * cosine + u * sine], axis=1)
        for part, piece in enumerate((key, value)):
            rounded = piece.astype(jnp.bfloat16).astype(jnp.float32)
            lanes = slice(part * head_length, (part + 1) * head_length)
            fresh_ref[part, pl.ds(g, row_count, stride=kv_heads)] = rounded
            kept = jnp.where(dead, 0.0, rounded)[: slots * steps]
            new_kv[:, :, g, lanes] = kept.reshape(slots, steps, head_length).astype(jnp.bfloat16)

    query_rows = queries.shape[1]
    heads = query_rows // steps
    cache_rows = cache.shape[1] * kv_heads
    new_rows = steps * kv_heads
    pad_rows = 16 - new_rows
    row = lax.broadcasted_iota(jnp.int32, (query_rows, 1), 0)
    step_of = row // heads
    group_of = row % heads // (heads // kv_heads)
    column = lax.broadcasted_iota(jnp.int32, (query_rows, cache_rows), 1)
    same = column % kv_heads == group_of
    past_row = column // kv_heads
    late = lax.broadcasted_iota(jnp.int32, (query_rows, 128), 1)
    allowed = jnp.logical_and(late % kv_heads == group_of, late // kv_heads <= step_of)
    allowed = jnp.logical_and(allowed, late < new_rows)
    scale = 1.0 / math.sqrt(head_length)

    def cached(n):
        stored = cache[n] if n < resident else arrived[n - resident]
        return stored.reshape(cache_rows, 2 * head_length)

    def fresh_rows(n, part):
        lines = fresh_ref[part, n * new_rows : (n + 1) * new_rows]
        blank = jnp.zeros((pad_rows, head_length), jnp.float32)
        return jnp.concatenate([lines, blank], axis=0).astype(jnp.bfloat16)

    def against(query, keys):
        return lax.dot_general(
            query, keys, (((1,), (1,)), ((), ())), preferred_element_type=jnp.float32
        )

    for n in range(slots):
        lines = slice(n * query_rows, (n + 1) * query_rows)
        query = queries[n]
        score = against(query, cached(n)[:, :head_length]) * scale
        score = jnp.where(jnp.logical_and(same, past_row < seen[n]), score, -jnp.inf)
        score_ref[lines, :cache_rows] = score
        keys = jnp.concatenate(
            [fresh_rows(n, 0), jnp.zeros((128 - 16, head_length), jnp.bfloat16)], axis=0
        )
        score = against(query, keys) * scale
        score_ref[lines, cache_rows:] = jnp.where(allowed, score, -jnp.inf)
    for n in range(slots):
        lines = slice(n * query_rows, (n + 1) * query_rows)
        score = score_ref[lines]
        term = jnp.exp(score - jnp.max(score, axis=1, keepdims=True))
        inverse = 1.0 / jnp.sum(term, axis=1, keepdims=True)
        weight_ref[lines] = (term * inverse).astype(jnp.bfloat16)
    for n in range(slots):
        lines = slice(n * query_rows, (n + 1) * query_rows)
        weight = weight_ref[lines]
        mixed = jnp.dot(
            weight[:, :cache_rows], cached(n)[:, head_length:], preferred_element_type=jnp.float32
        )
        mixed = mixed + jnp.dot(
            weight[:, cache_rows : cache_rows + 16],
            fresh_rows(n, 1),
            preferred_element_type=jnp.float32,
        )
        if n < resident:
            mixed = jnp.where(gone[n] != 0, 0.0, mixed)
        mixed_ref[lines] = mixed
    for n in range(slots):
        for head in range(heads):
            lanes = slice(head * head_length, (head + 1) * head_length)
            pair = mixed_ref[pl.ds(n * query_rows + head, steps, stride=heads)]
            out[n, :, lanes] = pair.astype(jnp.bfloat16)


def pairs_layer(
    hidden,
    queries,
    kv_cache,
    w_kv,
    store_a,
    store_b,
    lengths,
    arrival_from,
    arrival_slot,
    resident_adapter,
    arrival_adapter,
    hot_holder,
    hot_dest,
):
    me = lax.axis_index("replica")
    replicas = lax.axis_size("replica")
    shards = lax.axis_size("tensor")
    resident, cap, kv_heads, head_pair = kv_cache.shape
    arrive = arrival_from.shape[1]
    slots = resident + arrive
    steps, features = hidden.shape[1:]
    heads, head_length = queries.shape[2:]
    slot_total = store_a.shape[0]
    rank = store_a.shape[2]
    spans = hot_holder.shape[0] // COPIES
    row_a, row_b = store_a.shape[1:], store_b.shape[1:]
    columns = store_b.shape[3]
    masks = tuple(range(1, replicas))
    me_table = jnp.reshape(me, (1,)).astype(jnp.int32)
    shard_table = jnp.reshape(lax.axis_index("tensor"), (1,)).astype(jnp.int32)
    from_table, slot_table, choice_table = arrival_from.T, arrival_slot.T, arrival_adapter.T
    dest_table = hot_dest.T

    used = slots * steps
    padded = -(-used // 8) * 8
    first = resident * steps
    block = padded - first

    *leaving, rows_a, rows_b, rows, asking = copy_call(
        functools.partial(collect_kernel, spans, slot_total, masks),
        (me_table, from_table, slot_table, hot_holder),
        (kv_cache, store_a, store_b, hidden),
        [kv_cache.shape[1:]] * len(masks)
        + [(COPIES,) + row_a, (COPIES,) + row_b, (padded, features), (block, features)],
        [
            (len(masks),) + kv_cache.shape[1:],
            (COPIES,) + row_a,
            (COPIES,) + row_b,
            hidden.shape,
            (padded, features),
        ],
    )
    sibling_a = partner(rows_a, 1)
    sibling_b = partner(rows_b, 1)
    other_rows = [partner(asking, mask) for mask in masks]
    came = [partner(array, mask) for array, mask in zip(leaving, masks)]
    around = [rows] + [shifted(rows, step) for step in range(1, shards)]

    line_count = padded + len(masks) * block
    per_step = 2 if slot_total % 2 == 0 else 1
    partial, *sent = pl.pallas_call(
        functools.partial(project_kernel, spans, slot_total, resident, steps, masks),
        out_shape=[jax.ShapeDtypeStruct((padded, 2 * rank), jnp.float32)]
        + [jax.ShapeDtypeStruct((block, 2 * rank), jnp.float32)] * len(masks),
        grid=(slot_total // per_step,),
        in_specs=[SMEM] * 5
        + [pl.BlockSpec((padded, features), lambda i: (0, 0))]
        + [pl.BlockSpec((block, features), lambda i: (0, 0))] * len(masks)
        + [pl.BlockSpec((1, per_step * 2 * rank, features), lambda i: (i, 0, 0))],
        out_specs=[pl.BlockSpec((padded, 2 * rank), lambda i: (0, 0))]
        + [pl.BlockSpec((block, 2 * rank), lambda i: (0, 0))] * len(masks),
        scratch_shapes=[
            pltpu.VMEM((line_count, features), hidden.dtype),
            pltpu.VMEM((line_count, 2 * rank), jnp.int32),
            pltpu.VMEM((line_count, 2 * rank), jnp.float32),
        ],
        name="project",
    )(
        me_table,
        resident_adapter,
        choice_table,
        hot_holder,
        dest_table,
        rows,
        *other_rows,
        store_a.reshape(slot_total // per_step, per_step * 2 * rank, features),
    )
    returned = [partner(array, mask) for array, mask in zip(sent, masks)]
    unit_shape = row_a[1:]
    unit_total = 2 * COPIES
    across_b, *units, extra = copy_call(
        functools.partial(pack_kernel, spans, slot_total),
        (me_table, hot_holder, dest_table),
        (store_a, store_b, sibling_a, sibling_b),
        [(COPIES,) + row_b] + [(size,) + unit_shape for _, size in ALWAYS + AT_NEED],
        [(COPIES,) + row_b, (unit_total,) + unit_shape],
        [(1,)],
    )
    across_b = partner(across_b, 2)
    got = []
    for array in units[: len(ALWAYS)]:
        got.append(partner(array, 2))

    full, partial = pl.pallas_call(
        functools.partial(gather_kernel, shards),
        out_shape=[
            jax.ShapeDtypeStruct((padded, shards * features), hidden.dtype),
            jax.ShapeDtypeStruct(partial.shape, jnp.float32),
        ],
        in_specs=[SMEM] + [VMEM] * (shards + 1 + len(masks)),
        out_specs=[VMEM] * 2,
        name="gather",
    )(shard_table, *around, partial, *returned)
    parts = [partial] + [shifted(partial, step) for step in range(1, shards)]
    base = jnp.einsum("md,dgc->gmc", full, w_kv, preferred_element_type=jnp.float32)

    attn_out, new_kv, arrived, installed_b = pl.pallas_call(
        functools.partial(attend_kernel, spans, masks, resident, steps, kv_heads, head_length),
        out_shape=[
            jax.ShapeDtypeStruct((slots, steps, heads * head_length), jnp.bfloat16),
            jax.ShapeDtypeStruct((slots, steps, kv_heads, head_pair), jnp.bfloat16),
            jax.ShapeDtypeStruct((arrive,) + kv_cache.shape[1:], jnp.bfloat16),
            jax.ShapeDtypeStruct((COPIES, 2 * rank, columns), jnp.bfloat16),
        ],
        in_specs=[SMEM] * 8 + [VMEM] * (shards + len(masks) + 6),
        out_specs=[VMEM] * 4,
        scratch_shapes=[
            pltpu.VMEM((2, padded * kv_heads, head_length), jnp.float32),
            pltpu.VMEM((slots * steps * heads, head_length), jnp.float32),
            pltpu.VMEM((slots * steps * heads, cap * kv_heads + 128), jnp.float32),
            pltpu.VMEM((slots * steps * heads, cap * kv_heads + 128), jnp.bfloat16),
        ],
        name="attend",
    )(
        me_table,
        lengths,
        from_table,
        slot_table,
        resident_adapter,
        choice_table,
        hot_holder,
        dest_table,
        *parts,
        *came,
        store_b.reshape(slot_total, 2 * rank, columns),
        sibling_b.reshape(COPIES, 2 * rank, columns),
        across_b.reshape(COPIES, 2 * rank, columns),
        base,
        queries.reshape(slots, steps * heads, head_length),
        kv_cache,
    )
    installed_b = installed_b.reshape((COPIES,) + row_b)

    tables = (me_table, hot_holder, dest_table)
    early = len(ALWAYS) - 1
    other = [partner(array, 1) for array in got[:early]]
    (placed,) = copy_call(
        functools.partial(place_kernel, spans, slot_total, ALWAYS[:early]),
        tables,
        (sibling_a, *got[:early], *other),
        [(COPIES,) + row_a],
        [(unit_total,) + unit_shape],
    )

    def finish(count):
        def branch(placed, *arrays):
            late = [partner(array, 2) for array in arrays[1:][:count]]
            other = [partner(arrays[0], 1)]
            late = [arrays[0]] + late
            other += [partner(array, 1) for array in late[1:]]
            return copy_call(
                functools.partial(place_kernel, spans, slot_total, (ALWAYS + AT_NEED)[early:][: count + 1]),
                tables,
                (placed, *late, *other),
                [(COPIES,) + row_a],
                [(unit_total,) + unit_shape],
                aliases={len(tables): 0},
            )[0]

        return branch

    branches = [finish(count) for count in range(len(AT_NEED) + 1)]
    *rest, attn_out = lax.optimization_barrier((*units[len(ALWAYS) :], attn_out))
    installed_a = lax.switch(extra[0], branches, placed, got[early], *rest)
    return (attn_out, new_kv, arrived, installed_a, installed_b)


def local(*args):
    fan = args[-1].shape[1]
    if lax.axis_size("replica") == 4 and fan == 1:
        return pairs_layer(*args)
    return local_general(*args)


def solution(mesh):
    in_specs = (
        P(("parts", "replica"), None, "tensor"),
        P(("parts", "replica"), None, "tensor", None),
        P(("parts", "replica"), None, "tensor", None),
        P(None, "tensor", None),
        P(("parts", "replica"), None, None, "tensor"),
        P(("parts", "replica"), None, None, "tensor"),
        P("parts"),
        P("parts", None),
        P("parts", None),
        P("parts"),
        P("parts", None),
        P("parts"),
        P("parts", None),
    )
    out_specs = (
        P(("parts", "replica"), None, "tensor"),
        P(("parts", "replica"), None, "tensor", None),
        P(("parts", "replica"), None, "tensor", None),
        P(("parts", "replica"), None, None, "tensor"),
        P(("parts", "replica"), None, None, "tensor"),
    )
    return jax.shard_map(local, mesh=mesh, in_specs=in_specs, out_specs=out_specs, check_vma=False)
```

```python
import functools
import math

import jax
import jax.numpy as jnp
from jax import lax
from jax.experimental import pallas as pl
from jax.experimental.pallas import tpu as pltpu
from jax.sharding import PartitionSpec as P


COPIES = 4


ADAPTER_SCALE = 2.0
ROPE_BASE = 500000.0


def rotate_keys(key_rows, positions):
    head_length = key_rows.shape[-1]
    half_size = head_length // 2
    frequency = ROPE_BASE ** (-(jnp.arange(half_size, dtype=jnp.float32) * 2.0 / head_length))
    angles = positions.astype(jnp.float32)[:, :, None, None] * frequency
    cosine = jnp.cos(angles)
    sine_val = jnp.sin(angles)
    first_half = key_rows[..., :half_size]
    second_half = key_rows[..., half_size:]
    return jnp.concatenate(
        [
            first_half * cosine - second_half * sine_val,
            second_half * cosine + first_half * sine_val,
        ],
        axis=-1,
    )


def attend(queries, stored, lengths_now, fresh_kv):
    request_slot_count, decode_step_count, heads_local, head_length = queries.shape
    local_key_value = stored.shape[2]
    group_size = heads_local // local_key_value
    grouped = queries.reshape(
        request_slot_count, decode_step_count, local_key_value, group_size, head_length
    )
    score_scale = 1.0 / math.sqrt(head_length)
    past_scores = (
        jnp.einsum(
            "msgjd,mcgd->msgjc",
            grouped,
            stored[..., :head_length],
            preferred_element_type=jnp.float32,
        )
        * score_scale
    )
    recent_scores = (
        jnp.einsum(
            "msgjd,mtgd->msgjt",
            grouped,
            fresh_kv[..., :head_length],
            preferred_element_type=jnp.float32,
        )
        * score_scale
    )
    row_ids = jnp.arange(stored.shape[1], dtype=jnp.int32)
    past_ok = (row_ids[None, :] < lengths_now[:, None])[:, None, None, None, :]
    step_ids = jnp.arange(decode_step_count, dtype=jnp.int32)
    recent_ok = (step_ids[None, :] <= step_ids[:, None])[None, :, None, None, :]
    past_scores = jnp.where(past_ok, past_scores, -jnp.inf)
    recent_scores = jnp.where(recent_ok, recent_scores, -jnp.inf)
    peak_score = jnp.maximum(jnp.max(past_scores, -1), jnp.max(recent_scores, -1))[..., None]
    past_exp = jnp.exp(past_scores - peak_score)
    recent_exp = jnp.exp(recent_scores - peak_score)
    denom_sum = jnp.sum(past_exp, -1, keepdims=True) + jnp.sum(recent_exp, -1, keepdims=True)
    past_w = (past_exp / denom_sum).astype(jnp.bfloat16)
    recent_w = (recent_exp / denom_sum).astype(jnp.bfloat16)
    mixed_out = jnp.einsum(
        "msgjc,mcgd->msgjd", past_w, stored[..., head_length:], preferred_element_type=jnp.float32
    )
    mixed_out = mixed_out + jnp.einsum(
        "msgjt,mtgd->msgjd",
        recent_w,
        fresh_kv[..., head_length:],
        preferred_element_type=jnp.float32,
    )
    return mixed_out.reshape(request_slot_count, decode_step_count, heads_local * head_length)


def local_general(
    hidden,
    queries,
    kv_cache,
    w_kv,
    store_a,
    store_b,
    lengths,
    arrival_from,
    arrival_slot,
    resident_adapter,
    arrival_adapter,
    hot_holder,
    hot_dest,
):
    my_index = lax.axis_index("replica")
    replicas = lax.axis_size("replica")
    resident = kv_cache.shape[0]
    arrive = arrival_from.shape[1]
    request_slot_count = resident + arrive
    decode_step_count = hidden.shape[1]
    head_length = queries.shape[3]
    local_key_value = kv_cache.shape[2]
    slot_total = store_a.shape[0]
    hot_total = hot_holder.shape[0]
    spans = hot_total // COPIES
    my_from = lax.dynamic_index_in_dim(arrival_from, my_index, 0, keepdims=False)
    my_slot = lax.dynamic_index_in_dim(arrival_slot, my_index, 0, keepdims=False)
    own_ids = my_index * resident + jnp.arange(resident, dtype=jnp.int32)
    leaving_ids = (arrival_from * resident + arrival_slot).reshape(-1)
    staying = jnp.logical_not(jnp.any(own_ids[:, None] == leaving_ids[None, :], axis=1))
    live_mask = jnp.concatenate([staying, jnp.ones((arrive,), bool)])
    own_len = lax.dynamic_slice_in_dim(lengths, my_index * resident, resident)
    arrival_len = jnp.take(lengths, my_from * resident + my_slot)
    seen_len = jnp.concatenate([own_len, arrival_len])
    takes_mine = arrival_from == my_index
    sends_any = jnp.any(takes_mine, axis=1)
    send_slot = jnp.sum(jnp.where(takes_mine, arrival_slot, 0), axis=1)
    outgoing = jnp.take(kv_cache, send_slot, axis=0)
    outgoing = jnp.where(sends_any[:, None, None, None], outgoing, jnp.zeros((), jnp.bfloat16))
    incoming = lax.all_to_all(outgoing, "replica", split_axis=0, concat_axis=0, tiled=True)
    blocks = hot_dest.reshape(COPIES, spans, hot_dest.shape[1])
    holder_grid = hot_holder.reshape(COPIES, spans)
    holder_rep = holder_grid // slot_total
    mine = holder_rep == my_index
    has_one = jnp.any(mine, axis=1)
    local_pick = jnp.sum(jnp.where(mine, holder_grid % slot_total, 0), axis=1)

    def spread_rows(store):
        rows = jnp.take(store, local_pick, axis=0)
        rows = jnp.where(has_one[:, None, None, None], rows, jnp.zeros((), jnp.bfloat16))
        return rows.reshape(COPIES, replicas, -1).transpose(1, 0, 2)

    got_a, got_b = (
        lax.all_to_all(spread_rows(store_a), "replica", split_axis=0, concat_axis=0, tiled=True),
        lax.all_to_all(spread_rows(store_b), "replica", split_axis=0, concat_axis=0, tiled=True),
    )
    replica_ids = jnp.arange(replicas, dtype=jnp.int32)
    member = jnp.any(blocks[:, :, :, None] == replica_ids[None, None, None, :], axis=2).astype(
        jnp.int32
    )
    source_rep = jnp.sum(member * holder_rep[:, :, None], axis=1)
    copy_ids = jnp.arange(COPIES, dtype=jnp.int32)
    route_a = got_a[source_rep.T, copy_ids[None, :]]
    route_b = got_b[source_rep.T, copy_ids[None, :]]
    recv_a, recv_b = (
        lax.all_to_all(route_a, "replica", split_axis=0, concat_axis=0, tiled=True),
        lax.all_to_all(route_b, "replica", split_axis=0, concat_axis=0, tiled=True),
    )
    installed_a = recv_a.transpose(1, 0, 2).reshape((COPIES,) + store_a.shape[1:])
    installed_b = recv_b.transpose(1, 0, 2).reshape((COPIES,) + store_b.shape[1:])
    own_adapter = lax.dynamic_slice_in_dim(resident_adapter, my_index * resident, resident)
    my_choice = lax.dynamic_index_in_dim(arrival_adapter, my_index, 0, keepdims=False)
    adapt_a = jnp.concatenate(
        [jnp.take(store_a, own_adapter, axis=0), jnp.take(installed_a, my_choice, axis=0)]
    )
    adapter_up_weight = jnp.concatenate(
        [jnp.take(store_b, own_adapter, axis=0), jnp.take(installed_b, my_choice, axis=0)]
    )
    partial_value = jnp.einsum(
        "msd,mpkd->mspk", hidden, adapt_a, preferred_element_type=jnp.float32
    )
    base_projection = jnp.einsum(
        "msd,dgc->msgc",
        lax.all_gather(hidden, "tensor", axis=2, tiled=True),
        w_kv,
        preferred_element_type=jnp.float32,
    )
    down_projected = lax.psum(partial_value, "tensor")
    down_projected = down_projected.astype(jnp.bfloat16)
    adapter_update = jnp.einsum(
        "gnot,gote->gnoe", down_projected, adapter_up_weight, preferred_element_type=jnp.float32
    )
    adapter_update = (
        adapter_update.reshape(
            request_slot_count, decode_step_count, 2, local_key_value, head_length
        )
        .transpose(0, 1, 3, 2, 4)
        .reshape(request_slot_count, decode_step_count, local_key_value, 2 * head_length)
    )
    unrotated_key_value = base_projection + ADAPTER_SCALE * adapter_update
    positions = seen_len[:, None] + jnp.arange(decode_step_count, dtype=jnp.int32)[None, :]
    fresh_kv = jnp.concatenate(
        [
            rotate_keys(unrotated_key_value[..., :head_length], positions),
            unrotated_key_value[..., head_length:],
        ],
        axis=-1,
    ).astype(jnp.bfloat16)
    stay_out = attend(queries[:resident], kv_cache, own_len, fresh_kv[:resident])
    arrived = jnp.take(incoming, my_from, axis=0)
    row_ids = jnp.arange(kv_cache.shape[1], dtype=jnp.int32)
    arrived = jnp.where(
        (row_ids[None, :] < arrival_len[:, None])[:, :, None, None],
        arrived,
        jnp.zeros((), jnp.bfloat16),
    )
    move_out = attend(queries[resident:], arrived, arrival_len, fresh_kv[resident:])
    mixed_out = jnp.concatenate([stay_out, move_out], axis=0)
    attn_out = jnp.where(live_mask[:, None, None], mixed_out, 0.0).astype(jnp.bfloat16)
    new_kv = jnp.where(live_mask[:, None, None, None], fresh_kv, jnp.zeros((), jnp.bfloat16))
    return (attn_out, new_kv, arrived, installed_a, installed_b)


def partner(array, mask):
    return lax.ppermute(array, "replica", [(i, i ^ mask) for i in range(lax.axis_size("replica"))])


def shifted(array, step):
    size = lax.axis_size("tensor")
    return lax.ppermute(array, "tensor", [(i, (i + step) % size) for i in range(size)])


ALWAYS = ((0, 2), (2, 2), (4, 1))
AT_NEED = ((5, 1), (6, 1), (7, 1))
SMEM = pl.BlockSpec(memory_space=pltpu.SMEM)
VMEM = pl.BlockSpec(memory_space=pltpu.VMEM)


def wanted_by(holder, dest, spans, replica, copy_id):
    row = jnp.int32(0)
    for span in range(spans):
        at = copy_id * spans + span
        row += jnp.where(dest[0, at] == replica, holder[at], 0)
    return row


def crossing(holder, dest, spans, slot_total, chip):
    items, count = [], jnp.int32(0)
    for copy_id in range(COPIES):
        for core in range(2):
            row = wanted_by(holder, dest, spans, 2 * chip + core, copy_id)
            crosses = row // (2 * slot_total) != chip
            items.append((copy_id, core, row, crosses, count))
            count = count + crosses.astype(jnp.int32)
    return items


def staged(groups, meanwhile=None):
    def when(condition, action):
        if condition is None:
            action()
        else:
            pl.when(condition)(action)

    def begin(at, sources, buffer, sems):
        for condition, source in sources:
            when(condition, pltpu.make_async_copy(source, buffer.at[at], sems.at[0, at]).start)

    def forward(at, targets, buffer, sems):
        pltpu.make_async_copy(buffer.at[at], buffer.at[at], sems.at[0, at]).wait()
        for condition, target in targets:
            when(condition, pltpu.make_async_copy(buffer.at[at], target, sems.at[1, at]).start)

    def finish(at, buffer, sems):
        pltpu.make_async_copy(buffer.at[at], buffer.at[at], sems.at[1, at]).wait()

    for moves, buffer, sems in groups:
        for at, (condition, sources, _) in enumerate(moves):
            when(condition, functools.partial(begin, at, sources, buffer, sems))
    if meanwhile is not None:
        meanwhile()
    for moves, buffer, sems in groups:
        for at, (condition, _, targets) in enumerate(moves):
            when(condition, functools.partial(forward, at, targets, buffer, sems))
    for moves, buffer, sems in groups:
        for at, (condition, _, _) in enumerate(moves):
            when(condition, functools.partial(finish, at, buffer, sems))


def collect_kernel(spans, slot_total, masks, *refs):
    (me_ref, arrival_from, arrival_slot, holder, kv_cache, store_a, store_b, hidden) = refs[:8]
    *leaving, rows_a, rows_b, rows, asking = refs[8 : 12 + len(masks)]
    *buffers, raw, even = refs[12 + len(masks) : 17 + len(masks)]
    *semaphores, raw_sems, even_sems = refs[17 + len(masks) :]
    me = me_ref[0]
    moves = []
    for i, mask in enumerate(masks):
        to = me ^ mask
        slot = jnp.int32(0)
        for a in range(arrival_from.shape[0]):
            slot += jnp.where(arrival_from[a, to] == me, arrival_slot[a, to], 0)
        moves.append((None, [(None, kv_cache.at[slot])], [(None, leaving[i])]))
    groups = [moves]
    held = []
    for copy_id in range(COPIES):
        slot = jnp.int32(0)
        for span in range(spans):
            row = holder[copy_id * spans + span]
            slot += jnp.where(row // slot_total == me, row % slot_total, 0)
        held.append(slot)
    for table, target in ((store_a, rows_a), (store_b, rows_b)):
        groups.append(
            [
                (None, [(None, table.at[slot])], [(None, target.at[copy_id])])
                for copy_id, slot in enumerate(held)
            ]
        )

    start = rows.shape[0] - asking.shape[0]
    fetch = pltpu.make_async_copy(hidden, raw, raw_sems.at[0, 0])
    puts = [
        pltpu.make_async_copy(even, rows, even_sems.at[0, 0]),
        pltpu.make_async_copy(even.at[start:], asking, even_sems.at[1, 0]),
    ]

    def regroup():
        count = raw.shape[0] * raw.shape[1]
        blank = jnp.zeros((rows.shape[0] - count, rows.shape[1]), rows.dtype)
        fetch.wait()
        every = raw[...].reshape(count, rows.shape[1])
        even[...] = jnp.concatenate([every, blank], axis=0)
        for put in puts:
            put.start()

    fetch.start()
    staged(list(zip(groups, buffers, semaphores)), regroup)
    for put in puts:
        put.wait()


def pack_kernel(spans, slot_total, *refs):
    (me_ref, holder, dest, store_a, store_b, sibling_a, sibling_b) = refs[:7]
    across_b, *units = refs[7:-5]
    spread = ALWAYS + AT_NEED
    extra, buffer_b, buffer_a, sems_b, sems_a = refs[-5:]
    me = me_ref[0]
    core = me % 2
    chip = 1 - me // 2
    items = crossing(holder, dest, spans, slot_total, chip)
    moves_b, moves_a = [], []
    for copy_id in range(COPIES):
        row = jnp.where(core == 0, items[2 * copy_id][2], items[2 * copy_id + 1][2])
        own = row // slot_total == me
        sources = [
            (own, store_b.at[row % slot_total]),
            (jnp.logical_not(own), sibling_b.at[copy_id]),
        ]
        moves_b.append((None, sources, [(None, across_b.at[copy_id])]))
    for at, (copy_id, _, row, crosses, unit) in enumerate(items):
        own = row // slot_total == me
        sources = [
            (own, store_a.at[row % slot_total, core]),
            (jnp.logical_not(own), sibling_a.at[copy_id, core]),
        ]
        targets = [
            (
                jnp.logical_and(unit >= start, unit < start + size),
                array.at[jnp.clip(unit - start, 0, size - 1)],
            )
            for array, (start, size) in zip(units, spread)
            if start <= at
        ]
        moves_a.append((crosses, sources, targets))
    count = items[-1][4] + items[-1][3].astype(jnp.int32)
    extra[0] = jnp.clip(count - AT_NEED[0][0], 0, len(AT_NEED))
    staged([(moves_b, buffer_b, sems_b), (moves_a, buffer_a, sems_a)])


def place_kernel(spans, slot_total, spread, *refs):
    (me_ref, holder, dest, earlier) = refs[:4]
    got, other = refs[4 : 4 + len(spread)], refs[4 + len(spread) : 4 + 2 * len(spread)]
    out, buffer, sems = refs[-3:]
    me = me_ref[0]
    core = me % 2
    first_unit = spread[0][0]
    past_unit = spread[-1][0] + spread[-1][1]
    items = crossing(holder, dest, spans, slot_total, me // 2)
    moves = []
    for copy_id in range(COPIES):
        one, two = items[2 * copy_id], items[2 * copy_id + 1]
        crosses = jnp.where(core == 0, one[3].astype(jnp.int32), two[3].astype(jnp.int32)) != 0
        unit = jnp.where(core == 0, one[4], two[4])
        possible = [i for i, (start, _) in enumerate(spread) if start <= 2 * copy_id + 1]
        if first_unit and not possible:
            continue
        here = jnp.logical_and(unit >= first_unit, unit < past_unit)
        for half, arrays in ((core, got), (1 - core, other)):
            sources = []
            active = jnp.logical_and(crosses, here)
            if not first_unit:
                near = jnp.logical_not(crosses)
                active = jnp.logical_or(near, here)
                sources.append((near, earlier.at[copy_id, half]))
            for i in possible:
                start, size = spread[i]
                hit = jnp.logical_and(unit >= start, unit < start + size)
                source = arrays[i].at[jnp.clip(unit - start, 0, size - 1)]
                sources.append((jnp.logical_and(crosses, hit), source))
            moves.append((active, sources, [(None, out.at[copy_id, half])]))
    staged([(moves, buffer, sems)])


def copy_call(kernel, tables, arrays, shapes, scratch, scalars=(), aliases=None):
    hbm = pl.BlockSpec(memory_space=pl.ANY)
    dtype = arrays[0].dtype
    return pl.pallas_call(
        kernel,
        out_shape=[pltpu.HBM(shape, dtype) for shape in shapes]
        + [jax.ShapeDtypeStruct(shape, jnp.int32) for shape in scalars],
        in_specs=[SMEM] * len(tables) + [hbm] * len(arrays),
        out_specs=[hbm] * len(shapes) + [SMEM] * len(scalars),
        scratch_shapes=[pltpu.VMEM(shape, dtype) for shape in scratch]
        + [pltpu.SemaphoreType.DMA((2, shape[0])) for shape in scratch],
        input_output_aliases=aliases or {},
    )(*tables, *arrays)


def project_kernel(spans, slot_total, resident, steps, masks, *refs):
    (me_ref, resident_adapter, arrival_adapter, holder, dest, hidden, *others) = refs[: 6 + len(masks)]
    store, *outs, left, adapters, sums = refs[6 + len(masks) :]
    me = me_ref[0]
    group = pl.program_id(0)
    base = hidden.shape[0]
    block = others[0].shape[0]
    width = sums.shape[1]
    per_step = store.shape[1] // width

    @pl.when(group == 0)
    def _():
        left[0:base] = hidden[...]
        for i, other in enumerate(others):
            left[base + i * block : base + (i + 1) * block] = other[...]
        sums[...] = jnp.zeros_like(sums)
        ids = lax.broadcasted_iota(jnp.int32, sums.shape, 0) // steps
        own = jnp.full(sums.shape, -1, jnp.int32)
        for slot in range(resident):
            own = jnp.where(ids == slot, resident_adapter[me * resident + slot], own)
        for i, mask in enumerate((0,) + masks):
            replica = me ^ mask
            first = resident if i == 0 else (base + (i - 1) * block) // steps
            for a in range(arrival_adapter.shape[0]):
                chosen = arrival_adapter[a, replica]
                row = jnp.int32(0)
                for span in range(spans):
                    at = chosen * spans + span
                    row += jnp.where(dest[0, at] == replica, holder[at], 0)
                here = jnp.where(row // slot_total == me, row % slot_total, -1)
                own = jnp.where(ids == first + a, here, own)
        adapters[...] = own

    product = lax.dot_general(
        left[...], store[0], (((1,), (1,)), ((), ())), preferred_element_type=jnp.float32
    )
    for i in range(per_step):
        hit = adapters[...] == group * per_step + i
        sums[...] += jnp.where(hit, product[:, i * width : (i + 1) * width], 0.0)

    @pl.when(group == pl.num_programs(0) - 1)
    def _():
        outs[0][...] = sums[0:base]
        for i, out in enumerate(outs[1:]):
            out[...] = sums[base + i * block : base + (i + 1) * block]


def gather_kernel(chunks, shard_ref, *refs):
    partial, *returned, out, total = refs[chunks:]
    width = refs[0].shape[1]
    for step, ref in enumerate(refs[:chunks]):
        source = lax.rem(shard_ref[0] + chunks - step, chunks)
        out[:, pl.ds(pl.multiple_of(source * width, width), width)] = ref[...]
    first = partial.shape[0] - returned[0].shape[0]
    last = partial[first:]
    for ref in returned:
        last = last + ref[...]
    total[:first] = partial[:first]
    total[first:] = last


def attend_kernel(spans, masks, resident, steps, kv_heads, head_length, *refs):
    (me_ref, lengths, arrival_from, arrival_slot, resident_adapter, arrival_adapter) = refs[:6]
    holder, dest, *parts = refs[6 : -14 - len(masks)]
    came = refs[-14 - len(masks) : -14]
    store_b, sibling_b, across_b, base, queries, cache = refs[-14:-8]
    out, new_kv, arrived, installed_b = refs[-8:-4]
    fresh_ref, mixed_ref, score_ref, weight_ref = refs[-4:]
    me = me_ref[0]
    arrive = arrival_from.shape[0]
    replicas = arrival_from.shape[1]
    slots = resident + arrive
    row_count = base.shape[1]
    rank = store_b.shape[1] // 2
    slot_total = store_b.shape[0]
    half = head_length // 2
    seen = [lengths[me * resident + slot] for slot in range(resident)]
    for a in range(arrive):
        seen.append(lengths[arrival_from[a, me] * resident + arrival_slot[a, me]])

    for a in range(arrive):
        for ref, mask in zip(came, masks):

            @pl.when(arrival_from[a, me] == me ^ mask)
            def _():
                arrived[a] = ref[...]

        def clear(row, carry):
            arrived[a, row] = jnp.zeros(arrived.shape[2:], arrived.dtype)
            return carry

        lax.fori_loop(seen[resident + a], arrived.shape[1], clear, 0)
    for copy_id in range(COPIES):
        near = wanted_by(holder, dest, spans, me, copy_id) // (2 * slot_total) == me // 2

        @pl.when(near)
        def _():
            installed_b[copy_id] = sibling_b[copy_id]

        @pl.when(jnp.logical_not(near))
        def _():
            installed_b[copy_id] = across_b[copy_id]

    total = parts[0][...]
    for part in parts[1:]:
        total = total + part[...]
    down = total.astype(jnp.bfloat16)

    ids = lax.broadcasted_iota(jnp.int32, (row_count, 1), 0) // steps
    adapters = jnp.zeros((row_count, 1), jnp.int32)
    position = lax.broadcasted_iota(jnp.int32, (row_count, 1), 0) % steps
    for slot in range(slots):
        if slot < resident:
            adapter = resident_adapter[me * resident + slot]
        else:
            adapter = store_b.shape[0] + arrival_adapter[slot - resident, me]
        adapters = jnp.where(ids == slot, adapter, adapters)
        position = jnp.where(ids == slot, position + seen[slot], position)
    deltas = [jnp.zeros((row_count, store_b.shape[2]), jnp.float32) for _ in range(2)]
    for adapter in range(store_b.shape[0] + COPIES):
        if adapter < store_b.shape[0]:
            table = store_b[adapter]
        else:
            table = installed_b[adapter - store_b.shape[0]]
        for part in range(2):
            product = jnp.dot(
                down[:, part * rank : (part + 1) * rank],
                table[part * rank : (part + 1) * rank],
                preferred_element_type=jnp.float32,
            )
            deltas[part] = jnp.where(adapters == adapter, product, deltas[part])

    lane = lax.broadcasted_iota(jnp.int32, (1, half), 1).astype(jnp.float32)
    frequency = jnp.exp(lane * (-2.0 * math.log(ROPE_BASE) / head_length))
    angles = position.astype(jnp.float32) * frequency
    cosine, sine = jnp.cos(angles), jnp.sin(angles)
    dead = jnp.zeros((row_count, 1), jnp.bool_)
    gone = [jnp.int32(0)] * resident
    for q in range(replicas):
        for a in range(arrive):
            mine = arrival_from[a, q] == me
            slot = arrival_slot[a, q]
            dead = jnp.logical_or(dead, jnp.logical_and(ids == slot, mine))
            for n in range(resident):
                gone[n] = jnp.where(jnp.logical_and(mine, slot == n), 1, gone[n])
    for g in range(kv_heads):
        columns = slice(g * head_length, (g + 1) * head_length)
        key = base[g, :, :head_length] + ADAPTER_SCALE * deltas[0][:, columns]
        value = base[g, :, head_length:] + ADAPTER_SCALE * deltas[1][:, columns]
        u, w = key[:, :half], key[:, half:]
        key = jnp.concatenate([u * cosine - w * sine, w * cosine + u * sine], axis=1)
        for part, piece in enumerate((key, value)):
            rounded = piece.astype(jnp.bfloat16).astype(jnp.float32)
            lanes = slice(part * head_length, (part + 1) * head_length)
            fresh_ref[part, pl.ds(g, row_count, stride=kv_heads)] = rounded
            kept = jnp.where(dead, 0.0, rounded)[: slots * steps]
            new_kv[:, :, g, lanes] = kept.reshape(slots, steps, head_length).astype(jnp.bfloat16)

    query_rows = queries.shape[1]
    heads = query_rows // steps
    cache_rows = cache.shape[1] * kv_heads
    new_rows = steps * kv_heads
    pad_rows = 16 - new_rows
    row = lax.broadcasted_iota(jnp.int32, (query_rows, 1), 0)
    step_of = row // heads
    group_of = row % heads // (heads // kv_heads)
    column = lax.broadcasted_iota(jnp.int32, (query_rows, cache_rows), 1)
    same = column % kv_heads == group_of
    past_row = column // kv_heads
    late = lax.broadcasted_iota(jnp.int32, (query_rows, 128), 1)
    allowed = jnp.logical_and(late % kv_heads == group_of, late // kv_heads <= step_of)
    allowed = jnp.logical_and(allowed, late < new_rows)
    scale = 1.0 / math.sqrt(head_length)

    def cached(n):
        stored = cache[n] if n < resident else arrived[n - resident]
        return stored.reshape(cache_rows, 2 * head_length)

    def fresh_rows(n, part):
        lines = fresh_ref[part, n * new_rows : (n + 1) * new_rows]
        blank = jnp.zeros((pad_rows, head_length), jnp.float32)
        return jnp.concatenate([lines, blank], axis=0).astype(jnp.bfloat16)

    def against(query, keys):
        return lax.dot_general(
            query, keys, (((1,), (1,)), ((), ())), preferred_element_type=jnp.float32
        )

    for n in range(slots):
        lines = slice(n * query_rows, (n + 1) * query_rows)
        query = queries[n]
        score = against(query, cached(n)[:, :head_length]) * scale
        score = jnp.where(jnp.logical_and(same, past_row < seen[n]), score, -jnp.inf)
        score_ref[lines, :cache_rows] = score
        keys = jnp.concatenate(
            [fresh_rows(n, 0), jnp.zeros((128 - 16, head_length), jnp.bfloat16)], axis=0
        )
        score = against(query, keys) * scale
        score_ref[lines, cache_rows:] = jnp.where(allowed, score, -jnp.inf)
    for n in range(slots):
        lines = slice(n * query_rows, (n + 1) * query_rows)
        score = score_ref[lines]
        term = jnp.exp(score - jnp.max(score, axis=1, keepdims=True))
        inverse = 1.0 / jnp.sum(term, axis=1, keepdims=True)
        weight_ref[lines] = (term * inverse).astype(jnp.bfloat16)
    for n in range(slots):
        lines = slice(n * query_rows, (n + 1) * query_rows)
        weight = weight_ref[lines]
        mixed = jnp.dot(
            weight[:, :cache_rows], cached(n)[:, head_length:], preferred_element_type=jnp.float32
        )
        mixed = mixed + jnp.dot(
            weight[:, cache_rows : cache_rows + 16],
            fresh_rows(n, 1),
            preferred_element_type=jnp.float32,
        )
        if n < resident:
            mixed = jnp.where(gone[n] != 0, 0.0, mixed)
        mixed_ref[lines] = mixed
    for n in range(slots):
        for head in range(heads):
            lanes = slice(head * head_length, (head + 1) * head_length)
            pair = mixed_ref[pl.ds(n * query_rows + head, steps, stride=heads)]
            out[n, :, lanes] = pair.astype(jnp.bfloat16)


def pairs_layer(
    hidden,
    queries,
    kv_cache,
    w_kv,
    store_a,
    store_b,
    lengths,
    arrival_from,
    arrival_slot,
    resident_adapter,
    arrival_adapter,
    hot_holder,
    hot_dest,
):
    me = lax.axis_index("replica")
    replicas = lax.axis_size("replica")
    shards = lax.axis_size("tensor")
    resident, cap, kv_heads, head_pair = kv_cache.shape
    arrive = arrival_from.shape[1]
    slots = resident + arrive
    steps, features = hidden.shape[1:]
    heads, head_length = queries.shape[2:]
    slot_total = store_a.shape[0]
    rank = store_a.shape[2]
    spans = hot_holder.shape[0] // COPIES
    row_a, row_b = store_a.shape[1:], store_b.shape[1:]
    columns = store_b.shape[3]
    masks = tuple(range(1, replicas))
    me_table = jnp.reshape(me, (1,)).astype(jnp.int32)
    shard_table = jnp.reshape(lax.axis_index("tensor"), (1,)).astype(jnp.int32)
    from_table, slot_table, choice_table = arrival_from.T, arrival_slot.T, arrival_adapter.T
    dest_table = hot_dest.T

    used = slots * steps
    padded = -(-used // 8) * 8
    first = resident * steps
    block = padded - first

    *leaving, rows_a, rows_b, rows, asking = copy_call(
        functools.partial(collect_kernel, spans, slot_total, masks),
        (me_table, from_table, slot_table, hot_holder),
        (kv_cache, store_a, store_b, hidden),
        [kv_cache.shape[1:]] * len(masks)
        + [(COPIES,) + row_a, (COPIES,) + row_b, (padded, features), (block, features)],
        [
            (len(masks),) + kv_cache.shape[1:],
            (COPIES,) + row_a,
            (COPIES,) + row_b,
            hidden.shape,
            (padded, features),
        ],
    )
    sibling_a = partner(rows_a, 1)
    sibling_b = partner(rows_b, 1)
    other_rows = [partner(asking, mask) for mask in masks]
    came = [partner(array, mask) for array, mask in zip(leaving, masks)]
    around = [rows] + [shifted(rows, step) for step in range(1, shards)]

    line_count = padded + len(masks) * block
    per_step = 2 if slot_total % 2 == 0 else 1
    partial, *sent = pl.pallas_call(
        functools.partial(project_kernel, spans, slot_total, resident, steps, masks),
        out_shape=[jax.ShapeDtypeStruct((padded, 2 * rank), jnp.float32)]
        + [jax.ShapeDtypeStruct((block, 2 * rank), jnp.float32)] * len(masks),
        grid=(slot_total // per_step,),
        in_specs=[SMEM] * 5
        + [pl.BlockSpec((padded, features), lambda i: (0, 0))]
        + [pl.BlockSpec((block, features), lambda i: (0, 0))] * len(masks)
        + [pl.BlockSpec((1, per_step * 2 * rank, features), lambda i: (i, 0, 0))],
        out_specs=[pl.BlockSpec((padded, 2 * rank), lambda i: (0, 0))]
        + [pl.BlockSpec((block, 2 * rank), lambda i: (0, 0))] * len(masks),
        scratch_shapes=[
            pltpu.VMEM((line_count, features), hidden.dtype),
            pltpu.VMEM((line_count, 2 * rank), jnp.int32),
            pltpu.VMEM((line_count, 2 * rank), jnp.float32),
        ],
        name="project",
    )(
        me_table,
        resident_adapter,
        choice_table,
        hot_holder,
        dest_table,
        rows,
        *other_rows,
        store_a.reshape(slot_total // per_step, per_step * 2 * rank, features),
    )
    returned = [partner(array, mask) for array, mask in zip(sent, masks)]
    unit_shape = row_a[1:]
    unit_total = 2 * COPIES
    across_b, *units, extra = copy_call(
        functools.partial(pack_kernel, spans, slot_total),
        (me_table, hot_holder, dest_table),
        (store_a, store_b, sibling_a, sibling_b),
        [(COPIES,) + row_b] + [(size,) + unit_shape for _, size in ALWAYS + AT_NEED],
        [(COPIES,) + row_b, (unit_total,) + unit_shape],
        [(1,)],
    )
    across_b = partner(across_b, 2)
    got = []
    for array in units[: len(ALWAYS)]:
        got.append(partner(array, 2))

    full, partial = pl.pallas_call(
        functools.partial(gather_kernel, shards),
        out_shape=[
            jax.ShapeDtypeStruct((padded, shards * features), hidden.dtype),
            jax.ShapeDtypeStruct(partial.shape, jnp.float32),
        ],
        in_specs=[SMEM] + [VMEM] * (shards + 1 + len(masks)),
        out_specs=[VMEM] * 2,
        name="gather",
    )(shard_table, *around, partial, *returned)
    parts = [partial] + [shifted(partial, step) for step in range(1, shards)]
    base = jnp.einsum("md,dgc->gmc", full, w_kv, preferred_element_type=jnp.float32)

    attn_out, new_kv, arrived, installed_b = pl.pallas_call(
        functools.partial(attend_kernel, spans, masks, resident, steps, kv_heads, head_length),
        out_shape=[
            jax.ShapeDtypeStruct((slots, steps, heads * head_length), jnp.bfloat16),
            jax.ShapeDtypeStruct((slots, steps, kv_heads, head_pair), jnp.bfloat16),
            jax.ShapeDtypeStruct((arrive,) + kv_cache.shape[1:], jnp.bfloat16),
            jax.ShapeDtypeStruct((COPIES, 2 * rank, columns), jnp.bfloat16),
        ],
        in_specs=[SMEM] * 8 + [VMEM] * (shards + len(masks) + 6),
        out_specs=[VMEM] * 4,
        scratch_shapes=[
            pltpu.VMEM((2, padded * kv_heads, head_length), jnp.float32),
            pltpu.VMEM((slots * steps * heads, head_length), jnp.float32),
            pltpu.VMEM((slots * steps * heads, cap * kv_heads + 128), jnp.float32),
            pltpu.VMEM((slots * steps * heads, cap * kv_heads + 128), jnp.bfloat16),
        ],
        name="attend",
    )(
        me_table,
        lengths,
        from_table,
        slot_table,
        resident_adapter,
        choice_table,
        hot_holder,
        dest_table,
        *parts,
        *came,
        store_b.reshape(slot_total, 2 * rank, columns),
        sibling_b.reshape(COPIES, 2 * rank, columns),
        across_b.reshape(COPIES, 2 * rank, columns),
        base,
        queries.reshape(slots, steps * heads, head_length),
        kv_cache,
    )
    installed_b = installed_b.reshape((COPIES,) + row_b)

    tables = (me_table, hot_holder, dest_table)
    early = len(ALWAYS) - 1

    def finish(count):
        def branch(sibling_a, *arrays):
            swapped, arrays = list(arrays[:early]), arrays[early:]
            got, rest = list(arrays[: len(ALWAYS)]), arrays[len(ALWAYS) :]
            late = [partner(array, 2) for array in rest[:count]]
            other = swapped + [partner(array, 1) for array in got[early:]]
            (placed,) = copy_call(
                functools.partial(place_kernel, spans, slot_total, ALWAYS),
                tables,
                (sibling_a, *got, *other),
                [(COPIES,) + row_a],
                [(unit_total,) + unit_shape],
            )
            if not count:
                return placed
            other = [partner(array, 1) for array in late]
            (placed,) = copy_call(
                functools.partial(place_kernel, spans, slot_total, AT_NEED[:count]),
                tables,
                (placed, *late, *other),
                [(COPIES,) + row_a],
                [(unit_total,) + unit_shape],
                aliases={len(tables): 0},
            )
            return placed

        return branch

    branches = [finish(count) for count in range(len(AT_NEED) + 1)]
    swapped = [partner(array, 1) for array in got[:early]]
    *rest, attn_out = lax.optimization_barrier((*units[len(ALWAYS) :], attn_out))
    installed_a = lax.switch(extra[0], branches, sibling_a, *swapped, *got, *rest)
    return (attn_out, new_kv, arrived, installed_a, installed_b)


def local(*args):
    fan = args[-1].shape[1]
    if lax.axis_size("replica") == 4 and fan == 1:
        return pairs_layer(*args)
    return local_general(*args)


def solution(mesh):
    in_specs = (
        P(("parts", "replica"), None, "tensor"),
        P(("parts", "replica"), None, "tensor", None),
        P(("parts", "replica"), None, "tensor", None),
        P(None, "tensor", None),
        P(("parts", "replica"), None, None, "tensor"),
        P(("parts", "replica"), None, None, "tensor"),
        P("parts"),
        P("parts", None),
        P("parts", None),
        P("parts"),
        P("parts", None),
        P("parts"),
        P("parts", None),
    )
    out_specs = (
        P(("parts", "replica"), None, "tensor"),
        P(("parts", "replica"), None, "tensor", None),
        P(("parts", "replica"), None, "tensor", None),
        P(("parts", "replica"), None, None, "tensor"),
        P(("parts", "replica"), None, None, "tensor"),
    )
    return jax.shard_map(local, mesh=mesh, in_specs=in_specs, out_specs=out_specs, check_vma=False)
```
